32 devices in a mesh: fsdp: 4 (over x, core), ctx: 4 (over z), tp: 2 (over y).
Axes of the slice: x: 2, y: 2, z: 4, core: 2. Of those that a mesh axis runs over, the one named last changes fastest.
Arguments:
- inputs: bfloat16 [12, 1024, 768], P('fsdp', 'ctx'), may hold values from -6 to 6
- segments: int32 [12, 1024], P('fsdp', 'ctx'), may hold values from 0 to 17, as said below
- cotangent: bfloat16 [12, 1024, 768], P('fsdp', 'ctx'), may hold values from -6 to 6
- query_weight: bfloat16 [768, 768], P(('fsdp', 'ctx'), 'tp'), may hold values from -0.21875 to 0.21875
- key_weight: bfloat16 [768, 768], P(('fsdp', 'ctx'), 'tp'), may hold values from -0.21875 to 0.21875
- value_weight: bfloat16 [768, 768], P(('fsdp', 'ctx'), 'tp'), may hold values from -0.21875 to 0.21875
- output_weight: bfloat16 [768, 768], P('tp', ('fsdp', 'ctx')), may hold values from -0.875 to 0.875
- up_weight: bfloat16 [768, 3072], P(('fsdp', 'ctx'), 'tp'), may hold values from -0.21875 to 0.21875
- down_weight: bfloat16 [3072, 768], P('tp', ('fsdp', 'ctx')), may hold values from -0.109375 to 0.109375
- query_bias: bfloat16 [768], P(('tp', 'fsdp', 'ctx')), may hold values from -3 to 3
- value_bias: bfloat16 [768], P(('tp', 'fsdp', 'ctx')), may hold values from -3 to 3
- up_bias: bfloat16 [3072], P(('tp', 'fsdp', 'ctx')), may hold values from -3 to 3
- output_bias: bfloat16 [768], P(('fsdp', 'ctx')), may hold values from -3 to 3
- down_bias: bfloat16 [768], P(('fsdp', 'ctx')), may hold values from -3 to 3
- first_gain: bfloat16 [768], P(('fsdp', 'ctx')), may hold values from 0.25 to 1.75
- first_shift: bfloat16 [768], P(('fsdp', 'ctx')), may hold values from -3 to 3
- second_gain: bfloat16 [768], P(('fsdp', 'ctx')), may hold values from 0.25 to 1.75
- second_shift: bfloat16 [768], P(('fsdp', 'ctx')), may hold values from -3 to 3
Outputs:
- output: bfloat16 [12, 1024, 768], P('fsdp', 'ctx')
- input_grad: float32 [12, 1024, 768], P('fsdp', 'ctx')
- query_weight_grad: float32 [768, 768], P(('fsdp', 'ctx'), 'tp')
- key_weight_grad: float32 [768, 768], P(('fsdp', 'ctx'), 'tp')
- value_weight_grad: float32 [768, 768], P(('fsdp', 'ctx'), 'tp')
- output_weight_grad: float32 [768, 768], P('tp', ('fsdp', 'ctx'))
- up_weight_grad: float32 [768, 3072], P(('fsdp', 'ctx'), 'tp')
- down_weight_grad: float32 [3072, 768], P('tp', ('fsdp', 'ctx'))
- query_bias_grad: float32 [768], P(('tp', 'fsdp', 'ctx'))
- value_bias_grad: float32 [768], P(('tp', 'fsdp', 'ctx'))
- up_bias_grad: float32 [3072], P(('tp', 'fsdp', 'ctx'))
- output_bias_grad: float32 [768], P(('fsdp', 'ctx'))
- down_bias_grad: float32 [768], P(('fsdp', 'ctx'))
- first_gain_grad: float32 [768], P(('fsdp', 'ctx'))
- first_shift_grad: float32 [768], P(('fsdp', 'ctx'))
- second_gain_grad: float32 [768], P(('fsdp', 'ctx'))
- second_shift_grad: float32 [768], P(('fsdp', 'ctx'))
The draws below stay inside these ranges and needn't reach their ends.
Inputs may be any that keep to these rules, and one draw needn't show every extreme that they name: `segments`: within each sequence the numbers start at 0 and rise by one where a document begins; every document except a sequence's last has 60 to 800 tokens, the last has at most 800; the first document of the first sequence has exactly 800 tokens, and every document of the last sequence except its last has exactly 60 tokens.
All inputs are finite; a program needn't handle non-finite values.
Results may differ from the reference program's by a relative error of at most 0.015.
Values may be sent and summed in bfloat16 or wider, within the bound.
A program may use at most 128 MiB of HBM per device.

```python
import math
import jax
import jax.numpy as jnp
from jax import lax

D = 768
HEADS = 12
HEAD = 64
FF = 3072
LEN = 1024
DOC_LEAST = 60
DOC_MOST = 800
SEQS = 12


def draw_segments(key, part):
    documents = LEN // DOC_LEAST + 1
    lengths = jax.random.randint(key, (SEQS, documents), DOC_LEAST, DOC_MOST + 1)
    lengths = lengths.at[SEQS - 1].set(DOC_LEAST)
    lengths = lengths.at[0, 0].set(DOC_MOST)
    ends = jnp.cumsum(lengths, axis=1)
    places = jnp.arange(LEN, dtype=jnp.int32)
    passed = (ends[:, None, :] <= places[None, :, None]).astype(jnp.int32)
    return jnp.sum(passed, axis=2).astype(jnp.int32)


def block_levels(rng, extent, cuts, low, top_value):
    def one(axis_at, blocks):
        heights = jax.random.uniform(jax.random.fold_in(jax.random.fold_in(rng, 6), axis_at), (blocks,), jnp.float32, low / len(cuts), top_value / len(cuts))
        return jnp.repeat(jnp.exp(heights), extent[axis_at] // blocks).reshape((-1,) + (1,) * (len(extent) - axis_at - 1))

    loudness = one(*cuts[0])
    for cut in cuts[1:]:
        loudness = loudness * one(*cut)
    return loudness


def gaussian(stream_key, dims, spread, bound, cuts=(), kind=jnp.bfloat16):
    array = spread * jax.random.normal(stream_key, dims, jnp.float32)
    if cuts:
        array = array * block_levels(stream_key, dims, cuts, -0.22, 0.18)
    return jnp.clip(array, -bound, bound).astype(kind)


def setup_inputs(seed: int = 0) -> dict:
    streams_of = jax.random.split(jax.random.key(seed), 19)
    return {
        "inputs": gaussian(streams_of[0], (SEQS, LEN, D), 1.0, 6.0, ((0, 4), (1, 4))),
        "segments": draw_segments(jax.random.fold_in(streams_of[18], 71), 0),
        "cotangent": gaussian(streams_of[2], (SEQS, LEN, D), 1.0, 6.0, ((0, 4), (1, 4))),
        "query_weight": gaussian(streams_of[3], (D, D), D ** -0.5, 0.21875, ((0, 16), (1, 2))),
        "key_weight": gaussian(streams_of[4], (D, D), D ** -0.5, 0.21875, ((0, 16), (1, 2))),
        "value_weight": gaussian(streams_of[5], (D, D), D ** -0.5, 0.21875, ((0, 16), (1, 2))),
        "output_weight": gaussian(streams_of[6], (D, D), (D // 16) ** -0.5, 0.875, ((0, 2), (1, 16))),
        "up_weight": gaussian(streams_of[7], (D, FF), D ** -0.5, 0.21875, ((0, 16), (1, 2))),
        "down_weight": gaussian(streams_of[8], (FF, D), FF ** -0.5, 0.109375, ((0, 2), (1, 16))),
        "query_bias": gaussian(streams_of[9], (D,), 0.5, 3.0, ((0, 32),)),
        "value_bias": gaussian(streams_of[10], (D,), 0.5, 3.0, ((0, 32),)),
        "up_bias": gaussian(streams_of[11], (FF,), 0.5, 3.0, ((0, 32),)),
        "output_bias": gaussian(streams_of[12], (D,), 0.5, 3.0, ((0, 16),)),
        "down_bias": gaussian(streams_of[13], (D,), 0.5, 3.0, ((0, 16),)),
        "first_gain": jnp.clip(1.0 + 0.15 * jax.random.normal(streams_of[14], (D,), jnp.float32), 0.25, 1.75).astype(jnp.bfloat16),
        "first_shift": gaussian(streams_of[15], (D,), 0.5, 3.0, ((0, 16),)),
        "second_gain": jnp.clip(1.0 + 0.15 * jax.random.normal(streams_of[16], (D,), jnp.float32), 0.25, 1.75).astype(jnp.bfloat16),
        "second_shift": gaussian(streams_of[17], (D,), 0.5, 3.0, ((0, 16),)),
    }


@jax.custom_vjp
def low(v):
    return lax.optimization_barrier(v.astype(jnp.bfloat16)).astype(jnp.float32)

@jax.custom_vjp
def low_back(v):
    return v

def low_keep(v):
    return (low(v), None)

def low_pass(kept, grad):
    return (grad,)

def back_keep(v):
    return (v, None)

def back_low(kept, grad):
    return (low(grad),)
low.defvjp(low_keep, low_pass)
low_back.defvjp(back_keep, back_low)
norm_eps = 1e-12
masked_score = -1000000000.0
highest = lax.Precision.HIGHEST

def normalize(value, gain, shift):
    centre = lax.optimization_barrier(jnp.mean(value, axis=-1, keepdims=True))
    centred = value - centre
    factor = lax.rsqrt(lax.optimization_barrier(jnp.mean(centred * centred, axis=-1, keepdims=True)) + norm_eps)
    return centred * factor * gain + shift

def layer_forward(params, block_in, block_segs):
    query_weight, key_weight, value_weight, output_weight, up_weight, down_weight, query_bias, value_bias, up_bias, output_bias, down_bias, first_gain, first_shift, second_gain, second_shift = params
    group = block_in.shape[0]
    flat = block_in.reshape(group * LEN, D)
    query_rows = low_back(low(jnp.dot(flat, query_weight, precision=highest) + query_bias))
    key_rows = low_back(low(jnp.dot(flat, key_weight, precision=highest)))
    value_rows = low_back(low(jnp.dot(flat, value_weight, precision=highest) + value_bias))
    shape = (group, LEN, HEADS, HEAD)
    raw = jnp.einsum('sqhd,skhd->shqk', query_rows.reshape(shape), key_rows.reshape(shape), precision=highest)
    scores = low_back(raw * HEAD ** (-0.5))
    same = block_segs[:, :, None] == block_segs[:, None, :]
    scores = jnp.where(same[:, None], scores, masked_score)
    peak = lax.optimization_barrier(jnp.max(scores, axis=-1, keepdims=True))
    expd = jnp.exp(scores - peak)
    probs = expd / lax.optimization_barrier(jnp.sum(expd, axis=-1, keepdims=True))
    attended = jnp.einsum('shqk,skhd->sqhd', low(probs), value_rows.reshape(shape), precision=highest)
    attended = low_back(low(attended.reshape(group * LEN, D)))
    branch = low_back(jnp.dot(attended, output_weight, precision=highest) + output_bias)
    mixed = normalize(flat + branch, first_gain, first_shift)
    hidden = low_back(jnp.dot(low(mixed), up_weight, precision=highest) + up_bias)
    active = low(jax.nn.gelu(hidden, approximate=False))
    ffn = low_back(jnp.dot(active, down_weight, precision=highest) + down_bias)
    return normalize(mixed + ffn, second_gain, second_shift).reshape(block_in.shape)

def reference(inputs, segments, cotangent, query_weight, key_weight, value_weight, output_weight, up_weight, down_weight, query_bias, value_bias, up_bias, output_bias, down_bias, first_gain, first_shift, second_gain, second_shift):
    params = tuple((item.astype(jnp.float32) for item in (query_weight, key_weight, value_weight, output_weight, up_weight, down_weight, query_bias, value_bias, up_bias, output_bias, down_bias, first_gain, first_shift, second_gain, second_shift)))
    group = math.gcd(SEQS, max(1, 4096 // LEN))
    blocks = SEQS // group
    block_inputs = inputs.astype(jnp.float32).reshape(blocks, group, LEN, D)
    block_segments = segments.reshape(blocks, group, LEN)
    block_cotangents = cotangent.astype(jnp.float32).reshape(blocks, group, LEN, D)

    def one_block(totals, pieces):
        block_in, block_segs, block_cot = pieces

        def applied(weights, values):
            return layer_forward(weights, values, block_segs)
        result, pull = jax.vjp(applied, params, block_in)
        weight_grads, input_piece = pull(block_cot)
        return (jax.tree.map(jnp.add, totals, weight_grads), (result.astype(jnp.bfloat16), input_piece))
    zeros = tuple((jnp.zeros(item.shape, jnp.float32) for item in params))
    totals, (results, input_pieces) = lax.scan(one_block, zeros, (block_inputs, block_segments, block_cotangents))
    grad_query, grad_key, grad_value, grad_output, grad_up, grad_down, grad_query_bias, grad_value_bias, grad_up_bias, grad_output_bias, grad_down_bias, grad_first_gain, grad_first_shift, grad_second_gain, grad_second_shift = totals
    return (results.reshape(SEQS, LEN, D), input_pieces.reshape(SEQS, LEN, D), grad_query, grad_key, grad_value, grad_output, grad_up, grad_down, grad_query_bias, grad_value_bias, grad_up_bias, grad_output_bias, grad_down_bias, grad_first_gain, grad_first_shift, grad_second_gain, grad_second_shift)
```

```python
import functools
import jax
import jax.numpy as jnp
from jax import lax
from jax.sharding import PartitionSpec as P
from jax.experimental import pallas as pl
from jax.experimental.pallas import tpu as pltpu

MESH = pl.DeviceIdType.MESH
ANY = pl.BlockSpec(memory_space=pl.ANY)
VM = pl.BlockSpec(memory_space=pltpu.VMEM)


class Place:
    def __init__(self, sizes):
        self.F, self.C, self.T = sizes
        self.X = self.F // 2
        f = lax.axis_index("fsdp")
        self.x = f // 2
        self.c = lax.rem(f, 2)
        self.z = lax.axis_index("ctx")
        self.y = lax.axis_index("tp")

    def dev(self, x=None, c=None, z=None, y=None):
        x = self.x if x is None else x
        c = self.c if c is None else c
        return (2 * x + c, self.z if z is None else z, self.y if y is None else y)

    def z_off(self, d):
        return lax.rem(self.z + d + self.C, self.C)

    def x_off(self, d):
        return lax.rem(self.x + d + self.X, self.X)

    def greet(self, chip_wide):
        bar = pltpu.get_barrier_semaphore()
        devs = [self.dev(c=1 - self.c), self.dev(y=1 - self.y)]
        devs += [self.dev(x=self.x_off(d)) for d in range(1, self.X)]
        for d in range(1, self.C):
            devs.append(self.dev(z=self.z_off(d)))
            if chip_wide:
                devs.append(self.dev(z=self.z_off(d), c=1 - self.c))
        for d in devs:
            pl.semaphore_signal(bar, inc=1, device_id=d, device_id_type=MESH)
        pl.semaphore_wait(bar, len(devs))


class Sends:
    def __init__(self, sems):
        self.sems, self.n, self.waits = sems, 0, []

    def go(self, src, dst, recv, dev, cond=None):
        cp = pltpu.make_async_remote_copy(
            src_ref=src, dst_ref=dst, send_sem=self.sems.at[self.n], recv_sem=recv,
            device_id=dev, device_id_type=MESH)
        self.n += 1
        cp.start()
        self.waits.append(cp)
        return cp

    def finish(self):
        for cp in self.waits:
            cp.wait_send()
        self.waits = []


def arrived(dst, recv, pl_):
    pltpu.make_async_remote_copy(
        src_ref=dst, dst_ref=dst, send_sem=recv, recv_sem=recv,
        device_id=pl_.dev(c=1 - pl_.c), device_id_type=MESH).wait_recv()


def gather_events(me, own, full, sends, recv, lsem):
    C, X = me.C, me.X
    sem = lambda t, x, c, z: recv.at[((t * X + x) * 2 + c) * C + z]
    slot = lambda t, x, c, z: full.at[t, x, c, z]

    def push(src, at, dev):
        sends.go(src, slot(*at), sem(*at), dev)

    def wait(at):
        arrived(slot(*at), sem(*at), me)

    core, side = me.dev(c=1 - me.c), me.dev(y=1 - me.y)
    xs = [(me.x_off(d), me.dev(x=me.x_off(d))) for d in range(1, X)]
    half = C // 2
    local = pltpu.make_async_copy(own, slot(me.y, me.x, me.c, me.z), lsem)
    events = []

    def first():
        at = (me.y, me.x, me.c, me.z)
        for d in range(1, C):
            push(own, at, me.dev(z=me.z_off(d)))
        for _, dev in xs:
            push(own, at, dev)
        push(own, at, side)
        push(own, at, core)
        local.start()

    events.append(first)
    for d in range(1, C):
        def along(d=d):
            at = (me.y, me.x, me.c, me.z_off(-d))
            wait(at)
            for _, dev in xs:
                push(slot(*at), at, dev)
            push(slot(*at), at, side)
            push(slot(*at), at, core)
        events.append(along)
    for j in range(C):
        def across(j=j):
            zj = me.z_off(-j)
            at = (1 - me.y, me.x, me.c, zj)
            wait(at)
            if j < half:
                for _, dev in xs:
                    push(slot(*at), at, dev)
            push(slot(*at), at, core)
            for xo, _ in xs:
                at = (me.y, xo, me.c, zj)
                wait(at)
                if j >= half:
                    push(slot(*at), at, side)
                push(slot(*at), at, core)
        events.append(across)
    for j in range(C):
        def corner(j=j):
            zj = me.z_off(-j)
            for xo, _ in xs:
                at = (1 - me.y, xo, me.c, zj)
                wait(at)
                push(slot(*at), at, core)
        events.append(corner)

    def last():
        for t in range(me.T):
            for xx in range(X):
                for zz in range(C):
                    wait((t, xx, 1 - me.c, zz))
        local.wait()

    events.append(last)
    return events


def gather_count(sizes):
    F, C, T = sizes
    X = F // 2
    return (C - 1) + X + 1 + (C - 1) * (X + 1) + (C // 2) * (X - 1) + C * X + (C - C // 2) * (X - 1) + C * (X - 1)


def home(me, seqs, y):
    lo = y * (me.C - seqs)
    return lo


def token_events(me, pieces, seqs, sends):
    C = me.C
    half = C // 2
    lo = home(me, seqs, me.y)
    busy = (me.z >= lo) & (me.z < lo + seqs)
    return lo, busy


class Tokens:
    def __init__(self, me, seqs):
        self.me, self.S = me, seqs
        self.half = me.C // 2
        self.lo = me.y * (me.C - seqs)
        self.busy = (me.z >= self.lo) & (me.z < self.lo + seqs)
        self.owner = me.c == me.y

    def out(self, src, dst, full, ssem, rsem, lsem):
        me, half = self.me, self.half
        k = me.z // half
        at = me.z if full else lax.rem(me.z, half)

        @pl.when(self.owner)
        def _():
            for s in range(self.S):
                here = (self.lo + s == me.z) & (k == me.c)

                @pl.when(here)
                def _():
                    pltpu.make_async_copy(src.at[s], dst.at[at], lsem).start()

                @pl.when(jnp.logical_not(here))
                def _():
                    pltpu.make_async_remote_copy(
                        src_ref=src.at[s], dst_ref=dst.at[at], send_sem=ssem.at[s],
                        recv_sem=rsem.at[lax.rem(me.z, half)],
                        device_id=me.dev(c=k, z=self.lo + s), device_id_type=MESH).start()

    def out_done(self, src, dst, full, ssem, rsem, lsem):
        me, half = self.me, self.half

        @pl.when(self.busy)
        def _():
            for i in range(half):
                zq = me.c * half + i
                at = zq if full else i
                here = (zq == me.z) & (me.c == me.y)

                @pl.when(here)
                def _():
                    pltpu.make_async_copy(src.at[0], dst.at[at], lsem).wait()

                @pl.when(jnp.logical_not(here))
                def _():
                    arrived(dst.at[at], rsem.at[i], me)

                if full:
                    pltpu.make_async_remote_copy(
                        src_ref=dst.at[at], dst_ref=dst.at[at], send_sem=ssem.at[self.S + i],
                        recv_sem=rsem.at[half + i], device_id=me.dev(c=1 - me.c),
                        device_id_type=MESH).start()

    def out_end(self, src, dst, full, ssem, rsem, lsem):
        me, half = self.me, self.half
        k = me.z // half

        @pl.when(self.owner)
        def _():
            for s in range(self.S):
                here = (self.lo + s == me.z) & (k == me.c)

                @pl.when(jnp.logical_not(here))
                def _():
                    pltpu.make_async_remote_copy(
                        src_ref=src.at[s], dst_ref=dst.at[0], send_sem=ssem.at[s],
                        recv_sem=rsem.at[0], device_id=me.dev(c=1 - me.c),
                        device_id_type=MESH).wait_send()

        if full:
            @pl.when(self.busy)
            def _():
                for i in range(half):
                    zq = (1 - me.c) * half + i
                    arrived(dst.at[zq], rsem.at[half + i], me)
                    pltpu.make_async_remote_copy(
                        src_ref=dst.at[0], dst_ref=dst.at[0], send_sem=ssem.at[self.S + i],
                        recv_sem=rsem.at[0], device_id=me.dev(c=1 - me.c),
                        device_id_type=MESH).wait_send()

    def back(self, src, dst, ssem, rsem, lsem):
        me, half = self.me, self.half

        @pl.when(self.busy)
        def _():
            for i in range(half):
                zq = me.c * half + i
                here = (zq == me.z) & (me.c == me.y)
                at = me.z - self.lo

                @pl.when(here)
                def _():
                    pltpu.make_async_copy(src.at[i], dst.at[at], lsem).start()

                @pl.when(jnp.logical_not(here))
                def _():
                    pltpu.make_async_remote_copy(
                        src_ref=src.at[i], dst_ref=dst.at[at], send_sem=ssem.at[i],
                        recv_sem=rsem.at[at], device_id=me.dev(c=me.y, z=zq),
                        device_id_type=MESH).start()

    def back_pass(self, src, dst, ssem, rsem, lsem):
        me, half = self.me, self.half
        k = me.z // half

        @pl.when(self.owner)
        def _():
            for s in range(self.S):
                here = (self.lo + s == me.z) & (k == me.c)

                @pl.when(here)
                def _():
                    pltpu.make_async_copy(src.at[0], dst.at[s], lsem).wait()

                @pl.when(jnp.logical_not(here))
                def _():
                    arrived(dst.at[s], rsem.at[s], me)

                pltpu.make_async_remote_copy(
                    src_ref=dst.at[s], dst_ref=dst.at[s], send_sem=ssem.at[half + s],
                    recv_sem=rsem.at[s], device_id=me.dev(y=1 - me.y),
                    device_id_type=MESH).start()

    def back_end(self, src, dst, ssem, rsem, lsem):
        me, half = self.me, self.half

        @pl.when(self.busy)
        def _():
            for i in range(half):
                zq = me.c * half + i
                here = (zq == me.z) & (me.c == me.y)

                @pl.when(jnp.logical_not(here))
                def _():
                    pltpu.make_async_remote_copy(
                        src_ref=src.at[i], dst_ref=dst.at[0], send_sem=ssem.at[i],
                        recv_sem=rsem.at[0], device_id=me.dev(c=1 - me.c),
                        device_id_type=MESH).wait_send()

        @pl.when(self.owner)
        def _():
            for s in range(self.S):
                pltpu.make_async_remote_copy(
                    src_ref=dst.at[s], dst_ref=dst.at[s], send_sem=ssem.at[half + s],
                    recv_sem=rsem.at[s], device_id=me.dev(y=1 - me.y),
                    device_id_type=MESH).wait_send()

        @pl.when(jnp.logical_not(self.owner))
        def _():
            for s in range(self.S):
                arrived(dst.at[s], rsem.at[s], me)


def reduce_events(me, grads, split, bufs, out, sends, recv, lsem):
    acc, rc, xd, yd, xr, yr, zr = bufs
    C, X = me.C, me.X
    half = C // 2
    core, side = me.dev(c=1 - me.c), me.dev(y=1 - me.y)
    s_core = lambda t, x: recv.at[t * X + x]
    base = me.T * X
    s_xd = lambda d, j: recv.at[base + (d - 1) * C + j]
    base2 = base + (X - 1) * C
    s_xr = lambda d, j: recv.at[base2 + (d - 1) * C + j]
    base3 = base2 + (X - 1) * C
    s_yr = lambda j: recv.at[base3 + j]
    s_zr = lambda j: recv.at[base3 + C + j]

    quads = ([(1 - me.y, me.x_off(d)) for d in range(1, X)] + [(1 - me.y, me.x)]
             + [(me.y, me.x_off(d)) for d in range(1, X)] + [(me.y, me.x)])
    locals_ = []

    def first():
        if split:
            for n, x in enumerate([me.x_off(d) for d in range(1, X)] + [me.x]):
                sends.go(grads.at[x, 1 - me.c], acc.at[me.c, x], s_core(me.c, x), core)
                cp = pltpu.make_async_copy(grads.at[x, me.c], acc.at[me.c, x], lsem.at[n])
                cp.start()
                locals_.append(cp)
        else:
            for n, (t, x) in enumerate(quads):
                sends.go(grads.at[t, x, 1 - me.c], rc.at[t, x], s_core(t, x), core)
                cp = pltpu.make_async_copy(grads.at[t, x, me.c], acc.at[t, x], lsem.at[n])
                cp.start()
                locals_.append(cp)

    def add(a, b):
        a[...] = a[...] + b[...]

    def ready(n):
        t, x = quads[n]
        if split:
            if n == 0:
                for cp in locals_:
                    cp.wait()
                for xo in [me.x_off(d) for d in range(1, X)] + [me.x]:
                    arrived(acc.at[1 - me.c, xo], s_core(1 - me.c, xo), me)
            return
        locals_[n].wait()
        arrived(rc.at[t, x], s_core(t, x), me)

        def body(i, _):
            add(acc.at[t, x, i], rc.at[t, x, i])
            return 0
        lax.fori_loop(0, C, body, 0)

    events = [first]

    def corner():
        for d in range(1, X):
            ready(d - 1)
            t, x = quads[d - 1]
            for j in range(C):
                zj = me.z_off(-j)
                if j < half:
                    sends.go(acc.at[t, x, zj], xd.at[d - 1, j], s_xd(d, j), me.dev(x=x))
                else:
                    sends.go(acc.at[t, x, zj], yd.at[d - 1, j - half], s_xd(d, j), side)
    events.append(corner)

    def to_side():
        ready(X - 1)
        t, x = 1 - me.y, me.x
        for j in reversed(range(C)):
            zj = me.z_off(-j)
            if j < half:
                for d in range(1, X):
                    arrived(xd.at[d - 1, j], s_xd(d, j), me)
                    add(acc.at[t, x, zj], xd.at[d - 1, j])
            sends.go(acc.at[t, x, zj], yr.at[j], s_yr(j), side)
    events.append(to_side)

    def to_x():
        for d in range(1, X):
            ready(X - 1 + d)
            t, x = me.y, me.x_off(d)
            for j in range(C):
                zj = me.z_off(-j)
                if j >= half:
                    arrived(yd.at[d - 1, j - half], s_xd(d, j), me)
                    add(acc.at[t, x, zj], yd.at[d - 1, j - half])
                sends.go(acc.at[t, x, zj], xr.at[d - 1, j], s_xr(d, j), me.dev(x=x))
    events.append(to_x)

    def to_z():
        ready(2 * X - 1)
        t, x = me.y, me.x
        for j in list(range(1, C)) + [0]:
            zj = me.z_off(-j)
            arrived(yr.at[j], s_yr(j), me)
            add(acc.at[t, x, zj], yr.at[j])
            for d in range(1, X):
                arrived(xr.at[d - 1, j], s_xr(d, j), me)
                add(acc.at[t, x, zj], xr.at[d - 1, j])
            if j:
                sends.go(acc.at[t, x, zj], zr.at[j - 1], s_zr(j - 1), me.dev(z=zj))
    events.append(to_z)

    def last():
        total = acc[me.y, me.x, me.z].astype(jnp.float32)
        for j in range(1, C):
            arrived(zr.at[j - 1], s_zr(j - 1), me)
            total = total + zr[j - 1].astype(jnp.float32)
        out[...] = total
    events.append(last)
    return events


def reduce_scratch(sizes, r, n, split):
    F, C, T = sizes
    X = F // 2
    half = C // 2
    b = jnp.bfloat16
    v = pltpu.VMEM
    small = (1, 1, 1, 16, 128)
    return [v((T, X, C, r, n), b), v(small if split else (T, X, C, r, n), b), v((max(X - 1, 1), half, r, n), b),
            v((max(X - 1, 1), C - half, r, n), b), v((max(X - 1, 1), C, r, n), b), v((C, r, n), b), v((C - 1, r, n), b)]


def reduce_sems(sizes):
    F, C, T = sizes
    X = F // 2
    return T * X + 2 * (X - 1) * C + 2 * C


def reduce_count(sizes, split):
    F, C, T = sizes
    X = F // 2
    return (X if split else T * X) + 2 * (X - 1) * C + C + C - 1


def total_events(me, own, bufs, out, sends, recv):
    C, X = me.C, me.X
    acc, got = bufs
    groups = [[me.dev(c=1 - me.c)], [me.dev(x=me.x_off(d)) for d in range(1, X)],
              [me.dev(y=1 - me.y)], [me.dev(z=me.z_off(d)) for d in range(1, C)]]
    bases = [sum(len(g) for g in groups[:i]) for i in range(len(groups))]

    def start(gi):
        for i, dev in enumerate(groups[gi]):
            sends.go(acc.at[gi], got.at[bases[gi] + i], recv.at[bases[gi] + i], dev)

    def first():
        acc[0] = own[...]
        start(0)

    events = [first]
    for gi in range(len(groups)):
        def step(gi=gi):
            total = acc[gi]
            for i in range(len(groups[gi])):
                arrived(got.at[bases[gi] + i], recv.at[bases[gi] + i], me)
                total = total + got[bases[gi] + i]
            if gi + 1 < len(groups):
                acc[gi + 1] = total
                start(gi + 1)
            else:
                out[...] = total
        events.append(step)
    return events


def total_count(sizes):
    F, C, T = sizes
    return 1 + F // 2 - 1 + 1 + C - 1

HEAD = 64
PAIR = 2 * HEAD
SCALE = HEAD ** (-0.5)
norm_eps = 1e-12
masked_score = -1000000000.0


def nt(a, b):
    return lax.dot_general(a, b, (((1,), (1,)), ((), ())), preferred_element_type=jnp.float32)


def nn(a, b):
    return lax.dot_general(a, b, (((1,), (0,)), ((), ())), preferred_element_type=jnp.float32)


def spread_segments(seg_ref, wide):
    C, _, R = seg_ref.shape
    for i in range(C):
        for j in range(0, R, 128):
            row = jnp.broadcast_to(seg_ref[i, 0:1, j:j + 128], (128, 128))
            wide[i * R + j:i * R + j + 128, :] = row.T


def lanes_of(h, like):
    lane = lax.broadcasted_iota(jnp.int32, like.shape, like.ndim - 1)
    return jnp.where(lane // HEAD == h, like, jnp.zeros_like(like))


def two_lanes(wide):
    return jnp.concatenate([wide, wide], axis=1)


def attend_block(q, k, v_t, seg_q, seg_k):
    same = seg_k == seg_q
    outs, logs = [], []
    for h in range(2):
        s = nt(k, lanes_of(h, q) * jnp.bfloat16(SCALE))
        s = jnp.where(same, s, masked_score)
        peak = jnp.max(s, axis=0, keepdims=True)
        e = jnp.exp(s - peak)
        total = jnp.sum(e, axis=0, keepdims=True)
        o = nn(v_t, e.astype(jnp.bfloat16))
        outs.append(o[h * HEAD:(h + 1) * HEAD] * (1.0 / total))
        logs.append(peak + jnp.log(total))
    return jnp.concatenate(outs, axis=0), logs


def attend_kernel(q_ref, k_ref, v_ref, seg_ref, o_ref, lse_ref, wide, v_t):
    i = pl.program_id(1)

    @pl.when((pl.program_id(0) == 0) & (i == 0))
    def _():
        spread_segments(seg_ref, wide)

    @pl.when(i == 0)
    def _():
        v_t[...] = v_ref[...].astype(jnp.float32).T.astype(jnp.bfloat16)

    seg_q = seg_ref[i, 0:1, :]
    o, logs = attend_block(q_ref[...], k_ref[...], v_t[...], seg_q, two_lanes(wide[...]))
    o_ref[...] = o.T.astype(jnp.bfloat16)
    lse_ref[0] = jnp.concatenate(logs + [jnp.zeros((6, logs[0].shape[1]), jnp.float32)], axis=0)


def attend(q, k, v, seg):
    L, W = q.shape
    C, _, R = seg.shape
    n = W // PAIR
    return pl.pallas_call(
        attend_kernel,
        grid=(n, C),
        in_specs=[pl.BlockSpec((R, PAIR), lambda p, i: (i, p)),
                  pl.BlockSpec((L, PAIR), lambda p, i: (0, p)),
                  pl.BlockSpec((L, PAIR), lambda p, i: (0, p)),
                  pl.BlockSpec((C, 8, R), lambda p, i: (0, 0, 0))],
        out_specs=[pl.BlockSpec((R, PAIR), lambda p, i: (i, p)),
                   pl.BlockSpec((1, 8, R), lambda p, i: (p, 0, i))],
        out_shape=[jax.ShapeDtypeStruct((L, W), jnp.bfloat16),
                   jax.ShapeDtypeStruct((n, 8, L), jnp.float32)],
        scratch_shapes=[pltpu.VMEM((L, 128), jnp.float32), pltpu.VMEM((PAIR, L), jnp.bfloat16)],
        compiler_params=pltpu.CompilerParams(vmem_limit_bytes=56 * 2**20),
    )(q, k, v, seg)


def attend_back_block(q, k, k_t, v, do, o, lse, seg_q, seg_k):
    same = seg_k == seg_q
    prod = (do.astype(jnp.float32) * o.astype(jnp.float32)).T
    dq, dk, dv = [], None, None
    for h in range(2):
        qh = lanes_of(h, q) * jnp.bfloat16(SCALE)
        doh = lanes_of(h, do)
        s = nt(k, qh)
        p = jnp.exp(jnp.where(same, s, masked_score) - lse[h:h + 1])
        dp = nt(v, doh)
        inner = jnp.sum(prod[h * HEAD:(h + 1) * HEAD], axis=0, keepdims=True)
        ds = (p * (dp - inner)).astype(jnp.bfloat16)
        dv_h = nn(p.astype(jnp.bfloat16), doh)
        dk_h = nn(ds, qh)
        dv = dv_h if dv is None else dv + dv_h
        dk = dk_h if dk is None else dk + dk_h
        dq.append(nn(k_t, ds)[h * HEAD:(h + 1) * HEAD])
    return jnp.concatenate(dq, axis=0).T * SCALE, dk, dv


def attend_back_kernel(q_ref, k_ref, v_ref, do_ref, o_ref, lse_ref, seg_ref,
                       dq_ref, dk_ref, dv_ref, wide, k_t, dk_sum, dv_sum):
    i = pl.program_id(1)

    @pl.when((pl.program_id(0) == 0) & (i == 0))
    def _():
        spread_segments(seg_ref, wide)

    @pl.when(i == 0)
    def _():
        k_t[...] = k_ref[...].astype(jnp.float32).T.astype(jnp.bfloat16)

    seg_q = seg_ref[i, 0:1, :]
    dq, dk, dv = attend_back_block(q_ref[...], k_ref[...], k_t[...], v_ref[...], do_ref[...],
                                   o_ref[...], lse_ref[0], seg_q, two_lanes(wide[...]))
    dq_ref[...] = dq.astype(jnp.bfloat16)

    @pl.when(i == 0)
    def _():
        dk_sum[...] = dk
        dv_sum[...] = dv

    @pl.when(i > 0)
    def _():
        dk_sum[...] += dk
        dv_sum[...] += dv

    @pl.when(i == pl.num_programs(1) - 1)
    def _():
        dk_ref[...] = dk_sum[...].astype(jnp.bfloat16)
        dv_ref[...] = dv_sum[...].astype(jnp.bfloat16)


def attend_back(q, k, v, do, o, lse, seg):
    L, W = q.shape
    C, _, R = seg.shape
    n = W // PAIR
    row = pl.BlockSpec((R, PAIR), lambda p, i: (i, p))
    all_rows = pl.BlockSpec((L, PAIR), lambda p, i: (0, p))
    b = jax.ShapeDtypeStruct((L, W), jnp.bfloat16)
    return pl.pallas_call(
        attend_back_kernel,
        grid=(n, C),
        in_specs=[row, all_rows, all_rows, row, row,
                  pl.BlockSpec((1, 8, R), lambda p, i: (p, 0, i)),
                  pl.BlockSpec((C, 8, R), lambda p, i: (0, 0, 0))],
        out_specs=[row, all_rows, all_rows],
        out_shape=[b, b, b],
        scratch_shapes=[pltpu.VMEM((L, 128), jnp.float32), pltpu.VMEM((PAIR, L), jnp.bfloat16),
                        pltpu.VMEM((L, PAIR), jnp.float32), pltpu.VMEM((L, PAIR), jnp.float32)],
        compiler_params=pltpu.CompilerParams(vmem_limit_bytes=56 * 2**20),
    )(q, k, v, do, o, lse, seg)


def normalize(value, gain, shift):
    centre = jnp.mean(value, axis=-1, keepdims=True)
    centred = value - centre
    factor = lax.rsqrt(jnp.mean(centred * centred, axis=-1, keepdims=True) + norm_eps)
    unit = centred * factor
    return (unit * gain + shift, unit, factor)


def normalize_back(upstream, unit, factor, gain):
    along = upstream * gain
    inner = (along - jnp.mean(along, axis=-1, keepdims=True)
             - unit * jnp.mean(along * unit, axis=-1, keepdims=True))
    return inner * factor, jnp.sum(upstream * unit, axis=0), jnp.sum(upstream, axis=0)


def gelu_exact(value):
    return jax.nn.gelu(value, approximate=False)


VEC = 128


def gather_kernel(sizes, seqs, x_ref, cot_ref, seg_ref, w1_ref, w2_ref,
                  xf_ref, cf_ref, sf_ref, g1_ref, g2_ref,
                  zero, zseg, ssem, r1, r2, lsem, tss, trs, tls):
    me = Place(sizes)
    me.greet(True)
    sends = Sends(ssem)
    tok = Tokens(me, seqs)
    items = [(x_ref, xf_ref, True, tss.at[0], trs.at[0], tls.at[0]),
             (seg_ref, sf_ref, True, tss.at[1], trs.at[1], tls.at[1]),
             (cot_ref, cf_ref, False, tss.at[2], trs.at[2], tls.at[2])]
    idle = jnp.logical_not(tok.busy)

    @pl.when(idle)
    def _():
        zero[...] = jnp.zeros_like(zero)
        zseg[...] = jnp.zeros_like(zseg)
        for i in range(me.C):
            pltpu.make_async_copy(zero, xf_ref.at[i], tls.at[3 + i]).start()
            pltpu.make_async_copy(zseg, sf_ref.at[i], tls.at[3 + me.C + i]).start()
        for i in range(me.C // 2):
            pltpu.make_async_copy(zero, cf_ref.at[i], tls.at[3 + 2 * me.C + i]).start()

    for it in items[:2]:
        tok.out(*it)
    ev1 = gather_events(me, w1_ref, g1_ref, sends, r1, lsem.at[0])
    ev2 = gather_events(me, w2_ref, g2_ref, sends, r2, lsem.at[1])
    ev1[0]()
    for it in items[:2]:
        tok.out_done(*it)
    for e in ev1[1:]:
        e()
    ev2[0]()
    tok.out(*items[2])
    for e in ev2[1:]:
        e()
    tok.out_done(*items[2])
    for it in items:
        tok.out_end(*it)

    @pl.when(idle)
    def _():
        for i in range(me.C):
            pltpu.make_async_copy(zero, xf_ref.at[i], tls.at[3 + i]).wait()
            pltpu.make_async_copy(zseg, sf_ref.at[i], tls.at[3 + me.C + i]).wait()
        for i in range(me.C // 2):
            pltpu.make_async_copy(zero, cf_ref.at[i], tls.at[3 + 2 * me.C + i]).wait()

    sends.finish()


def gather_all(sizes, x, cot, seg, w1, w2):
    F, C, T = sizes
    S, R, D = x.shape
    X = F // 2
    b = jnp.bfloat16
    dma = pltpu.SemaphoreType.DMA
    r = w1.shape[0]
    return pl.pallas_call(
        functools.partial(gather_kernel, sizes, S),
        in_specs=[ANY] * 5,
        out_specs=[ANY] * 5,
        out_shape=[jax.ShapeDtypeStruct((C, R, D), b), jax.ShapeDtypeStruct((C // 2, R, D), b),
                   jax.ShapeDtypeStruct((C, 8, R), jnp.float32),
                   jax.ShapeDtypeStruct((T, X, 2, C, r, w1.shape[1]), b),
                   jax.ShapeDtypeStruct((T, X, 2, C, r, w2.shape[1]), b)],
        scratch_shapes=[pltpu.VMEM((R, D), b), pltpu.VMEM((8, R), jnp.float32),
                        dma((2 * gather_count(sizes),)), dma((T * F * C,)), dma((T * F * C,)), dma((2,)),
                        dma((3, S + C // 2)), dma((3, C)), dma((3 + 3 * C,))],
        compiler_params=pltpu.CompilerParams(collective_id=0, has_side_effects=True),
    )(x, cot, seg, w1, w2)


def scatter_kernel(sizes, seqs, res_ref, ing_ref, ga_ref, gb_ref, vec_ref,
                   res_out, ing_out, oa_ref, ob_ref, vec_out, *scr):
    ba, bb, (acc, got) = scr[:7], scr[7:14], scr[14:16]
    ssem, ra, rb, rv, la, lb, tss, trs, tls = scr[16:]
    me = Place(sizes)
    me.greet(True)
    sends = Sends(ssem)
    tok = Tokens(me, seqs)
    back = [(res_ref, res_out, tss.at[0], trs.at[0], tls.at[0]),
            (ing_ref, ing_out, tss.at[1], trs.at[1], tls.at[1])]
    ev = total_events(me, vec_ref, (acc, got), vec_out, sends, rv)
    ea = reduce_events(me, ga_ref, False, ba, oa_ref, sends, ra, la)
    eb = reduce_events(me, gb_ref, True, bb, ob_ref, sends, rb, lb)
    for b in back:
        tok.back(*b)
    ea[0]()
    eb[0]()
    ev[0]()
    for i in range(1, len(ea)):
        ea[i]()
        eb[i]()
        if i < len(ev):
            ev[i]()
    for e in ev[len(ea):]:
        e()
    for b in back:
        tok.back_pass(*b)
    for b in back:
        tok.back_end(*b)
    sends.finish()


def scatter_all(sizes, res, ing, ga, gb, vec, seqs):
    F, C, T = sizes
    X = F // 2
    half, R, D = res.shape
    r, na = ga.shape[-2:]
    nb = gb.shape[-1]
    b = jnp.bfloat16
    f = jnp.float32
    dma = pltpu.SemaphoreType.DMA
    steps = total_count(sizes)
    return pl.pallas_call(
        functools.partial(scatter_kernel, sizes, seqs),
        in_specs=[ANY] * 4 + [VM],
        out_specs=[ANY, ANY, VM, VM, VM],
        out_shape=[jax.ShapeDtypeStruct((seqs, R, D), b), jax.ShapeDtypeStruct((seqs, R, D), b),
                   jax.ShapeDtypeStruct((r, na), f), jax.ShapeDtypeStruct((r, nb), f),
                   jax.ShapeDtypeStruct(vec.shape, f)],
        scratch_shapes=reduce_scratch(sizes, r, na, False) + reduce_scratch(sizes, r, nb, True)
        + [pltpu.VMEM((4,) + vec.shape, f), pltpu.VMEM((steps,) + vec.shape, f),
           dma((reduce_count(sizes, False) + reduce_count(sizes, True) + steps,)),
           dma((reduce_sems(sizes),)), dma((reduce_sems(sizes),)), dma((steps,)),
           dma((T * X,)), dma((X,)), dma((2, half + seqs)), dma((2, seqs)), dma((2,))],
        compiler_params=pltpu.CompilerParams(collective_id=1, has_side_effects=True,
                                             vmem_limit_bytes=60 * 2**20),
    )(res, ing, ga, gb, vec)


def at(piece, index, total):
    return lax.dynamic_update_slice(jnp.zeros((total,), piece.dtype), piece, (index * piece.shape[0],))


def on_device(sizes, inputs, segments, cotangent, query_weight, key_weight, value_weight,
              output_weight, up_weight, down_weight, query_bias, value_bias, up_bias,
              output_bias, down_bias, first_gain, first_shift, second_gain, second_shift):
    F, C, T = sizes
    X = F // 2
    S, R, D = inputs.shape
    W = query_weight.shape[1]
    H = up_weight.shape[1]
    r = query_weight.shape[0]
    L = C * R
    half = L // 2
    f = lax.axis_index("fsdp")
    z = lax.axis_index("ctx")
    y = lax.axis_index("tp")
    c = lax.rem(f, 2)
    fz = f * C + z
    tfz = y * F * C + fz
    b16 = jnp.bfloat16
    f32 = jnp.float32

    w1 = jnp.concatenate([query_weight, key_weight, value_weight], axis=1)
    w2 = jnp.concatenate([output_weight.T, up_weight, down_weight.T], axis=1)
    flat_vec = jnp.concatenate(
        [at(query_bias, tfz, T * W), at(value_bias, tfz, T * W), at(up_bias, tfz, T * H)]
        + [jnp.where(y == 0, at(v, fz, D), jnp.zeros((D,), b16)) for v in
           (output_bias, down_bias, first_gain, first_shift, second_gain, second_shift)])
    nv = flat_vec.shape[0]
    cols = -(-nv // (r * VEC)) * VEC
    vec_block = jnp.pad(flat_vec, (0, r * cols - nv)).reshape(r, cols)
    w1 = jnp.concatenate([w1, vec_block], axis=1)
    seg = jnp.broadcast_to(segments.astype(f32)[:, None, :], (S, 8, R))
    xf, cf, sf, g1, g2 = gather_all(sizes, inputs, cotangent, seg, w1, w2)
    xf = xf.reshape(L, D)
    vecs = jnp.sum(g1[..., 3 * W:].astype(f32), axis=(0, 1, 2, 3)).reshape(-1)
    offs = [0]
    for n in [T * W, T * W, T * H] + [D] * 6:
        offs.append(offs[-1] + n)
    qb, vb, ub, ob, db, ga1, sh1, ga2, sh2 = [vecs[offs[i]:offs[i + 1]] for i in range(9)]
    mine1 = lax.dynamic_index_in_dim(g1, c, 0, False).reshape(D, -1)
    w2f = g2.reshape(T, D, -1)
    qkv = nn(xf, mine1[:, :3 * W])
    mineb = lambda v: lax.dynamic_slice(v, (c * W,), (W,))
    q = (qkv[:, :W] + mineb(qb)).astype(b16)
    k = qkv[:, W:2 * W].astype(b16)
    v = (qkv[:, 2 * W:] + mineb(vb)).astype(b16)
    att, lse = attend(q, k, v, sf)

    def swap(t):
        return lax.ppermute(t, "fsdp", [(i, i ^ 1) for i in range(F)])

    rows_of = lambda t, who: lax.dynamic_slice(t, (who * half, 0), (half, t.shape[1]))
    att_mine = rows_of(att, c)
    att_other = swap(rows_of(att, 1 - c))
    w_mine = lax.dynamic_index_in_dim(w2f, c, 0, False)
    w_other = lax.dynamic_index_in_dim(w2f, 1 - c, 0, False)
    branch = nt(att_mine, w_mine[:, :W]) + nt(att_other, w_other[:, :W]) + ob
    x_mine = rows_of(xf, c)
    mixed, unit1, fac1 = normalize(x_mine.astype(f32) + branch, ga1, sh1)
    mixed_low = mixed.astype(b16)
    ups = [w2f[t, :, W:W + H] for t in range(T)]
    downs = [w2f[t, :, W + H:] for t in range(T)]
    acts, pulls = [], []
    ffn = db[None]
    for t in range(T):
        hid = nn(mixed_low, ups[t]) + ub[t * H:(t + 1) * H]
        a, pull = jax.vjp(gelu_exact, hid)
        acts.append(a.astype(b16))
        pulls.append(pull)
        ffn = ffn + nt(acts[t], downs[t])
    result, unit2, fac2 = normalize(mixed + ffn, ga2, sh2)
    up_g = cf.reshape(half, D).astype(f32)
    grad2, g_ga2, g_sh2 = normalize_back(up_g, unit2, fac2, ga2)
    ffn_low = grad2.astype(b16)
    g_db = jnp.sum(ffn_low.astype(f32), axis=0)
    tn = lambda a, b: lax.dot_general(a, b, (((0,), (0,)), ((), ())), preferred_element_type=f32).astype(b16)
    mixed_grad = grad2
    parts = []
    g_ub = []
    for t in range(T):
        hl = pulls[t](nn(ffn_low, downs[t]))[0].astype(b16)
        g_ub.append(jnp.sum(hl.astype(f32), axis=0))
        parts.append((tn(mixed_low, hl), tn(ffn_low, acts[t])))
        mixed_grad = mixed_grad + nt(hl, ups[t])
    grad1, g_ga1, g_sh1 = normalize_back(mixed_grad, unit1, fac1, ga1)
    branch_low = grad1.astype(b16)
    g_ob = jnp.sum(branch_low.astype(f32), axis=0)
    go_mine, go_other = tn(branch_low, att_mine), tn(branch_low, att_other)
    g_out = [jnp.where(c == t, go_mine, go_other) for t in range(T)]
    ga = jnp.stack([jnp.concatenate([g_out[t], parts[t][0], parts[t][1]], axis=1) for t in range(T)])
    do_mine = nn(branch_low, w_mine[:, :W]).astype(b16)
    do_other = swap(nn(branch_low, w_other[:, :W]).astype(b16))
    lower = jnp.where(c == 0, do_mine, do_other)
    upper = jnp.where(c == 0, do_other, do_mine)
    do = jnp.concatenate([lower, upper], axis=0)
    dq, dk, dv = attend_back(q, k, v, do, att, lse, sf)
    dqkv = jnp.concatenate([dq, dk, dv], axis=1)
    gb = tn(xf, dqkv)
    back = nt(dqkv, mine1[:, :3 * W]).astype(b16)
    ing = grad1 + rows_of(back, c).astype(f32) + swap(rows_of(back, 1 - c)).astype(f32)
    wide = lambda v: lax.dynamic_update_slice(jnp.zeros((T * W,), f32), v, (c * W,))
    vec = jnp.concatenate([wide(jnp.sum(dq.astype(f32), axis=0)), wide(jnp.sum(dv.astype(f32), axis=0))]
                          + g_ub + [g_ob, g_db, g_ga1, g_sh1, g_ga2, g_sh2])
    pad = -nv % (8 * VEC)
    vec = jnp.pad(vec, (0, pad)).reshape(-1, VEC)
    res_out, ing_out, oa, ob_, vs = scatter_all(
        sizes, result.astype(b16).reshape(C // 2, R, D), ing.astype(b16).reshape(C // 2, R, D),
        ga.reshape(T, X, 2, C, r, -1), gb.reshape(X, 2, C, r, -1), vec, S)
    vs = vs.reshape(-1)
    widths = [query_bias.shape[0]] * 2 + [up_bias.shape[0]] + [r] * 6
    where = [tfz] * 3 + [fz] * 6
    small = [lax.dynamic_slice(vs, (offs[i] + where[i] * widths[i],), (widths[i],)) for i in range(9)]
    return (res_out, ing_out.astype(f32), ob_[:, :W], ob_[:, W:2 * W], ob_[:, 2 * W:], oa[:, :W].T,
            oa[:, W:W + H], oa[:, W + H:].T) + tuple(small)


def solution(mesh):
    sizes = (mesh.shape["fsdp"], mesh.shape["ctx"], mesh.shape["tp"])
    every = ("fsdp", "ctx")
    rows, cols, one, three = P(every, "tp"), P("tp", every), P(every), P(("tp",) + every)
    token = P("fsdp", "ctx", None)
    weights = (rows, rows, rows, cols, rows, cols)
    vectors = (three, three, three) + (one,) * 6
    return jax.shard_map(
        functools.partial(on_device, sizes), mesh=mesh,
        in_specs=(token, P("fsdp", "ctx"), token) + weights + vectors,
        out_specs=(token, token) + weights + vectors, check_vma=False)
```

```python
import functools
import jax
import jax.numpy as jnp
from jax import lax
from jax.sharding import PartitionSpec as P
from jax.experimental import pallas as pl
from jax.experimental.pallas import tpu as pltpu

MESH = pl.DeviceIdType.MESH
ANY = pl.BlockSpec(memory_space=pl.ANY)
VM = pl.BlockSpec(memory_space=pltpu.VMEM)


class Place:
    def __init__(self, sizes):
        self.F, self.C, self.T = sizes
        self.X = self.F // 2
        f = lax.axis_index("fsdp")
        self.x = f // 2
        self.c = lax.rem(f, 2)
        self.z = lax.axis_index("ctx")
        self.y = lax.axis_index("tp")

    def dev(self, x=None, c=None, z=None, y=None):
        x = self.x if x is None else x
        c = self.c if c is None else c
        return (2 * x + c, self.z if z is None else z, self.y if y is None else y)

    def z_off(self, d):
        return lax.rem(self.z + d + self.C, self.C)

    def x_off(self, d):
        return lax.rem(self.x + d + self.X, self.X)

    def greet(self, chip_wide):
        bar = pltpu.get_barrier_semaphore()
        devs = [self.dev(c=1 - self.c), self.dev(y=1 - self.y)]
        devs += [self.dev(x=self.x_off(d)) for d in range(1, self.X)]
        for d in range(1, self.C):
            devs.append(self.dev(z=self.z_off(d)))
            if chip_wide:
                devs.append(self.dev(z=self.z_off(d), c=1 - self.c))
        for d in devs:
            pl.semaphore_signal(bar, inc=1, device_id=d, device_id_type=MESH)
        pl.semaphore_wait(bar, len(devs))


class Sends:
    def __init__(self, sems):
        self.sems, self.n, self.waits = sems, 0, []

    def go(self, src, dst, recv, dev, like=None):
        pltpu.make_async_remote_copy(
            src_ref=src, dst_ref=dst, send_sem=self.sems.at[self.n], recv_sem=recv,
            device_id=dev, device_id_type=MESH).start()
        self.n += 1
        self.waits.append(src if like is None else like)

    def finish(self, me):
        for n, like in enumerate(self.waits):
            pltpu.make_async_remote_copy(
                src_ref=like, dst_ref=like, send_sem=self.sems.at[n], recv_sem=self.sems.at[n],
                device_id=me.dev(c=1 - me.c), device_id_type=MESH).wait_send()
        self.waits = []


def arrived(dst, recv, pl_):
    pltpu.make_async_remote_copy(
        src_ref=dst, dst_ref=dst, send_sem=recv, recv_sem=recv,
        device_id=pl_.dev(c=1 - pl_.c), device_id_type=MESH).wait_recv()


def gather_events(me, own, full, sends, recv, lsem):
    C, X = me.C, me.X
    sem = lambda t, x, c, z: recv.at[((t * X + x) * 2 + c) * C + z]
    slot = lambda t, x, c, z: full.at[t, x, c, z]
    like = slot(0, 0, 0, 0)

    def push(src, at, dev):
        sends.go(src, slot(*at), sem(*at), dev, like)

    def wait(at):
        arrived(slot(*at), sem(*at), me)

    core, side = me.dev(c=1 - me.c), me.dev(y=1 - me.y)
    xs = [(me.x_off(d), me.dev(x=me.x_off(d))) for d in range(1, X)]
    half = C // 2
    local = pltpu.make_async_copy(own, slot(me.y, me.x, me.c, me.z), lsem)
    events = []

    def first():
        at = (me.y, me.x, me.c, me.z)
        for d in range(1, C):
            push(own, at, me.dev(z=me.z_off(d)))
        for _, dev in xs:
            push(own, at, dev)
        push(own, at, side)
        push(own, at, core)
        local.start()

    events.append(first)
    for d in range(1, C):
        def along(d=d):
            at = (me.y, me.x, me.c, me.z_off(-d))
            wait(at)
            for _, dev in xs:
                push(slot(*at), at, dev)
            push(slot(*at), at, side)
            push(slot(*at), at, core)
        events.append(along)
    for j in range(C):
        def across(j=j):
            zj = me.z_off(-j)
            at = (1 - me.y, me.x, me.c, zj)
            wait(at)
            if j < half:
                for _, dev in xs:
                    push(slot(*at), at, dev)
            push(slot(*at), at, core)
            for xo, _ in xs:
                at = (me.y, xo, me.c, zj)
                wait(at)
                if j >= half:
                    push(slot(*at), at, side)
                push(slot(*at), at, core)
        events.append(across)
    for j in range(C):
        def corner(j=j):
            zj = me.z_off(-j)
            for xo, _ in xs:
                at = (1 - me.y, xo, me.c, zj)
                wait(at)
                push(slot(*at), at, core)
        events.append(corner)

    def last():
        for t in range(me.T):
            for xx in range(X):
                for zz in range(C):
                    wait((t, xx, 1 - me.c, zz))
        local.wait()

    events.append(last)
    return events


def gather_count(sizes):
    F, C, T = sizes
    X = F // 2
    return (C - 1) + X + 1 + (C - 1) * (X + 1) + (C // 2) * (X - 1) + C * X + (C - C // 2) * (X - 1) + C * (X - 1)


def home(me, seqs, y):
    lo = y * (me.C - seqs)
    return lo


def token_events(me, pieces, seqs, sends):
    C = me.C
    half = C // 2
    lo = home(me, seqs, me.y)
    busy = (me.z >= lo) & (me.z < lo + seqs)
    return lo, busy


class Tokens:
    def __init__(self, me, seqs):
        self.me, self.S = me, seqs
        self.half = me.C // 2
        self.lo = me.y * (me.C - seqs)
        self.busy = (me.z >= self.lo) & (me.z < self.lo + seqs)
        self.owner = me.c == me.y

    def out(self, src, dst, full, ssem, rsem, lsem):
        me, half = self.me, self.half
        k = me.z // half
        at = me.z if full else lax.rem(me.z, half)

        @pl.when(self.owner)
        def _():
            for s in range(self.S):
                here = (self.lo + s == me.z) & (k == me.c)

                @pl.when(here)
                def _():
                    pltpu.make_async_copy(src.at[s], dst.at[at], lsem).start()

                @pl.when(jnp.logical_not(here))
                def _():
                    pltpu.make_async_remote_copy(
                        src_ref=src.at[s], dst_ref=dst.at[at], send_sem=ssem.at[s],
                        recv_sem=rsem.at[lax.rem(me.z, half)],
                        device_id=me.dev(c=k, z=self.lo + s), device_id_type=MESH).start()

    def out_done(self, src, dst, full, ssem, rsem, lsem):
        me, half = self.me, self.half

        @pl.when(self.busy)
        def _():
            for i in range(half):
                zq = me.c * half + i
                at = zq if full else i
                here = (zq == me.z) & (me.c == me.y)

                @pl.when(here)
                def _():
                    pltpu.make_async_copy(src.at[0], dst.at[at], lsem).wait()

                @pl.when(jnp.logical_not(here))
                def _():
                    arrived(dst.at[at], rsem.at[i], me)

                if full:
                    pltpu.make_async_remote_copy(
                        src_ref=dst.at[at], dst_ref=dst.at[at], send_sem=ssem.at[self.S + i],
                        recv_sem=rsem.at[half + i], device_id=me.dev(c=1 - me.c),
                        device_id_type=MESH).start()

    def out_end(self, src, dst, full, ssem, rsem, lsem):
        me, half = self.me, self.half
        k = me.z // half

        @pl.when(self.owner)
        def _():
            for s in range(self.S):
                here = (self.lo + s == me.z) & (k == me.c)

                @pl.when(jnp.logical_not(here))
                def _():
                    pltpu.make_async_remote_copy(
                        src_ref=src.at[s], dst_ref=dst.at[0], send_sem=ssem.at[s],
                        recv_sem=rsem.at[0], device_id=me.dev(c=1 - me.c),
                        device_id_type=MESH).wait_send()

        if full:
            @pl.when(self.busy)
            def _():
                for i in range(half):
                    zq = (1 - me.c) * half + i
                    arrived(dst.at[zq], rsem.at[half + i], me)
                    pltpu.make_async_remote_copy(
                        src_ref=dst.at[0], dst_ref=dst.at[0], send_sem=ssem.at[self.S + i],
                        recv_sem=rsem.at[0], device_id=me.dev(c=1 - me.c),
                        device_id_type=MESH).wait_send()

    def back(self, src, dst, ssem, rsem, lsem):
        me, half = self.me, self.half

        @pl.when(self.busy)
        def _():
            for i in range(half):
                zq = me.c * half + i
                here = (zq == me.z) & (me.c == me.y)
                at = me.z - self.lo

                @pl.when(here)
                def _():
                    pltpu.make_async_copy(src.at[i], dst.at[at], lsem).start()

                @pl.when(jnp.logical_not(here))
                def _():
                    pltpu.make_async_remote_copy(
                        src_ref=src.at[i], dst_ref=dst.at[at], send_sem=ssem.at[i],
                        recv_sem=rsem.at[at], device_id=me.dev(c=me.y, z=zq),
                        device_id_type=MESH).start()

    def back_pass(self, src, dst, ssem, rsem, lsem):
        me, half = self.me, self.half
        k = me.z // half

        @pl.when(self.owner)
        def _():
            for s in range(self.S):
                here = (self.lo + s == me.z) & (k == me.c)

                @pl.when(here)
                def _():
                    pltpu.make_async_copy(src.at[0], dst.at[s], lsem).wait()

                @pl.when(jnp.logical_not(here))
                def _():
                    arrived(dst.at[s], rsem.at[s], me)

                pltpu.make_async_remote_copy(
                    src_ref=dst.at[s], dst_ref=dst.at[s], send_sem=ssem.at[half + s],
                    recv_sem=rsem.at[s], device_id=me.dev(y=1 - me.y),
                    device_id_type=MESH).start()

    def back_end(self, src, dst, ssem, rsem, lsem):
        me, half = self.me, self.half

        @pl.when(self.busy)
        def _():
            for i in range(half):
                zq = me.c * half + i
                here = (zq == me.z) & (me.c == me.y)

                @pl.when(jnp.logical_not(here))
                def _():
                    pltpu.make_async_remote_copy(
                        src_ref=src.at[i], dst_ref=dst.at[0], send_sem=ssem.at[i],
                        recv_sem=rsem.at[0], device_id=me.dev(c=1 - me.c),
                        device_id_type=MESH).wait_send()

        @pl.when(self.owner)
        def _():
            for s in range(self.S):
                pltpu.make_async_remote_copy(
                    src_ref=dst.at[s], dst_ref=dst.at[s], send_sem=ssem.at[half + s],
                    recv_sem=rsem.at[s], device_id=me.dev(y=1 - me.y),
                    device_id_type=MESH).wait_send()

        @pl.when(jnp.logical_not(self.owner))
        def _():
            for s in range(self.S):
                arrived(dst.at[s], rsem.at[s], me)


def reduce_events(me, grads, split, bufs, sends, recv, lsem, finish):
    acc, rc, xd, yd, xr, yr, zr = bufs
    C, X = me.C, me.X
    half = C // 2
    n_cols = acc.shape[2]
    like, like_all = acc.at[0, 0, :, 0], acc.at[0, 0]
    core, side = me.dev(c=1 - me.c), me.dev(y=1 - me.y)
    s_core = lambda t, x: recv.at[t * X + x]
    base = me.T * X
    s_d = lambda d, j: recv.at[base + (d - 1) * C + j]
    base2 = base + (X - 1) * C
    s_xr = lambda d, j: recv.at[base2 + (d - 1) * C + j]
    base3 = base2 + (X - 1) * C
    s_yr = lambda j: recv.at[base3 + j]
    s_zr = lambda j: recv.at[base3 + C + j]
    quads = ([(1 - me.y, me.x_off(d)) for d in range(1, X)] + [(1 - me.y, me.x)]
             + [(me.y, me.x_off(d)) for d in range(1, X)] + [(me.y, me.x)])
    locals_ = []

    def first():
        if split:
            for n, x in enumerate([me.x_off(d) for d in range(1, X)] + [me.x]):
                sends.go(grads.at[:, x, 1 - me.c], acc.at[me.c, x], s_core(me.c, x), core, like_all)
                cp = pltpu.make_async_copy(grads.at[:, x, me.c], acc.at[me.c, x], lsem.at[n])
                cp.start()
                locals_.append(cp)
        else:
            for n, (t, x) in enumerate(quads):
                sends.go(grads.at[t, :, x, 1 - me.c], rc.at[t, x], s_core(t, x), core, like_all)
                cp = pltpu.make_async_copy(grads.at[t, :, x, me.c], acc.at[t, x], lsem.at[n])
                cp.start()
                locals_.append(cp)

    def add(a, b):
        def body(i, carry):
            a[i] = a[i] + b[i]
            return carry
        lax.fori_loop(0, n_cols, body, 0)

    def ready(n):
        t, x = quads[n]
        if split:
            if n == 0:
                for cp in locals_:
                    cp.wait()
                for xo in [me.x_off(d) for d in range(1, X)] + [me.x]:
                    arrived(acc.at[1 - me.c, xo], s_core(1 - me.c, xo), me)
            return
        locals_[n].wait()
        arrived(rc.at[t, x], s_core(t, x), me)

        def body(i, carry):
            for z in range(C):
                acc[t, x, i, z] = acc[t, x, i, z] + rc[t, x, i, z]
            return carry
        lax.fori_loop(0, n_cols, body, 0)

    events = [first]

    def corner():
        for d in range(1, X):
            ready(d - 1)
            t, x = quads[d - 1]
            for j in range(C):
                zj = me.z_off(-j)
                if j < half:
                    sends.go(acc.at[t, x, :, zj], xd.at[d - 1, j], s_d(d, j), me.dev(x=x), like)
                else:
                    sends.go(acc.at[t, x, :, zj], yd.at[d - 1, j - half], s_d(d, j), side, like)
    events.append(corner)

    def side_early():
        ready(X - 1)
        t, x = 1 - me.y, me.x
        for j in range(half, C):
            zj = me.z_off(-j)
            sends.go(acc.at[t, x, :, zj], yr.at[j], s_yr(j), side, like)
    events.append(side_early)

    def x_early():
        for d in range(1, X):
            ready(X - 1 + d)
            t, x = me.y, me.x_off(d)
            for j in range(half):
                zj = me.z_off(-j)
                sends.go(acc.at[t, x, :, zj], xr.at[d - 1, j], s_xr(d, j), me.dev(x=x), like)
    events.append(x_early)

    def side_late():
        t, x = 1 - me.y, me.x
        for j in range(half):
            zj = me.z_off(-j)
            for d in range(1, X):
                arrived(xd.at[d - 1, j], s_d(d, j), me)
                add(acc.at[t, x, :, zj], xd.at[d - 1, j])
            sends.go(acc.at[t, x, :, zj], yr.at[j], s_yr(j), side, like)
    events.append(side_late)

    def x_late():
        for d in range(1, X):
            t, x = me.y, me.x_off(d)
            for j in range(half, C):
                zj = me.z_off(-j)
                arrived(yd.at[d - 1, j - half], s_d(d, j), me)
                add(acc.at[t, x, :, zj], yd.at[d - 1, j - half])
                sends.go(acc.at[t, x, :, zj], xr.at[d - 1, j], s_xr(d, j), me.dev(x=x), like)
    events.append(x_late)
    for n, j in enumerate(list(range(1, C)) + [0]):
        def to_z(n=n, j=j):
            if n == 0:
                ready(2 * X - 1)
            t, x = me.y, me.x
            zj = me.z_off(-j)
            arrived(yr.at[j], s_yr(j), me)
            add(acc.at[t, x, :, zj], yr.at[j])
            for d in range(1, X):
                arrived(xr.at[d - 1, j], s_xr(d, j), me)
                add(acc.at[t, x, :, zj], xr.at[d - 1, j])
            if j:
                sends.go(acc.at[t, x, :, zj], zr.at[j - 1], s_zr(j - 1), me.dev(z=zj), like)
        events.append(to_z)

    def last():
        for j in range(1, C):
            arrived(zr.at[j - 1], s_zr(j - 1), me)
        for i in range(n_cols):
            total = acc[me.y, me.x, i, me.z].astype(jnp.float32)
            for j in range(1, C):
                total = total + zr[j - 1, i].astype(jnp.float32)
            finish(i, total)
    events.append(last)
    return events


def reduce_scratch(sizes, n, r, w, split):
    F, C, T = sizes
    X = F // 2
    half = C // 2
    v = lambda shape: pltpu.VMEM(shape, jnp.bfloat16)
    return [v((T, X, n, C, r, w)), v((1, 1, 1, 1, 16, 128) if split else (T, X, n, C, r, w)),
            v((X - 1, half, n, r, w)), v((X - 1, C - half, n, r, w)), v((X - 1, C, n, r, w)),
            v((C, n, r, w)), v((C - 1, n, r, w))]


def reduce_sems(sizes):
    F, C, T = sizes
    X = F // 2
    return T * X + 2 * (X - 1) * C + 2 * C


def reduce_count(sizes, split):
    F, C, T = sizes
    X = F // 2
    return (X if split else T * X) + 2 * (X - 1) * C + C + C - 1


def total_events(me, own, bufs, out, sends, recv):
    C, X = me.C, me.X
    acc, got = bufs
    groups = [[me.dev(c=1 - me.c)], [me.dev(x=me.x_off(d)) for d in range(1, X)],
              [me.dev(y=1 - me.y)], [me.dev(z=me.z_off(d)) for d in range(1, C)]]
    like = acc.at[0]
    bases = [sum(len(g) for g in groups[:i]) for i in range(len(groups))]

    def start(gi):
        for i, dev in enumerate(groups[gi]):
            sends.go(acc.at[gi], got.at[bases[gi] + i], recv.at[bases[gi] + i], dev, like)

    def first():
        acc[0] = own[...]
        start(0)

    events = [first]
    for gi in range(len(groups)):
        def step(gi=gi):
            total = acc[gi]
            for i in range(len(groups[gi])):
                arrived(got.at[bases[gi] + i], recv.at[bases[gi] + i], me)
                total = total + got[bases[gi] + i]
            if gi + 1 < len(groups):
                acc[gi + 1] = total
                start(gi + 1)
            else:
                out[...] = total
        events.append(step)
    return events


def total_count(sizes):
    F, C, T = sizes
    return 1 + F // 2 - 1 + 1 + C - 1

HEAD = 64
PAIR = 2 * HEAD
SCALE = HEAD ** (-0.5)
norm_eps = 1e-12
masked_score = -1000000000.0


def nt(a, b):
    return lax.dot_general(a, b, (((1,), (1,)), ((), ())), preferred_element_type=jnp.float32)


def nn(a, b):
    return lax.dot_general(a, b, (((1,), (0,)), ((), ())), preferred_element_type=jnp.float32)


def spread_segments(seg_ref, wide):
    C, _, R = seg_ref.shape
    for i in range(C):
        for j in range(0, R, 128):
            row = jnp.broadcast_to(seg_ref[i, 0:1, j:j + 128], (128, 128))
            wide[i * R + j:i * R + j + 128, :] = row.T


def lanes_of(h, like):
    lane = lax.broadcasted_iota(jnp.int32, like.shape, like.ndim - 1)
    return jnp.where(lane // HEAD == h, like, jnp.zeros_like(like))


def two_lanes(wide):
    return jnp.concatenate([wide, wide], axis=1)


def attend_block(q, k, v_t, seg_q, seg_k):
    same = seg_k == seg_q
    outs, logs = [], []
    for h in range(2):
        s = nt(k, lanes_of(h, q) * jnp.bfloat16(SCALE))
        s = jnp.where(same, s, masked_score)
        peak = jnp.max(s, axis=0, keepdims=True)
        e = jnp.exp(s - peak)
        total = jnp.sum(e, axis=0, keepdims=True)
        o = nn(v_t, e.astype(jnp.bfloat16))
        outs.append(o[h * HEAD:(h + 1) * HEAD] * (1.0 / total))
        logs.append(peak + jnp.log(total))
    return jnp.concatenate(outs, axis=0), logs


def attend_kernel(q_ref, k_ref, v_ref, seg_ref, o_ref, lse_ref, wide, v_t):
    i = pl.program_id(1)

    @pl.when((pl.program_id(0) == 0) & (i == 0))
    def _():
        spread_segments(seg_ref, wide)

    @pl.when(i == 0)
    def _():
        v_t[...] = v_ref[...].astype(jnp.float32).T.astype(jnp.bfloat16)

    seg_q = seg_ref[i, 0:1, :]
    o, logs = attend_block(q_ref[...], k_ref[...], v_t[...], seg_q, two_lanes(wide[...]))
    o_ref[...] = o.T.astype(jnp.bfloat16)
    lse_ref[0] = jnp.concatenate(logs + [jnp.zeros((6, logs[0].shape[1]), jnp.float32)], axis=0)


def attend(q, k, v, seg):
    L, W = q.shape
    C, _, R = seg.shape
    n = W // PAIR
    return pl.pallas_call(
        attend_kernel,
        grid=(n, C),
        in_specs=[pl.BlockSpec((R, PAIR), lambda p, i: (i, p)),
                  pl.BlockSpec((L, PAIR), lambda p, i: (0, p)),
                  pl.BlockSpec((L, PAIR), lambda p, i: (0, p)),
                  pl.BlockSpec((C, 8, R), lambda p, i: (0, 0, 0))],
        out_specs=[pl.BlockSpec((R, PAIR), lambda p, i: (i, p)),
                   pl.BlockSpec((1, 8, R), lambda p, i: (p, 0, i))],
        out_shape=[jax.ShapeDtypeStruct((L, W), jnp.bfloat16),
                   jax.ShapeDtypeStruct((n, 8, L), jnp.float32)],
        scratch_shapes=[pltpu.VMEM((L, 128), jnp.float32), pltpu.VMEM((PAIR, L), jnp.bfloat16)],
        compiler_params=pltpu.CompilerParams(vmem_limit_bytes=56 * 2**20),
    )(q, k, v, seg)


def attend_back_block(q, k, k_t, v, do, o, lse, seg_q, seg_k):
    same = seg_k == seg_q
    prod = (do.astype(jnp.float32) * o.astype(jnp.float32)).T
    dq, dk, dv = [], None, None
    for h in range(2):
        qh = lanes_of(h, q) * jnp.bfloat16(SCALE)
        doh = lanes_of(h, do)
        s = nt(k, qh)
        p = jnp.exp(jnp.where(same, s, masked_score) - lse[h:h + 1])
        dp = nt(v, doh)
        inner = jnp.sum(prod[h * HEAD:(h + 1) * HEAD], axis=0, keepdims=True)
        ds = (p * (dp - inner)).astype(jnp.bfloat16)
        dv_h = nn(p.astype(jnp.bfloat16), doh)
        dk_h = nn(ds, qh)
        dv = dv_h if dv is None else dv + dv_h
        dk = dk_h if dk is None else dk + dk_h
        dq.append(nn(k_t, ds)[h * HEAD:(h + 1) * HEAD])
    return jnp.concatenate(dq, axis=0).T * SCALE, dk, dv


def attend_back_kernel(q_ref, k_ref, v_ref, do_ref, o_ref, lse_ref, seg_ref,
                       dq_ref, dk_ref, dv_ref, wide, k_t, dk_sum, dv_sum):
    i = pl.program_id(1)

    @pl.when((pl.program_id(0) == 0) & (i == 0))
    def _():
        spread_segments(seg_ref, wide)

    @pl.when(i == 0)
    def _():
        k_t[...] = k_ref[...].astype(jnp.float32).T.astype(jnp.bfloat16)

    seg_q = seg_ref[i, 0:1, :]
    dq, dk, dv = attend_back_block(q_ref[...], k_ref[...], k_t[...], v_ref[...], do_ref[...],
                                   o_ref[...], lse_ref[0], seg_q, two_lanes(wide[...]))
    dq_ref[...] = dq.astype(jnp.bfloat16)

    @pl.when(i == 0)
    def _():
        dk_sum[...] = dk
        dv_sum[...] = dv

    @pl.when(i > 0)
    def _():
        dk_sum[...] += dk
        dv_sum[...] += dv

    @pl.when(i == pl.num_programs(1) - 1)
    def _():
        dk_ref[...] = dk_sum[...].astype(jnp.bfloat16)
        dv_ref[...] = dv_sum[...].astype(jnp.bfloat16)


def attend_back(q, k, v, do, o, lse, seg):
    L, W = q.shape
    C, _, R = seg.shape
    n = W // PAIR
    row = pl.BlockSpec((R, PAIR), lambda p, i: (i, p))
    all_rows = pl.BlockSpec((L, PAIR), lambda p, i: (0, p))
    b = jax.ShapeDtypeStruct((L, W), jnp.bfloat16)
    return pl.pallas_call(
        attend_back_kernel,
        grid=(n, C),
        in_specs=[row, all_rows, all_rows, row, row,
                  pl.BlockSpec((1, 8, R), lambda p, i: (p, 0, i)),
                  pl.BlockSpec((C, 8, R), lambda p, i: (0, 0, 0))],
        out_specs=[row, all_rows, all_rows],
        out_shape=[b, b, b],
        scratch_shapes=[pltpu.VMEM((L, 128), jnp.float32), pltpu.VMEM((PAIR, L), jnp.bfloat16),
                        pltpu.VMEM((L, PAIR), jnp.float32), pltpu.VMEM((L, PAIR), jnp.float32)],
        compiler_params=pltpu.CompilerParams(vmem_limit_bytes=56 * 2**20),
    )(q, k, v, do, o, lse, seg)


STRIP = 64


def strips(rows, body):
    def step(i, carry):
        body(pl.ds(pl.multiple_of(i * STRIP, STRIP), STRIP))
        return carry
    lax.fori_loop(0, rows // STRIP, step, 0)


def fold(value):
    total = value[0:8]
    for i in range(8, value.shape[0], 8):
        total = total + value[i:i + 8]
    return total


def mean(value):
    return jnp.mean(value, axis=-1, keepdims=True)


def unit_of(value):
    centred = value - mean(value)
    factor = lax.rsqrt(mean(centred * centred) + norm_eps)
    return centred * factor, factor


def back_of(upstream, unit, factor, gain):
    along = upstream * gain
    return factor * (along - mean(along) - unit * mean(along * unit))


def flip(ref, out):
    rows = ref.shape[0]
    for i in range(0, rows, 128):
        out[:, i:i + 128] = ref[i:i + 128, :].astype(jnp.float32).T.astype(jnp.bfloat16)


def middle_kernel(T, J, x_ref, att_ref, cot_ref, wu_ref, wd_ref, wo_ref, vec_ref, ub_ref,
                  res_ref, one_ref, do_ref, gff_ref, go_ref, gvec_ref, gub_ref,
                  unit, mixed, fac, low, low_t, acc, two, fl, fl_t, hid, act, slope, hl, sums):
    s = pl.program_id(0)
    n = T * J
    rows, D = x_ref.shape
    W = wo_ref.shape[2]
    f32, b16 = jnp.float32, jnp.bfloat16
    row = lambda i: vec_ref[i:i + 1, :]

    @pl.when(s == 0)
    def _():
        for t in range(T):
            part = nt(att_ref[:, t * W:(t + 1) * W], wo_ref[t])
            acc[...] = part if t == 0 else acc[...] + part

        def body(at):
            u, factor = unit_of(x_ref[at, :].astype(f32) + acc[at, :] + row(0))
            m = u * row(2) + row(3)
            unit[at, :] = u
            fac[at, :] = jnp.broadcast_to(factor, (STRIP, 128))
            mixed[at, :] = m
            low[at, :] = m.astype(b16)
            acc[at, :] = jnp.zeros((STRIP, D), f32)
        strips(rows, body)
        flip(low, low_t)

    @pl.when(s < n)
    def _():
        hid[...] = nn(low[...], wu_ref[0])

        def body(at):
            h = hid[at, :] + ub_ref[0]
            phi = 0.5 + 0.5 * lax.erf(h * (0.5 ** 0.5))
            dens = jnp.exp(-0.5 * h * h) * 0.3989422804014327
            act[s, at, :] = (h * phi).astype(b16)
            slope[s, at, :] = phi + h * dens
        strips(rows, body)
        acc[...] += nt(act[s], wd_ref[0])

    @pl.when(s == n)
    def _():
        sums[...] = jnp.zeros_like(sums)

        def body(at):
            u, factor = unit_of(mixed[at, :] + acc[at, :] + row(1))
            res_ref[at, :] = (u * row(4) + row(5)).astype(b16)
            g = cot_ref[at, :].astype(f32)
            g2 = back_of(g, u, factor, row(4))
            l2 = g2.astype(b16)
            fl[at, :] = l2
            acc[at, :] = g2
            sums[1] += fold(l2.astype(f32))
            sums[4] += fold(g * u)
            sums[5] += fold(g)
        strips(rows, body)
        flip(fl, fl_t)

    @pl.when(s >= n)
    def _():
        j = 2 * n - 1 - s
        hid[...] = nn(fl[...], wd_ref[0])
        gub_ref[0] = jnp.zeros_like(gub_ref[0])

        def body(at):
            v = (hid[at, :] * slope[j, at, :]).astype(b16)
            hl[at, :] = v
            gub_ref[0] += fold(v.astype(f32))
        strips(rows, body)
        acc[...] += nt(hl[...], wu_ref[0])
        gff_ref[0, 0, 0] = nn(low_t[...], hl[...]).astype(b16)
        gff_ref[0, 0, 1] = nn(fl_t[...], act[j]).astype(b16)

    @pl.when(s == 2 * n - 1)
    def _():
        def body(at):
            g = acc[at, :]
            u = unit[at, :]
            g1 = back_of(g, u, fac[at, 0:1], row(2))
            one_ref[at, :] = g1
            l1 = g1.astype(b16)
            fl[at, :] = l1
            sums[0] += fold(l1.astype(f32))
            sums[2] += fold(g * u)
            sums[3] += fold(g)
        strips(rows, body)
        flip(fl, fl_t)
        for t in range(T):
            go_ref[t] = nn(fl_t[...], att_ref[:, t * W:(t + 1) * W]).astype(b16)
            do_ref[:, t * W:(t + 1) * W] = nn(fl[...], wo_ref[t]).astype(b16)
        for i in range(6):
            gvec_ref[i:i + 1, :] = jnp.sum(sums[i], axis=0, keepdims=True)


def middle(T, x, att, cot, w2, vec, ub, chunk):
    rows, D = x.shape
    W = att.shape[1] // T
    J = ub.shape[0] // T
    H = J * chunk
    n = T * J
    f32, b16 = jnp.float32, jnp.bfloat16
    which = lambda s: jnp.where(s < n, s, 2 * n - 1 - s)
    whole = lambda shape: pl.BlockSpec(shape, lambda s: (0,) * len(shape), pipeline_mode=pl.Buffered(1))
    up = pl.BlockSpec((1, D, chunk), lambda s: (which(s) // J, 0, lax.rem(which(s), J)))
    down = pl.BlockSpec((1, D, chunk), lambda s: (which(s) // J, 0, J + lax.rem(which(s), J)))
    wo = pl.BlockSpec((T, D, W), lambda s: (0, 0, 2 * H // W), pipeline_mode=pl.Buffered(1))
    late = lambda s: jnp.where(s < n, n - 1, 2 * n - 1 - s)
    return pl.pallas_call(
        functools.partial(middle_kernel, T, J),
        grid=(2 * n,),
        in_specs=[whole((rows, D)), whole((rows, T * W)), whole((rows, D)), up, down, wo, whole(vec.shape),
                  pl.BlockSpec((1, 1, chunk), lambda s: (which(s), 0, 0))],
        out_specs=[whole((rows, D)), whole((rows, D)), whole((rows, T * W)),
                   pl.BlockSpec((1, 1, 2, D, chunk), lambda s: (late(s) // J, lax.rem(late(s), J), 0, 0, 0)),
                   whole((T, D, W)), whole((8, D)),
                   pl.BlockSpec((1, 8, chunk), lambda s: (late(s), 0, 0))],
        out_shape=[jax.ShapeDtypeStruct((rows, D), b16), jax.ShapeDtypeStruct((rows, D), f32),
                   jax.ShapeDtypeStruct((rows, T * W), b16), jax.ShapeDtypeStruct((T, J, 2, D, chunk), b16),
                   jax.ShapeDtypeStruct((T, D, W), b16), jax.ShapeDtypeStruct((8, D), f32),
                   jax.ShapeDtypeStruct((n, 8, chunk), f32)],
        scratch_shapes=[pltpu.VMEM((rows, D), f32), pltpu.VMEM((rows, D), f32), pltpu.VMEM((rows, 128), f32),
                        pltpu.VMEM((rows, D), b16), pltpu.VMEM((D, rows), b16), pltpu.VMEM((rows, D), f32),
                        pltpu.VMEM((8, 128), f32), pltpu.VMEM((rows, D), b16), pltpu.VMEM((D, rows), b16),
                        pltpu.VMEM((rows, chunk), f32), pltpu.VMEM((n, rows, chunk), b16),
                        pltpu.VMEM((n, rows, chunk), f32), pltpu.VMEM((rows, chunk), b16),
                        pltpu.VMEM((6, 8, D), f32)],
        compiler_params=pltpu.CompilerParams(vmem_limit_bytes=60 * 2**20),
    )(x, att, cot, w2, w2, w2, vec, ub)


VEC = 128


def spread_pieces(blocks, width, first, total, copies):
    n, lanes = blocks.shape
    i = lax.broadcasted_iota(jnp.int32, (lanes, total), 0)
    col = lax.broadcasted_iota(jnp.int32, (lanes, total), 1)
    pick = jnp.where(i - first == lax.rem(col, width), 1.0, 0.0).astype(jnp.bfloat16)
    wide = nn(blocks, pick)
    dev = lax.broadcasted_iota(jnp.int32, (n, total), 0)
    col = lax.broadcasted_iota(jnp.int32, (n, total), 1)
    return jnp.sum(jnp.where(dev == col // width, wide, 0.0), axis=0, keepdims=True)


def front_kernel(cfg, x_ref, cot_ref, seg_ref, w1_ref, w2_ref,
                 q_ref, k_ref, v_ref, ah_ref, ar_ref, lse_ref, xf_ref, cf_ref, sf_ref, g1_ref, g2_ref,
                 vec_ref, ub_ref,
                 zero, zseg, xv, wv, pv, sv, wide, v_t,
                 ssem, r1, r2, lsem, tss, trs, tls, csem):
    sizes, S, W, H, chunk = cfg
    me = Place(sizes)
    C, X, T = me.C, me.X, me.T
    R, D = xv.shape[1:]
    r = wv.shape[3]
    L = C * R
    f32, b16 = jnp.float32, jnp.bfloat16
    me.greet(True)
    sends = Sends(ssem)
    tok = Tokens(me, S)
    items = [(x_ref, xf_ref, True, tss.at[0], trs.at[0], tls.at[0]),
             (seg_ref, sf_ref, True, tss.at[1], trs.at[1], tls.at[1]),
             (cot_ref, cf_ref, False, tss.at[2], trs.at[2], tls.at[2])]
    idle = jnp.logical_not(tok.busy)
    fills = ([(zero, xf_ref.at[i]) for i in range(C)] + [(zseg, sf_ref.at[i]) for i in range(C)]
             + [(zero, cf_ref.at[i]) for i in range(C // 2)])

    @pl.when(idle)
    def _():
        zero[...] = jnp.zeros_like(zero)
        zseg[...] = jnp.zeros_like(zseg)
        for i, (a, b) in enumerate(fills):
            pltpu.make_async_copy(a, b, tls.at[3 + i]).start()

    ev1 = gather_events(me, w1_ref, g1_ref, sends, r1, lsem.at[0])
    ev2 = gather_events(me, w2_ref, g2_ref, sends, r2, lsem.at[1])
    ev1[0]()
    for it in items[:2]:
        tok.out(*it)
    ev2[0]()
    for e in ev1[1:C]:
        e()
    for it in items[:2]:
        tok.out_done(*it)
    tok.out(*items[2])
    for e in ev1[C:]:
        e()
    for it in items[:2]:
        tok.out_end(*it)

    @pl.when(idle)
    def _():
        for i, (a, b) in enumerate(fills):
            pltpu.make_async_copy(a, b, tls.at[3 + i]).wait()

    loads = [(xf_ref, xv), (sf_ref, sv), (g1_ref.at[me.c], wv)]
    pieces = [(g1_ref.at[t, xx, cc, zz, :, pl.ds(3 * W, VEC)], pv.at[((t * X + xx) * 2 + cc) * C + zz])
              for t in range(T) for xx in range(X) for cc in range(2) for zz in range(C)]
    loads = [pltpu.make_async_copy(a, b, csem.at[i]) for i, (a, b) in enumerate(loads + pieces)]
    for cp in loads:
        cp.start()
    for cp in loads:
        cp.wait()
    ev2[1]()
    per = pv.shape[1]
    blocks = jnp.concatenate([pv[:, i, :] for i in range(min(per, 4))], axis=1)
    n_dev = blocks.shape[0]
    qw, uw = T * W // n_dev, T * H // n_dev
    qb = spread_pieces(blocks, qw, 0, T * W, 1)
    vb = spread_pieces(blocks, qw, qw, T * W, 1)
    ub = spread_pieces(blocks, uw, 2 * qw, T * H, 1)
    for i in range(T * H // chunk):
        ub_ref[i] = ub[:, i * chunk:(i + 1) * chunk]
    once = blocks[:n_dev // T]
    for i in range(6):
        vec_ref[i:i + 1, :] = spread_pieces(once, r, 2 * qw + uw + i * r, D, T)
    vec_ref[6:8, :] = jnp.zeros((2, D), f32)
    first = me.c == 0
    qb = jnp.where(first, qb[:, :W], qb[:, W:])
    vb = jnp.where(first, vb[:, :W], vb[:, W:])
    weights = wv[...].reshape(D, wv.shape[-1])

    def project(i, carry):
        at = pl.ds(pl.multiple_of(i * R, R), R)
        out = nn(xv[i], weights[:, :3 * W])
        q_ref[at, :] = (out[:, :W] + qb).astype(b16)
        k_ref[at, :] = out[:, W:2 * W].astype(b16)
        v_ref[at, :] = (out[:, 2 * W:] + vb).astype(b16)
        return carry
    lax.fori_loop(0, C, project, 0)
    ev2[2]()
    spread_segments(sv, wide)
    n_pairs = W // PAIR
    for p in range(n_pairs):
        v_t[p] = v_ref[:, p * PAIR:(p + 1) * PAIR].astype(f32).T.astype(b16)
    ev2[3]()

    late = ev2[4:]
    n_it = n_pairs * C

    def run(lo, hi):
        def body(it, carry):
            p, i = it // C, lax.rem(it, C)
            at = pl.ds(pl.multiple_of(i * R, R), R)
            cols = pl.ds(pl.multiple_of(p * PAIR, PAIR), PAIR)
            o, logs = attend_block(q_ref[at, cols], k_ref[:, cols], v_t[p], sv[i, 0:1, :],
                                   two_lanes(wide[...]))
            ah_ref[at, cols] = o.T.astype(b16)
            lse_ref[p, :, at] = jnp.concatenate(logs + [jnp.zeros((6, R), f32)], axis=0)
            for e, ev in enumerate(late):
                @pl.when(it == e + 1)
                def _():
                    ev()
            return carry
        lax.fori_loop(lo, hi, body, 0)

    run(0, n_it)
    half = L // 2
    mine = pl.ds(pl.multiple_of(me.c * half, half), half)
    theirs = pl.ds(pl.multiple_of((1 - me.c) * half, half), half)
    heads = pl.ds(pl.multiple_of(me.c * W, W), W)
    sends.go(ah_ref.at[theirs, :], ar_ref.at[:, heads], csem.at[0], me.dev(c=1 - me.c))
    ar_ref[:, heads] = ah_ref[mine, :]
    for e in late[n_it - 1:]:
        e()
    tok.out_done(*items[2])
    tok.out_end(*items[2])
    arrived(ar_ref.at[:, heads], csem.at[0], me)
    sends.finish(me)


def front(cfg, x, cot, seg, w1, w2):
    sizes, S, W, H, chunk = cfg
    F, C, T = sizes
    _, R, D = x.shape
    X = F // 2
    L = C * R
    n = T * H // chunk
    f32, b = jnp.float32, jnp.bfloat16
    dma = pltpu.SemaphoreType.DMA
    r = w1.shape[0]
    sds = jax.ShapeDtypeStruct
    v = pltpu.VMEM
    return pl.pallas_call(
        functools.partial(front_kernel, cfg),
        in_specs=[ANY] * 5,
        out_specs=[VM] * 6 + [ANY] * 5 + [VM] * 2,
        out_shape=[sds((L, W), b)] * 4 + [sds((L // 2, T * W), b), sds((W // PAIR, 8, L), f32),
                                          sds((C, R, D), b), sds((C // 2, R, D), b), sds((C, 8, R), f32),
                                          sds((T, X, 2, C, r, w1.shape[1]), b),
                                          sds((T, X, 2, C, r, w2.shape[1]), b),
                                          sds((8, D), f32), sds((n, 1, chunk), f32)],
        scratch_shapes=[v((R, D), b), v((8, R), f32), v((C, R, D), b), v((X, 2, C, r, w1.shape[1]), b),
                        v((T * F * C, r, VEC), b), v((C, 8, R), f32), v((L, 128), f32), v((W // PAIR, PAIR, L), b),
                        dma((2 * gather_count(sizes) + 1,)), dma((T * F * C,)), dma((T * F * C,)), dma((2,)),
                        dma((3, S + C // 2)), dma((3, C)), dma((3 + 3 * C,)), dma((3 + T * F * C,))],
        compiler_params=pltpu.CompilerParams(collective_id=0, has_side_effects=True,
                                             vmem_limit_bytes=60 * 2**20),
    )(x, cot, seg, w1, w2)


def take(vec, index, width):
    n = vec.shape[1]
    wide = jnp.broadcast_to(vec, (8, n))
    return pltpu.roll(wide, lax.rem(n - index * width, n), 1)[0:1, :max(128, -(-width // 128) * 128)]


def back_kernel(cfg, q_ref, k_ref, v_ref, ah_ref, lse_ref, sf_ref, do_ref, one_ref, res_ref, xf_ref, g1_ref,
                gff_ref, go_ref, gvec_ref, gub_ref,
                res_out, ing_out, oq_ref, oup_ref, odn_ref, oo_ref, vq_ref, vv_ref, vu_ref, vs_ref,
                doh, dqkv, k_t, wide, dk_sum, dv_sum, xt, xv, wv, gq, one_v, part, got_part, ing, ing_in,
                vec, vacc, vgot, *scr):
    sizes, S, W, H, chunk = cfg
    bf, bo, bq = scr[:7], scr[7:14], scr[14:21]
    ssem, rf, ro, rq, rv, lf, lo, lq, tss, trs, tls, csem = scr[21:]
    me = Place(sizes)
    C, X, T = me.C, me.X, me.T
    R, D = xv.shape[1:]
    L = C * R
    half = L // 2
    f32, b16 = jnp.float32, jnp.bfloat16
    me.greet(True)
    sends = Sends(ssem)
    tok = Tokens(me, S)
    J = H // chunk
    other = me.dev(c=1 - me.c)
    mine = pl.ds(pl.multiple_of(me.c * half, half), half)
    theirs = pl.ds(pl.multiple_of((1 - me.c) * half, half), half)
    heads = pl.ds(pl.multiple_of(me.c * W, W), W)
    their_heads = pl.ds(pl.multiple_of((1 - me.c) * W, W), W)

    sends.go(do_ref.at[:, their_heads], doh.at[mine, :], csem.at[0], other)
    loads = [(do_ref.at[:, heads], doh.at[mine, :]), (xf_ref, xv), (g1_ref.at[me.c], wv), (one_ref, one_v)]
    loads = [pltpu.make_async_copy(a, b, csem.at[2 + i]) for i, (a, b) in enumerate(loads)]
    for cp in loads:
        cp.start()
    res_item = (res_ref, res_out, tss.at[0], trs.at[0], tls.at[0])

    def put_ff(i, total):
        j, kind = i // 2, i % 2
        (oup_ref, odn_ref)[kind][:, j * chunk:(j + 1) * chunk] = total

    def put_o(i, total):
        oo_ref[...] = total

    def put_q(i, total):
        oq_ref[...] = total

    ef = reduce_events(me, gff_ref, False, bf, sends, rf, lf, put_ff)
    eo = reduce_events(me, go_ref, False, bo, sends, ro, lo, put_o)
    eq = reduce_events(me, gq, True, bq, sends, rq, lq, put_q)
    n_vec = vec.shape[0]
    evt = total_events(me, vec, (vacc, vgot), vec, sends, rv)
    ef[0]()
    eo[0]()
    spread_segments(sf_ref, wide)
    n_pairs = W // PAIR
    for p in range(n_pairs):
        k_t[p] = k_ref[:, p * PAIR:(p + 1) * PAIR].astype(f32).T.astype(b16)
    loads[0].wait()
    arrived(doh.at[theirs, :], csem.at[0], me)
    tok.back(*res_item)

    plan = []
    for a, b in zip(ef, eo):
        plan += [a, b]
    plan = plan[2:]
    n_it = n_pairs * C
    per = -(-len(plan) // n_it)

    def body(it, carry):
        p, i = it // C, lax.rem(it, C)
        at = pl.ds(pl.multiple_of(i * R, R), R)
        cols = pl.ds(pl.multiple_of(p * PAIR, PAIR), PAIR)
        dq, dk, dv = attend_back_block(q_ref[at, cols], k_ref[:, cols], k_t[p], v_ref[:, cols], doh[at, cols],
                                       ah_ref[at, cols], lse_ref[p, :, at], sf_ref[i, 0:1, :],
                                       two_lanes(wide[...]))
        dqkv[at, cols] = dq.astype(b16)

        @pl.when(i == 0)
        def _():
            dk_sum[...] = dk
            dv_sum[...] = dv

        @pl.when(i > 0)
        def _():
            dk_sum[...] += dk
            dv_sum[...] += dv

        @pl.when(i == C - 1)
        def _():
            dqkv[:, pl.ds(pl.multiple_of(W + p * PAIR, PAIR), PAIR)] = dk_sum[...].astype(b16)
            dqkv[:, pl.ds(pl.multiple_of(2 * W + p * PAIR, PAIR), PAIR)] = dv_sum[...].astype(b16)

        for n in range(n_it):
            evs = plan[n * per:(n + 1) * per]
            if evs:
                @pl.when(it == n)
                def _():
                    for e in evs:
                        e()
        return carry
    lax.fori_loop(0, n_it, body, 0)

    for cp in loads[1:]:
        cp.wait()
    for i in range(C):
        for j in range(0, R, 128):
            xt[:, i * R + j:i * R + j + 128] = xv[i, j:j + 128, :].astype(f32).T.astype(b16)
    r = gq.shape[4]
    step = D // (2 * X)

    def grads(i, carry):
        rows = pl.ds(pl.multiple_of(i * step, step), step)
        out = nn(xt[rows, :], dqkv[...]).astype(b16)
        gq[0, i // 2, lax.rem(i, 2)] = out.reshape(C, r, 3 * W)
        return carry
    lax.fori_loop(0, 2 * X, grads, 0)
    eq[0]()
    weights = wv[...].reshape(D, wv.shape[-1])[:, :3 * W]
    part[...] = nt(dqkv[theirs, :], weights).astype(b16)
    sends.go(part, got_part, csem.at[1], other)
    zeros = jnp.zeros((1, W), f32)
    ones = jnp.ones((8, L), b16)
    sums = nn(ones, dqkv[...])[0:1]
    first = me.c == 0
    place = lambda v: [jnp.where(first, v, zeros), jnp.where(first, zeros, v)]
    flat = place(sums[:, :W]) + place(sums[:, 2 * W:])
    flat += [jnp.sum(gub_ref[i], axis=0, keepdims=True) for i in range(T * J)]
    flat += [gvec_ref[i:i + 1, :] for i in range(6)]
    flat = jnp.concatenate(flat, axis=1)
    n_flat = flat.shape[1]
    for i in range(n_flat // 128):
        vec[i:i + 1, :] = flat[:, i * 128:(i + 1) * 128]
    if n_vec * 128 > n_flat:
        vec[n_flat // 128:, :] = jnp.zeros((n_vec - n_flat // 128, 128), f32)
    evt[0]()
    eq[1]()
    own = nt(dqkv[mine, :], weights)
    evt[1]()
    eq[2]()
    eq[3]()
    arrived(got_part, csem.at[1], me)
    for i in range(C // 2):
        at = slice(i * R, (i + 1) * R)
        ing[i] = (own[at] + got_part[at, :].astype(f32) + one_v[at, :]).astype(b16)
    ing_item = (ing, ing_in, tss.at[1], trs.at[1], tls.at[1])
    tok.back(*ing_item)
    evt[2]()
    eq[4]()
    eq[5]()
    evt[3]()
    for e in eq[6:]:
        e()
    for e in evt[4:]:
        e()
    tok.back_pass(*res_item)
    tok.back_pass(*ing_item)
    tok.back_end(*ing_item)
    for s in range(S):
        ing_out[s] = ing_in[s].astype(f32)
    tok.back_end(*res_item)
    total = jnp.concatenate([vec[i:i + 1, :] for i in range(n_flat // 128)], axis=1)
    fz = (2 * me.x + me.c) * C + me.z
    tfz = me.y * (X * 2 * C) + fz
    n_dev = T * X * 2 * C
    qw, uw = T * W // n_dev, T * H // n_dev
    vq_ref[...] = take(total[:, :T * W], tfz, qw)
    vv_ref[...] = take(total[:, T * W:2 * T * W], tfz, qw)
    vu_ref[...] = take(total[:, 2 * T * W:2 * T * W + T * H], tfz, uw)
    base = 2 * T * W + T * H
    for i in range(6):
        vs_ref[i:i + 1, :] = take(total[:, base + i * D:base + (i + 1) * D], fz, r)
    sends.finish(me)


def back(cfg, q, k, v, ah, lse, sf, do, one, res, xf, g1, gff, go, gvec, gub):
    sizes, S, W, H, chunk = cfg
    F, C, T = sizes
    X = F // 2
    _, R, D = xf.shape
    L = C * R
    J = H // chunk
    r = g1.shape[4]
    f32, b = jnp.float32, jnp.bfloat16
    dma = pltpu.SemaphoreType.DMA
    sds = jax.ShapeDtypeStruct
    vm = pltpu.VMEM
    steps = total_count(sizes)
    n_vec = -(-(2 * T * W + T * H + 6 * D) // 1024) * 8
    lanes = lambda w: max(128, -(-w // 128) * 128)
    n_dev = T * F * C
    sems = reduce_sems(sizes)
    return pl.pallas_call(
        functools.partial(back_kernel, cfg),
        in_specs=[VM] * 6 + [ANY] * 7 + [VM] * 2,
        out_specs=[ANY] + [VM] * 9,
        out_shape=[sds((S, R, D), b), sds((S, R, D), f32), sds((r, 3 * W), f32), sds((r, H), f32), sds((r, H), f32),
                   sds((r, W), f32), sds((1, lanes(T * W // n_dev)), f32), sds((1, lanes(T * W // n_dev)), f32),
                   sds((1, lanes(T * H // n_dev)), f32), sds((6, lanes(r)), f32)],
        scratch_shapes=[vm((L, W), b), vm((L, 3 * W), b), vm((W // PAIR, PAIR, L), b), vm((L, 128), f32),
                        vm((L, PAIR), f32), vm((L, PAIR), f32), vm((D, L), b), vm((C, R, D), b),
                        vm((X, 2, C, r, g1.shape[5]), b), vm((1, X, 2, C, r, 3 * W), b), vm((L // 2, D), f32),
                        vm((L // 2, D), b), vm((L // 2, D), b), vm((C // 2, R, D), b), vm((S, R, D), b),
                        vm((n_vec, 128), f32), vm((4, n_vec, 128), f32), vm((steps, n_vec, 128), f32)]
        + reduce_scratch(sizes, 2 * J, r, chunk, False) + reduce_scratch(sizes, 1, r, W, False)
        + reduce_scratch(sizes, 1, r, 3 * W, True)
        + [dma((2 * reduce_count(sizes, False) + reduce_count(sizes, True) + steps + 2,)),
           dma((sems,)), dma((sems,)), dma((sems,)), dma((steps,)), dma((T * X,)), dma((T * X,)), dma((X,)),
           dma((2, C // 2 + S)), dma((2, S)), dma((2,)), dma((6,))],
        compiler_params=pltpu.CompilerParams(collective_id=1, has_side_effects=True,
                                             vmem_limit_bytes=62 * 2**20),
    )(q, k, v, ah, lse, sf, do, one, res, xf, g1, gff, go, gvec, gub)


def chunk_of(H):
    for w in (512, 384, 256, 128):
        if H % w == 0:
            return w
    return H


def on_device(sizes, inputs, segments, cotangent, query_weight, key_weight, value_weight,
              output_weight, up_weight, down_weight, query_bias, value_bias, up_bias,
              output_bias, down_bias, first_gain, first_shift, second_gain, second_shift):
    F, C, T = sizes
    X = F // 2
    S, R, D = inputs.shape
    W = query_weight.shape[1]
    H = up_weight.shape[1]
    r = query_weight.shape[0]
    L = C * R
    half = L // 2
    chunk = chunk_of(H)
    J = H // chunk
    c = lax.rem(lax.axis_index("fsdp"), 2)
    f32 = jnp.float32
    small = jnp.concatenate([query_bias, value_bias, up_bias, output_bias, down_bias, first_gain,
                             first_shift, second_gain, second_shift])
    rows = -(-small.shape[0] // VEC)
    small = jnp.pad(small, (0, rows * VEC - small.shape[0])).reshape(rows, VEC)
    small = jnp.pad(small, ((0, r - rows), (0, 0)))
    w1 = jnp.concatenate([query_weight, key_weight, value_weight, small], axis=1)
    w2 = jnp.concatenate([up_weight, down_weight.T, output_weight.T], axis=1)
    seg = jnp.broadcast_to(segments.astype(f32)[:, None, :], (S, 8, R))
    cfg = (sizes, S, W, H, chunk)
    q, k, v, ah, ar, lse, xf, cf, sf, g1, g2, vec, ub = front(cfg, inputs, cotangent, seg, w1, w2)
    x_mine = lax.dynamic_slice(xf.reshape(L, D), (c * half, 0), (half, D))
    res, one, do, gff, go, gvec, gub = middle(
        T, x_mine, ar, cf.reshape(half, D), g2.reshape(T, D, -1), vec, ub, chunk)
    outs = back(cfg, q, k, v, ah, lse, sf, do, one, res.reshape(C // 2, R, D), xf, g1,
                gff.reshape(T, 2 * J, X, 2, C, r, chunk), go.reshape(T, 1, X, 2, C, r, W), gvec, gub)
    res_out, ing_out, oq, oup, odn, oo, vq, vv, vu, vs = outs
    qw, uw = query_bias.shape[0], up_bias.shape[0]
    return (res_out, ing_out, oq[:, :W], oq[:, W:2 * W], oq[:, 2 * W:], oo.T, oup, odn.T,
            vq[0, :qw], vv[0, :qw], vu[0, :uw]) + tuple(vs[i, :r] for i in range(6))


def solution(mesh):
    sizes = (mesh.shape["fsdp"], mesh.shape["ctx"], mesh.shape["tp"])
    every = ("fsdp", "ctx")
    rows, cols, one, three = P(every, "tp"), P("tp", every), P(every), P(("tp",) + every)
    token = P("fsdp", "ctx", None)
    weights = (rows, rows, rows, cols, rows, cols)
    vectors = (three, three, three) + (one,) * 6
    return jax.shard_map(
        functools.partial(on_device, sizes), mesh=mesh,
        in_specs=(token, P("fsdp", "ctx"), token) + weights + vectors,
        out_specs=(token, token) + weights + vectors, check_vma=False)
```

```python
import functools
import jax
import jax.numpy as jnp
from jax import lax
from jax.sharding import PartitionSpec as P
from jax.experimental import pallas as pl
from jax.experimental.pallas import tpu as pltpu

MESH = pl.DeviceIdType.MESH
ANY = pl.BlockSpec(memory_space=pl.ANY)
VM = pl.BlockSpec(memory_space=pltpu.VMEM)


class Place:
    def __init__(self, sizes):
        self.F, self.C, self.T = sizes
        self.X = self.F // 2
        f = lax.axis_index("fsdp")
        self.x = f // 2
        self.c = lax.rem(f, 2)
        self.z = lax.axis_index("ctx")
        self.y = lax.axis_index("tp")

    def dev(self, x=None, c=None, z=None, y=None):
        x = self.x if x is None else x
        c = self.c if c is None else c
        return (2 * x + c, self.z if z is None else z, self.y if y is None else y)

    def z_off(self, d):
        return lax.rem(self.z + d + self.C, self.C)

    def x_off(self, d):
        return lax.rem(self.x + d + self.X, self.X)

    def greet(self, chip_wide):
        bar = pltpu.get_barrier_semaphore()
        devs = [self.dev(c=1 - self.c), self.dev(y=1 - self.y)]
        devs += [self.dev(x=self.x_off(d)) for d in range(1, self.X)]
        for d in range(1, self.C):
            devs.append(self.dev(z=self.z_off(d)))
            if chip_wide:
                devs.append(self.dev(z=self.z_off(d), c=1 - self.c))
        for d in devs:
            pl.semaphore_signal(bar, inc=1, device_id=d, device_id_type=MESH)
        pl.semaphore_wait(bar, len(devs))


class Sends:
    def __init__(self, sems):
        self.sems, self.n, self.waits = sems, 0, []

    def go(self, src, dst, recv, dev, like=None, when=None):
        pltpu.make_async_remote_copy(
            src_ref=src, dst_ref=dst, send_sem=self.sems.at[self.n], recv_sem=recv,
            device_id=dev, device_id_type=MESH).start()
        self.n += 1
        self.waits.append((src if like is None else like, when))

    def finish(self, me):
        for n, (like, when) in enumerate(self.waits):
            def wait():
                pltpu.make_async_remote_copy(
                    src_ref=like, dst_ref=like, send_sem=self.sems.at[n], recv_sem=self.sems.at[n],
                    device_id=me.dev(c=1 - me.c), device_id_type=MESH).wait_send()
            given(when, wait)
        self.waits = []


def given(when, body):
    if when is None:
        body()
    else:
        pl.when(when())(body)


def arrived(dst, recv, pl_):
    pltpu.make_async_remote_copy(
        src_ref=dst, dst_ref=dst, send_sem=recv, recv_sem=recv,
        device_id=pl_.dev(c=1 - pl_.c), device_id_type=MESH).wait_recv()


def line_order(C, z):
    return [z] + [z + sign * k for k in range(1, C) for sign in (-1, 1) if 0 <= z + sign * k < C]


def pick(index, table):
    out = table[-1]
    for i in reversed(range(len(table) - 1)):
        out = jnp.where(index == i, table[i], out)
    return jnp.int32(out)


def gather_events(me, own, full, sends, recv, lsem):
    C, X = me.C, me.X
    sem = lambda t, x, c, z: recv.at[((t * X + x) * 2 + c) * C + z]
    slot = lambda t, x, c, z: full.at[t, x, c, z]
    like = slot(0, 0, 0, 0)
    orders = [line_order(C, z) for z in range(C)]
    where = lambda m: pick(me.z, [o[m] for o in orders])

    def push(src, at, dev, when=None):
        sends.go(src, slot(*at), sem(*at), dev, like, when)

    def wait(at):
        arrived(slot(*at), sem(*at), me)

    core, side = me.dev(c=1 - me.c), me.dev(y=1 - me.y)
    xs = [(me.x_off(d), me.dev(x=me.x_off(d))) for d in range(1, X)]
    local = pltpu.make_async_copy(own, slot(me.y, me.x, me.c, me.z), lsem)

    def along(m):
        def run():
            zz = where(m)
            at = (me.y, me.x, me.c, zz)
            src = slot(*at) if m else own
            if m:
                wait(at)
            for sign in (-1, 1):
                def onward(sign=sign):
                    zz = where(m)
                    return ((zz - me.z) * sign <= 0) & (me.z + sign >= 0) & (me.z + sign < C)

                @pl.when(onward())
                def _():
                    push(src, at, me.dev(z=me.z + sign), onward)
            for _, dev in xs:
                push(src, at, dev)
            push(src, at, side)
            push(src, at, core)
            if not m:
                local.start()
        return run

    def across(m):
        def run():
            zz = where(m)
            at = (1 - me.y, me.x, me.c, zz)
            wait(at)
            if m < C // 2:
                for _, dev in xs:
                    push(slot(*at), at, dev)
            push(slot(*at), at, core)
            for xo, _ in xs:
                at = (me.y, xo, me.c, zz)
                wait(at)
                if m >= C // 2:
                    push(slot(*at), at, side)
                push(slot(*at), at, core)
        return run

    def corner(m):
        def run():
            zz = where(m)
            for xo, _ in xs:
                at = (1 - me.y, xo, me.c, zz)
                wait(at)
                push(slot(*at), at, core)
        return run

    def last():
        for t in range(me.T):
            for xx in range(X):
                for zz in range(C):
                    wait((t, xx, 1 - me.c, zz))
        local.wait()

    steps = {"l": last}
    for m in range(C):
        steps["a%d" % m] = along(m)
        steps["x%d" % m] = across(m)
        steps["c%d" % m] = corner(m)
    return steps


def gather_count(sizes):
    F, C, T = sizes
    X = F // 2
    return C * (4 * X + 4)


class Tokens:
    def __init__(self, me, seqs):
        self.me, self.S = me, seqs
        self.half = me.C // 2
        self.lo = me.y * (me.C - seqs)
        self.busy = (me.z >= self.lo) & (me.z < self.lo + seqs)
        self.owner = me.c == me.y

    def out(self, src, dst, full, ssem, rsem, lsem):
        me, half = self.me, self.half
        k = me.z // half
        at = me.z if full else lax.rem(me.z, half)

        @pl.when(self.owner)
        def _():
            for s in range(self.S):
                here = (self.lo + s == me.z) & (k == me.c)

                @pl.when(here)
                def _():
                    pltpu.make_async_copy(src.at[s], dst.at[at], lsem).start()

                @pl.when(jnp.logical_not(here))
                def _():
                    pltpu.make_async_remote_copy(
                        src_ref=src.at[s], dst_ref=dst.at[at], send_sem=ssem.at[s],
                        recv_sem=rsem.at[lax.rem(me.z, half)],
                        device_id=me.dev(c=k, z=self.lo + s), device_id_type=MESH).start()

    def out_done(self, src, dst, full, ssem, rsem, lsem):
        me, half = self.me, self.half

        @pl.when(self.busy)
        def _():
            for i in range(half):
                zq = me.c * half + i
                at = zq if full else i
                here = (zq == me.z) & (me.c == me.y)

                @pl.when(here)
                def _():
                    pltpu.make_async_copy(src.at[0], dst.at[at], lsem).wait()

                @pl.when(jnp.logical_not(here))
                def _():
                    arrived(dst.at[at], rsem.at[i], me)

                if full:
                    pltpu.make_async_remote_copy(
                        src_ref=dst.at[at], dst_ref=dst.at[at], send_sem=ssem.at[self.S + i],
                        recv_sem=rsem.at[half + i], device_id=me.dev(c=1 - me.c),
                        device_id_type=MESH).start()

    def out_end(self, src, dst, full, ssem, rsem, lsem):
        me, half = self.me, self.half
        k = me.z // half

        @pl.when(self.owner)
        def _():
            for s in range(self.S):
                here = (self.lo + s == me.z) & (k == me.c)

                @pl.when(jnp.logical_not(here))
                def _():
                    pltpu.make_async_remote_copy(
                        src_ref=src.at[s], dst_ref=dst.at[0], send_sem=ssem.at[s],
                        recv_sem=rsem.at[0], device_id=me.dev(c=1 - me.c),
                        device_id_type=MESH).wait_send()

        if full:
            @pl.when(self.busy)
            def _():
                for i in range(half):
                    zq = (1 - me.c) * half + i
                    arrived(dst.at[zq], rsem.at[half + i], me)
                    pltpu.make_async_remote_copy(
                        src_ref=dst.at[0], dst_ref=dst.at[0], send_sem=ssem.at[self.S + i],
                        recv_sem=rsem.at[0], device_id=me.dev(c=1 - me.c),
                        device_id_type=MESH).wait_send()

    def back(self, src, dst, ssem, rsem, lsem):
        me, half = self.me, self.half

        @pl.when(self.busy)
        def _():
            for i in range(half):
                zq = me.c * half + i
                here = (zq == me.z) & (me.c == me.y)
                at = me.z - self.lo

                @pl.when(here)
                def _():
                    pltpu.make_async_copy(src.at[i], dst.at[at], lsem).start()

                @pl.when(jnp.logical_not(here))
                def _():
                    pltpu.make_async_remote_copy(
                        src_ref=src.at[i], dst_ref=dst.at[at], send_sem=ssem.at[i],
                        recv_sem=rsem.at[at], device_id=me.dev(c=me.y, z=zq),
                        device_id_type=MESH).start()

    def back_pass(self, src, dst, ssem, rsem, lsem):
        me, half = self.me, self.half
        k = me.z // half

        @pl.when(self.owner)
        def _():
            for s in range(self.S):
                here = (self.lo + s == me.z) & (k == me.c)

                @pl.when(here)
                def _():
                    pltpu.make_async_copy(src.at[0], dst.at[s], lsem).wait()

                @pl.when(jnp.logical_not(here))
                def _():
                    arrived(dst.at[s], rsem.at[s], me)

                pltpu.make_async_remote_copy(
                    src_ref=dst.at[s], dst_ref=dst.at[s], send_sem=ssem.at[half + s],
                    recv_sem=rsem.at[s], device_id=me.dev(y=1 - me.y),
                    device_id_type=MESH).start()

    def back_end(self, src, dst, ssem, rsem, lsem):
        me, half = self.me, self.half

        @pl.when(self.busy)
        def _():
            for i in range(half):
                zq = me.c * half + i
                here = (zq == me.z) & (me.c == me.y)

                @pl.when(jnp.logical_not(here))
                def _():
                    pltpu.make_async_remote_copy(
                        src_ref=src.at[i], dst_ref=dst.at[0], send_sem=ssem.at[i],
                        recv_sem=rsem.at[0], device_id=me.dev(c=1 - me.c),
                        device_id_type=MESH).wait_send()

        @pl.when(self.owner)
        def _():
            for s in range(self.S):
                pltpu.make_async_remote_copy(
                    src_ref=dst.at[s], dst_ref=dst.at[s], send_sem=ssem.at[half + s],
                    recv_sem=rsem.at[s], device_id=me.dev(y=1 - me.y),
                    device_id_type=MESH).wait_send()

        @pl.when(jnp.logical_not(self.owner))
        def _():
            for s in range(self.S):
                arrived(dst.at[s], rsem.at[s], me)


def reduce_events(me, grads, split, bufs, sends, recv, lsem, finish):
    acc, rc, xd, yd, xr, yr, zr = bufs
    C, X = me.C, me.X
    half = C // 2
    n_cols = acc.shape[2]
    like, like_all = acc.at[0, 0, :, 0], acc.at[0, 0]
    core, side = me.dev(c=1 - me.c), me.dev(y=1 - me.y)
    s_core = lambda t, x: recv.at[t * X + x]
    base = me.T * X
    s_d = lambda d, j: recv.at[base + (d - 1) * C + j]
    base2 = base + (X - 1) * C
    s_xr = lambda d, j: recv.at[base2 + (d - 1) * C + j]
    base3 = base2 + (X - 1) * C
    s_yr = lambda j: recv.at[base3 + j]
    s_zr = lambda j: recv.at[base3 + C + j]
    quads = ([(1 - me.y, me.x_off(d)) for d in range(1, X)] + [(1 - me.y, me.x)]
             + [(me.y, me.x_off(d)) for d in range(1, X)] + [(me.y, me.x)])
    locals_ = []

    def first():
        if split:
            for n, x in enumerate([me.x_off(d) for d in range(1, X)] + [me.x]):
                sends.go(grads.at[:, x, 1 - me.c], acc.at[me.c, x], s_core(me.c, x), core, like_all)
                cp = pltpu.make_async_copy(grads.at[:, x, me.c], acc.at[me.c, x], lsem.at[n])
                cp.start()
                locals_.append(cp)
        else:
            for n, (t, x) in enumerate(quads):
                sends.go(grads.at[t, :, x, 1 - me.c], rc.at[t, x], s_core(t, x), core, like_all)
                cp = pltpu.make_async_copy(grads.at[t, :, x, me.c], acc.at[t, x], lsem.at[n])
                cp.start()
                locals_.append(cp)

    def add(a, b):
        def body(i, carry):
            a[i] = a[i] + b[i]
            return carry
        lax.fori_loop(0, n_cols, body, 0)

    def ready(n):
        t, x = quads[n]
        if split:
            if n == 0:
                for cp in locals_:
                    cp.wait()
                for xo in [me.x_off(d) for d in range(1, X)] + [me.x]:
                    arrived(acc.at[1 - me.c, xo], s_core(1 - me.c, xo), me)
            return
        locals_[n].wait()
        arrived(rc.at[t, x], s_core(t, x), me)

        def body(i, carry):
            for z in range(C):
                acc[t, x, i, z] = acc[t, x, i, z] + rc[t, x, i, z]
            return carry
        lax.fori_loop(0, n_cols, body, 0)

    by_x = range(1, C)
    order = list(range(1, C)) + [0]

    def corner():
        for d in range(1, X):
            ready(d - 1)
            t, x = quads[d - 1]
            for j in order:
                zj = me.z_off(-j)
                if j in by_x:
                    sends.go(acc.at[t, x, :, zj], xd.at[d - 1, j], s_d(d, j), me.dev(x=x), like)
                else:
                    sends.go(acc.at[t, x, :, zj], yd.at[d - 1, j], s_d(d, j), side, like)

    def ready_sides():
        for n in range(X - 1, 2 * X - 1):
            ready(n)

    def spread(j):
        def run():
            zj = me.z_off(-j)
            t, x = me.y, me.x
            for d in range(1, X):
                xo = me.x_off(d)
                if j not in by_x:
                    arrived(yd.at[d - 1, j], s_d(d, j), me)
                    add(acc.at[t, xo, :, zj], yd.at[d - 1, j])
                sends.go(acc.at[t, xo, :, zj], xr.at[d - 1, j], s_xr(d, j), me.dev(x=xo), like)
            t = 1 - me.y
            for d in range(1, X):
                if j in by_x:
                    arrived(xd.at[d - 1, j], s_d(d, j), me)
                    add(acc.at[t, x, :, zj], xd.at[d - 1, j])
            sends.go(acc.at[t, x, :, zj], yr.at[j], s_yr(j), side, like)
        return run

    def to_z(j):
        def run():
            t, x = me.y, me.x
            zj = me.z_off(-j)
            for d in range(1, X):
                arrived(xr.at[d - 1, j], s_xr(d, j), me)
                add(acc.at[t, x, :, zj], xr.at[d - 1, j])
            arrived(yr.at[j], s_yr(j), me)
            add(acc.at[t, x, :, zj], yr.at[j])
            if j:
                sends.go(acc.at[t, x, :, zj], zr.at[j - 1], s_zr(j - 1), me.dev(z=zj), like)
        return run

    def last():
        for j in range(1, C):
            arrived(zr.at[j - 1], s_zr(j - 1), me)
        for i in range(n_cols):
            total = acc[me.y, me.x, i, me.z].astype(jnp.float32)
            for j in range(1, C):
                total = total + zr[j - 1, i].astype(jnp.float32)
            finish(i, total)

    steps = {"f": first, "d": corner, "r": ready_sides, "o": lambda: ready(2 * X - 1), "l": last}
    for j in range(C):
        steps["s%d" % j] = spread(j)
        steps["z%d" % j] = to_z(j)
    return steps


def reduce_scratch(sizes, n, r, w, split):
    F, C, T = sizes
    X = F // 2
    half = C // 2
    v = lambda shape: pltpu.VMEM(shape, jnp.bfloat16)
    return [v((T, X, n, C, r, w)), v((1, 1, 1, 1, 16, 128) if split else (T, X, n, C, r, w)),
            v((X - 1, C, n, r, w)), v((X - 1, C, n, r, w)), v((X - 1, C, n, r, w)),
            v((C, n, r, w)), v((C - 1, n, r, w))]


def reduce_sems(sizes):
    F, C, T = sizes
    X = F // 2
    return T * X + 2 * (X - 1) * C + 2 * C


def reduce_count(sizes, split):
    F, C, T = sizes
    X = F // 2
    return (X if split else T * X) + 2 * (X - 1) * C + C + C - 1


def total_events(me, own, bufs, out, sends, recv):
    C, X = me.C, me.X
    acc, got = bufs
    groups = [[me.dev(c=1 - me.c)], [me.dev(x=me.x_off(d)) for d in range(1, X)],
              [me.dev(y=1 - me.y)], [me.dev(z=me.z_off(d)) for d in range(1, C)]]
    like = acc.at[0]
    bases = [sum(len(g) for g in groups[:i]) for i in range(len(groups))]

    def start(gi):
        for i, dev in enumerate(groups[gi]):
            sends.go(acc.at[gi], got.at[bases[gi] + i], recv.at[bases[gi] + i], dev, like)

    def first():
        acc[0] = own[...]
        start(0)

    steps = {"0": first}
    for gi in range(len(groups)):
        def step(gi=gi):
            total = acc[gi]
            for i in range(len(groups[gi])):
                arrived(got.at[bases[gi] + i], recv.at[bases[gi] + i], me)
                total = total + got[bases[gi] + i]
            if gi + 1 < len(groups):
                acc[gi + 1] = total
                start(gi + 1)
            else:
                out[...] = total
        steps[str(gi + 1)] = step
    return steps


def total_count(sizes):
    F, C, T = sizes
    return 1 + F // 2 - 1 + 1 + C - 1

HEAD = 64
PAIR = 2 * HEAD
SCALE = HEAD ** (-0.5)
norm_eps = 1e-12
masked_score = -1000000000.0


def nt(a, b):
    return lax.dot_general(a, b, (((1,), (1,)), ((), ())), preferred_element_type=jnp.float32)


def nn(a, b):
    return lax.dot_general(a, b, (((1,), (0,)), ((), ())), preferred_element_type=jnp.float32)


def spread_segments(seg_ref, wide):
    C, _, R = seg_ref.shape
    for i in range(C):
        for j in range(0, R, 128):
            row = jnp.broadcast_to(seg_ref[i, 0:1, j:j + 128], (128, 128))
            wide[i * R + j:i * R + j + 128, :] = row.T


def lanes_of(h, like):
    lane = lax.broadcasted_iota(jnp.int32, like.shape, like.ndim - 1)
    return jnp.where(lane // HEAD == h, like, jnp.zeros_like(like))


def two_lanes(wide):
    return jnp.concatenate([wide, wide], axis=1)


def attend_block(q, k, v_t, seg_q, seg_k):
    same = seg_k == seg_q
    outs, logs = [], []
    for h in range(2):
        s = nt(k, lanes_of(h, q) * jnp.bfloat16(SCALE))
        s = jnp.where(same, s, masked_score)
        peak = jnp.max(s, axis=0, keepdims=True)
        e = jnp.exp(s - peak)
        total = jnp.sum(e, axis=0, keepdims=True)
        o = nn(v_t, e.astype(jnp.bfloat16))
        outs.append(o[h * HEAD:(h + 1) * HEAD] * (1.0 / total))
        logs.append(peak + jnp.log(total))
    return jnp.concatenate(outs, axis=0), logs


def attend_kernel(q_ref, k_ref, v_ref, seg_ref, o_ref, lse_ref, wide, v_t):
    i = pl.program_id(1)

    @pl.when((pl.program_id(0) == 0) & (i == 0))
    def _():
        spread_segments(seg_ref, wide)

    @pl.when(i == 0)
    def _():
        v_t[...] = v_ref[...].astype(jnp.float32).T.astype(jnp.bfloat16)

    seg_q = seg_ref[i, 0:1, :]
    o, logs = attend_block(q_ref[...], k_ref[...], v_t[...], seg_q, two_lanes(wide[...]))
    o_ref[...] = o.T.astype(jnp.bfloat16)
    lse_ref[0] = jnp.concatenate(logs + [jnp.zeros((6, logs[0].shape[1]), jnp.float32)], axis=0)


def attend(q, k, v, seg):
    L, W = q.shape
    C, _, R = seg.shape
    n = W // PAIR
    return pl.pallas_call(
        attend_kernel,
        grid=(n, C),
        in_specs=[pl.BlockSpec((R, PAIR), lambda p, i: (i, p)),
                  pl.BlockSpec((L, PAIR), lambda p, i: (0, p)),
                  pl.BlockSpec((L, PAIR), lambda p, i: (0, p)),
                  pl.BlockSpec((C, 8, R), lambda p, i: (0, 0, 0))],
        out_specs=[pl.BlockSpec((R, PAIR), lambda p, i: (i, p)),
                   pl.BlockSpec((1, 8, R), lambda p, i: (p, 0, i))],
        out_shape=[jax.ShapeDtypeStruct((L, W), jnp.bfloat16),
                   jax.ShapeDtypeStruct((n, 8, L), jnp.float32)],
        scratch_shapes=[pltpu.VMEM((L, 128), jnp.float32), pltpu.VMEM((PAIR, L), jnp.bfloat16)],
        compiler_params=pltpu.CompilerParams(vmem_limit_bytes=56 * 2**20),
    )(q, k, v, seg)


def attend_back_block(q, k, k_t, v, do, o, lse, seg_q, seg_k):
    same = seg_k == seg_q
    prod = (do.astype(jnp.float32) * o.astype(jnp.float32)).T
    dq, dk, dv = [], None, None
    for h in range(2):
        qh = lanes_of(h, q) * jnp.bfloat16(SCALE)
        doh = lanes_of(h, do)
        s = nt(k, qh)
        p = jnp.exp(jnp.where(same, s, masked_score) - lse[h:h + 1])
        dp = nt(v, doh)
        inner = jnp.sum(prod[h * HEAD:(h + 1) * HEAD], axis=0, keepdims=True)
        ds = (p * (dp - inner)).astype(jnp.bfloat16)
        dv_h = nn(p.astype(jnp.bfloat16), doh)
        dk_h = nn(ds, qh)
        dv = dv_h if dv is None else dv + dv_h
        dk = dk_h if dk is None else dk + dk_h
        dq.append(nn(k_t, ds)[h * HEAD:(h + 1) * HEAD])
    return jnp.concatenate(dq, axis=0).T * SCALE, dk, dv


def attend_back_kernel(q_ref, k_ref, v_ref, do_ref, o_ref, lse_ref, seg_ref,
                       dq_ref, dk_ref, dv_ref, wide, k_t, dk_sum, dv_sum):
    i = pl.program_id(1)

    @pl.when((pl.program_id(0) == 0) & (i == 0))
    def _():
        spread_segments(seg_ref, wide)

    @pl.when(i == 0)
    def _():
        k_t[...] = k_ref[...].astype(jnp.float32).T.astype(jnp.bfloat16)

    seg_q = seg_ref[i, 0:1, :]
    dq, dk, dv = attend_back_block(q_ref[...], k_ref[...], k_t[...], v_ref[...], do_ref[...],
                                   o_ref[...], lse_ref[0], seg_q, two_lanes(wide[...]))
    dq_ref[...] = dq.astype(jnp.bfloat16)

    @pl.when(i == 0)
    def _():
        dk_sum[...] = dk
        dv_sum[...] = dv

    @pl.when(i > 0)
    def _():
        dk_sum[...] += dk
        dv_sum[...] += dv

    @pl.when(i == pl.num_programs(1) - 1)
    def _():
        dk_ref[...] = dk_sum[...].astype(jnp.bfloat16)
        dv_ref[...] = dv_sum[...].astype(jnp.bfloat16)


def attend_back(q, k, v, do, o, lse, seg):
    L, W = q.shape
    C, _, R = seg.shape
    n = W // PAIR
    row = pl.BlockSpec((R, PAIR), lambda p, i: (i, p))
    all_rows = pl.BlockSpec((L, PAIR), lambda p, i: (0, p))
    b = jax.ShapeDtypeStruct((L, W), jnp.bfloat16)
    return pl.pallas_call(
        attend_back_kernel,
        grid=(n, C),
        in_specs=[row, all_rows, all_rows, row, row,
                  pl.BlockSpec((1, 8, R), lambda p, i: (p, 0, i)),
                  pl.BlockSpec((C, 8, R), lambda p, i: (0, 0, 0))],
        out_specs=[row, all_rows, all_rows],
        out_shape=[b, b, b],
        scratch_shapes=[pltpu.VMEM((L, 128), jnp.float32), pltpu.VMEM((PAIR, L), jnp.bfloat16),
                        pltpu.VMEM((L, PAIR), jnp.float32), pltpu.VMEM((L, PAIR), jnp.float32)],
        compiler_params=pltpu.CompilerParams(vmem_limit_bytes=56 * 2**20),
    )(q, k, v, do, o, lse, seg)


STRIP = 64


def strips(rows, body):
    def step(i, carry):
        body(pl.ds(pl.multiple_of(i * STRIP, STRIP), STRIP))
        return carry
    lax.fori_loop(0, rows // STRIP, step, 0)


def fold(value):
    total = value[0:8]
    for i in range(8, value.shape[0], 8):
        total = total + value[i:i + 8]
    return total


def mean(value):
    return jnp.mean(value, axis=-1, keepdims=True)


def unit_of(value):
    centred = value - mean(value)
    factor = lax.rsqrt(mean(centred * centred) + norm_eps)
    return centred * factor, factor


def back_of(upstream, unit, factor, gain):
    along = upstream * gain
    return factor * (along - mean(along) - unit * mean(along * unit))


def flip(ref, out):
    rows = ref.shape[0]
    for i in range(0, rows, 128):
        out[:, i:i + 128] = ref[i:i + 128, :].astype(jnp.float32).T.astype(jnp.bfloat16)


def middle_kernel(T, J, x_ref, att_ref, cot_ref, wu_ref, wd_ref, wo_ref, vec_ref, ub_ref,
                  res_ref, one_ref, do_ref, gff_ref, go_ref, gvec_ref, gub_ref,
                  unit, mixed, fac, low, low_t, acc, two, fl, fl_t, hid, act, slope, hl, sums):
    s = pl.program_id(0)
    n = T * J
    rows, D = x_ref.shape
    W = wo_ref.shape[2]
    f32, b16 = jnp.float32, jnp.bfloat16
    row = lambda i: vec_ref[i:i + 1, :]

    @pl.when(s == 0)
    def _():
        for t in range(T):
            part = nt(att_ref[:, t * W:(t + 1) * W], wo_ref[t])
            acc[...] = part if t == 0 else acc[...] + part

        def body(at):
            u, factor = unit_of(x_ref[at, :].astype(f32) + acc[at, :] + row(0))
            m = u * row(2) + row(3)
            unit[at, :] = u
            fac[at, :] = jnp.broadcast_to(factor, (STRIP, 128))
            mixed[at, :] = m
            low[at, :] = m.astype(b16)
            acc[at, :] = jnp.zeros((STRIP, D), f32)
        strips(rows, body)
        flip(low, low_t)

    @pl.when(s < n)
    def _():
        hid[...] = nn(low[...], wu_ref[0])

        def body(at):
            h = hid[at, :] + ub_ref[0]
            phi = 0.5 + 0.5 * lax.erf(h * (0.5 ** 0.5))
            dens = jnp.exp(-0.5 * h * h) * 0.3989422804014327
            act[s, at, :] = (h * phi).astype(b16)
            slope[s, at, :] = phi + h * dens
        strips(rows, body)
        acc[...] += nt(act[s], wd_ref[0])

    @pl.when(s == n)
    def _():
        sums[...] = jnp.zeros_like(sums)

        def body(at):
            u, factor = unit_of(mixed[at, :] + acc[at, :] + row(1))
            res_ref[at, :] = (u * row(4) + row(5)).astype(b16)
            g = cot_ref[at, :].astype(f32)
            g2 = back_of(g, u, factor, row(4))
            l2 = g2.astype(b16)
            fl[at, :] = l2
            acc[at, :] = g2
            sums[1] += fold(l2.astype(f32))
            sums[4] += fold(g * u)
            sums[5] += fold(g)
        strips(rows, body)
        flip(fl, fl_t)

    @pl.when(s >= n)
    def _():
        j = 2 * n - 1 - s
        hid[...] = nn(fl[...], wd_ref[0])
        gub_ref[0] = jnp.zeros_like(gub_ref[0])

        def body(at):
            v = (hid[at, :] * slope[j, at, :]).astype(b16)
            hl[at, :] = v
            gub_ref[0] += fold(v.astype(f32))
        strips(rows, body)
        acc[...] += nt(hl[...], wu_ref[0])
        gff_ref[0, 0, 0] = nn(low_t[...], hl[...]).astype(b16)
        gff_ref[0, 0, 1] = nn(fl_t[...], act[j]).astype(b16)

    @pl.when(s == 2 * n - 1)
    def _():
        def body(at):
            g = acc[at, :]
            u = unit[at, :]
            g1 = back_of(g, u, fac[at, 0:1], row(2))
            one_ref[at, :] = g1
            l1 = g1.astype(b16)
            fl[at, :] = l1
            sums[0] += fold(l1.astype(f32))
            sums[2] += fold(g * u)
            sums[3] += fold(g)
        strips(rows, body)
        flip(fl, fl_t)
        for t in range(T):
            go_ref[t] = nn(fl_t[...], att_ref[:, t * W:(t + 1) * W]).astype(b16)
            do_ref[:, t * W:(t + 1) * W] = nn(fl[...], wo_ref[t]).astype(b16)
        for i in range(6):
            gvec_ref[i:i + 1, :] = jnp.sum(sums[i], axis=0, keepdims=True)


def middle(T, x, att, cot, w2, vec, ub, chunk):
    rows, D = x.shape
    W = att.shape[1] // T
    J = ub.shape[0] // T
    H = J * chunk
    n = T * J
    f32, b16 = jnp.float32, jnp.bfloat16
    which = lambda s: jnp.where(s < n, s, 2 * n - 1 - s)
    whole = lambda shape: pl.BlockSpec(shape, lambda s: (0,) * len(shape), pipeline_mode=pl.Buffered(1))
    up = pl.BlockSpec((1, D, chunk), lambda s: (which(s) // J, 0, lax.rem(which(s), J)))
    down = pl.BlockSpec((1, D, chunk), lambda s: (which(s) // J, 0, J + lax.rem(which(s), J)))
    wo = pl.BlockSpec((T, D, W), lambda s: (0, 0, 2 * H // W), pipeline_mode=pl.Buffered(1))
    late = lambda s: jnp.where(s < n, n - 1, 2 * n - 1 - s)
    return pl.pallas_call(
        functools.partial(middle_kernel, T, J),
        grid=(2 * n,),
        in_specs=[whole((rows, D)), whole((rows, T * W)), whole((rows, D)), up, down, wo, whole(vec.shape),
                  pl.BlockSpec((1, 1, chunk), lambda s: (which(s), 0, 0))],
        out_specs=[whole((rows, D)), whole((rows, D)), whole((rows, T * W)),
                   pl.BlockSpec((1, 1, 2, D, chunk), lambda s: (late(s) // J, lax.rem(late(s), J), 0, 0, 0)),
                   whole((T, D, W)), whole((8, D)),
                   pl.BlockSpec((1, 8, chunk), lambda s: (late(s), 0, 0))],
        out_shape=[jax.ShapeDtypeStruct((rows, D), b16), jax.ShapeDtypeStruct((rows, D), f32),
                   jax.ShapeDtypeStruct((rows, T * W), b16), jax.ShapeDtypeStruct((T, J, 2, D, chunk), b16),
                   jax.ShapeDtypeStruct((T, D, W), b16), jax.ShapeDtypeStruct((8, D), f32),
                   jax.ShapeDtypeStruct((n, 8, chunk), f32)],
        scratch_shapes=[pltpu.VMEM((rows, D), f32), pltpu.VMEM((rows, D), f32), pltpu.VMEM((rows, 128), f32),
                        pltpu.VMEM((rows, D), b16), pltpu.VMEM((D, rows), b16), pltpu.VMEM((rows, D), f32),
                        pltpu.VMEM((8, 128), f32), pltpu.VMEM((rows, D), b16), pltpu.VMEM((D, rows), b16),
                        pltpu.VMEM((rows, chunk), f32), pltpu.VMEM((n, rows, chunk), b16),
                        pltpu.VMEM((n, rows, chunk), f32), pltpu.VMEM((rows, chunk), b16),
                        pltpu.VMEM((6, 8, D), f32)],
        compiler_params=pltpu.CompilerParams(vmem_limit_bytes=60 * 2**20),
    )(x, att, cot, w2, w2, w2, vec, ub)


VEC = 128


def spread_pieces(blocks, width, first, total):
    n, lanes = blocks.shape
    i = lax.broadcasted_iota(jnp.int32, (lanes, total), 0)
    col = lax.broadcasted_iota(jnp.int32, (lanes, total), 1)
    pick = jnp.where(i - first == lax.rem(col, width), 1.0, 0.0).astype(jnp.bfloat16)
    wide = nn(blocks, pick)
    dev = lax.broadcasted_iota(jnp.int32, (n, total), 0)
    col = lax.broadcasted_iota(jnp.int32, (n, total), 1)
    return jnp.sum(jnp.where(dev == col // width, wide, 0.0), axis=0, keepdims=True)


def front_kernel(cfg, x_ref, cot_ref, seg_ref, w1_ref, w2_ref,
                 q_ref, k_ref, v_ref, ah_ref, ar_ref, lse_ref, xf_ref, cf_ref, sf_ref, g1_ref, g2_ref,
                 vec_ref, ub_ref,
                 zero, zseg, xv, wv, pv, sv, wide, v_t,
                 ssem, r1, r2, lsem, tss, trs, tls, csem):
    sizes, S, W, H, chunk = cfg
    me = Place(sizes)
    C, X, T = me.C, me.X, me.T
    R, D = xv.shape[1:]
    r = wv.shape[3]
    L = C * R
    f32, b16 = jnp.float32, jnp.bfloat16
    me.greet(True)
    sends = Sends(ssem)
    tok = Tokens(me, S)
    items = [(x_ref, xf_ref, True, tss.at[0], trs.at[0], tls.at[0]),
             (seg_ref, sf_ref, True, tss.at[1], trs.at[1], tls.at[1]),
             (cot_ref, cf_ref, False, tss.at[2], trs.at[2], tls.at[2])]
    idle = jnp.logical_not(tok.busy)
    fills = ([(zero, xf_ref.at[i]) for i in range(C)] + [(zseg, sf_ref.at[i]) for i in range(C)]
             + [(zero, cf_ref.at[i]) for i in range(C // 2)])

    @pl.when(idle)
    def _():
        zero[...] = jnp.zeros_like(zero)
        zseg[...] = jnp.zeros_like(zseg)
        for i, (a, b) in enumerate(fills):
            pltpu.make_async_copy(a, b, tls.at[3 + i]).start()

    steps = {}
    for group, w_ref, g_ref, recv, n in (("1", w1_ref, g1_ref, r1, 0), ("2", w2_ref, g2_ref, r2, 1)):
        for name, step in gather_events(me, w_ref, g_ref, sends, recv, lsem.at[n]).items():
            steps[group + name] = step
    half = L // 2

    def each(f, its):
        return lambda: [f(*it) for it in its]

    for name, its in (("X", items[:2]), ("C", items[2:])):
        steps[name + "o"] = each(tok.out, its)
        steps[name + "w"] = each(tok.out_done, its)
        steps[name + "e"] = each(tok.out_end, its)

    def filled():
        @pl.when(idle)
        def _():
            for i, (a, b) in enumerate(fills):
                pltpu.make_async_copy(a, b, tls.at[3 + i]).wait()
    steps["filled"] = filled

    loads = [(xf_ref, xv), (sf_ref, sv), (g1_ref.at[me.c], wv)]
    pieces = [(g1_ref.at[t, xx, cc, zz, :, pl.ds(3 * W, VEC)], pv.at[((t * X + xx) * 2 + cc) * C + zz])
              for t in range(T) for xx in range(X) for cc in range(2) for zz in range(C)]
    loads = [pltpu.make_async_copy(a, b, csem.at[i]) for i, (a, b) in enumerate(loads + pieces)]

    def load():
        for cp in loads:
            cp.start()
    steps["load"] = load

    def vectors():
        for cp in loads:
            cp.wait()
        per = pv.shape[1]
        blocks = jnp.concatenate([pv[:, i, :] for i in range(min(per, 4))], axis=1)
        n_dev = blocks.shape[0]
        qw, uw = T * W // n_dev, T * H // n_dev
        qb = spread_pieces(blocks, qw, 0, T * W)
        vb = spread_pieces(blocks, qw, qw, T * W)
        ub = spread_pieces(blocks, uw, 2 * qw, T * H)
        for i in range(T * H // chunk):
            ub_ref[i] = ub[:, i * chunk:(i + 1) * chunk]
        once = blocks[:n_dev // T]
        for i in range(6):
            vec_ref[i:i + 1, :] = spread_pieces(once, r, 2 * qw + uw + i * r, D)
        first = me.c == 0
        vec_ref[6:7, :W] = jnp.where(first, qb[:, :W], qb[:, W:])
        vec_ref[7:8, :W] = jnp.where(first, vb[:, :W], vb[:, W:])
    steps["vectors"] = vectors

    def project():
        weights = wv[...].reshape(D, wv.shape[-1])

        def body(i, carry):
            at = pl.ds(pl.multiple_of(i * R, R), R)
            out = nn(xv[i], weights[:, :3 * W])
            q_ref[at, :] = (out[:, :W] + vec_ref[6:7, :W]).astype(b16)
            k_ref[at, :] = out[:, W:2 * W].astype(b16)
            v_ref[at, :] = (out[:, 2 * W:] + vec_ref[7:8, :W]).astype(b16)
            return carry
        lax.fori_loop(0, C, body, 0)
    steps["project"] = project

    def ready():
        spread_segments(sv, wide)
        for p in range(W // PAIR):
            v_t[p] = v_ref[:, p * PAIR:(p + 1) * PAIR].astype(f32).T.astype(b16)
    steps["ready"] = ready

    def attention(late):
        def body(it, carry):
            p, i = it // C, lax.rem(it, C)
            at = pl.ds(pl.multiple_of(i * R, R), R)
            cols = pl.ds(pl.multiple_of(p * PAIR, PAIR), PAIR)
            o, logs = attend_block(q_ref[at, cols], k_ref[:, cols], v_t[p], sv[i, 0:1, :],
                                   two_lanes(wide[...]))
            ah_ref[at, cols] = o.T.astype(b16)
            lse_ref[p, :, at] = jnp.concatenate(logs + [jnp.zeros((6, R), f32)], axis=0)
            for n, names in enumerate(late):
                if names:
                    @pl.when(it == n)
                    def _():
                        for name in names:
                            steps[name]()
            return carry
        lax.fori_loop(0, W // PAIR * C, body, 0)

    mine = pl.ds(pl.multiple_of(me.c * half, half), half)
    theirs = pl.ds(pl.multiple_of((1 - me.c) * half, half), half)
    heads = pl.ds(pl.multiple_of(me.c * W, W), W)

    def swap():
        sends.go(ah_ref.at[theirs, :], ar_ref.at[:, heads], csem.at[len(loads)], me.dev(c=1 - me.c))
        ar_ref[:, heads] = ah_ref[mine, :]
    steps["swap"] = swap
    early, late, end = FRONT_PLAN
    for name in early:
        steps[name]()
    attention(late)
    for name in end:
        steps[name]()
    arrived(ar_ref.at[:, heads], csem.at[len(loads)], me)
    sends.finish(me)


FRONT_PLAN = (
    ('1a0', '1a1', '1a2', '1a3', '1x0', '2a0', '1x1', '2a1', '1x2', '2a2', 'Xo', '1x3', '2a3', '1c0', '2x0',
     '1c1', '2x1', '1c2', '1c3', 'Xw', '1l', 'Xe', 'filled', 'load', '2x2', 'vectors', 'project', 'ready'),
    (('2x3',), (), ('Co',), ('2c0',), (), ('2c1',), (), ('2c2',), ('2c3',)),
    ('swap', '2l', 'Cw', 'Ce'),
)


def front(cfg, x, cot, seg, w1, w2):
    sizes, S, W, H, chunk = cfg
    F, C, T = sizes
    _, R, D = x.shape
    X = F // 2
    L = C * R
    n = T * H // chunk
    f32, b = jnp.float32, jnp.bfloat16
    dma = pltpu.SemaphoreType.DMA
    r = w1.shape[0]
    sds = jax.ShapeDtypeStruct
    v = pltpu.VMEM
    return pl.pallas_call(
        functools.partial(front_kernel, cfg),
        in_specs=[ANY] * 5,
        out_specs=[VM] * 6 + [ANY] * 5 + [VM] * 2,
        out_shape=[sds((L, W), b)] * 4 + [sds((L // 2, T * W), b), sds((W // PAIR, 8, L), f32),
                                          sds((C, R, D), b), sds((C // 2, R, D), b), sds((C, 8, R), f32),
                                          sds((T, X, 2, C, r, w1.shape[1]), b),
                                          sds((T, X, 2, C, r, w2.shape[1]), b),
                                          sds((8, D), f32), sds((n, 1, chunk), f32)],
        scratch_shapes=[v((R, D), b), v((8, R), f32), v((C, R, D), b), v((X, 2, C, r, w1.shape[1]), b),
                        v((T * F * C, r, VEC), b), v((C, 8, R), f32), v((L, 128), f32), v((W // PAIR, PAIR, L), b),
                        dma((2 * gather_count(sizes) + 1,)), dma((T * F * C,)), dma((T * F * C,)), dma((2,)),
                        dma((3, S + C // 2)), dma((3, C)), dma((3 + 3 * C,)), dma((4 + T * F * C,))],
        compiler_params=pltpu.CompilerParams(collective_id=0, has_side_effects=True,
                                             vmem_limit_bytes=60 * 2**20),
    )(x, cot, seg, w1, w2)


def take(vec, index, width):
    n = vec.shape[1]
    wide = jnp.broadcast_to(vec, (8, n))
    return pltpu.roll(wide, lax.rem(n - index * width, n), 1)[0:1, :max(128, -(-width // 128) * 128)]


def back_kernel(cfg, q_ref, k_ref, v_ref, ah_ref, lse_ref, sf_ref, do_ref, one_ref, res_ref, xf_ref, g1_ref,
                gff_ref, go_ref, gvec_ref, gub_ref,
                res_out, ing_out, oq_ref, oup_ref, odn_ref, oo_ref, vq_ref, vv_ref, vu_ref, vs_ref,
                doh, dqkv, k_t, wide, dk_sum, dv_sum, xt, xv, wv, gq, one_v, part, got_part, ing, ing_in,
                vec, vacc, vgot, *scr):
    sizes, S, W, H, chunk = cfg
    bf, bo, bq = scr[:7], scr[7:14], scr[14:21]
    ssem, rf, ro, rq, rv, lf, lo, lq, tss, trs, tls, csem = scr[21:]
    me = Place(sizes)
    C, X, T = me.C, me.X, me.T
    R, D = xv.shape[1:]
    L = C * R
    half = L // 2
    f32, b16 = jnp.float32, jnp.bfloat16
    me.greet(True)
    sends = Sends(ssem)
    tok = Tokens(me, S)
    J = H // chunk
    other = me.dev(c=1 - me.c)
    mine = pl.ds(pl.multiple_of(me.c * half, half), half)
    theirs = pl.ds(pl.multiple_of((1 - me.c) * half, half), half)
    heads = pl.ds(pl.multiple_of(me.c * W, W), W)
    their_heads = pl.ds(pl.multiple_of((1 - me.c) * W, W), W)

    sends.go(do_ref.at[:, their_heads], doh.at[mine, :], csem.at[0], other)
    loads = [(do_ref.at[:, heads], doh.at[mine, :]), (xf_ref, xv), (g1_ref.at[me.c], wv), (one_ref, one_v)]
    loads = [pltpu.make_async_copy(a, b, csem.at[2 + i]) for i, (a, b) in enumerate(loads)]
    for cp in loads:
        cp.start()
    def put_ff(i, total):
        j, kind = i // 2, i % 2
        (oup_ref, odn_ref)[kind][:, j * chunk:(j + 1) * chunk] = total

    def put_o(i, total):
        oo_ref[...] = total

    def put_q(i, total):
        oq_ref[...] = total

    steps = {}
    for name, group in (("f", reduce_events(me, gff_ref, False, bf, sends, rf, lf, put_ff)),
                        ("o", reduce_events(me, go_ref, False, bo, sends, ro, lo, put_o)),
                        ("q", reduce_events(me, gq, True, bq, sends, rq, lq, put_q)),
                        ("t", total_events(me, vec, (vacc, vgot), vec, sends, rv))):
        for key, step in group.items():
            steps[name + key] = step
    n_vec = vec.shape[0]
    n_pairs = W // PAIR
    r = gq.shape[4]
    res_item = (res_ref, res_out, tss.at[0], trs.at[0], tls.at[0])
    ing_item = (ing, ing_in, tss.at[1], trs.at[1], tls.at[1])
    for name, item in (("R", res_item), ("I", ing_item)):
        steps[name + "o"] = lambda item=item: tok.back(*item)
        steps[name + "p"] = lambda item=item: tok.back_pass(*item)
        steps[name + "e"] = lambda item=item: tok.back_end(*item)

    def keys():
        spread_segments(sf_ref, wide)
        for p in range(n_pairs):
            k_t[p] = k_ref[:, p * PAIR:(p + 1) * PAIR].astype(f32).T.astype(b16)
    steps["keys"] = keys

    def upstream():
        loads[0].wait()
        arrived(doh.at[theirs, :], csem.at[0], me)
    steps["upstream"] = upstream

    def attention(late):
        def body(it, carry):
            p, i = it // C, lax.rem(it, C)
            at = pl.ds(pl.multiple_of(i * R, R), R)
            cols = pl.ds(pl.multiple_of(p * PAIR, PAIR), PAIR)
            dq, dk, dv = attend_back_block(q_ref[at, cols], k_ref[:, cols], k_t[p], v_ref[:, cols], doh[at, cols],
                                           ah_ref[at, cols], lse_ref[p, :, at], sf_ref[i, 0:1, :],
                                           two_lanes(wide[...]))
            dqkv[at, cols] = dq.astype(b16)

            @pl.when(i == 0)
            def _():
                dk_sum[...] = dk
                dv_sum[...] = dv

            @pl.when(i > 0)
            def _():
                dk_sum[...] += dk
                dv_sum[...] += dv

            @pl.when(i == C - 1)
            def _():
                dqkv[:, pl.ds(pl.multiple_of(W + p * PAIR, PAIR), PAIR)] = dk_sum[...].astype(b16)
                dqkv[:, pl.ds(pl.multiple_of(2 * W + p * PAIR, PAIR), PAIR)] = dv_sum[...].astype(b16)

            for n, names in enumerate(late):
                if names:
                    @pl.when(it == n)
                    def _():
                        for name in names:
                            steps[name]()
            return carry
        lax.fori_loop(0, n_pairs * C, body, 0)

    def inputs_turned():
        for cp in loads[1:]:
            cp.wait()
        for i in range(C):
            for j in range(0, R, 128):
                xt[:, i * R + j:i * R + j + 128] = xv[i, j:j + 128, :].astype(f32).T.astype(b16)
    steps["xt"] = inputs_turned

    def projections():
        step = D // (2 * X)

        def body(i, carry):
            rows = pl.ds(pl.multiple_of(i * step, step), step)
            out = nn(xt[rows, :], dqkv[...]).astype(b16)
            gq[0, i // 2, lax.rem(i, 2)] = out.reshape(C, r, 3 * W)
            return carry
        lax.fori_loop(0, 2 * X, body, 0)
    steps["gq"] = projections

    def back_project(rows):
        return nt(dqkv[rows, :], wv[...].reshape(D, wv.shape[-1])[:, :3 * W])

    def give():
        part[...] = back_project(theirs).astype(b16)
        sends.go(part, got_part, csem.at[1], other)
    steps["give"] = give

    def keep():
        one_v[...] += back_project(mine)
    steps["keep"] = keep

    def join():
        arrived(got_part, csem.at[1], me)
        for i in range(C // 2):
            at = slice(i * R, (i + 1) * R)
            ing[i] = (one_v[at, :] + got_part[at, :].astype(f32)).astype(b16)
    steps["join"] = join
    n_flat = 2 * T * W + T * H + 6 * D

    def sums():
        zeros = jnp.zeros((1, W), f32)
        total = nn(jnp.ones((8, L), b16), dqkv[...])[0:1]
        first = me.c == 0
        place = lambda v: [jnp.where(first, v, zeros), jnp.where(first, zeros, v)]
        flat = place(total[:, :W]) + place(total[:, 2 * W:])
        flat += [jnp.sum(gub_ref[i], axis=0, keepdims=True) for i in range(T * J)]
        flat += [gvec_ref[i:i + 1, :] for i in range(6)]
        flat = jnp.concatenate(flat, axis=1)
        for i in range(n_flat // 128):
            vec[i:i + 1, :] = flat[:, i * 128:(i + 1) * 128]
        if n_vec * 128 > n_flat:
            vec[n_flat // 128:, :] = jnp.zeros((n_vec - n_flat // 128, 128), f32)
    steps["sums"] = sums

    def vectors():
        total = jnp.concatenate([vec[i:i + 1, :] for i in range(n_flat // 128)], axis=1)
        fz = (2 * me.x + me.c) * C + me.z
        tfz = me.y * (X * 2 * C) + fz
        n_dev = T * X * 2 * C
        qw, uw = T * W // n_dev, T * H // n_dev
        vq_ref[...] = take(total[:, :T * W], tfz, qw)
        vv_ref[...] = take(total[:, T * W:2 * T * W], tfz, qw)
        vu_ref[...] = take(total[:, 2 * T * W:2 * T * W + T * H], tfz, uw)
        base = 2 * T * W + T * H
        for i in range(6):
            vs_ref[i:i + 1, :] = take(total[:, base + i * D:base + (i + 1) * D], fz, r)
    steps["vectors"] = vectors

    def widen():
        for s in range(S):
            ing_out[s] = ing_in[s].astype(f32)
    steps["widen"] = widen

    early, late, end = BACK_PLAN
    for name in early:
        steps[name]()
    attention(late)
    for name in end:
        steps[name]()
    sends.finish(me)


BACK_PLAN = (
    ('ff', 'of', 'Ro', 'keys', 'upstream', 'fd', 'fr', 'od', 'or'),
    (('fs1', 'os1'), ('fs2',), ('fs3', 'fo'), ('fz1',), ('fs0',), ('fz2', 'oo'), ('fz3', 'oz1'), ('Rp',),
     ('os2',), ('os3', 'oz2'), ('os0', 'oz3'), ('fz0', 'xt')),
    ('gq', 'qf', 'give', 'qd', 'qr', 'keep', 'sums', 't0', 'qs1', 'qs2', 'qs3', 'qo', 'join', 'Io', 'qs0', 't1',
     'qz1', 'qz2', 't2', 'qz3', 'qz0', 'oz0', 'fl', 'ol', 't3', 'ql', 't4', 'vectors', 'Ip', 'Re', 'Ie',
     'widen'),
)


def back(cfg, q, k, v, ah, lse, sf, do, one, res, xf, g1, gff, go, gvec, gub):
    sizes, S, W, H, chunk = cfg
    F, C, T = sizes
    X = F // 2
    _, R, D = xf.shape
    L = C * R
    J = H // chunk
    r = g1.shape[4]
    f32, b = jnp.float32, jnp.bfloat16
    dma = pltpu.SemaphoreType.DMA
    sds = jax.ShapeDtypeStruct
    vm = pltpu.VMEM
    steps = total_count(sizes)
    n_vec = -(-(2 * T * W + T * H + 6 * D) // 1024) * 8
    lanes = lambda w: max(128, -(-w // 128) * 128)
    n_dev = T * F * C
    sems = reduce_sems(sizes)
    return pl.pallas_call(
        functools.partial(back_kernel, cfg),
        in_specs=[VM] * 6 + [ANY] * 7 + [VM] * 2,
        out_specs=[ANY] + [VM] * 9,
        out_shape=[sds((S, R, D), b), sds((S, R, D), f32), sds((r, 3 * W), f32), sds((r, H), f32), sds((r, H), f32),
                   sds((r, W), f32), sds((1, lanes(T * W // n_dev)), f32), sds((1, lanes(T * W // n_dev)), f32),
                   sds((1, lanes(T * H // n_dev)), f32), sds((6, lanes(r)), f32)],
        scratch_shapes=[vm((L, W), b), vm((L, 3 * W), b), vm((W // PAIR, PAIR, L), b), vm((L, 128), f32),
                        vm((L, PAIR), f32), vm((L, PAIR), f32), vm((D, L), b), vm((C, R, D), b),
                        vm((X, 2, C, r, g1.shape[5]), b), vm((1, X, 2, C, r, 3 * W), b), vm((L // 2, D), f32),
                        vm((L // 2, D), b), vm((L // 2, D), b), vm((C // 2, R, D), b), vm((S, R, D), b),
                        vm((n_vec, 128), f32), vm((4, n_vec, 128), f32), vm((steps, n_vec, 128), f32)]
        + reduce_scratch(sizes, 2 * J, r, chunk, False) + reduce_scratch(sizes, 1, r, W, False)
        + reduce_scratch(sizes, 1, r, 3 * W, True)
        + [dma((2 * reduce_count(sizes, False) + reduce_count(sizes, True) + steps + 2,)),
           dma((sems,)), dma((sems,)), dma((sems,)), dma((steps,)), dma((T * X,)), dma((T * X,)), dma((X,)),
           dma((2, C // 2 + S)), dma((2, S)), dma((2,)), dma((6,))],
        compiler_params=pltpu.CompilerParams(collective_id=1, has_side_effects=True,
                                             vmem_limit_bytes=62 * 2**20),
    )(q, k, v, ah, lse, sf, do, one, res, xf, g1, gff, go, gvec, gub)


def chunk_of(H):
    for w in (512, 384, 256, 128):
        if H % w == 0:
            return w
    return H


def on_device(sizes, inputs, segments, cotangent, query_weight, key_weight, value_weight,
              output_weight, up_weight, down_weight, query_bias, value_bias, up_bias,
              output_bias, down_bias, first_gain, first_shift, second_gain, second_shift):
    F, C, T = sizes
    X = F // 2
    S, R, D = inputs.shape
    W = query_weight.shape[1]
    H = up_weight.shape[1]
    r = query_weight.shape[0]
    L = C * R
    half = L // 2
    chunk = chunk_of(H)
    J = H // chunk
    c = lax.rem(lax.axis_index("fsdp"), 2)
    f32 = jnp.float32
    small = jnp.concatenate([query_bias, value_bias, up_bias, output_bias, down_bias, first_gain,
                             first_shift, second_gain, second_shift])
    rows = -(-small.shape[0] // VEC)
    small = jnp.pad(small, (0, rows * VEC - small.shape[0])).reshape(rows, VEC)
    small = jnp.pad(small, ((0, r - rows), (0, 0)))
    w1 = jnp.concatenate([query_weight, key_weight, value_weight, small], axis=1)
    w2 = jnp.concatenate([up_weight, down_weight.T, output_weight.T], axis=1)
    seg = jnp.broadcast_to(segments.astype(f32)[:, None, :], (S, 8, R))
    cfg = (sizes, S, W, H, chunk)
    q, k, v, ah, ar, lse, xf, cf, sf, g1, g2, vec, ub = front(cfg, inputs, cotangent, seg, w1, w2)
    x_mine = lax.dynamic_slice(xf.reshape(L, D), (c * half, 0), (half, D))
    res, one, do, gff, go, gvec, gub = middle(
        T, x_mine, ar, cf.reshape(half, D), g2.reshape(T, D, -1), vec, ub, chunk)
    outs = back(cfg, q, k, v, ah, lse, sf, do, one, res.reshape(C // 2, R, D), xf, g1,
                gff.reshape(T, 2 * J, X, 2, C, r, chunk), go.reshape(T, 1, X, 2, C, r, W), gvec, gub)
    res_out, ing_out, oq, oup, odn, oo, vq, vv, vu, vs = outs
    qw, uw = query_bias.shape[0], up_bias.shape[0]
    return (res_out, ing_out, oq[:, :W], oq[:, W:2 * W], oq[:, 2 * W:], oo.T, oup, odn.T,
            vq[0, :qw], vv[0, :qw], vu[0, :uw]) + tuple(vs[i, :r] for i in range(6))


def solution(mesh):
    sizes = (mesh.shape["fsdp"], mesh.shape["ctx"], mesh.shape["tp"])
    every = ("fsdp", "ctx")
    rows, cols, one, three = P(every, "tp"), P("tp", every), P(every), P(("tp",) + every)
    token = P("fsdp", "ctx", None)
    weights = (rows, rows, rows, cols, rows, cols)
    vectors = (three, three, three) + (one,) * 6
    return jax.shard_map(
        functools.partial(on_device, sizes), mesh=mesh,
        in_specs=(token, P("fsdp", "ctx"), token) + weights + vectors,
        out_specs=(token, token) + weights + vectors, check_vma=False)
```

```python
import functools
import jax
import jax.numpy as jnp
from jax import lax
from jax.sharding import PartitionSpec as P
from jax.experimental import pallas as pl
from jax.experimental.pallas import tpu as pltpu

MESH = pl.DeviceIdType.MESH
ANY = pl.BlockSpec(memory_space=pl.ANY)
VM = pl.BlockSpec(memory_space=pltpu.VMEM)


class Place:
    def __init__(self, sizes):
        self.F, self.C, self.T = sizes
        self.X = self.F // 2
        f = lax.axis_index("fsdp")
        self.x = f // 2
        self.c = lax.rem(f, 2)
        self.z = lax.axis_index("ctx")
        self.y = lax.axis_index("tp")

    def dev(self, x=None, c=None, z=None, y=None):
        x = self.x if x is None else x
        c = self.c if c is None else c
        return (2 * x + c, self.z if z is None else z, self.y if y is None else y)

    def z_off(self, d):
        return lax.rem(self.z + d + self.C, self.C)

    def x_off(self, d):
        return lax.rem(self.x + d + self.X, self.X)

    def greet(self, chip_wide):
        bar = pltpu.get_barrier_semaphore()
        devs = [self.dev(c=1 - self.c), self.dev(y=1 - self.y)]
        devs += [self.dev(x=self.x_off(d)) for d in range(1, self.X)]
        for d in range(1, self.C):
            devs.append(self.dev(z=self.z_off(d)))
            if chip_wide:
                devs.append(self.dev(z=self.z_off(d), c=1 - self.c))
        for d in devs:
            pl.semaphore_signal(bar, inc=1, device_id=d, device_id_type=MESH)
        pl.semaphore_wait(bar, len(devs))


class Sends:
    def __init__(self, sems):
        self.sems, self.n, self.waits = sems, 0, []

    def go(self, src, dst, recv, dev, like=None, when=None):
        pltpu.make_async_remote_copy(
            src_ref=src, dst_ref=dst, send_sem=self.sems.at[self.n], recv_sem=recv,
            device_id=dev, device_id_type=MESH).start()
        self.n += 1
        self.waits.append((src if like is None else like, when))

    def finish(self, me):
        for n, (like, when) in enumerate(self.waits):
            def wait():
                pltpu.make_async_remote_copy(
                    src_ref=like, dst_ref=like, send_sem=self.sems.at[n], recv_sem=self.sems.at[n],
                    device_id=me.dev(c=1 - me.c), device_id_type=MESH).wait_send()
            given(when, wait)
        self.waits = []


def given(when, body):
    if when is None:
        body()
    else:
        pl.when(when())(body)


def arrived(dst, recv, pl_):
    pltpu.make_async_remote_copy(
        src_ref=dst, dst_ref=dst, send_sem=recv, recv_sem=recv,
        device_id=pl_.dev(c=1 - pl_.c), device_id_type=MESH).wait_recv()


def line_order(C, z):
    return [z] + [z + sign * k for k in range(1, C) for sign in (-1, 1) if 0 <= z + sign * k < C]


def pick(index, table):
    out = table[-1]
    for i in reversed(range(len(table) - 1)):
        out = jnp.where(index == i, table[i], out)
    return jnp.int32(out)


def gather_events(me, own, full, sends, recv, lsem):
    C, X = me.C, me.X
    sem = lambda t, x, c, z: recv.at[((t * X + x) * 2 + c) * C + z]
    slot = lambda t, x, c, z: full.at[t, x, c, z]
    like = slot(0, 0, 0, 0)
    orders = [line_order(C, z) for z in range(C)]
    where = lambda m: pick(me.z, [o[m] for o in orders])

    def push(src, at, dev, when=None):
        sends.go(src, slot(*at), sem(*at), dev, like, when)

    def wait(at):
        arrived(slot(*at), sem(*at), me)

    core, side = me.dev(c=1 - me.c), me.dev(y=1 - me.y)
    xs = [(me.x_off(d), me.dev(x=me.x_off(d))) for d in range(1, X)]
    local = pltpu.make_async_copy(own, slot(me.y, me.x, me.c, me.z), lsem)

    def along(m):
        def run():
            zz = where(m)
            at = (me.y, me.x, me.c, zz)
            src = slot(*at) if m else own
            if m:
                wait(at)
            for sign in (-1, 1):
                def onward(sign=sign):
                    zz = where(m)
                    return ((zz - me.z) * sign <= 0) & (me.z + sign >= 0) & (me.z + sign < C)

                @pl.when(onward())
                def _():
                    push(src, at, me.dev(z=me.z + sign), onward)
            for _, dev in xs:
                push(src, at, dev)
            push(src, at, side)
            push(src, at, core)
            if not m:
                local.start()
        return run

    def across(m):
        def run():
            zz = where(m)
            at = (1 - me.y, me.x, me.c, zz)
            wait(at)
            if m < C // 2:
                for _, dev in xs:
                    push(slot(*at), at, dev)
            push(slot(*at), at, core)
            for xo, _ in xs:
                at = (me.y, xo, me.c, zz)
                wait(at)
                if m >= C // 2:
                    push(slot(*at), at, side)
                push(slot(*at), at, core)
        return run

    def corner(m):
        def run():
            zz = where(m)
            for xo, _ in xs:
                at = (1 - me.y, xo, me.c, zz)
                wait(at)
                push(slot(*at), at, core)
        return run

    def last():
        for t in range(me.T):
            for xx in range(X):
                for zz in range(C):
                    wait((t, xx, 1 - me.c, zz))
        local.wait()

    steps = {"l": last}
    for m in range(C):
        steps["a%d" % m] = along(m)
        steps["x%d" % m] = across(m)
        steps["c%d" % m] = corner(m)
    return steps


def gather_count(sizes):
    F, C, T = sizes
    X = F // 2
    return C * (4 * X + 4)


class Tokens:
    def __init__(self, me, seqs):
        self.me, self.S = me, seqs
        self.half = me.C // 2
        self.lo = me.y * (me.C - seqs)
        self.busy = (me.z >= self.lo) & (me.z < self.lo + seqs)
        self.owner = me.c == me.y

    def out(self, src, dst, full, ssem, rsem, lsem):
        me, half = self.me, self.half
        k = me.z // half
        at = me.z if full else lax.rem(me.z, half)

        @pl.when(self.owner)
        def _():
            for s in range(self.S):
                here = (self.lo + s == me.z) & (k == me.c)

                @pl.when(here)
                def _():
                    pltpu.make_async_copy(src.at[s], dst.at[at], lsem).start()

                @pl.when(jnp.logical_not(here))
                def _():
                    pltpu.make_async_remote_copy(
                        src_ref=src.at[s], dst_ref=dst.at[at], send_sem=ssem.at[s],
                        recv_sem=rsem.at[lax.rem(me.z, half)],
                        device_id=me.dev(c=k, z=self.lo + s), device_id_type=MESH).start()

    def out_done(self, src, dst, full, ssem, rsem, lsem):
        me, half = self.me, self.half

        @pl.when(self.busy)
        def _():
            for i in range(half):
                zq = me.c * half + i
                at = zq if full else i
                here = (zq == me.z) & (me.c == me.y)

                @pl.when(here)
                def _():
                    pltpu.make_async_copy(src.at[0], dst.at[at], lsem).wait()

                @pl.when(jnp.logical_not(here))
                def _():
                    arrived(dst.at[at], rsem.at[i], me)

                if full:
                    pltpu.make_async_remote_copy(
                        src_ref=dst.at[at], dst_ref=dst.at[at], send_sem=ssem.at[self.S + i],
                        recv_sem=rsem.at[half + i], device_id=me.dev(c=1 - me.c),
                        device_id_type=MESH).start()

    def out_end(self, src, dst, full, ssem, rsem, lsem):
        me, half = self.me, self.half
        k = me.z // half

        @pl.when(self.owner)
        def _():
            for s in range(self.S):
                here = (self.lo + s == me.z) & (k == me.c)

                @pl.when(jnp.logical_not(here))
                def _():
                    pltpu.make_async_remote_copy(
                        src_ref=src.at[s], dst_ref=dst.at[0], send_sem=ssem.at[s],
                        recv_sem=rsem.at[0], device_id=me.dev(c=1 - me.c),
                        device_id_type=MESH).wait_send()

        if full:
            @pl.when(self.busy)
            def _():
                for i in range(half):
                    zq = (1 - me.c) * half + i
                    arrived(dst.at[zq], rsem.at[half + i], me)
                    pltpu.make_async_remote_copy(
                        src_ref=dst.at[0], dst_ref=dst.at[0], send_sem=ssem.at[self.S + i],
                        recv_sem=rsem.at[0], device_id=me.dev(c=1 - me.c),
                        device_id_type=MESH).wait_send()

    def back(self, src, dst, ssem, rsem, lsem):
        me, half = self.me, self.half

        @pl.when(self.busy)
        def _():
            for i in range(half):
                zq = me.c * half + i
                here = (zq == me.z) & (me.c == me.y)
                at = me.z - self.lo

                @pl.when(here)
                def _():
                    pltpu.make_async_copy(src.at[i], dst.at[at], lsem).start()

                @pl.when(jnp.logical_not(here))
                def _():
                    pltpu.make_async_remote_copy(
                        src_ref=src.at[i], dst_ref=dst.at[at], send_sem=ssem.at[i],
                        recv_sem=rsem.at[at], device_id=me.dev(c=me.y, z=zq),
                        device_id_type=MESH).start()

    def back_pass(self, src, dst, ssem, rsem, lsem):
        me, half = self.me, self.half
        k = me.z // half

        @pl.when(self.owner)
        def _():
            for s in range(self.S):
                here = (self.lo + s == me.z) & (k == me.c)

                @pl.when(here)
                def _():
                    pltpu.make_async_copy(src.at[0], dst.at[s], lsem).wait()

                @pl.when(jnp.logical_not(here))
                def _():
                    arrived(dst.at[s], rsem.at[s], me)

                pltpu.make_async_remote_copy(
                    src_ref=dst.at[s], dst_ref=dst.at[s], send_sem=ssem.at[half + s],
                    recv_sem=rsem.at[s], device_id=me.dev(y=1 - me.y),
                    device_id_type=MESH).start()

    def back_end(self, src, dst, ssem, rsem, lsem):
        me, half = self.me, self.half

        @pl.when(self.busy)
        def _():
            for i in range(half):
                zq = me.c * half + i
                here = (zq == me.z) & (me.c == me.y)

                @pl.when(jnp.logical_not(here))
                def _():
                    pltpu.make_async_remote_copy(
                        src_ref=src.at[i], dst_ref=dst.at[0], send_sem=ssem.at[i],
                        recv_sem=rsem.at[0], device_id=me.dev(c=1 - me.c),
                        device_id_type=MESH).wait_send()

        @pl.when(self.owner)
        def _():
            for s in range(self.S):
                pltpu.make_async_remote_copy(
                    src_ref=dst.at[s], dst_ref=dst.at[s], send_sem=ssem.at[half + s],
                    recv_sem=rsem.at[s], device_id=me.dev(y=1 - me.y),
                    device_id_type=MESH).wait_send()

        @pl.when(jnp.logical_not(self.owner))
        def _():
            for s in range(self.S):
                arrived(dst.at[s], rsem.at[s], me)


def reduce_events(me, grads, split, bufs, sends, recv, lsem, finish):
    acc, rc, xd, yd, xr, yr, zr = bufs
    C, X = me.C, me.X
    half = C // 2
    n_cols = acc.shape[2]
    like, like_all = acc.at[0, 0, :, 0], acc.at[0, 0]
    core, side = me.dev(c=1 - me.c), me.dev(y=1 - me.y)
    s_core = lambda t, x: recv.at[t * X + x]
    base = me.T * X
    s_d = lambda d, j: recv.at[base + (d - 1) * C + j]
    base2 = base + (X - 1) * C
    s_xr = lambda d, j: recv.at[base2 + (d - 1) * C + j]
    base3 = base2 + (X - 1) * C
    s_yr = lambda j: recv.at[base3 + j]
    s_zr = lambda j: recv.at[base3 + C + j]
    quads = ([(1 - me.y, me.x_off(d)) for d in range(1, X)] + [(1 - me.y, me.x)]
             + [(me.y, me.x_off(d)) for d in range(1, X)] + [(me.y, me.x)])
    locals_ = []

    def first():
        if split:
            for n, x in enumerate([me.x_off(d) for d in range(1, X)] + [me.x]):
                sends.go(grads.at[:, x, 1 - me.c], acc.at[me.c, x], s_core(me.c, x), core, like_all)
                cp = pltpu.make_async_copy(grads.at[:, x, me.c], acc.at[me.c, x], lsem.at[n])
                cp.start()
                locals_.append(cp)
        else:
            for n, (t, x) in enumerate(quads):
                sends.go(grads.at[t, :, x, 1 - me.c], rc.at[t, x], s_core(t, x), core, like_all)
                cp = pltpu.make_async_copy(grads.at[t, :, x, me.c], acc.at[t, x], lsem.at[n])
                cp.start()
                locals_.append(cp)

    def add(a, b):
        def body(i, carry):
            a[i] = a[i] + b[i]
            return carry
        lax.fori_loop(0, n_cols, body, 0)

    def ready(n):
        t, x = quads[n]
        if split:
            if n == 0:
                for cp in locals_:
                    cp.wait()
                for xo in [me.x_off(d) for d in range(1, X)] + [me.x]:
                    arrived(acc.at[1 - me.c, xo], s_core(1 - me.c, xo), me)
            return
        locals_[n].wait()
        arrived(rc.at[t, x], s_core(t, x), me)

        def body(i, carry):
            for z in range(C):
                acc[t, x, i, z] = acc[t, x, i, z] + rc[t, x, i, z]
            return carry
        lax.fori_loop(0, n_cols, body, 0)

    by_x = range(1, C)
    order = list(range(1, C)) + [0]

    def corner():
        for d in range(1, X):
            ready(d - 1)
            t, x = quads[d - 1]
            for j in order:
                zj = me.z_off(-j)
                if j in by_x:
                    sends.go(acc.at[t, x, :, zj], xd.at[d - 1, j], s_d(d, j), me.dev(x=x), like)
                else:
                    sends.go(acc.at[t, x, :, zj], yd.at[d - 1, j], s_d(d, j), side, like)

    def ready_sides():
        for n in range(X - 1, 2 * X - 1):
            ready(n)

    def spread(j):
        def run():
            zj = me.z_off(-j)
            t, x = me.y, me.x
            for d in range(1, X):
                xo = me.x_off(d)
                if j not in by_x:
                    arrived(yd.at[d - 1, j], s_d(d, j), me)
                    add(acc.at[t, xo, :, zj], yd.at[d - 1, j])
                sends.go(acc.at[t, xo, :, zj], xr.at[d - 1, j], s_xr(d, j), me.dev(x=xo), like)
            t = 1 - me.y
            for d in range(1, X):
                if j in by_x:
                    arrived(xd.at[d - 1, j], s_d(d, j), me)
                    add(acc.at[t, x, :, zj], xd.at[d - 1, j])
            sends.go(acc.at[t, x, :, zj], yr.at[j], s_yr(j), side, like)
        return run

    def to_z(j):
        def run():
            t, x = me.y, me.x
            zj = me.z_off(-j)
            for d in range(1, X):
                arrived(xr.at[d - 1, j], s_xr(d, j), me)
                add(acc.at[t, x, :, zj], xr.at[d - 1, j])
            arrived(yr.at[j], s_yr(j), me)
            add(acc.at[t, x, :, zj], yr.at[j])
            if j:
                sends.go(acc.at[t, x, :, zj], zr.at[j - 1], s_zr(j - 1), me.dev(z=zj), like)
        return run

    def last():
        for j in range(1, C):
            arrived(zr.at[j - 1], s_zr(j - 1), me)
        for i in range(n_cols):
            total = acc[me.y, me.x, i, me.z].astype(jnp.float32)
            for j in range(1, C):
                total = total + zr[j - 1, i].astype(jnp.float32)
            finish(i, total)

    steps = {"f": first, "d": corner, "r": ready_sides, "o": lambda: ready(2 * X - 1), "l": last}
    for j in range(C):
        steps["s%d" % j] = spread(j)
        steps["z%d" % j] = to_z(j)
    return steps


def reduce_scratch(sizes, n, r, w, split):
    F, C, T = sizes
    X = F // 2
    half = C // 2
    v = lambda shape: pltpu.VMEM(shape, jnp.bfloat16)
    return [v((T, X, n, C, r, w)), v((1, 1, 1, 1, 16, 128) if split else (T, X, n, C, r, w)),
            v((X - 1, C, n, r, w)), v((X - 1, C, n, r, w)), v((X - 1, C, n, r, w)),
            v((C, n, r, w)), v((C - 1, n, r, w))]


def reduce_sems(sizes):
    F, C, T = sizes
    X = F // 2
    return T * X + 2 * (X - 1) * C + 2 * C


def reduce_count(sizes, split):
    F, C, T = sizes
    X = F // 2
    return (X if split else T * X) + 2 * (X - 1) * C + C + C - 1


def total_events(me, own, bufs, out, sends, recv):
    C, X = me.C, me.X
    acc, got = bufs
    groups = [[me.dev(c=1 - me.c)], [me.dev(x=me.x_off(d)) for d in range(1, X)],
              [me.dev(y=1 - me.y)], [me.dev(z=me.z_off(d)) for d in range(1, C)]]
    like = acc.at[0]
    bases = [sum(len(g) for g in groups[:i]) for i in range(len(groups))]

    def start(gi):
        for i, dev in enumerate(groups[gi]):
            sends.go(acc.at[gi], got.at[bases[gi] + i], recv.at[bases[gi] + i], dev, like)

    def first():
        acc[0] = own[...]
        start(0)

    steps = {"0": first}
    for gi in range(len(groups)):
        def step(gi=gi):
            total = acc[gi]
            for i in range(len(groups[gi])):
                arrived(got.at[bases[gi] + i], recv.at[bases[gi] + i], me)
                total = total + got[bases[gi] + i]
            if gi + 1 < len(groups):
                acc[gi + 1] = total
                start(gi + 1)
            else:
                out[...] = total
        steps[str(gi + 1)] = step
    return steps


def total_count(sizes):
    F, C, T = sizes
    return 1 + F // 2 - 1 + 1 + C - 1

HEAD = 64
PAIR = 2 * HEAD
SCALE = HEAD ** (-0.5)
norm_eps = 1e-12
masked_score = -1000000000.0


def nt(a, b):
    return lax.dot_general(a, b, (((1,), (1,)), ((), ())), preferred_element_type=jnp.float32)


def nn(a, b):
    return lax.dot_general(a, b, (((1,), (0,)), ((), ())), preferred_element_type=jnp.float32)


def spread_segments(seg_ref, wide):
    C, _, R = seg_ref.shape
    for i in range(C):
        for j in range(0, R, 128):
            row = jnp.broadcast_to(seg_ref[i, 0:1, j:j + 128], (128, 128))
            wide[i * R + j:i * R + j + 128, :] = row.T


def lanes_of(h, like):
    lane = lax.broadcasted_iota(jnp.int32, like.shape, like.ndim - 1)
    return jnp.where(lane // HEAD == h, like, jnp.zeros_like(like))


def two_lanes(wide):
    return jnp.concatenate([wide, wide], axis=1)


def attend_block(q, k, v_t, seg_q, seg_k):
    same = seg_k == seg_q
    outs, logs = [], []
    for h in range(2):
        s = nt(k, lanes_of(h, q) * jnp.bfloat16(SCALE))
        s = jnp.where(same, s, masked_score)
        peak = jnp.max(s, axis=0, keepdims=True)
        e = jnp.exp(s - peak)
        total = jnp.sum(e, axis=0, keepdims=True)
        o = nn(v_t, e.astype(jnp.bfloat16))
        outs.append(o[h * HEAD:(h + 1) * HEAD] * (1.0 / total))
        logs.append(peak + jnp.log(total))
    return jnp.concatenate(outs, axis=0), logs


def attend_kernel(q_ref, k_ref, v_ref, seg_ref, o_ref, lse_ref, wide, v_t):
    i = pl.program_id(1)

    @pl.when((pl.program_id(0) == 0) & (i == 0))
    def _():
        spread_segments(seg_ref, wide)

    @pl.when(i == 0)
    def _():
        v_t[...] = v_ref[...].astype(jnp.float32).T.astype(jnp.bfloat16)

    seg_q = seg_ref[i, 0:1, :]
    o, logs = attend_block(q_ref[...], k_ref[...], v_t[...], seg_q, two_lanes(wide[...]))
    o_ref[...] = o.T.astype(jnp.bfloat16)
    lse_ref[0] = jnp.concatenate(logs + [jnp.zeros((6, logs[0].shape[1]), jnp.float32)], axis=0)


def attend(q, k, v, seg):
    L, W = q.shape
    C, _, R = seg.shape
    n = W // PAIR
    return pl.pallas_call(
        attend_kernel,
        grid=(n, C),
        in_specs=[pl.BlockSpec((R, PAIR), lambda p, i: (i, p)),
                  pl.BlockSpec((L, PAIR), lambda p, i: (0, p)),
                  pl.BlockSpec((L, PAIR), lambda p, i: (0, p)),
                  pl.BlockSpec((C, 8, R), lambda p, i: (0, 0, 0))],
        out_specs=[pl.BlockSpec((R, PAIR), lambda p, i: (i, p)),
                   pl.BlockSpec((1, 8, R), lambda p, i: (p, 0, i))],
        out_shape=[jax.ShapeDtypeStruct((L, W), jnp.bfloat16),
                   jax.ShapeDtypeStruct((n, 8, L), jnp.float32)],
        scratch_shapes=[pltpu.VMEM((L, 128), jnp.float32), pltpu.VMEM((PAIR, L), jnp.bfloat16)],
        compiler_params=pltpu.CompilerParams(vmem_limit_bytes=56 * 2**20),
    )(q, k, v, seg)


def attend_back_block(q, k, k_t, v, do, o, lse, seg_q, seg_k):
    same = seg_k == seg_q
    prod = (do.astype(jnp.float32) * o.astype(jnp.float32)).T
    dq, dk, dv = [], None, None
    for h in range(2):
        qh = lanes_of(h, q) * jnp.bfloat16(SCALE)
        doh = lanes_of(h, do)
        s = nt(k, qh)
        p = jnp.exp(jnp.where(same, s, masked_score) - lse[h:h + 1])
        dp = nt(v, doh)
        inner = jnp.sum(prod[h * HEAD:(h + 1) * HEAD], axis=0, keepdims=True)
        ds = (p * (dp - inner)).astype(jnp.bfloat16)
        dv_h = nn(p.astype(jnp.bfloat16), doh)
        dk_h = nn(ds, qh)
        dv = dv_h if dv is None else dv + dv_h
        dk = dk_h if dk is None else dk + dk_h
        dq.append(nn(k_t, ds)[h * HEAD:(h + 1) * HEAD])
    return jnp.concatenate(dq, axis=0).T * SCALE, dk, dv


def attend_back_kernel(q_ref, k_ref, v_ref, do_ref, o_ref, lse_ref, seg_ref,
                       dq_ref, dk_ref, dv_ref, wide, k_t, dk_sum, dv_sum):
    i = pl.program_id(1)

    @pl.when((pl.program_id(0) == 0) & (i == 0))
    def _():
        spread_segments(seg_ref, wide)

    @pl.when(i == 0)
    def _():
        k_t[...] = k_ref[...].astype(jnp.float32).T.astype(jnp.bfloat16)

    seg_q = seg_ref[i, 0:1, :]
    dq, dk, dv = attend_back_block(q_ref[...], k_ref[...], k_t[...], v_ref[...], do_ref[...],
                                   o_ref[...], lse_ref[0], seg_q, two_lanes(wide[...]))
    dq_ref[...] = dq.astype(jnp.bfloat16)

    @pl.when(i == 0)
    def _():
        dk_sum[...] = dk
        dv_sum[...] = dv

    @pl.when(i > 0)
    def _():
        dk_sum[...] += dk
        dv_sum[...] += dv

    @pl.when(i == pl.num_programs(1) - 1)
    def _():
        dk_ref[...] = dk_sum[...].astype(jnp.bfloat16)
        dv_ref[...] = dv_sum[...].astype(jnp.bfloat16)


def attend_back(q, k, v, do, o, lse, seg):
    L, W = q.shape
    C, _, R = seg.shape
    n = W // PAIR
    row = pl.BlockSpec((R, PAIR), lambda p, i: (i, p))
    all_rows = pl.BlockSpec((L, PAIR), lambda p, i: (0, p))
    b = jax.ShapeDtypeStruct((L, W), jnp.bfloat16)
    return pl.pallas_call(
        attend_back_kernel,
        grid=(n, C),
        in_specs=[row, all_rows, all_rows, row, row,
                  pl.BlockSpec((1, 8, R), lambda p, i: (p, 0, i)),
                  pl.BlockSpec((C, 8, R), lambda p, i: (0, 0, 0))],
        out_specs=[row, all_rows, all_rows],
        out_shape=[b, b, b],
        scratch_shapes=[pltpu.VMEM((L, 128), jnp.float32), pltpu.VMEM((PAIR, L), jnp.bfloat16),
                        pltpu.VMEM((L, PAIR), jnp.float32), pltpu.VMEM((L, PAIR), jnp.float32)],
        compiler_params=pltpu.CompilerParams(vmem_limit_bytes=56 * 2**20),
    )(q, k, v, do, o, lse, seg)


STRIP = 64


def strips(rows, body):
    def step(i, carry):
        body(pl.ds(pl.multiple_of(i * STRIP, STRIP), STRIP))
        return carry
    lax.fori_loop(0, rows // STRIP, step, 0)


def fold(value):
    total = value[0:8]
    for i in range(8, value.shape[0], 8):
        total = total + value[i:i + 8]
    return total


def mean(value):
    return jnp.mean(value, axis=-1, keepdims=True)


def unit_of(value):
    centred = value - mean(value)
    factor = lax.rsqrt(mean(centred * centred) + norm_eps)
    return centred * factor, factor


def back_of(upstream, unit, factor, gain):
    along = upstream * gain
    return factor * (along - mean(along) - unit * mean(along * unit))


def flip(ref, out):
    rows = ref.shape[0]
    for i in range(0, rows, 128):
        out[:, i:i + 128] = ref[i:i + 128, :].astype(jnp.float32).T.astype(jnp.bfloat16)


def middle_kernel(T, J, x_ref, att_ref, cot_ref, wu_ref, wd_ref, wo_ref, vec_ref, ub_ref,
                  res_ref, one_ref, do_ref, gff_ref, go_ref, gvec_ref, gub_ref,
                  unit, mixed, fac, low, low_t, acc, two, fl, fl_t, hid, act, slope, hl, sums):
    s = pl.program_id(0)
    n = T * J
    rows, D = x_ref.shape
    W = wo_ref.shape[2]
    f32, b16 = jnp.float32, jnp.bfloat16
    row = lambda i: vec_ref[i:i + 1, :]

    @pl.when(s == 0)
    def _():
        for t in range(T):
            part = nt(att_ref[:, t * W:(t + 1) * W], wo_ref[t])
            acc[...] = part if t == 0 else acc[...] + part

        def body(at):
            u, factor = unit_of(x_ref[at, :].astype(f32) + acc[at, :] + row(0))
            m = u * row(2) + row(3)
            unit[at, :] = u
            fac[at, :] = jnp.broadcast_to(factor, (STRIP, 128))
            mixed[at, :] = m
            low[at, :] = m.astype(b16)
            acc[at, :] = jnp.zeros((STRIP, D), f32)
        strips(rows, body)
        flip(low, low_t)

    @pl.when(s < n)
    def _():
        hid[...] = nn(low[...], wu_ref[0])

        def body(at):
            h = hid[at, :] + ub_ref[0]
            phi = 0.5 + 0.5 * lax.erf(h * (0.5 ** 0.5))
            dens = jnp.exp(-0.5 * h * h) * 0.3989422804014327
            act[s, at, :] = (h * phi).astype(b16)
            slope[s, at, :] = phi + h * dens
        strips(rows, body)
        acc[...] += nt(act[s], wd_ref[0])

    @pl.when(s == n)
    def _():
        sums[...] = jnp.zeros_like(sums)

        def body(at):
            u, factor = unit_of(mixed[at, :] + acc[at, :] + row(1))
            res_ref[at, :] = (u * row(4) + row(5)).astype(b16)
            g = cot_ref[at, :].astype(f32)
            g2 = back_of(g, u, factor, row(4))
            l2 = g2.astype(b16)
            fl[at, :] = l2
            acc[at, :] = g2
            sums[1] += fold(l2.astype(f32))
            sums[4] += fold(g * u)
            sums[5] += fold(g)
        strips(rows, body)
        flip(fl, fl_t)

    @pl.when(s >= n)
    def _():
        j = 2 * n - 1 - s
        hid[...] = nn(fl[...], wd_ref[0])
        gub_ref[0] = jnp.zeros_like(gub_ref[0])

        def body(at):
            v = (hid[at, :] * slope[j, at, :]).astype(b16)
            hl[at, :] = v
            gub_ref[0] += fold(v.astype(f32))
        strips(rows, body)
        acc[...] += nt(hl[...], wu_ref[0])
        gff_ref[0, 0, 0] = nn(low_t[...], hl[...]).astype(b16)
        gff_ref[0, 0, 1] = nn(fl_t[...], act[j]).astype(b16)

    @pl.when(s == 2 * n - 1)
    def _():
        def body(at):
            g = acc[at, :]
            u = unit[at, :]
            g1 = back_of(g, u, fac[at, 0:1], row(2))
            one_ref[at, :] = g1
            l1 = g1.astype(b16)
            fl[at, :] = l1
            sums[0] += fold(l1.astype(f32))
            sums[2] += fold(g * u)
            sums[3] += fold(g)
        strips(rows, body)
        flip(fl, fl_t)
        for t in range(T):
            go_ref[t] = nn(fl_t[...], att_ref[:, t * W:(t + 1) * W]).astype(b16)
            do_ref[:, t * W:(t + 1) * W] = nn(fl[...], wo_ref[t]).astype(b16)
        for i in range(6):
            gvec_ref[i:i + 1, :] = jnp.sum(sums[i], axis=0, keepdims=True)


def middle(T, x, att, cot, w2, vec, ub, chunk):
    rows, D = x.shape
    W = att.shape[1] // T
    J = ub.shape[0] // T
    H = J * chunk
    n = T * J
    f32, b16 = jnp.float32, jnp.bfloat16
    which = lambda s: jnp.where(s < n, s, 2 * n - 1 - s)
    whole = lambda shape: pl.BlockSpec(shape, lambda s: (0,) * len(shape), pipeline_mode=pl.Buffered(1))
    up = pl.BlockSpec((1, D, chunk), lambda s: (which(s) // J, 0, lax.rem(which(s), J)))
    down = pl.BlockSpec((1, D, chunk), lambda s: (which(s) // J, 0, J + lax.rem(which(s), J)))
    wo = pl.BlockSpec((T, D, W), lambda s: (0, 0, 2 * H // W), pipeline_mode=pl.Buffered(1))
    late = lambda s: jnp.where(s < n, n - 1, 2 * n - 1 - s)
    return pl.pallas_call(
        functools.partial(middle_kernel, T, J),
        grid=(2 * n,),
        in_specs=[whole((rows, D)), whole((rows, T * W)), whole((rows, D)), up, down, wo, whole(vec.shape),
                  pl.BlockSpec((1, 1, chunk), lambda s: (which(s), 0, 0))],
        out_specs=[whole((rows, D)), whole((rows, D)), whole((rows, T * W)),
                   pl.BlockSpec((1, 1, 2, D, chunk), lambda s: (late(s) // J, lax.rem(late(s), J), 0, 0, 0)),
                   whole((T, D, W)), whole((8, D)),
                   pl.BlockSpec((1, 8, chunk), lambda s: (late(s), 0, 0))],
        out_shape=[jax.ShapeDtypeStruct((rows, D), b16), jax.ShapeDtypeStruct((rows, D), f32),
                   jax.ShapeDtypeStruct((rows, T * W), b16), jax.ShapeDtypeStruct((T, J, 2, D, chunk), b16),
                   jax.ShapeDtypeStruct((T, D, W), b16), jax.ShapeDtypeStruct((8, D), f32),
                   jax.ShapeDtypeStruct((n, 8, chunk), f32)],
        scratch_shapes=[pltpu.VMEM((rows, D), f32), pltpu.VMEM((rows, D), f32), pltpu.VMEM((rows, 128), f32),
                        pltpu.VMEM((rows, D), b16), pltpu.VMEM((D, rows), b16), pltpu.VMEM((rows, D), f32),
                        pltpu.VMEM((8, 128), f32), pltpu.VMEM((rows, D), b16), pltpu.VMEM((D, rows), b16),
                        pltpu.VMEM((rows, chunk), f32), pltpu.VMEM((n, rows, chunk), b16),
                        pltpu.VMEM((n, rows, chunk), f32), pltpu.VMEM((rows, chunk), b16),
                        pltpu.VMEM((6, 8, D), f32)],
        compiler_params=pltpu.CompilerParams(vmem_limit_bytes=60 * 2**20),
    )(x, att, cot, w2, w2, w2, vec, ub)


VEC = 128


def spread_pieces(blocks, width, first, total):
    n, lanes = blocks.shape
    i = lax.broadcasted_iota(jnp.int32, (lanes, total), 0)
    col = lax.broadcasted_iota(jnp.int32, (lanes, total), 1)
    pick = jnp.where(i - first == lax.rem(col, width), 1.0, 0.0).astype(jnp.bfloat16)
    wide = nn(blocks, pick)
    dev = lax.broadcasted_iota(jnp.int32, (n, total), 0)
    col = lax.broadcasted_iota(jnp.int32, (n, total), 1)
    return jnp.sum(jnp.where(dev == col // width, wide, 0.0), axis=0, keepdims=True)


def pack(widths):
    offs, at = [], 0
    for w in widths:
        if at % VEC + w > VEC:
            at += VEC - at % VEC
        offs.append(at)
        at += w
    return offs, -(-at // VEC)


def small_widths(sizes, D, W, H):
    F, C, T = sizes
    n_dev = T * F * C
    return [T * W // n_dev, T * W // n_dev, T * H // n_dev] + [D // (F * C)] * 6


def front_kernel(cfg, *refs):
    sizes, S, W, H, chunk = cfg
    x_ref, cot_ref, segs_ref, wq_in, wk_in, wv_in, wo_in, up_in, dn_in = refs[:9]
    small_refs = refs[9:18]
    (q_ref, k_ref, v_ref, ah_ref, ar_ref, lse_ref, xf_ref, cf_ref, sf_ref, g1_ref, g2_ref,
     vec_ref, ub_ref, xm_ref, zero, zseg, xv, wv, pv, sv, wide, v_t, w1_ref, w2_ref, seg_ref, rows,
     ssem, r1, r2, lsem, tss, trs, tls, csem) = refs[18:]
    me = Place(sizes)
    C, X, T = me.C, me.X, me.T
    R, D = xv.shape[1:]
    r = wv.shape[3]
    L = C * R
    f32, b16 = jnp.float32, jnp.bfloat16
    offs, n_rows = pack([ref.shape[1] for ref in small_refs])
    w1_ref[:, :W] = wq_in[...]
    w1_ref[:, W:2 * W] = wk_in[...]
    w1_ref[:, 2 * W:3 * W] = wv_in[...]
    w2_ref[:, :H] = up_in[...]
    w2_ref[:, H:2 * H] = dn_in[...]
    w2_ref[:, 2 * H:] = wo_in[...]
    rows[...] = jnp.zeros_like(rows)
    for i, ref in enumerate(small_refs):
        rows[i:i + 1, :ref.shape[1]] = ref[...].astype(f32)
    block = [jnp.zeros((1, VEC), f32) for _ in range(n_rows)]
    for i, off in enumerate(offs):
        one = jnp.broadcast_to(rows[i:i + 1, :], (8, VEC))
        block[off // VEC] += (pltpu.roll(one, off % VEC, 1) if off % VEC else one)[0:1]
    pad = [jnp.zeros((r - n_rows, VEC), f32)] if r > n_rows else []
    w1_ref[:, 3 * W:] = jnp.concatenate(block + pad, axis=0).astype(b16)
    for i in range(S):
        seg_ref[i] = jnp.broadcast_to(segs_ref[i:i + 1, :].astype(f32), (8, R))
    me.greet(True)
    sends = Sends(ssem)
    tok = Tokens(me, S)
    items = [(x_ref, xf_ref, True, tss.at[0], trs.at[0], tls.at[0]),
             (seg_ref, sf_ref, True, tss.at[1], trs.at[1], tls.at[1]),
             (cot_ref, cf_ref, False, tss.at[2], trs.at[2], tls.at[2])]
    idle = jnp.logical_not(tok.busy)
    fills = ([(zero, xf_ref.at[i]) for i in range(C)] + [(zseg, sf_ref.at[i]) for i in range(C)]
             + [(zero, cf_ref.at[i]) for i in range(C // 2)])

    @pl.when(idle)
    def _():
        zero[...] = jnp.zeros_like(zero)
        zseg[...] = jnp.zeros_like(zseg)
        for i, (a, b) in enumerate(fills):
            pltpu.make_async_copy(a, b, tls.at[3 + i]).start()

    steps = {}
    for group, w_ref, g_ref, recv, n in (("1", w1_ref, g1_ref, r1, 0), ("2", w2_ref, g2_ref, r2, 1)):
        for name, step in gather_events(me, w_ref, g_ref, sends, recv, lsem.at[n]).items():
            steps[group + name] = step
    half = L // 2

    def each(f, its):
        return lambda: [f(*it) for it in its]

    for name, its in (("X", items[:2]), ("C", items[2:])):
        steps[name + "o"] = each(tok.out, its)
        steps[name + "w"] = each(tok.out_done, its)
        steps[name + "e"] = each(tok.out_end, its)

    def filled():
        @pl.when(idle)
        def _():
            for i, (a, b) in enumerate(fills):
                pltpu.make_async_copy(a, b, tls.at[3 + i]).wait()
    steps["filled"] = filled

    loads = [(xf_ref, xv), (sf_ref, sv), (g1_ref.at[me.c], wv)]
    pieces = [(g1_ref.at[t, xx, cc, zz, :, pl.ds(3 * W, VEC)], pv.at[((t * X + xx) * 2 + cc) * C + zz])
              for t in range(T) for xx in range(X) for cc in range(2) for zz in range(C)]
    loads = [pltpu.make_async_copy(a, b, csem.at[i]) for i, (a, b) in enumerate(loads + pieces)]

    def load():
        for cp in loads:
            cp.start()
    steps["load"] = load

    def vectors():
        for cp in loads:
            cp.wait()
        blocks = jnp.concatenate([pv[:, i, :] for i in range(n_rows)], axis=1)
        n_dev = blocks.shape[0]
        qw, uw = T * W // n_dev, T * H // n_dev
        qb = spread_pieces(blocks, qw, offs[0], T * W)
        vb = spread_pieces(blocks, qw, offs[1], T * W)
        ub = spread_pieces(blocks, uw, offs[2], T * H)
        for i in range(T * H // chunk):
            ub_ref[i] = ub[:, i * chunk:(i + 1) * chunk]
        once = blocks[:n_dev // T]
        for i in range(6):
            vec_ref[i:i + 1, :] = spread_pieces(once, r, offs[3 + i], D)
        first = me.c == 0
        vec_ref[6:7, :W] = jnp.where(first, qb[:, :W], qb[:, W:])
        vec_ref[7:8, :W] = jnp.where(first, vb[:, :W], vb[:, W:])
    steps["vectors"] = vectors

    def project():
        weights = wv[...].reshape(D, wv.shape[-1])

        def body(i, carry):
            at = pl.ds(pl.multiple_of(i * R, R), R)
            out = nn(xv[i], weights[:, :3 * W])
            q_ref[at, :] = (out[:, :W] + vec_ref[6:7, :W]).astype(b16)
            k_ref[at, :] = out[:, W:2 * W].astype(b16)
            v_ref[at, :] = (out[:, 2 * W:] + vec_ref[7:8, :W]).astype(b16)
            return carry
        lax.fori_loop(0, C, body, 0)
        out = pltpu.make_async_copy(xv.at[pl.ds(me.c * (C // 2), C // 2)], xm_ref, csem.at[len(loads) + 1])
        out.start()
        out.wait()
    steps["project"] = project

    def ready():
        spread_segments(sv, wide)
        for p in range(W // PAIR):
            v_t[p] = v_ref[:, p * PAIR:(p + 1) * PAIR].astype(f32).T.astype(b16)
    steps["ready"] = ready

    def attention(late):
        def body(it, carry):
            p, i = it // C, lax.rem(it, C)
            at = pl.ds(pl.multiple_of(i * R, R), R)
            cols = pl.ds(pl.multiple_of(p * PAIR, PAIR), PAIR)
            o, logs = attend_block(q_ref[at, cols], k_ref[:, cols], v_t[p], sv[i, 0:1, :],
                                   two_lanes(wide[...]))
            ah_ref[at, cols] = o.T.astype(b16)
            lse_ref[p, :, at] = jnp.concatenate(logs + [jnp.zeros((6, R), f32)], axis=0)
            for n, names in enumerate(late):
                if names:
                    @pl.when(it == n)
                    def _():
                        for name in names:
                            steps[name]()
            return carry
        lax.fori_loop(0, W // PAIR * C, body, 0)

    mine = pl.ds(pl.multiple_of(me.c * half, half), half)
    theirs = pl.ds(pl.multiple_of((1 - me.c) * half, half), half)
    heads = pl.ds(pl.multiple_of(me.c * W, W), W)

    def swap():
        sends.go(ah_ref.at[theirs, :], ar_ref.at[:, heads], csem.at[len(loads)], me.dev(c=1 - me.c))
        ar_ref[:, heads] = ah_ref[mine, :]
    steps["swap"] = swap
    early, late, end = FRONT_PLAN
    for name in early:
        steps[name]()
    attention(late)
    for name in end:
        steps[name]()
    arrived(ar_ref.at[:, heads], csem.at[len(loads)], me)
    sends.finish(me)


FRONT_PLAN = (
    ('1a0', '1a1', '1a2', '1a3', '1x0', '2a0', '1x1', '2a1', '1x2', '2a2', 'Xo', '1x3', '2a3', '1c0', '2x0',
     '1c1', '2x1', '1c2', '1c3', 'Xw', '1l', 'Xe', 'filled', 'load', '2x2', 'vectors', 'project', 'ready'),
    (('2x3',), (), ('Co',), ('2c0',), (), ('2c1',), (), ('2c2',), ('2c3',)),
    ('swap', '2l', 'Cw', 'Ce'),
)


def front(cfg, x, cot, segs, weights, small):
    sizes, S, W, H, chunk = cfg
    F, C, T = sizes
    _, R, D = x.shape
    X = F // 2
    L = C * R
    n = T * H // chunk
    f32, b = jnp.float32, jnp.bfloat16
    dma = pltpu.SemaphoreType.DMA
    r = weights[0].shape[0]
    n1, n2 = 3 * W + VEC, 2 * H + W
    sds = jax.ShapeDtypeStruct
    v = pltpu.VMEM
    return pl.pallas_call(
        functools.partial(front_kernel, cfg),
        in_specs=[ANY] * 2 + [VM] * (1 + len(weights) + len(small)),
        out_specs=[VM] * 6 + [ANY] * 5 + [VM] * 2 + [ANY],
        out_shape=[sds((L, W), b)] * 4 + [sds((L // 2, T * W), b), sds((W // PAIR, 8, L), f32),
                                          sds((C, R, D), b), sds((C // 2, R, D), b), sds((C, 8, R), f32),
                                          sds((T, X, 2, C, r, n1), b), sds((T, X, 2, C, r, n2), b),
                                          sds((8, D), f32), sds((n, 1, chunk), f32), sds((C // 2, R, D), b)],
        scratch_shapes=[v((R, D), b), v((8, R), f32), v((C, R, D), b), v((X, 2, C, r, n1), b),
                        v((T * F * C, r, VEC), b), v((C, 8, R), f32), v((L, 128), f32), v((W // PAIR, PAIR, L), b),
                        v((r, n1), b), v((r, n2), b), v((S, 8, R), f32), v((16, VEC), f32),
                        dma((2 * gather_count(sizes) + 1,)), dma((T * F * C,)), dma((T * F * C,)), dma((2,)),
                        dma((3, S + C // 2)), dma((3, C)), dma((3 + 3 * C,)), dma((5 + T * F * C,))],
        compiler_params=pltpu.CompilerParams(collective_id=0, has_side_effects=True,
                                             vmem_limit_bytes=60 * 2**20),
    )(x, cot, segs, *weights, *small)


def take(vec, index, width):
    n = vec.shape[1]
    wide = jnp.broadcast_to(vec, (8, n))
    return pltpu.roll(wide, lax.rem(n - index * width, n), 1)[0:1, :VEC]


def back_kernel(cfg, q_ref, k_ref, v_ref, ah_ref, lse_ref, sf_ref, do_ref, one_ref, res_ref, xf_ref, g1_ref,
                gff_ref, go_ref, gvec_ref, gub_ref,
                res_out, ing_out, oq_ref, oup_ref, odn_ref, oo_ref, vs_ref,
                doh, dqkv, k_t, wide, dk_sum, dv_sum, xt, xv, wv, gq, one_v, part, got_part, ing,
                vec, vacc, vgot, *scr):
    sizes, S, W, H, chunk = cfg
    bf, bo, bq = scr[:7], scr[7:14], scr[14:21]
    ssem, rf, ro, rq, rv, lf, lo, lq, tss, trs, tls, csem = scr[21:]
    me = Place(sizes)
    C, X, T = me.C, me.X, me.T
    R, D = xv.shape[1:]
    L = C * R
    half = L // 2
    f32, b16 = jnp.float32, jnp.bfloat16
    me.greet(True)
    sends = Sends(ssem)
    tok = Tokens(me, S)
    J = H // chunk
    other = me.dev(c=1 - me.c)
    mine = pl.ds(pl.multiple_of(me.c * half, half), half)
    theirs = pl.ds(pl.multiple_of((1 - me.c) * half, half), half)
    heads = pl.ds(pl.multiple_of(me.c * W, W), W)
    their_heads = pl.ds(pl.multiple_of((1 - me.c) * W, W), W)

    sends.go(do_ref.at[:, their_heads], doh.at[mine, :], csem.at[0], other)
    loads = [(do_ref.at[:, heads], doh.at[mine, :]), (xf_ref, xv), (g1_ref.at[me.c], wv), (one_ref, one_v)]
    loads = [pltpu.make_async_copy(a, b, csem.at[2 + i]) for i, (a, b) in enumerate(loads)]
    for cp in loads:
        cp.start()
    def put_ff(i, total):
        j, kind = i // 2, i % 2
        (oup_ref, odn_ref)[kind][:, j * chunk:(j + 1) * chunk] = total

    def put_o(i, total):
        oo_ref[...] = total

    def put_q(i, total):
        oq_ref[...] = total

    steps = {}
    for name, group in (("f", reduce_events(me, gff_ref, False, bf, sends, rf, lf, put_ff)),
                        ("o", reduce_events(me, go_ref, False, bo, sends, ro, lo, put_o)),
                        ("q", reduce_events(me, gq, True, bq, sends, rq, lq, put_q)),
                        ("t", total_events(me, vec, (vacc, vgot), vec, sends, rv))):
        for key, step in group.items():
            steps[name + key] = step
    n_vec = vec.shape[0]
    n_pairs = W // PAIR
    r = gq.shape[4]
    res_item = (res_ref, res_out, tss.at[0], trs.at[0], tls.at[0])
    ing_item = (ing, ing_out, tss.at[1], trs.at[1], tls.at[1])
    for name, item in (("R", res_item), ("I", ing_item)):
        steps[name + "o"] = lambda item=item: tok.back(*item)
        steps[name + "p"] = lambda item=item: tok.back_pass(*item)
        steps[name + "e"] = lambda item=item: tok.back_end(*item)

    def keys():
        spread_segments(sf_ref, wide)
        for p in range(n_pairs):
            k_t[p] = k_ref[:, p * PAIR:(p + 1) * PAIR].astype(f32).T.astype(b16)
    steps["keys"] = keys

    def upstream():
        loads[0].wait()
        arrived(doh.at[theirs, :], csem.at[0], me)
    steps["upstream"] = upstream

    def attention(late):
        def body(it, carry):
            p, i = it // C, lax.rem(it, C)
            at = pl.ds(pl.multiple_of(i * R, R), R)
            cols = pl.ds(pl.multiple_of(p * PAIR, PAIR), PAIR)
            dq, dk, dv = attend_back_block(q_ref[at, cols], k_ref[:, cols], k_t[p], v_ref[:, cols], doh[at, cols],
                                           ah_ref[at, cols], lse_ref[p, :, at], sf_ref[i, 0:1, :],
                                           two_lanes(wide[...]))
            dqkv[at, cols] = dq.astype(b16)

            @pl.when(i == 0)
            def _():
                dk_sum[...] = dk
                dv_sum[...] = dv

            @pl.when(i > 0)
            def _():
                dk_sum[...] += dk
                dv_sum[...] += dv

            @pl.when(i == C - 1)
            def _():
                dqkv[:, pl.ds(pl.multiple_of(W + p * PAIR, PAIR), PAIR)] = dk_sum[...].astype(b16)
                dqkv[:, pl.ds(pl.multiple_of(2 * W + p * PAIR, PAIR), PAIR)] = dv_sum[...].astype(b16)

            for n, names in enumerate(late):
                if names:
                    @pl.when(it == n)
                    def _():
                        for name in names:
                            steps[name]()
            return carry
        lax.fori_loop(0, n_pairs * C, body, 0)

    def inputs_turned():
        for cp in loads[1:]:
            cp.wait()
        for i in range(C):
            for j in range(0, R, 128):
                xt[:, i * R + j:i * R + j + 128] = xv[i, j:j + 128, :].astype(f32).T.astype(b16)
    steps["xt"] = inputs_turned

    def projections():
        step = D // (2 * X)

        def body(i, carry):
            rows = pl.ds(pl.multiple_of(i * step, step), step)
            out = nn(xt[rows, :], dqkv[...]).astype(b16)
            gq[0, i // 2, lax.rem(i, 2)] = out.reshape(C, r, 3 * W)
            return carry
        lax.fori_loop(0, 2 * X, body, 0)
    steps["gq"] = projections

    def back_project(rows):
        return nt(dqkv[rows, :], wv[...].reshape(D, wv.shape[-1])[:, :3 * W])

    def give():
        part[...] = back_project(theirs).astype(b16)
        sends.go(part, got_part, csem.at[1], other)
    steps["give"] = give

    def keep():
        one_v[...] += back_project(mine)
    steps["keep"] = keep

    def join():
        arrived(got_part, csem.at[1], me)
        for i in range(C // 2):
            at = slice(i * R, (i + 1) * R)
            ing[i] = (one_v[at, :] + got_part[at, :].astype(f32)).astype(b16)
    steps["join"] = join
    n_flat = 2 * T * W + T * H + 6 * D

    def sums():
        zeros = jnp.zeros((1, W), f32)
        total = nn(jnp.ones((8, L), b16), dqkv[...])[0:1]
        first = me.c == 0
        place = lambda v: [jnp.where(first, v, zeros), jnp.where(first, zeros, v)]
        flat = place(total[:, :W]) + place(total[:, 2 * W:])
        flat += [jnp.sum(gub_ref[i], axis=0, keepdims=True) for i in range(T * J)]
        flat += [gvec_ref[i:i + 1, :] for i in range(6)]
        flat = jnp.concatenate(flat, axis=1)
        for i in range(n_flat // 128):
            vec[i:i + 1, :] = flat[:, i * 128:(i + 1) * 128]
        if n_vec * 128 > n_flat:
            vec[n_flat // 128:, :] = jnp.zeros((n_vec - n_flat // 128, 128), f32)
    steps["sums"] = sums

    def vectors():
        total = jnp.concatenate([vec[i:i + 1, :] for i in range(n_flat // 128)], axis=1)
        fz = (2 * me.x + me.c) * C + me.z
        tfz = me.y * (X * 2 * C) + fz
        n_dev = T * X * 2 * C
        qw, uw = T * W // n_dev, T * H // n_dev
        at = 0
        for i, (n, w, here) in enumerate([(T * W, qw, tfz)] * 2 + [(T * H, uw, tfz)] + [(D, r, fz)] * 6):
            vs_ref[i:i + 1, :] = take(total[:, at:at + n], here, w)
            at += n
    steps["vectors"] = vectors

    early, late, end = BACK_PLAN
    for name in early:
        steps[name]()
    attention(late)
    for name in end:
        steps[name]()
    sends.finish(me)


BACK_PLAN = (
    ('ff', 'of', 'Ro', 'keys', 'upstream', 'fd', 'fr', 'od', 'or'),
    (('fs1', 'os1'), ('fs2',), ('fs3', 'fo'), ('fz1',), ('fs0',), ('fz2', 'oo'), ('fz3', 'oz1'), ('Rp',),
     ('os2',), ('os3', 'oz2'), ('os0', 'oz3'), ('fz0', 'xt')),
    ('gq', 'qf', 'give', 'qd', 'qr', 'keep', 'sums', 't0', 'qs1', 'qs2', 'qs3', 'qo', 'join', 'Io', 'qs0', 't1',
     'qz1', 'qz2', 't2', 'qz3', 'qz0', 'oz0', 'fl', 'ol', 't3', 'ql', 't4', 'vectors', 'Ip', 'Re', 'Ie'),
)


def back(cfg, q, k, v, ah, lse, sf, do, one, res, xf, g1, gff, go, gvec, gub):
    sizes, S, W, H, chunk = cfg
    F, C, T = sizes
    X = F // 2
    _, R, D = xf.shape
    L = C * R
    J = H // chunk
    r = g1.shape[4]
    f32, b = jnp.float32, jnp.bfloat16
    dma = pltpu.SemaphoreType.DMA
    sds = jax.ShapeDtypeStruct
    vm = pltpu.VMEM
    steps = total_count(sizes)
    n_vec = -(-(2 * T * W + T * H + 6 * D) // 1024) * 8
    sems = reduce_sems(sizes)
    return pl.pallas_call(
        functools.partial(back_kernel, cfg),
        in_specs=[VM] * 6 + [ANY] * 7 + [VM] * 2,
        out_specs=[ANY] * 2 + [VM] * 5,
        out_shape=[sds((S, R, D), b), sds((S, R, D), b), sds((r, 3 * W), f32), sds((r, H), f32), sds((r, H), f32),
                   sds((r, W), f32), sds((16, VEC), f32)],
        scratch_shapes=[vm((L, W), b), vm((L, 3 * W), b), vm((W // PAIR, PAIR, L), b), vm((L, 128), f32),
                        vm((L, PAIR), f32), vm((L, PAIR), f32), vm((D, L), b), vm((C, R, D), b),
                        vm((X, 2, C, r, g1.shape[5]), b), vm((1, X, 2, C, r, 3 * W), b), vm((L // 2, D), f32),
                        vm((L // 2, D), b), vm((L // 2, D), b), vm((C // 2, R, D), b),
                        vm((n_vec, 128), f32), vm((4, n_vec, 128), f32), vm((steps, n_vec, 128), f32)]
        + reduce_scratch(sizes, 2 * J, r, chunk, False) + reduce_scratch(sizes, 1, r, W, False)
        + reduce_scratch(sizes, 1, r, 3 * W, True)
        + [dma((2 * reduce_count(sizes, False) + reduce_count(sizes, True) + steps + 2,)),
           dma((sems,)), dma((sems,)), dma((sems,)), dma((steps,)), dma((T * X,)), dma((T * X,)), dma((X,)),
           dma((2, C // 2 + S)), dma((2, S)), dma((2,)), dma((6,))],
        compiler_params=pltpu.CompilerParams(collective_id=1, has_side_effects=True,
                                             vmem_limit_bytes=62 * 2**20),
    )(q, k, v, ah, lse, sf, do, one, res, xf, g1, gff, go, gvec, gub)


def finish_kernel(W, res_in, ing_in, oq_in, oup_in, odn_in, oo_in, vs_in,
                  res, ing, oq, ok, ov, oo, oup, odn, *small):
    res[...] = res_in[...]
    ing[...] = ing_in[...].astype(jnp.float32)

    @pl.when(pl.program_id(0) == 0)
    def _():
        oq[...] = oq_in[:, :W]
        ok[...] = oq_in[:, W:2 * W]
        ov[...] = oq_in[:, 2 * W:]
        oup[...] = oup_in[...]
        oo[...] = oo_in[...]
        odn[...] = odn_in[...]
        for i, ref in enumerate(small):
            ref[...] = vs_in[i:i + 1, :ref.shape[1]]


def finish(cfg, widths, *arrays):
    sizes, S, W, H, chunk = cfg
    res, ing, oq = arrays[:3]
    r = oq.shape[0]
    R, D = res.shape[1:]
    f32 = jnp.float32
    token = pl.BlockSpec((1, R, D), lambda i: (i, 0, 0))
    whole = lambda shape: pl.BlockSpec(shape, lambda i: (0,) * len(shape))
    shapes = [(r, W)] * 4 + [(r, H), (r, H)] + [(1, w) for w in widths]
    return pl.pallas_call(
        functools.partial(finish_kernel, W),
        grid=(S,),
        in_specs=[token, token] + [whole(a.shape) for a in arrays[2:]],
        out_specs=[token, token] + [whole(shape) for shape in shapes],
        out_shape=[jax.ShapeDtypeStruct((S, R, D), jnp.bfloat16), jax.ShapeDtypeStruct((S, R, D), f32)]
        + [jax.ShapeDtypeStruct(shape, f32) for shape in shapes],
        compiler_params=pltpu.CompilerParams(vmem_limit_bytes=62 * 2**20),
    )(*arrays)


def chunk_of(H):
    for w in (512, 384, 256, 128):
        if H % w == 0:
            return w
    return H


def on_device(sizes, inputs, segments, cotangent, query_weight, key_weight, value_weight,
              output_weight, up_weight, down_weight, *small):
    F, C, T = sizes
    X = F // 2
    S, R, D = inputs.shape
    W = query_weight.shape[1]
    H = up_weight.shape[1]
    r = query_weight.shape[0]
    half = C * R // 2
    chunk = chunk_of(H)
    J = H // chunk
    cfg = (sizes, S, W, H, chunk)
    weights = (query_weight, key_weight, value_weight, output_weight.T, up_weight, down_weight.T)
    widths = [v.shape[0] for v in small]
    small = [v.reshape(1, -1) for v in small]
    q, k, v, ah, ar, lse, xf, cf, sf, g1, g2, vec, ub, xm = front(
        cfg, inputs, cotangent, segments, weights, small)
    res, one, do, gff, go, gvec, gub = middle(
        T, xm.reshape(half, D), ar, cf.reshape(half, D), g2.reshape(T, D, -1), vec, ub, chunk)
    landed = back(cfg, q, k, v, ah, lse, sf, do, one, res.reshape(C // 2, R, D), xf, g1,
                  gff.reshape(T, 2 * J, X, 2, C, r, chunk), go.reshape(T, 1, X, 2, C, r, W), gvec, gub)
    outs = finish(cfg, widths, *landed)
    return tuple(outs[:5]) + (outs[5].T, outs[6], outs[7].T) + tuple(v.reshape(-1) for v in outs[8:])


def solution(mesh):
    sizes = (mesh.shape["fsdp"], mesh.shape["ctx"], mesh.shape["tp"])
    every = ("fsdp", "ctx")
    rows, cols, one, three = P(every, "tp"), P("tp", every), P(every), P(("tp",) + every)
    token = P("fsdp", "ctx", None)
    weights = (rows, rows, rows, cols, rows, cols)
    vectors = (three, three, three) + (one,) * 6
    return jax.shard_map(
        functools.partial(on_device, sizes), mesh=mesh,
        in_specs=(token, P("fsdp", "ctx"), token) + weights + vectors,
        out_specs=(token, token) + weights + vectors, check_vma=False)
```

```python
import functools
import jax
import jax.numpy as jnp
from jax import lax
from jax.sharding import PartitionSpec as P
from jax.experimental import pallas as pl
from jax.experimental.pallas import tpu as pltpu

MESH = pl.DeviceIdType.MESH
ANY = pl.BlockSpec(memory_space=pl.ANY)
VM = pl.BlockSpec(memory_space=pltpu.VMEM)


class Place:
    def __init__(self, sizes):
        self.F, self.C, self.T = sizes
        self.X = self.F // 2
        f = lax.axis_index("fsdp")
        self.x = f // 2
        self.c = lax.rem(f, 2)
        self.z = lax.axis_index("ctx")
        self.y = lax.axis_index("tp")

    def dev(self, x=None, c=None, z=None, y=None):
        x = self.x if x is None else x
        c = self.c if c is None else c
        return (2 * x + c, self.z if z is None else z, self.y if y is None else y)

    def z_off(self, d):
        return lax.rem(self.z + d + self.C, self.C)

    def x_off(self, d):
        return lax.rem(self.x + d + self.X, self.X)

    def greet(self, chip_wide):
        bar = pltpu.get_barrier_semaphore()
        devs = [self.dev(c=1 - self.c), self.dev(y=1 - self.y)]
        devs += [self.dev(x=self.x_off(d)) for d in range(1, self.X)]
        for d in range(1, self.C):
            devs.append(self.dev(z=self.z_off(d)))
            if chip_wide:
                devs.append(self.dev(z=self.z_off(d), c=1 - self.c))
        for d in devs:
            pl.semaphore_signal(bar, inc=1, device_id=d, device_id_type=MESH)
        pl.semaphore_wait(bar, len(devs))


class Sends:
    def __init__(self, sems):
        self.sems, self.n, self.waits = sems, 0, []

    def go(self, src, dst, recv, dev, like=None, when=None):
        pltpu.make_async_remote_copy(
            src_ref=src, dst_ref=dst, send_sem=self.sems.at[self.n], recv_sem=recv,
            device_id=dev, device_id_type=MESH).start()
        self.n += 1
        self.waits.append((src if like is None else like, when))

    def finish(self, me):
        for n, (like, when) in enumerate(self.waits):
            def wait():
                pltpu.make_async_remote_copy(
                    src_ref=like, dst_ref=like, send_sem=self.sems.at[n], recv_sem=self.sems.at[n],
                    device_id=me.dev(c=1 - me.c), device_id_type=MESH).wait_send()
            given(when, wait)
        self.waits = []


def given(when, body):
    if when is None:
        body()
    else:
        pl.when(when())(body)


def arrived(dst, recv, pl_):
    pltpu.make_async_remote_copy(
        src_ref=dst, dst_ref=dst, send_sem=recv, recv_sem=recv,
        device_id=pl_.dev(c=1 - pl_.c), device_id_type=MESH).wait_recv()


def line_order(C, z):
    return [z] + [z + sign * k for k in range(1, C) for sign in (-1, 1) if 0 <= z + sign * k < C]


def pick(index, table):
    out = table[-1]
    for i in reversed(range(len(table) - 1)):
        out = jnp.where(index == i, table[i], out)
    return jnp.int32(out)


def gather_events(me, own, full, sends, recv, lsem):
    C, X = me.C, me.X
    sem = lambda t, x, c, z: recv.at[((t * X + x) * 2 + c) * C + z]
    slot = lambda t, x, c, z: full.at[t, x, c, z]
    like = slot(0, 0, 0, 0)
    orders = [line_order(C, z) for z in range(C)]
    where = lambda m: pick(me.z, [o[m] for o in orders])

    def push(src, at, dev, when=None):
        sends.go(src, slot(*at), sem(*at), dev, like, when)

    def wait(at):
        arrived(slot(*at), sem(*at), me)

    core, side = me.dev(c=1 - me.c), me.dev(y=1 - me.y)
    xs = [(me.x_off(d), me.dev(x=me.x_off(d))) for d in range(1, X)]
    local = pltpu.make_async_copy(own, slot(me.y, me.x, me.c, me.z), lsem)

    def along(m):
        def run():
            zz = where(m)
            at = (me.y, me.x, me.c, zz)
            src = slot(*at) if m else own
            if m:
                wait(at)
            for sign in (-1, 1):
                def onward(sign=sign):
                    zz = where(m)
                    return ((zz - me.z) * sign <= 0) & (me.z + sign >= 0) & (me.z + sign < C)

                @pl.when(onward())
                def _():
                    push(src, at, me.dev(z=me.z + sign), onward)
            for _, dev in xs:
                push(src, at, dev)
            push(src, at, side)
            push(src, at, core)
            if not m:
                local.start()
        return run

    def across(m):
        def run():
            zz = where(m)
            at = (1 - me.y, me.x, me.c, zz)
            wait(at)
            if m < C // 2:
                for _, dev in xs:
                    push(slot(*at), at, dev)
            push(slot(*at), at, core)
            for xo, _ in xs:
                at = (me.y, xo, me.c, zz)
                wait(at)
                if m >= C // 2:
                    push(slot(*at), at, side)
                push(slot(*at), at, core)
        return run

    def corner(m):
        def run():
            zz = where(m)
            for xo, _ in xs:
                at = (1 - me.y, xo, me.c, zz)
                wait(at)
                push(slot(*at), at, core)
        return run

    def last():
        for t in range(me.T):
            for xx in range(X):
                for zz in range(C):
                    wait((t, xx, 1 - me.c, zz))
        local.wait()

    steps = {"l": last}
    for m in range(C):
        steps["a%d" % m] = along(m)
        steps["x%d" % m] = across(m)
        steps["c%d" % m] = corner(m)
    return steps


def gather_count(sizes):
    F, C, T = sizes
    X = F // 2
    return C * (4 * X + 4)


class Tokens:
    def __init__(self, me, seqs):
        self.me, self.S = me, seqs
        self.half = me.C // 2
        self.lo = me.y * (me.C - seqs)
        self.busy = (me.z >= self.lo) & (me.z < self.lo + seqs)
        self.owner = me.c == me.y

    def out(self, src, dst, full, ssem, rsem, lsem):
        me, half = self.me, self.half
        k = me.z // half
        at = me.z if full else lax.rem(me.z, half)

        @pl.when(self.owner)
        def _():
            for s in range(self.S):
                here = (self.lo + s == me.z) & (k == me.c)

                @pl.when(here)
                def _():
                    pltpu.make_async_copy(src.at[s], dst.at[at], lsem).start()

                @pl.when(jnp.logical_not(here))
                def _():
                    pltpu.make_async_remote_copy(
                        src_ref=src.at[s], dst_ref=dst.at[at], send_sem=ssem.at[s],
                        recv_sem=rsem.at[lax.rem(me.z, half)],
                        device_id=me.dev(c=k, z=self.lo + s), device_id_type=MESH).start()

    def out_done(self, src, dst, full, ssem, rsem, lsem):
        me, half = self.me, self.half

        @pl.when(self.busy)
        def _():
            for i in range(half):
                zq = me.c * half + i
                at = zq if full else i
                here = (zq == me.z) & (me.c == me.y)

                @pl.when(here)
                def _():
                    pltpu.make_async_copy(src.at[0], dst.at[at], lsem).wait()

                @pl.when(jnp.logical_not(here))
                def _():
                    arrived(dst.at[at], rsem.at[i], me)

                if full:
                    pltpu.make_async_remote_copy(
                        src_ref=dst.at[at], dst_ref=dst.at[at], send_sem=ssem.at[self.S + i],
                        recv_sem=rsem.at[half + i], device_id=me.dev(c=1 - me.c),
                        device_id_type=MESH).start()

    def out_end(self, src, dst, full, ssem, rsem, lsem):
        me, half = self.me, self.half
        k = me.z // half

        @pl.when(self.owner)
        def _():
            for s in range(self.S):
                here = (self.lo + s == me.z) & (k == me.c)

                @pl.when(jnp.logical_not(here))
                def _():
                    pltpu.make_async_remote_copy(
                        src_ref=src.at[s], dst_ref=dst.at[0], send_sem=ssem.at[s],
                        recv_sem=rsem.at[0], device_id=me.dev(c=1 - me.c),
                        device_id_type=MESH).wait_send()

        if full:
            @pl.when(self.busy)
            def _():
                for i in range(half):
                    zq = (1 - me.c) * half + i
                    arrived(dst.at[zq], rsem.at[half + i], me)
                    pltpu.make_async_remote_copy(
                        src_ref=dst.at[0], dst_ref=dst.at[0], send_sem=ssem.at[self.S + i],
                        recv_sem=rsem.at[0], device_id=me.dev(c=1 - me.c),
                        device_id_type=MESH).wait_send()

    def back(self, src, dst, ssem, rsem, lsem):
        me, half = self.me, self.half

        @pl.when(self.busy)
        def _():
            for i in range(half):
                zq = me.c * half + i
                here = (zq == me.z) & (me.c == me.y)
                at = me.z - self.lo

                @pl.when(here)
                def _():
                    pltpu.make_async_copy(src.at[i], dst.at[at], lsem).start()

                @pl.when(jnp.logical_not(here))
                def _():
                    pltpu.make_async_remote_copy(
                        src_ref=src.at[i], dst_ref=dst.at[at], send_sem=ssem.at[i],
                        recv_sem=rsem.at[at], device_id=me.dev(c=me.y, z=zq),
                        device_id_type=MESH).start()

    def back_pass(self, src, dst, ssem, rsem, lsem):
        me, half = self.me, self.half
        k = me.z // half

        @pl.when(self.owner)
        def _():
            for s in range(self.S):
                here = (self.lo + s == me.z) & (k == me.c)

                @pl.when(here)
                def _():
                    pltpu.make_async_copy(src.at[0], dst.at[s], lsem).wait()

                @pl.when(jnp.logical_not(here))
                def _():
                    arrived(dst.at[s], rsem.at[s], me)

                pltpu.make_async_remote_copy(
                    src_ref=dst.at[s], dst_ref=dst.at[s], send_sem=ssem.at[half + s],
                    recv_sem=rsem.at[s], device_id=me.dev(y=1 - me.y),
                    device_id_type=MESH).start()

    def back_end(self, src, dst, ssem, rsem, lsem):
        me, half = self.me, self.half

        @pl.when(self.busy)
        def _():
            for i in range(half):
                zq = me.c * half + i
                here = (zq == me.z) & (me.c == me.y)

                @pl.when(jnp.logical_not(here))
                def _():
                    pltpu.make_async_remote_copy(
                        src_ref=src.at[i], dst_ref=dst.at[0], send_sem=ssem.at[i],
                        recv_sem=rsem.at[0], device_id=me.dev(c=1 - me.c),
                        device_id_type=MESH).wait_send()

        @pl.when(self.owner)
        def _():
            for s in range(self.S):
                pltpu.make_async_remote_copy(
                    src_ref=dst.at[s], dst_ref=dst.at[s], send_sem=ssem.at[half + s],
                    recv_sem=rsem.at[s], device_id=me.dev(y=1 - me.y),
                    device_id_type=MESH).wait_send()

        @pl.when(jnp.logical_not(self.owner))
        def _():
            for s in range(self.S):
                arrived(dst.at[s], rsem.at[s], me)


def reduce_events(me, split, bufs, sends, recv, finish, parts):
    acc, rc, xd, yd, xr, yr, zr = bufs
    C, X = me.C, me.X
    half = C // 2
    n_cols = acc.shape[2]
    like = acc.at[0, 0, :, 0]
    side = me.dev(y=1 - me.y)
    base = 0
    s_d = lambda d, j: recv.at[base + (d - 1) * C + j]
    base2 = base + (X - 1) * C
    s_xr = lambda d, j: recv.at[base2 + (d - 1) * C + j]
    base3 = base2 + (X - 1) * C
    s_yr = lambda j: recv.at[base3 + j]
    s_zr = lambda j: recv.at[base3 + C + j]
    quads = ([(1 - me.y, me.x_off(d)) for d in range(1, X)] + [(1 - me.y, me.x)]
             + [(me.y, me.x_off(d)) for d in range(1, X)] + [(me.y, me.x)])

    def add(a, b):
        def body(i, carry):
            a[i] = a[i] + b[i]
            return carry
        lax.fori_loop(0, n_cols, body, 0)

    def ready(n):
        t, x = quads[n]
        if split:
            if n == 0:
                for xo in [me.x_off(d) for d in range(1, X)] + [me.x]:
                    for view, sem in parts(1 - me.c, xo):
                        arrived(view, sem, me)
            return
        for view, sem in parts(t, x):
            arrived(view, sem, me)

        def body(i, carry):
            for z in range(C):
                acc[t, x, i, z] = acc[t, x, i, z] + rc[t, x, i, z]
            return carry
        lax.fori_loop(0, n_cols, body, 0)

    by_x = range(1, C)
    order = list(range(1, C)) + [0]

    def corner():
        for d in range(1, X):
            ready(d - 1)
            t, x = quads[d - 1]
            for j in order:
                zj = me.z_off(-j)
                if j in by_x:
                    sends.go(acc.at[t, x, :, zj], xd.at[d - 1, j - 1], s_d(d, j), me.dev(x=x), like)
                else:
                    sends.go(acc.at[t, x, :, zj], yd.at[d - 1, 0], s_d(d, j), side, like)

    def ready_sides():
        for n in range(X - 1, 2 * X - 1):
            ready(n)

    def spread(j):
        def run():
            zj = me.z_off(-j)
            t, x = me.y, me.x
            for d in range(1, X):
                xo = me.x_off(d)
                if j not in by_x:
                    arrived(yd.at[d - 1, 0], s_d(d, j), me)
                    add(acc.at[t, xo, :, zj], yd.at[d - 1, 0])
                sends.go(acc.at[t, xo, :, zj], xr.at[d - 1, j], s_xr(d, j), me.dev(x=xo), like)
            t = 1 - me.y
            for d in range(1, X):
                if j in by_x:
                    arrived(xd.at[d - 1, j - 1], s_d(d, j), me)
                    add(acc.at[t, x, :, zj], xd.at[d - 1, j - 1])
            sends.go(acc.at[t, x, :, zj], yr.at[j], s_yr(j), side, like)
        return run

    def to_z(j):
        def run():
            t, x = me.y, me.x
            zj = me.z_off(-j)
            for d in range(1, X):
                arrived(xr.at[d - 1, j], s_xr(d, j), me)
                add(acc.at[t, x, :, zj], xr.at[d - 1, j])
            arrived(yr.at[j], s_yr(j), me)
            add(acc.at[t, x, :, zj], yr.at[j])
            if j:
                sends.go(acc.at[t, x, :, zj], zr.at[j - 1], s_zr(j - 1), me.dev(z=zj), like)
        return run

    def last():
        for j in range(1, C):
            arrived(zr.at[j - 1], s_zr(j - 1), me)
        for i in range(n_cols):
            total = acc[me.y, me.x, i, me.z].astype(jnp.float32)
            for j in range(1, C):
                total = total + zr[j - 1, i].astype(jnp.float32)
            finish(i, total)

    steps = {"d": corner, "r": ready_sides, "o": lambda: ready(2 * X - 1), "l": last}
    for j in range(C):
        steps["s%d" % j] = spread(j)
        steps["z%d" % j] = to_z(j)
    return steps


def reduce_scratch(sizes, n, r, w, split):
    F, C, T = sizes
    X = F // 2
    half = C // 2
    v = lambda shape: pltpu.VMEM(shape, jnp.bfloat16)
    return [v((T, X, n, C, r, w)), v((1, 1, 1, 1, 16, 128) if split else (T, X, n, C, r, w)),
            v((X - 1, C - 1, n, r, w)), v((X - 1, 1, n, r, w)), v((X - 1, C, n, r, w)),
            v((C, n, r, w)), v((C - 1, n, r, w))]


def reduce_sems(sizes):
    F, C, T = sizes
    X = F // 2
    return 2 * (X - 1) * C + 2 * C


def reduce_count(sizes):
    F, C, T = sizes
    X = F // 2
    return 2 * (X - 1) * C + C + C - 1


def total_events(me, own, bufs, out, sends, recv):
    C, X = me.C, me.X
    acc, got = bufs
    groups = [[me.dev(c=1 - me.c)], [me.dev(x=me.x_off(d)) for d in range(1, X)],
              [me.dev(y=1 - me.y)], [me.dev(z=me.z_off(d)) for d in range(1, C)]]
    like = acc.at[0]
    bases = [sum(len(g) for g in groups[:i]) for i in range(len(groups))]

    def start(gi):
        for i, dev in enumerate(groups[gi]):
            sends.go(acc.at[gi], got.at[bases[gi] + i], recv.at[bases[gi] + i], dev, like)

    def first():
        acc[0] = own[...]
        start(0)

    steps = {"0": first}
    for gi in range(len(groups)):
        def step(gi=gi):
            total = acc[gi]
            for i in range(len(groups[gi])):
                arrived(got.at[bases[gi] + i], recv.at[bases[gi] + i], me)
                total = total + got[bases[gi] + i]
            if gi + 1 < len(groups):
                acc[gi + 1] = total
                start(gi + 1)
            else:
                out[...] = total
        steps[str(gi + 1)] = step
    return steps


def total_count(sizes):
    F, C, T = sizes
    return 1 + F // 2 - 1 + 1 + C - 1

HEAD = 64
PAIR = 2 * HEAD
SCALE = HEAD ** (-0.5)
norm_eps = 1e-12
masked_score = -1000000000.0


def nt(a, b):
    return lax.dot_general(a, b, (((1,), (1,)), ((), ())), preferred_element_type=jnp.float32)


def nn(a, b):
    return lax.dot_general(a, b, (((1,), (0,)), ((), ())), preferred_element_type=jnp.float32)


def spread_segments(seg_ref, wide):
    C, _, R = seg_ref.shape
    for i in range(C):
        for j in range(0, R, 128):
            row = jnp.broadcast_to(seg_ref[i, 0:1, j:j + 128], (128, 128))
            wide[i * R + j:i * R + j + 128, :] = row.T


def lanes_of(h, like):
    lane = lax.broadcasted_iota(jnp.int32, like.shape, like.ndim - 1)
    return jnp.where(lane // HEAD == h, like, jnp.zeros_like(like))


def two_lanes(wide):
    return jnp.concatenate([wide, wide], axis=1)


def attend_block(q, k, v_t, seg_q, seg_k):
    same = seg_k == seg_q
    outs, logs = [], []
    for h in range(2):
        s = nt(k, lanes_of(h, q) * jnp.bfloat16(SCALE))
        s = jnp.where(same, s, masked_score)
        peak = jnp.max(s, axis=0, keepdims=True)
        e = jnp.exp(s - peak)
        total = jnp.sum(e, axis=0, keepdims=True)
        o = nn(v_t, e.astype(jnp.bfloat16))
        outs.append(o[h * HEAD:(h + 1) * HEAD] * (1.0 / total))
        logs.append(peak + jnp.log(total))
    return jnp.concatenate(outs, axis=0), logs


def attend_back_block(q, k, k_t, v, do, o, lse, seg_q, seg_k):
    same = seg_k == seg_q
    prod = (do.astype(jnp.float32) * o.astype(jnp.float32)).T
    dq, dk, dv = [], None, None
    for h in range(2):
        qh = lanes_of(h, q) * jnp.bfloat16(SCALE)
        doh = lanes_of(h, do)
        s = nt(k, qh)
        p = jnp.exp(jnp.where(same, s, masked_score) - lse[h:h + 1])
        dp = nt(v, doh)
        inner = jnp.sum(prod[h * HEAD:(h + 1) * HEAD], axis=0, keepdims=True)
        ds = (p * (dp - inner)).astype(jnp.bfloat16)
        dv_h = nn(p.astype(jnp.bfloat16), doh)
        dk_h = nn(ds, qh)
        dv = dv_h if dv is None else dv + dv_h
        dk = dk_h if dk is None else dk + dk_h
        dq.append(nn(k_t, ds)[h * HEAD:(h + 1) * HEAD])
    return jnp.concatenate(dq, axis=0).T * SCALE, dk, dv

STRIP = 64


def fold(value):
    total = value[0:8]
    for i in range(8, value.shape[0], 8):
        total = total + value[i:i + 8]
    return total


def mean(value):
    return jnp.mean(value, axis=-1, keepdims=True)


def unit_of(value):
    centred = value - mean(value)
    factor = lax.rsqrt(mean(centred * centred) + norm_eps)
    return centred * factor, factor


def back_of(upstream, unit, factor, gain):
    along = upstream * gain
    return factor * (along - mean(along) - unit * mean(along * unit))


def flip(ref, out):
    rows = ref.shape[0]
    for i in range(0, rows, 128):
        out[:, i:i + 128] = ref[i:i + 128, :].astype(jnp.float32).T.astype(jnp.bfloat16)


VEC = 128


def spread_pieces(blocks, width, first, total):
    n, lanes = blocks.shape
    i = lax.broadcasted_iota(jnp.int32, (lanes, total), 0)
    col = lax.broadcasted_iota(jnp.int32, (lanes, total), 1)
    pick = jnp.where(i - first == lax.rem(col, width), 1.0, 0.0).astype(jnp.bfloat16)
    wide = nn(blocks, pick)
    dev = lax.broadcasted_iota(jnp.int32, (n, total), 0)
    col = lax.broadcasted_iota(jnp.int32, (n, total), 1)
    return jnp.sum(jnp.where(dev == col // width, wide, 0.0), axis=0, keepdims=True)


def pack(widths):
    offs, at = [], 0
    for w in widths:
        if at % VEC + w > VEC:
            at += VEC - at % VEC
        offs.append(at)
        at += w
    return offs, -(-at // VEC)


def small_widths(sizes, D, W, H):
    F, C, T = sizes
    n_dev = T * F * C
    return [T * W // n_dev, T * W // n_dev, T * H // n_dev] + [D // (F * C)] * 6


def front_kernel(cfg, *refs):
    sizes, S, W, H, chunk = cfg
    x_ref, cot_ref, segs_ref, wq_in, wk_in, wv_in, wo_in, up_in, dn_in = refs[:9]
    small_refs = refs[9:18]
    (q_ref, k_ref, v_ref, ah_ref, ar_ref, lse_ref, xf_ref, cf_ref, sf_ref, g1_ref, g2_ref,
     vec_ref, ub_ref, xm_ref, zero, zseg, xv, wv, pv, sv, wide, v_t, w1_ref, w2_ref, seg_ref, rows,
     ssem, r1, r2, lsem, tss, trs, tls, csem) = refs[18:]
    me = Place(sizes)
    C, X, T = me.C, me.X, me.T
    R, D = xv.shape[1:]
    r = wv.shape[3]
    L = C * R
    f32, b16 = jnp.float32, jnp.bfloat16
    offs, n_rows = pack([ref.shape[1] for ref in small_refs])
    w1_ref[:, :W] = wq_in[...]
    w1_ref[:, W:2 * W] = wk_in[...]
    w1_ref[:, 2 * W:3 * W] = wv_in[...]
    w2_ref[:, :H] = up_in[...]
    w2_ref[:, H:2 * H] = dn_in[...]
    w2_ref[:, 2 * H:] = wo_in[...]
    rows[...] = jnp.zeros_like(rows)
    for i, ref in enumerate(small_refs):
        rows[i:i + 1, :ref.shape[1]] = ref[...].astype(f32)
    block = [jnp.zeros((1, VEC), f32) for _ in range(n_rows)]
    for i, off in enumerate(offs):
        one = jnp.broadcast_to(rows[i:i + 1, :], (8, VEC))
        block[off // VEC] += (pltpu.roll(one, off % VEC, 1) if off % VEC else one)[0:1]
    pad = [jnp.zeros((r - n_rows, VEC), f32)] if r > n_rows else []
    w1_ref[:, 3 * W:] = jnp.concatenate(block + pad, axis=0).astype(b16)
    for i in range(S):
        seg_ref[i] = jnp.broadcast_to(segs_ref[i:i + 1, :].astype(f32), (8, R))
    me.greet(True)
    sends = Sends(ssem)
    tok = Tokens(me, S)
    items = [(x_ref, xf_ref, True, tss.at[0], trs.at[0], tls.at[0]),
             (seg_ref, sf_ref, True, tss.at[1], trs.at[1], tls.at[1]),
             (cot_ref, cf_ref, False, tss.at[2], trs.at[2], tls.at[2])]
    idle = jnp.logical_not(tok.busy)
    fills = ([(zero, xf_ref.at[i]) for i in range(C)] + [(zseg, sf_ref.at[i]) for i in range(C)]
             + [(zero, cf_ref.at[i]) for i in range(C // 2)])

    @pl.when(idle)
    def _():
        zero[...] = jnp.zeros_like(zero)
        zseg[...] = jnp.zeros_like(zseg)
        for i, (a, b) in enumerate(fills):
            pltpu.make_async_copy(a, b, tls.at[3 + i]).start()

    steps = {}
    for group, w_ref, g_ref, recv, n in (("1", w1_ref, g1_ref, r1, 0), ("2", w2_ref, g2_ref, r2, 1)):
        for name, step in gather_events(me, w_ref, g_ref, sends, recv, lsem.at[n]).items():
            steps[group + name] = step
    half = L // 2

    def each(f, its):
        return lambda: [f(*it) for it in its]

    for name, its in (("X", items[:2]), ("C", items[2:])):
        steps[name + "o"] = each(tok.out, its)
        steps[name + "w"] = each(tok.out_done, its)
        steps[name + "e"] = each(tok.out_end, its)

    def filled():
        @pl.when(idle)
        def _():
            for i, (a, b) in enumerate(fills):
                pltpu.make_async_copy(a, b, tls.at[3 + i]).wait()
    steps["filled"] = filled

    loads = [(xf_ref, xv), (sf_ref, sv), (g1_ref.at[me.c], wv)]
    pieces = [(g1_ref.at[t, xx, cc, zz, :, pl.ds(3 * W, VEC)], pv.at[((t * X + xx) * 2 + cc) * C + zz])
              for t in range(T) for xx in range(X) for cc in range(2) for zz in range(C)]
    loads = [pltpu.make_async_copy(a, b, csem.at[i]) for i, (a, b) in enumerate(loads + pieces)]

    def load():
        for cp in loads:
            cp.start()
    steps["load"] = load

    def vectors():
        for cp in loads:
            cp.wait()
        blocks = jnp.concatenate([pv[:, i, :] for i in range(n_rows)], axis=1)
        n_dev = blocks.shape[0]
        qw, uw = T * W // n_dev, T * H // n_dev
        qb = spread_pieces(blocks, qw, offs[0], T * W)
        vb = spread_pieces(blocks, qw, offs[1], T * W)
        ub = spread_pieces(blocks, uw, offs[2], T * H)
        for i in range(T * H // chunk):
            ub_ref[i] = ub[:, i * chunk:(i + 1) * chunk]
        once = blocks[:n_dev // T]
        for i in range(6):
            vec_ref[i:i + 1, :] = spread_pieces(once, r, offs[3 + i], D)
        first = me.c == 0
        vec_ref[6:7, :W] = jnp.where(first, qb[:, :W], qb[:, W:])
        vec_ref[7:8, :W] = jnp.where(first, vb[:, :W], vb[:, W:])
    steps["vectors"] = vectors

    def project():
        weights = wv[...].reshape(D, wv.shape[-1])

        def body(i, carry):
            at = pl.ds(pl.multiple_of(i * R, R), R)
            out = nn(xv[i], weights[:, :3 * W])
            q_ref[at, :] = (out[:, :W] + vec_ref[6:7, :W]).astype(b16)
            k_ref[at, :] = out[:, W:2 * W].astype(b16)
            v_ref[at, :] = (out[:, 2 * W:] + vec_ref[7:8, :W]).astype(b16)
            return carry
        lax.fori_loop(0, C, body, 0)
        out = pltpu.make_async_copy(xv.at[pl.ds(me.c * (C // 2), C // 2)], xm_ref, csem.at[len(loads) + 1])
        out.start()
        out.wait()
    steps["project"] = project

    def ready():
        spread_segments(sv, wide)
        for p in range(W // PAIR):
            v_t[p] = v_ref[:, p * PAIR:(p + 1) * PAIR].astype(f32).T.astype(b16)
    steps["ready"] = ready

    def attention(late):
        def body(it, carry):
            p, i = it // C, lax.rem(it, C)
            at = pl.ds(pl.multiple_of(i * R, R), R)
            cols = pl.ds(pl.multiple_of(p * PAIR, PAIR), PAIR)
            o, logs = attend_block(q_ref[at, cols], k_ref[:, cols], v_t[p], sv[i, 0:1, :],
                                   two_lanes(wide[...]))
            ah_ref[at, cols] = o.T.astype(b16)
            lse_ref[p, :, at] = jnp.concatenate(logs + [jnp.zeros((6, R), f32)], axis=0)
            for n, names in enumerate(late):
                if names:
                    @pl.when(it == n)
                    def _():
                        for name in names:
                            steps[name]()
            return carry
        lax.fori_loop(0, W // PAIR * C, body, 0)

    mine = pl.ds(pl.multiple_of(me.c * half, half), half)
    theirs = pl.ds(pl.multiple_of((1 - me.c) * half, half), half)
    heads = pl.ds(pl.multiple_of(me.c * W, W), W)

    def swap():
        sends.go(ah_ref.at[theirs, :], ar_ref.at[:, heads], csem.at[len(loads)], me.dev(c=1 - me.c))
        ar_ref[:, heads] = ah_ref[mine, :]
    steps["swap"] = swap
    early, late, end = FRONT_PLAN
    for name in early:
        steps[name]()
    attention(late)
    for name in end:
        steps[name]()
    arrived(ar_ref.at[:, heads], csem.at[len(loads)], me)
    sends.finish(me)


FRONT_PLAN = (
    ('1a0', '1a1', '1a2', '1a3', '1x0', '2a0', '1x1', '2a1', '1x2', '2a2', 'Xo', '1x3', '2a3', '1c0', '2x0',
     '1c1', '2x1', '1c2', '1c3', 'Xw', '1l', 'Xe', 'filled', 'load', '2x2', 'vectors', 'project', 'ready'),
    (('2x3',), (), ('Co',), ('2c0',), (), ('2c1',), (), ('2c2',), ('2c3',)),
    ('swap', '2l', 'Cw', 'Ce'),
)


def front(cfg, x, cot, segs, weights, small):
    sizes, S, W, H, chunk = cfg
    F, C, T = sizes
    _, R, D = x.shape
    X = F // 2
    L = C * R
    n = T * H // chunk
    f32, b = jnp.float32, jnp.bfloat16
    dma = pltpu.SemaphoreType.DMA
    r = weights[0].shape[0]
    n1, n2 = 3 * W + VEC, 2 * H + W
    sds = jax.ShapeDtypeStruct
    v = pltpu.VMEM
    return pl.pallas_call(
        functools.partial(front_kernel, cfg),
        in_specs=[ANY] * 2 + [VM] * (1 + len(weights) + len(small)),
        out_specs=[VM] * 6 + [ANY] * 5 + [VM] * 2 + [ANY],
        out_shape=[sds((L, W), b)] * 4 + [sds((L // 2, T * W), b), sds((W // PAIR, 8, L), f32),
                                          sds((C, R, D), b), sds((C // 2, R, D), b), sds((C, 8, R), f32),
                                          sds((T, X, 2, C, r, n1), b), sds((T, X, 2, C, r, n2), b),
                                          sds((8, D), f32), sds((n, 1, chunk), f32), sds((C // 2, R, D), b)],
        scratch_shapes=[v((R, D), b), v((8, R), f32), v((C, R, D), b), v((X, 2, C, r, n1), b),
                        v((T * F * C, r, VEC), b), v((C, 8, R), f32), v((L, 128), f32), v((W // PAIR, PAIR, L), b),
                        v((r, n1), b), v((r, n2), b), v((S, 8, R), f32), v((16, VEC), f32),
                        dma((2 * gather_count(sizes) + 1,)), dma((T * F * C,)), dma((T * F * C,)), dma((2,)),
                        dma((3, S + C // 2)), dma((3, C)), dma((3 + 3 * C,)), dma((5 + T * F * C,))],
        compiler_params=pltpu.CompilerParams(collective_id=0, has_side_effects=True,
                                             vmem_limit_bytes=60 * 2**20),
    )(x, cot, segs, *weights, *small)


def take(vec, index, width):
    n = vec.shape[1]
    wide = jnp.broadcast_to(vec, (8, n))
    return pltpu.roll(wide, lax.rem(n - index * width, n), 1)[0:1, :VEC]


def rest_kernel(cfg, q_ref, k_ref, v_ref, ah_ref, lse_ref, sf_ref, ar_ref, vec_ref, ub_ref,
                xm_ref, cf_ref, xf_ref, g1_ref, g2_ref,
                res_out, ing_out, oq_ref, oup_ref, odn_ref, oo_ref, vs_ref,
                xb, cb, unit, fac, low, low_t, acc, fl, fl_t, hid, act, slope, hl, wbuf, wo, sums, gub, tmp, stage,
                doh, away_o, away_q, got_part, vec, vacc, vgot, *scr):
    sizes, S, W, H, chunk = cfg
    bf, bo, bq = scr[:7], scr[7:14], scr[14:21]
    ssem, rf, ro, rq, rv, fc, fs, oc, qc, tss, trs, tls, csem, wsem = scr[21:]
    me = Place(sizes)
    C, X, T = me.C, me.X, me.T
    R, D = xb.shape[1:]
    L = C * R
    half = L // 2
    J = H // chunk
    n = T * J
    r = away_q.shape[3]
    f32, b16 = jnp.float32, jnp.bfloat16
    n_pairs = W // PAIR
    row = lambda i: vec_ref[i:i + 1, :]
    me.greet(True)
    sends = Sends(ssem)
    tok = Tokens(me, S)
    other = me.dev(c=1 - me.c)
    mine = pl.ds(pl.multiple_of(me.c * half, half), half)
    theirs = pl.ds(pl.multiple_of((1 - me.c) * half, half), half)
    heads = pl.ds(pl.multiple_of(me.c * W, W), W)

    def which(i):
        return jnp.where(i < J, 1 - me.y, me.y), lax.rem(i, J)

    def fetch(i, slot):
        t, j = which(i)
        return [pltpu.make_async_copy(
            g2_ref.at[t, :, pl.ds(pl.multiple_of(kind * H + j * chunk, chunk), chunk)],
            wbuf.at[2 * slot + kind], wsem.at[2 * slot + kind]) for kind in range(2)]

    loads = [pltpu.make_async_copy(a, b, csem.at[2 + i]) for i, (a, b) in enumerate(
        [(xm_ref, xb), (cf_ref, cb)] + [(g2_ref.at[t, :, pl.ds(2 * H, W)], wo.at[t]) for t in range(T)])]
    for cp in loads:
        cp.start()
    for cp in fetch(0, 0):
        cp.start()

    def put_ff(i, total):
        j, kind = i // 2, i % 2
        (oup_ref, odn_ref)[kind][:, j * chunk:(j + 1) * chunk] = total

    def put_o(i, total):
        oo_ref[...] = total

    def put_q(i, total):
        oq_ref[...] = total

    acc_f, rc_f = bf[:2]
    acc_o, rc_o = bo[:2]
    acc_q = bq[0]

    def parts_f(t, x):
        return [(rc_f.at[t, x, pl.ds(2 * j, 2)], fc.at[(t * X + x) * J + j]) for j in range(J)]

    def parts_o(t, x):
        return [(rc_o.at[t, x], oc.at[t * X + x])]

    def parts_q(t, x):
        return [(acc_q.at[t, x], qc.at[x])]

    def deal(cols, own_to, away_to):
        rows = C * r
        for x in range(X):
            own = pl.ds(pl.multiple_of((2 * x + me.c) * rows, r), rows)
            away = pl.ds(pl.multiple_of((2 * x + 1 - me.c) * rows, r), rows)
            own_to(x, tmp[own, :cols].reshape(C, r, cols))
            away_to(x, tmp[away, :cols].reshape(C, r, cols))

    def store(ref, *index):
        def put(x, block):
            ref[tuple(x if i is None else i for i in index)] = block
        return put

    steps = {}
    for name, group in (("f", reduce_events(me, False, bf, sends, rf, put_ff, parts_f)),
                        ("o", reduce_events(me, False, bo, sends, ro, put_o, parts_o)),
                        ("q", reduce_events(me, True, bq, sends, rq, put_q, parts_q)),
                        ("t", total_events(me, vec, (vacc, vgot), vec, sends, rv))):
        for key, step in group.items():
            steps[name + key] = step
    n_vec = vec.shape[0]
    for name, item in (("R", (xb, res_out, tss.at[0], trs.at[0], tls.at[0])),
                       ("I", (cb, ing_out, tss.at[1], trs.at[1], tls.at[1]))):
        steps[name + "o"] = lambda item=item: tok.back(*item)
        steps[name + "p"] = lambda item=item: tok.back_pass(*item)
        steps[name + "e"] = lambda item=item: tok.back_end(*item)
    mid_plan, gap_plan, att_plan, end_plan = REST_PLAN

    def at_step(i, plan):
        for m, names in enumerate(plan):
            if names:
                @pl.when(i == m)
                def _():
                    for name in names:
                        steps[name]()

    def strips(body):
        per = R // STRIP

        def step(i, carry):
            at = pl.ds(pl.multiple_of(i * STRIP, STRIP), STRIP)
            body(at, (i // per, pl.ds(pl.multiple_of(lax.rem(i, per) * STRIP, STRIP), STRIP)))
            return carry
        lax.fori_loop(0, half // STRIP, step, 0)

    for cp in loads:
        cp.wait()
    for t in range(T):
        part = nt(ar_ref[:, t * W:(t + 1) * W], wo[t])
        acc[...] = part if t == 0 else acc[...] + part

    def first_norm(at, qat):
        u, factor = unit_of(xb[qat].astype(f32) + acc[at, :] + row(0))
        unit[at, :] = u
        fac[at, :] = jnp.broadcast_to(factor, (STRIP, 128))
        low[at, :] = (u * row(2) + row(3)).astype(b16)
        acc[at, :] = jnp.zeros((STRIP, D), f32)
    strips(first_norm)
    flip(low, low_t)

    def forward(i, carry):
        slot = lax.rem(i, 2)
        t, j = which(i)
        for cp in fetch(i, slot):
            cp.wait()
        for cp in fetch(lax.rem(i + 1, n), 1 - slot):
            cp.start()
        hid[...] = nn(low[...], wbuf[2 * slot])
        bias = ub_ref[t * J + j]
        base = i * half

        def units(at, qat):
            h = hid[at, :] + bias
            phi = 0.5 + 0.5 * lax.erf(h * (0.5 ** 0.5))
            dens = jnp.exp(-0.5 * h * h) * 0.3989422804014327
            to = pl.ds(pl.multiple_of(base + at.start, STRIP), STRIP)
            act[to, :] = (h * phi).astype(b16)
            slope[to, :] = (phi + h * dens).astype(b16)
        strips(units)
        acc[...] += nt(act[pl.ds(pl.multiple_of(base, half), half), :], wbuf[2 * slot + 1])
        return carry
    lax.fori_loop(0, n, forward, 0)

    sums[...] = jnp.zeros_like(sums)

    def second_norm(at, qat):
        u, factor = unit_of(unit[at, :] * row(2) + row(3) + acc[at, :] + row(1))
        g = cb[qat].astype(f32)
        xb[qat] = (u * row(4) + row(5)).astype(b16)
        g2 = back_of(g, u, factor, row(4))
        l2 = g2.astype(b16)
        fl[at, :] = l2
        acc[at, :] = g2
        sums[1] += fold(l2.astype(f32))
        sums[4] += fold(g * u)
        sums[5] += fold(g)
    strips(second_norm)
    flip(fl, fl_t)
    steps["Ro"]()

    def stage_copy(i, x):
        t, j = which(i)
        slot = lax.rem(i, 2)
        return pltpu.make_async_remote_copy(
            src_ref=stage.at[slot, x], dst_ref=rc_f.at[t, x, pl.ds(2 * j, 2)], send_sem=fs.at[slot * X + x],
            recv_sem=fc.at[(t * X + x) * J + j], device_id=other, device_id_type=MESH)

    def backward(i, carry):
        slot = lax.rem(i, 2)
        t, j = which(i)
        for cp in fetch(i, slot):
            cp.wait()

        @pl.when(i + 1 < n)
        def _():
            for cp in fetch(i + 1, 1 - slot):
                cp.start()
        hid[...] = nn(fl[...], wbuf[2 * slot + 1])
        base = i * half
        gub[t * J + j] = jnp.zeros_like(gub[0])

        def units(at, qat):
            to = pl.ds(pl.multiple_of(base + at.start, STRIP), STRIP)
            v = (hid[at, :] * slope[to, :].astype(f32)).astype(b16)
            hl[at, :] = v
            gub[t * J + j] += fold(v.astype(f32))
        strips(units)

        @pl.when(i >= 2)
        def _():
            for x in range(X):
                stage_copy(i, x).wait_send()
        for kind in range(2):
            if kind == 0:
                tmp[...] = nn(low_t[...], hl[...]).astype(b16)
            else:
                tmp[...] = nn(fl_t[...], act[pl.ds(pl.multiple_of(base, half), half), :]).astype(b16)
            deal(chunk, store(acc_f, t, None, 2 * j + kind), store(stage, slot, None, kind))
        for x in range(X):
            stage_copy(i, x).start()
        acc[...] += nt(hl[...], wbuf[2 * slot])
        at_step(i, mid_plan)
        return carry
    lax.fori_loop(0, n, backward, 0)

    def first_back(at, qat):
        g = acc[at, :]
        u = unit[at, :]
        g1 = back_of(g, u, fac[at, 0:1], row(2))
        acc[at, :] = g1
        l1 = g1.astype(b16)
        fl[at, :] = l1
        sums[0] += fold(l1.astype(f32))
        sums[2] += fold(g * u)
        sums[3] += fold(g)
    strips(first_back)
    hl[:, :W] = nn(fl[...], wo[1 - me.c]).astype(b16)
    sends.go(hl.at[:, pl.ds(0, W)], doh.at[mine, :], csem.at[0], other)
    doh[mine, :] = nn(fl[...], wo[me.c]).astype(b16)
    flip(fl, fl_t)
    for t in range(T):
        tmp[:, :W] = nn(fl_t[...], ar_ref[:, t * W:(t + 1) * W]).astype(b16)
        deal(W, store(acc_o, t, None, 0), store(away_o, t, None, 0))
        for x in range(X):
            sends.go(away_o.at[t, x], rc_o.at[t, x], oc.at[t * X + x], other)
    for i in (n - 2, n - 1):
        for x in range(X):
            stage_copy(i, x).wait_send()
    turn = [pltpu.make_async_copy(g1_ref.at[me.c, :, pl.ds(m * W, W)], wbuf.at[m, :, pl.ds(0, W)], wsem.at[m])
            for m in range(3)]
    for cp in turn:
        cp.start()
    for h in range(2):
        for i in range(0, half, 128):
            a, b = (h * half + i) // R, (h * half + i) % R
            unit[i:i + 128, (4 + h) * PAIR:(5 + h) * PAIR] = jnp.broadcast_to(sf_ref[a, 0:1, b:b + 128], (128, 128)).T
        for p in range(n_pairs):
            low_t[(2 * p + h) * PAIR:(2 * p + h + 1) * PAIR, :] = (
                k_ref[h * half:(h + 1) * half, p * PAIR:(p + 1) * PAIR].astype(f32).T.astype(b16))
    def tokens(h):
        return [pltpu.make_async_copy(xf_ref.at[h * (C // 2) + i], low.at[pl.ds(i * R, R), :], csem.at[2 + i])
                for i in range(C // 2)]

    def turn_tokens(h):
        def run():
            for cp in tokens(h):
                cp.wait()
            for i in range(0, half, 128):
                at = h * half + i
                act[at // chunk * D:(at // chunk + 1) * D, at % chunk:at % chunk + 128] = (
                    low[i:i + 128, :].astype(f32).T.astype(b16))
            if h == 0:
                for cp in tokens(1):
                    cp.start()
        return run
    steps["x0"] = turn_tokens(0)
    steps["x1"] = turn_tokens(1)
    for cp in tokens(0):
        cp.start()

    def projections():
        for m in range(3):
            out = None
            for h in range(L // chunk):
                term = nn(act[h * D:(h + 1) * D, :], slope[m * L + h * chunk:m * L + (h + 1) * chunk, :W])
                out = term if out is None else out + term
            tmp[:, :W] = out.astype(b16)
            cols = slice(m * W, (m + 1) * W)
            every = slice(None)
            deal(W, store(acc_q, me.c, None, 0, every, every, cols), store(away_q, None, 0, every, every, cols))
        for x in range(X):
            sends.go(away_q.at[x], acc_q.at[me.c, x], qc.at[x], other)
    steps["gq"] = projections

    def back_project(who):
        out = None
        for m in range(3):
            rows = pl.ds(pl.multiple_of(m * L + who * half, half), half)
            term = nt(slope[rows, :W], wbuf[m, :, :W])
            out = term if out is None else out + term
        return out

    def give():
        for cp in turn:
            cp.wait()
        fl[...] = back_project(1 - me.c).astype(b16)
        sends.go(fl, got_part, csem.at[1], other)
    steps["give"] = give

    def keep():
        acc[...] += back_project(me.c)
    steps["keep"] = keep

    def join():
        arrived(got_part, csem.at[1], me)
        for i in range(C // 2):
            at = slice(i * R, (i + 1) * R)
            cb[i] = (acc[at, :] + got_part[at, :].astype(f32)).astype(b16)
    steps["join"] = join
    n_flat = 2 * T * W + T * H + 6 * D

    def token_sums():
        zeros = jnp.zeros((1, W), f32)
        ones = jnp.ones((8, L), b16)
        first = me.c == 0
        flat = []
        for m in (0, 2):
            v = nn(ones, slope[m * L:(m + 1) * L, :W])[0:1]
            flat += [jnp.where(first, v, zeros), jnp.where(first, zeros, v)]
        flat += [jnp.sum(gub[i], axis=0, keepdims=True) for i in range(n)]
        flat += [jnp.sum(sums[i], axis=0, keepdims=True) for i in range(6)]
        flat = jnp.concatenate(flat, axis=1)
        for i in range(n_flat // 128):
            vec[i:i + 1, :] = flat[:, i * 128:(i + 1) * 128]
        if n_vec * 128 > n_flat:
            vec[n_flat // 128:, :] = jnp.zeros((n_vec - n_flat // 128, 128), f32)
    steps["sums"] = token_sums

    def vectors():
        total = jnp.concatenate([vec[i:i + 1, :] for i in range(n_flat // 128)], axis=1)
        fz = (2 * me.x + me.c) * C + me.z
        tfz = me.y * (X * 2 * C) + fz
        n_dev = T * X * 2 * C
        qw, uw = T * W // n_dev, T * H // n_dev
        at = 0
        for i, (m, w, here) in enumerate([(T * W, qw, tfz)] * 2 + [(T * H, uw, tfz)] + [(D, r, fz)] * 6):
            vs_ref[i:i + 1, :] = take(total[:, at:at + m], here, w)
            at += m
    steps["vectors"] = vectors
    for name in gap_plan:
        steps[name]()
    arrived(doh.at[theirs, :], csem.at[0], me)

    def attention(it, carry):
        p, i = it // C, lax.rem(it, C)
        at = pl.ds(pl.multiple_of(i * R, R), R)
        cols = pl.ds(pl.multiple_of(p * PAIR, PAIR), PAIR)
        wide = jnp.concatenate([unit[:, (4 + h) * PAIR:(5 + h) * PAIR] for h in range(2)], axis=0)
        k_t = jnp.concatenate([low_t[pl.ds(pl.multiple_of((2 * p + h) * PAIR, PAIR), PAIR), :] for h in range(2)],
                              axis=1)
        dq, dk, dv = attend_back_block(q_ref[at, cols], k_ref[:, cols], k_t, v_ref[:, cols], doh[at, cols],
                                       ah_ref[at, cols], lse_ref[p, :, at], sf_ref[i, 0:1, :], two_lanes(wide))
        slope[at, cols] = dq.astype(b16)
        lanes = [slice(m * PAIR, (m + 1) * PAIR) for m in range(4)]
        halves = [dk[:half], dk[half:], dv[:half], dv[half:]]

        @pl.when(i == 0)
        def _():
            for m in range(4):
                unit[:, lanes[m]] = halves[m]

        @pl.when(i > 0)
        def _():
            for m in range(4):
                unit[:, lanes[m]] += halves[m]

        @pl.when(i == C - 1)
        def _():
            for m in range(4):
                slope[L + m * half:L + (m + 1) * half, cols] = unit[:, lanes[m]].astype(b16)

        at_step(it, att_plan)
        return carry
    lax.fori_loop(0, n_pairs * C, attention, 0)

    for name in end_plan:
        steps[name]()
    sends.finish(me)


REST_PLAN = (
    ((), (), (), ('fd',), (), ('Rp',)),
    ('fr',),
    (('fs1', 'od'), ('fs2',), ('or', 'fs3'), ('fo', 'fz1'), ('fs0', 'oo'), ('fz2',), ('os1', 'os2'), ('fz3',
     'os3'), ('oz1', 'os0'), ('fz0', 'oz2'), ('oz3', 'x0'), ('x1',)),
    ('gq', 'give', 'qd', 'qr', 'keep', 'sums', 't0', 'qs1', 'qs2', 'qs3', 'qo', 'join', 'Io', 'qs0', 't1', 'qz1',
     'qz2', 't2', 'qz3', 'qz0', 'oz0', 'fl', 'ol', 't3', 'ql', 't4', 'vectors', 'Ip', 'Re', 'Ie'),
)


def rest(cfg, q, k, v, ah, lse, sf, ar, vec, ub, xm, cf, xf, g1, g2):
    sizes, S, W, H, chunk = cfg
    F, C, T = sizes
    X = F // 2
    _, R, D = xf.shape
    L = C * R
    half = L // 2
    J = H // chunk
    n = T * J
    r = D // (F * C)
    f32, b = jnp.float32, jnp.bfloat16
    dma = pltpu.SemaphoreType.DMA
    sds = jax.ShapeDtypeStruct
    vm = pltpu.VMEM
    steps = total_count(sizes)
    n_vec = -(-(2 * T * W + T * H + 6 * D) // 1024) * 8
    sems = reduce_sems(sizes)
    tall = max(n * half, 3 * L, L // chunk * D)
    return pl.pallas_call(
        functools.partial(rest_kernel, cfg),
        in_specs=[VM] * 9 + [ANY] * 5,
        out_specs=[ANY] * 2 + [VM] * 5,
        out_shape=[sds((S, R, D), b), sds((S, R, D), b), sds((r, 3 * W), f32), sds((r, H), f32), sds((r, H), f32),
                   sds((r, W), f32), sds((16, VEC), f32)],
        scratch_shapes=[vm((C // 2, R, D), b), vm((C // 2, R, D), b), vm((half, D), f32), vm((half, 128), f32),
                        vm((half, D), b), vm((D, half), b), vm((half, D), f32), vm((half, D), b), vm((D, half), b),
                        vm((half, chunk), f32), vm((tall, chunk), b), vm((tall, chunk), b), vm((half, chunk), b),
                        vm((4, D, chunk), b), vm((T, D, W), b), vm((6, 8, D), f32), vm((n, 8, chunk), f32),
                        vm((D, chunk), b), vm((2, X, 2, C, r, chunk), b),
                        vm((L, W), b), vm((T, X, 1, C, r, W), b),
                        vm((X, 1, C, r, 3 * W), b), vm((half, D), b),
                        vm((n_vec, 128), f32), vm((4, n_vec, 128), f32), vm((steps, n_vec, 128), f32)]
        + reduce_scratch(sizes, 2 * J, r, chunk, False) + reduce_scratch(sizes, 1, r, W, False)
        + reduce_scratch(sizes, 1, r, 3 * W, True)
        + [dma((3 * reduce_count(sizes) + T * X + X + steps + 2,)),
           dma((sems,)), dma((sems,)), dma((sems,)), dma((steps,)), dma((T * X * J,)), dma((2 * X,)),
           dma((T * X,)), dma((X,)), dma((2, C // 2 + S)), dma((2, S)), dma((2,)), dma((4 + T + C,)), dma((4,))],
        compiler_params=pltpu.CompilerParams(collective_id=1, has_side_effects=True,
                                             vmem_limit_bytes=60 * 2**20 + 512 * 2**10),
    )(q, k, v, ah, lse, sf, ar, vec, ub, xm, cf, xf, g1, g2)


def finish_kernel(W, res_in, ing_in, oq_in, oup_in, odn_in, oo_in, vs_in,
                  res, ing, oq, ok, ov, oo, oup, odn, *small):
    res[...] = res_in[...]
    ing[...] = ing_in[...].astype(jnp.float32)

    @pl.when(pl.program_id(0) == 0)
    def _():
        oq[...] = oq_in[:, :W]
        ok[...] = oq_in[:, W:2 * W]
        ov[...] = oq_in[:, 2 * W:]
        oup[...] = oup_in[...]
        oo[...] = oo_in[...]
        odn[...] = odn_in[...]
        for i, ref in enumerate(small):
            ref[...] = vs_in[i:i + 1, :ref.shape[1]]


def finish(cfg, widths, *arrays):
    sizes, S, W, H, chunk = cfg
    res, ing, oq = arrays[:3]
    r = oq.shape[0]
    R, D = res.shape[1:]
    f32 = jnp.float32
    token = pl.BlockSpec((1, R, D), lambda i: (i, 0, 0))
    whole = lambda shape: pl.BlockSpec(shape, lambda i: (0,) * len(shape))
    shapes = [(r, W)] * 4 + [(r, H), (r, H)] + [(1, w) for w in widths]
    return pl.pallas_call(
        functools.partial(finish_kernel, W),
        grid=(S,),
        in_specs=[token, token] + [whole(a.shape) for a in arrays[2:]],
        out_specs=[token, token] + [whole(shape) for shape in shapes],
        out_shape=[jax.ShapeDtypeStruct((S, R, D), jnp.bfloat16), jax.ShapeDtypeStruct((S, R, D), f32)]
        + [jax.ShapeDtypeStruct(shape, f32) for shape in shapes],
        compiler_params=pltpu.CompilerParams(vmem_limit_bytes=62 * 2**20),
    )(*arrays)


def chunk_of(H):
    for w in (512, 384, 256, 128):
        if H % w == 0:
            return w
    return H


def on_device(sizes, inputs, segments, cotangent, query_weight, key_weight, value_weight,
              output_weight, up_weight, down_weight, *small):
    F, C, T = sizes
    X = F // 2
    S, R, D = inputs.shape
    W = query_weight.shape[1]
    H = up_weight.shape[1]
    r = query_weight.shape[0]
    chunk = chunk_of(H)
    cfg = (sizes, S, W, H, chunk)
    weights = (query_weight, key_weight, value_weight, output_weight.T, up_weight, down_weight.T)
    widths = [v.shape[0] for v in small]
    small = [v.reshape(1, -1) for v in small]
    q, k, v, ah, ar, lse, xf, cf, sf, g1, g2, vec, ub, xm = front(
        cfg, inputs, cotangent, segments, weights, small)
    landed = rest(cfg, q, k, v, ah, lse, sf, ar, vec, ub, xm, cf, xf,
                  g1.reshape(T, D, -1), g2.reshape(T, D, -1))
    outs = finish(cfg, widths, *landed)
    return tuple(outs[:5]) + (outs[5].T, outs[6], outs[7].T) + tuple(v.reshape(-1) for v in outs[8:])


def solution(mesh):
    sizes = (mesh.shape["fsdp"], mesh.shape["ctx"], mesh.shape["tp"])
    every = ("fsdp", "ctx")
    rows, cols, one, three = P(every, "tp"), P("tp", every), P(every), P(("tp",) + every)
    token = P("fsdp", "ctx", None)
    weights = (rows, rows, rows, cols, rows, cols)
    vectors = (three, three, three) + (one,) * 6
    return jax.shard_map(
        functools.partial(on_device, sizes), mesh=mesh,
        in_specs=(token, P("fsdp", "ctx"), token) + weights + vectors,
        out_specs=(token, token) + weights + vectors, check_vma=False)
```

```python
import functools
import jax
import jax.numpy as jnp
from jax import lax
from jax.sharding import PartitionSpec as P
from jax.experimental import pallas as pl
from jax.experimental.pallas import tpu as pltpu

MESH = pl.DeviceIdType.MESH
ANY = pl.BlockSpec(memory_space=pl.ANY)
VM = pl.BlockSpec(memory_space=pltpu.VMEM)


class Place:
    def __init__(self, sizes):
        self.F, self.C, self.T = sizes
        self.X = self.F // 2
        f = lax.axis_index("fsdp")
        self.x = f // 2
        self.c = lax.rem(f, 2)
        self.z = lax.axis_index("ctx")
        self.y = lax.axis_index("tp")

    def dev(self, x=None, c=None, z=None, y=None):
        x = self.x if x is None else x
        c = self.c if c is None else c
        return (2 * x + c, self.z if z is None else z, self.y if y is None else y)

    def z_off(self, d):
        return lax.rem(self.z + d + self.C, self.C)

    def x_off(self, d):
        return lax.rem(self.x + d + self.X, self.X)

    def greet(self, chip_wide):
        bar = pltpu.get_barrier_semaphore()
        devs = [self.dev(c=1 - self.c), self.dev(y=1 - self.y)]
        devs += [self.dev(x=self.x_off(d)) for d in range(1, self.X)]
        for d in range(1, self.C):
            devs.append(self.dev(z=self.z_off(d)))
            if chip_wide:
                devs.append(self.dev(z=self.z_off(d), c=1 - self.c))
        for d in devs:
            pl.semaphore_signal(bar, inc=1, device_id=d, device_id_type=MESH)
        pl.semaphore_wait(bar, len(devs))


class Sends:
    def __init__(self, sems):
        self.sems, self.n, self.waits = sems, 0, []

    def go(self, src, dst, recv, dev, like=None, when=None):
        pltpu.make_async_remote_copy(
            src_ref=src, dst_ref=dst, send_sem=self.sems.at[self.n], recv_sem=recv,
            device_id=dev, device_id_type=MESH).start()
        self.n += 1
        self.waits.append((src if like is None else like, when))

    def finish(self, me):
        for n, (like, when) in enumerate(self.waits):
            def wait():
                pltpu.make_async_remote_copy(
                    src_ref=like, dst_ref=like, send_sem=self.sems.at[n], recv_sem=self.sems.at[n],
                    device_id=me.dev(c=1 - me.c), device_id_type=MESH).wait_send()
            given(when, wait)
        self.waits = []


def given(when, body):
    if when is None:
        body()
    else:
        pl.when(when())(body)


def arrived(dst, recv, pl_):
    pltpu.make_async_remote_copy(
        src_ref=dst, dst_ref=dst, send_sem=recv, recv_sem=recv,
        device_id=pl_.dev(c=1 - pl_.c), device_id_type=MESH).wait_recv()


def line_order(C, z):
    return [z] + [z + sign * k for k in range(1, C) for sign in (-1, 1) if 0 <= z + sign * k < C]


def pick(index, table):
    out = table[-1]
    for i in reversed(range(len(table) - 1)):
        out = jnp.where(index == i, table[i], out)
    return jnp.int32(out)


def gather_events(me, own, full, sends, recv, lsem):
    C, X = me.C, me.X
    sem = lambda t, x, c, z: recv.at[((t * X + x) * 2 + c) * C + z]
    slot = lambda t, x, c, z: full.at[t, x, c, z]
    like = slot(0, 0, 0, 0)
    orders = [line_order(C, z) for z in range(C)]
    where = lambda m: pick(me.z, [o[m] for o in orders])

    def push(src, at, dev, when=None):
        sends.go(src, slot(*at), sem(*at), dev, like, when)

    def wait(at):
        arrived(slot(*at), sem(*at), me)

    core, side = me.dev(c=1 - me.c), me.dev(y=1 - me.y)
    xs = [(me.x_off(d), me.dev(x=me.x_off(d))) for d in range(1, X)]
    local = pltpu.make_async_copy(own, slot(me.y, me.x, me.c, me.z), lsem)

    def along(m):
        def run():
            zz = where(m)
            at = (me.y, me.x, me.c, zz)
            src = slot(*at) if m else own
            if m:
                wait(at)
            for sign in (-1, 1):
                def onward(sign=sign):
                    zz = where(m)
                    return ((zz - me.z) * sign <= 0) & (me.z + sign >= 0) & (me.z + sign < C)

                @pl.when(onward())
                def _():
                    push(src, at, me.dev(z=me.z + sign), onward)
            for _, dev in xs:
                push(src, at, dev)
            push(src, at, side)
            push(src, at, core)
            if not m:
                local.start()
        return run

    def across(m):
        def run():
            zz = where(m)
            at = (1 - me.y, me.x, me.c, zz)
            wait(at)
            if m < C // 2:
                for _, dev in xs:
                    push(slot(*at), at, dev)
            push(slot(*at), at, core)
            for xo, _ in xs:
                at = (me.y, xo, me.c, zz)
                wait(at)
                if m >= C // 2:
                    push(slot(*at), at, side)
                push(slot(*at), at, core)
        return run

    def corner(m):
        def run():
            zz = where(m)
            for xo, _ in xs:
                at = (1 - me.y, xo, me.c, zz)
                wait(at)
                push(slot(*at), at, core)
        return run

    def last():
        for t in range(me.T):
            for xx in range(X):
                for zz in range(C):
                    wait((t, xx, 1 - me.c, zz))
        local.wait()

    steps = {"l": last}
    for m in range(C):
        steps["a%d" % m] = along(m)
        steps["x%d" % m] = across(m)
        steps["c%d" % m] = corner(m)
    return steps


def gather_count(sizes):
    F, C, T = sizes
    X = F // 2
    return C * (4 * X + 4)


CUT = 2


class Tokens:
    def __init__(self, me, seqs):
        self.me, self.S = me, seqs
        self.half = me.C // 2
        self.lo = me.y * (me.C - seqs)
        self.busy = (me.z >= self.lo) & (me.z < self.lo + seqs)
        self.owner = me.c == me.y

    def out(self, src, dst, full, ssem, rsem, lsem):
        me, half = self.me, self.half
        k = me.z // half
        at = me.z if full else lax.rem(me.z, half)

        @pl.when(self.owner)
        def _():
            for s in range(self.S):
                here = (self.lo + s == me.z) & (k == me.c)

                @pl.when(here)
                def _():
                    pltpu.make_async_copy(src.at[s], dst.at[at], lsem).start()

                @pl.when(jnp.logical_not(here))
                def _():
                    pltpu.make_async_remote_copy(
                        src_ref=src.at[s], dst_ref=dst.at[at], send_sem=ssem.at[s],
                        recv_sem=rsem.at[lax.rem(me.z, half)],
                        device_id=me.dev(c=k, z=self.lo + s), device_id_type=MESH).start()

    def out_done(self, src, dst, full, ssem, rsem, lsem):
        me, half = self.me, self.half

        @pl.when(self.busy)
        def _():
            for i in range(half):
                zq = me.c * half + i
                at = zq if full else i
                here = (zq == me.z) & (me.c == me.y)

                @pl.when(here)
                def _():
                    pltpu.make_async_copy(src.at[0], dst.at[at], lsem).wait()

                @pl.when(jnp.logical_not(here))
                def _():
                    arrived(dst.at[at], rsem.at[i], me)

                if full:
                    pltpu.make_async_remote_copy(
                        src_ref=dst.at[at], dst_ref=dst.at[at], send_sem=ssem.at[self.S + i],
                        recv_sem=rsem.at[half + i], device_id=me.dev(c=1 - me.c),
                        device_id_type=MESH).start()

    def out_end(self, src, dst, full, ssem, rsem, lsem):
        me, half = self.me, self.half
        k = me.z // half

        @pl.when(self.owner)
        def _():
            for s in range(self.S):
                here = (self.lo + s == me.z) & (k == me.c)

                @pl.when(jnp.logical_not(here))
                def _():
                    pltpu.make_async_remote_copy(
                        src_ref=src.at[s], dst_ref=dst.at[0], send_sem=ssem.at[s],
                        recv_sem=rsem.at[0], device_id=me.dev(c=1 - me.c),
                        device_id_type=MESH).wait_send()

        if full:
            @pl.when(self.busy)
            def _():
                for i in range(half):
                    zq = (1 - me.c) * half + i
                    arrived(dst.at[zq], rsem.at[half + i], me)
                    pltpu.make_async_remote_copy(
                        src_ref=dst.at[0], dst_ref=dst.at[0], send_sem=ssem.at[self.S + i],
                        recv_sem=rsem.at[0], device_id=me.dev(c=1 - me.c),
                        device_id_type=MESH).wait_send()

    def back(self, src, dst, ssem, rsem, lsem):
        me, half = self.me, self.half
        size = src.shape[1] // CUT

        @pl.when(self.busy)
        def _():
            at = me.z - self.lo
            for h in range(CUT):
                piece = pl.ds(h * size, size)
                for i in range(half):
                    zq = me.c * half + i
                    here = (zq == me.z) & (me.c == me.y)

                    @pl.when(here)
                    def _():
                        if h == 0:
                            pltpu.make_async_copy(src.at[i], dst.at[at], lsem).start()

                    @pl.when(jnp.logical_not(here))
                    def _():
                        pltpu.make_async_remote_copy(
                            src_ref=src.at[i, piece], dst_ref=dst.at[at, piece], send_sem=ssem.at[i * CUT + h],
                            recv_sem=rsem.at[at * CUT + h], device_id=me.dev(c=me.y, z=zq),
                            device_id_type=MESH).start()

    def back_pass(self, s, h, src, dst, ssem, rsem, lsem):
        me, half = self.me, self.half
        size = src.shape[1] // CUT
        piece = pl.ds(h * size, size)

        @pl.when(self.owner)
        def _():
            here = (self.lo + s == me.z) & (me.z // half == me.c)

            @pl.when(here)
            def _():
                if h == 0:
                    pltpu.make_async_copy(src.at[0], dst.at[s], lsem).wait()

            @pl.when(jnp.logical_not(here))
            def _():
                arrived(dst.at[s, piece], rsem.at[s * CUT + h], me)

            pltpu.make_async_remote_copy(
                src_ref=dst.at[s, piece], dst_ref=dst.at[s, piece], send_sem=ssem.at[(half + s) * CUT + h],
                recv_sem=rsem.at[s * CUT + h], device_id=me.dev(y=1 - me.y), device_id_type=MESH).start()

    def back_end(self, src, dst, ssem, rsem, lsem):
        me, half = self.me, self.half
        size = src.shape[1] // CUT
        piece = pl.ds(0, size)

        @pl.when(self.busy)
        def _():
            for i in range(half):
                here = (me.c * half + i == me.z) & (me.c == me.y)

                @pl.when(jnp.logical_not(here))
                def _():
                    for h in range(CUT):
                        pltpu.make_async_remote_copy(
                            src_ref=src.at[i, piece], dst_ref=dst.at[0, piece], send_sem=ssem.at[i * CUT + h],
                            recv_sem=rsem.at[0], device_id=me.dev(c=1 - me.c), device_id_type=MESH).wait_send()

        @pl.when(self.owner)
        def _():
            for n in range(self.S * CUT):
                pltpu.make_async_remote_copy(
                    src_ref=dst.at[0, piece], dst_ref=dst.at[0, piece], send_sem=ssem.at[half * CUT + n],
                    recv_sem=rsem.at[0], device_id=me.dev(y=1 - me.y), device_id_type=MESH).wait_send()

        @pl.when(jnp.logical_not(self.owner))
        def _():
            for n in range(self.S * CUT):
                arrived(dst.at[n // CUT, pl.ds(n % CUT * size, size)], rsem.at[n], me)


def reduce_events(me, split, bufs, sends, recv, finish, parts):
    acc, rc, xd, yd, xr, yr, zr = bufs
    C, X = me.C, me.X
    half = C // 2
    n_cols = acc.shape[2]
    like = acc.at[0, 0, :, 0]
    side = me.dev(y=1 - me.y)
    base = 0
    s_d = lambda d, j: recv.at[base + (d - 1) * C + j]
    base2 = base + (X - 1) * C
    s_xr = lambda d, j: recv.at[base2 + (d - 1) * C + j]
    base3 = base2 + (X - 1) * C
    s_yr = lambda j: recv.at[base3 + j]
    s_zr = lambda j: recv.at[base3 + C + j]
    quads = ([(1 - me.y, me.x_off(d)) for d in range(1, X)] + [(1 - me.y, me.x)]
             + [(me.y, me.x_off(d)) for d in range(1, X)] + [(me.y, me.x)])

    def add(a, b):
        def body(i, carry):
            a[i] = a[i] + b[i]
            return carry
        lax.fori_loop(0, n_cols, body, 0)

    def ready(n):
        t, x = quads[n]
        if split:
            if n == 0:
                for xo in [me.x_off(d) for d in range(1, X)] + [me.x]:
                    for view, sem in parts(1 - me.c, xo):
                        arrived(view, sem, me)
            return
        for view, sem in parts(t, x):
            arrived(view, sem, me)

        def body(i, carry):
            for z in range(C):
                acc[t, x, i, z] = acc[t, x, i, z] + rc[t, x, i, z]
            return carry
        lax.fori_loop(0, n_cols, body, 0)

    by_x = range(1, C)

    def ready_corner():
        for d in range(1, X):
            ready(d - 1)

    def corner(j):
        def run():
            zj = me.z_off(-j)
            for d in range(1, X):
                t, x = quads[d - 1]
                if j in by_x:
                    sends.go(acc.at[t, x, :, zj], xd.at[d - 1, j - 1], s_d(d, j), me.dev(x=x), like)
                else:
                    sends.go(acc.at[t, x, :, zj], yd.at[d - 1, 0], s_d(d, j), side, like)
        return run

    def ready_x():
        for n in range(X, 2 * X - 1):
            ready(n)

    def over_x(j):
        def run():
            zj = me.z_off(-j)
            for d in range(1, X):
                xo = me.x_off(d)
                if j not in by_x:
                    arrived(yd.at[d - 1, 0], s_d(d, j), me)
                    add(acc.at[me.y, xo, :, zj], yd.at[d - 1, 0])
                sends.go(acc.at[me.y, xo, :, zj], xr.at[d - 1, j], s_xr(d, j), me.dev(x=xo), like)
        return run

    def over_y(j):
        def run():
            zj = me.z_off(-j)
            if j in by_x:
                for d in range(1, X):
                    arrived(xd.at[d - 1, j - 1], s_d(d, j), me)
                    add(acc.at[1 - me.y, me.x, :, zj], xd.at[d - 1, j - 1])
            sends.go(acc.at[1 - me.y, me.x, :, zj], yr.at[j], s_yr(j), side, like)
        return run

    def to_z(j):
        def run():
            t, x = me.y, me.x
            zj = me.z_off(-j)
            for d in range(1, X):
                arrived(xr.at[d - 1, j], s_xr(d, j), me)
                add(acc.at[t, x, :, zj], xr.at[d - 1, j])
            arrived(yr.at[j], s_yr(j), me)
            add(acc.at[t, x, :, zj], yr.at[j])
            if j:
                sends.go(acc.at[t, x, :, zj], zr.at[j - 1], s_zr(j - 1), me.dev(z=zj), like)
        return run

    def last():
        for j in range(1, C):
            arrived(zr.at[j - 1], s_zr(j - 1), me)
        for i in range(n_cols):
            total = acc[me.y, me.x, i, me.z].astype(jnp.float32)
            for j in range(1, C):
                total = total + zr[j - 1, i].astype(jnp.float32)
            finish(i, total)

    steps = {"c": ready_corner, "a": lambda: ready(X - 1), "b": ready_x, "o": lambda: ready(2 * X - 1), "l": last}
    for j in range(C):
        steps["d%d" % j] = corner(j)
        steps["w%d" % j] = over_x(j)
        steps["y%d" % j] = over_y(j)
        steps["z%d" % j] = to_z(j)
    return steps


def reduce_scratch(sizes, n, r, w, split):
    F, C, T = sizes
    X = F // 2
    half = C // 2
    v = lambda shape: pltpu.VMEM(shape, jnp.bfloat16)
    return [v((T, X, n, C, r, w)), v((1, 1, 1, 1, 16, 128) if split else (T, X, n, C, r, w)),
            v((X - 1, C - 1, n, r, w)), v((X - 1, 1, n, r, w)), v((X - 1, C, n, r, w)),
            v((C, n, r, w)), v((C - 1, n, r, w))]


def reduce_sems(sizes):
    F, C, T = sizes
    X = F // 2
    return 2 * (X - 1) * C + 2 * C


def reduce_count(sizes):
    F, C, T = sizes
    X = F // 2
    return 2 * (X - 1) * C + C + C - 1


def total_events(me, own, bufs, out, sends, recv):
    C, X = me.C, me.X
    acc, got = bufs
    groups = [[me.dev(c=1 - me.c)], [me.dev(x=me.x_off(d)) for d in range(1, X)],
              [me.dev(y=1 - me.y)], [me.dev(z=me.z_off(d)) for d in range(1, C)]]
    like = acc.at[0]
    bases = [sum(len(g) for g in groups[:i]) for i in range(len(groups))]

    def start(gi):
        for i, dev in enumerate(groups[gi]):
            sends.go(acc.at[gi], got.at[bases[gi] + i], recv.at[bases[gi] + i], dev, like)

    def first():
        acc[0] = own[...]
        start(0)

    steps = {"0": first}
    for gi in range(len(groups)):
        def step(gi=gi):
            total = acc[gi]
            for i in range(len(groups[gi])):
                arrived(got.at[bases[gi] + i], recv.at[bases[gi] + i], me)
                total = total + got[bases[gi] + i]
            if gi + 1 < len(groups):
                acc[gi + 1] = total
                start(gi + 1)
            else:
                out[...] = total
        steps[str(gi + 1)] = step
    return steps


def total_count(sizes):
    F, C, T = sizes
    return 1 + F // 2 - 1 + 1 + C - 1

HEAD = 64
PAIR = 2 * HEAD
SCALE = HEAD ** (-0.5)
norm_eps = 1e-12
masked_score = -1000000000.0


def nt(a, b):
    return lax.dot_general(a, b, (((1,), (1,)), ((), ())), preferred_element_type=jnp.float32)


def nn(a, b):
    return lax.dot_general(a, b, (((1,), (0,)), ((), ())), preferred_element_type=jnp.float32)


def spread_segments(seg_ref, wide):
    C, _, R = seg_ref.shape
    for i in range(C):
        for j in range(0, R, 128):
            row = jnp.broadcast_to(seg_ref[i, 0:1, j:j + 128], (128, 128))
            wide[i * R + j:i * R + j + 128, :] = row.T


def lanes_of(h, like):
    lane = lax.broadcasted_iota(jnp.int32, like.shape, like.ndim - 1)
    return jnp.where(lane // HEAD == h, like, jnp.zeros_like(like))


def two_lanes(wide):
    return jnp.concatenate([wide, wide], axis=1)


def attend_block(q, k, v_t, seg_q, seg_k):
    same = seg_k == seg_q
    outs, logs = [], []
    for h in range(2):
        s = nt(k, lanes_of(h, q) * jnp.bfloat16(SCALE))
        s = jnp.where(same, s, masked_score)
        peak = jnp.max(s, axis=0, keepdims=True)
        e = jnp.exp(s - peak)
        total = jnp.sum(e, axis=0, keepdims=True)
        o = nn(v_t, e.astype(jnp.bfloat16))
        outs.append(o[h * HEAD:(h + 1) * HEAD] * (1.0 / total))
        logs.append(peak + jnp.log(total))
    return jnp.concatenate(outs, axis=0), logs


def attend_back_block(q, k, k_t, v, do, o, lse, seg_q, seg_k):
    same = seg_k == seg_q
    prod = (do.astype(jnp.float32) * o.astype(jnp.float32)).T
    dq, dk, dv = [], None, None
    for h in range(2):
        qh = lanes_of(h, q) * jnp.bfloat16(SCALE)
        doh = lanes_of(h, do)
        s = nt(k, qh)
        p = jnp.exp(jnp.where(same, s, masked_score) - lse[h:h + 1])
        dp = nt(v, doh)
        inner = jnp.sum(prod[h * HEAD:(h + 1) * HEAD], axis=0, keepdims=True)
        ds = (p * (dp - inner)).astype(jnp.bfloat16)
        dv_h = nn(p.astype(jnp.bfloat16), doh)
        dk_h = nn(ds, qh)
        dv = dv_h if dv is None else dv + dv_h
        dk = dk_h if dk is None else dk + dk_h
        dq.append(nn(k_t, ds)[h * HEAD:(h + 1) * HEAD])
    return jnp.concatenate(dq, axis=0).T * SCALE, dk, dv

STRIP = 64


def fold(value):
    total = value[0:8]
    for i in range(8, value.shape[0], 8):
        total = total + value[i:i + 8]
    return total


def mean(value):
    return jnp.mean(value, axis=-1, keepdims=True)


def unit_of(value):
    centred = value - mean(value)
    factor = lax.rsqrt(mean(centred * centred) + norm_eps)
    return centred * factor, factor


def back_of(upstream, unit, factor, gain):
    along = upstream * gain
    return factor * (along - mean(along) - unit * mean(along * unit))


def flip(ref, out):
    rows = ref.shape[0]
    for i in range(0, rows, 128):
        out[:, i:i + 128] = ref[i:i + 128, :].astype(jnp.float32).T.astype(jnp.bfloat16)


VEC = 128


def spread_pieces(blocks, width, first, total):
    n, lanes = blocks.shape
    i = lax.broadcasted_iota(jnp.int32, (lanes, total), 0)
    col = lax.broadcasted_iota(jnp.int32, (lanes, total), 1)
    pick = jnp.where(i - first == lax.rem(col, width), 1.0, 0.0).astype(jnp.bfloat16)
    wide = nn(blocks, pick)
    dev = lax.broadcasted_iota(jnp.int32, (n, total), 0)
    col = lax.broadcasted_iota(jnp.int32, (n, total), 1)
    return jnp.sum(jnp.where(dev == col // width, wide, 0.0), axis=0, keepdims=True)


def pack(widths):
    offs, at = [], 0
    for w in widths:
        if at % VEC + w > VEC:
            at += VEC - at % VEC
        offs.append(at)
        at += w
    return offs, -(-at // VEC)


def small_widths(sizes, D, W, H):
    F, C, T = sizes
    n_dev = T * F * C
    return [T * W // n_dev, T * W // n_dev, T * H // n_dev] + [D // (F * C)] * 6


def front_kernel(cfg, *refs):
    sizes, S, W, H, chunk = cfg
    x_ref, cot_ref, segs_ref, wq_in, wk_in, wv_in, wo_in, up_in, dn_in = refs[:9]
    small_refs = refs[9:18]
    (q_ref, k_ref, v_ref, ah_ref, ar_ref, lse_ref, xf_ref, cf_ref, sf_ref, g1_ref, g2_ref,
     vec_ref, ub_ref, xm_ref, zero, zseg, xv, wv, pv, sv, wide, v_t, w1_ref, w2_ref, seg_ref, rows,
     ssem, r1, r2, lsem, tss, trs, tls, csem) = refs[18:]
    me = Place(sizes)
    C, X, T = me.C, me.X, me.T
    R, D = xv.shape[1:]
    r = wv.shape[3]
    L = C * R
    f32, b16 = jnp.float32, jnp.bfloat16
    offs, n_rows = pack([ref.shape[1] for ref in small_refs])
    w1_ref[:, :W] = wq_in[...]
    w1_ref[:, W:2 * W] = wk_in[...]
    w1_ref[:, 2 * W:3 * W] = wv_in[...]
    w2_ref[:, :H] = up_in[...]
    w2_ref[:, H:2 * H] = dn_in[...]
    w2_ref[:, 2 * H:] = wo_in[...]
    rows[...] = jnp.zeros_like(rows)
    for i, ref in enumerate(small_refs):
        rows[i:i + 1, :ref.shape[1]] = ref[...].astype(f32)
    block = [jnp.zeros((1, VEC), f32) for _ in range(n_rows)]
    for i, off in enumerate(offs):
        one = jnp.broadcast_to(rows[i:i + 1, :], (8, VEC))
        block[off // VEC] += (pltpu.roll(one, off % VEC, 1) if off % VEC else one)[0:1]
    pad = [jnp.zeros((r - n_rows, VEC), f32)] if r > n_rows else []
    w1_ref[:, 3 * W:] = jnp.concatenate(block + pad, axis=0).astype(b16)
    for i in range(S):
        seg_ref[i] = jnp.broadcast_to(segs_ref[i:i + 1, :].astype(f32), (8, R))
    me.greet(True)
    sends = Sends(ssem)
    tok = Tokens(me, S)
    items = [(x_ref, xf_ref, True, tss.at[0], trs.at[0], tls.at[0]),
             (seg_ref, sf_ref, True, tss.at[1], trs.at[1], tls.at[1]),
             (cot_ref, cf_ref, False, tss.at[2], trs.at[2], tls.at[2])]
    idle = jnp.logical_not(tok.busy)
    fills = ([(zero, xf_ref.at[i]) for i in range(C)] + [(zseg, sf_ref.at[i]) for i in range(C)]
             + [(zero, cf_ref.at[i]) for i in range(C // 2)])

    @pl.when(idle)
    def _():
        zero[...] = jnp.zeros_like(zero)
        zseg[...] = jnp.zeros_like(zseg)
        for i, (a, b) in enumerate(fills):
            pltpu.make_async_copy(a, b, tls.at[3 + i]).start()

    steps = {}
    for group, w_ref, g_ref, recv, n in (("1", w1_ref, g1_ref, r1, 0), ("2", w2_ref, g2_ref, r2, 1)):
        for name, step in gather_events(me, w_ref, g_ref, sends, recv, lsem.at[n]).items():
            steps[group + name] = step
    half = L // 2

    def each(f, its):
        return lambda: [f(*it) for it in its]

    for name, its in (("X", items[:2]), ("C", items[2:])):
        steps[name + "o"] = each(tok.out, its)
        steps[name + "w"] = each(tok.out_done, its)
        steps[name + "e"] = each(tok.out_end, its)

    def filled():
        @pl.when(idle)
        def _():
            for i, (a, b) in enumerate(fills):
                pltpu.make_async_copy(a, b, tls.at[3 + i]).wait()
    steps["filled"] = filled

    loads = [(xf_ref, xv), (sf_ref, sv), (g1_ref.at[me.c], wv)]
    pieces = [(g1_ref.at[t, xx, cc, zz, :, pl.ds(3 * W, VEC)], pv.at[((t * X + xx) * 2 + cc) * C + zz])
              for t in range(T) for xx in range(X) for cc in range(2) for zz in range(C)]
    loads = [pltpu.make_async_copy(a, b, csem.at[i]) for i, (a, b) in enumerate(loads + pieces)]

    def load():
        for cp in loads:
            cp.start()
    steps["load"] = load

    def vectors():
        for cp in loads:
            cp.wait()
        blocks = jnp.concatenate([pv[:, i, :] for i in range(n_rows)], axis=1)
        n_dev = blocks.shape[0]
        qw, uw = T * W // n_dev, T * H // n_dev
        qb = spread_pieces(blocks, qw, offs[0], T * W)
        vb = spread_pieces(blocks, qw, offs[1], T * W)
        ub = spread_pieces(blocks, uw, offs[2], T * H)
        for i in range(T * H // chunk):
            ub_ref[i] = ub[:, i * chunk:(i + 1) * chunk]
        once = blocks[:n_dev // T]
        for i in range(6):
            vec_ref[i:i + 1, :] = spread_pieces(once, r, offs[3 + i], D)
        first = me.c == 0
        vec_ref[6:7, :W] = jnp.where(first, qb[:, :W], qb[:, W:])
        vec_ref[7:8, :W] = jnp.where(first, vb[:, :W], vb[:, W:])
    steps["vectors"] = vectors

    def project():
        weights = wv[...].reshape(D, wv.shape[-1])

        def body(i, carry):
            at = pl.ds(pl.multiple_of(i * R, R), R)
            out = nn(xv[i], weights[:, :3 * W])
            q_ref[at, :] = (out[:, :W] + vec_ref[6:7, :W]).astype(b16)
            k_ref[at, :] = out[:, W:2 * W].astype(b16)
            v_ref[at, :] = (out[:, 2 * W:] + vec_ref[7:8, :W]).astype(b16)
            return carry
        lax.fori_loop(0, C, body, 0)
        out = pltpu.make_async_copy(xv.at[pl.ds(me.c * (C // 2), C // 2)], xm_ref, csem.at[len(loads) + 1])
        out.start()
        out.wait()
    steps["project"] = project

    def ready():
        spread_segments(sv, wide)
        for p in range(W // PAIR):
            v_t[p] = v_ref[:, p * PAIR:(p + 1) * PAIR].astype(f32).T.astype(b16)
    steps["ready"] = ready

    def attention(late):
        def body(it, carry):
            p, i = it // C, lax.rem(it, C)
            at = pl.ds(pl.multiple_of(i * R, R), R)
            cols = pl.ds(pl.multiple_of(p * PAIR, PAIR), PAIR)
            o, logs = attend_block(q_ref[at, cols], k_ref[:, cols], v_t[p], sv[i, 0:1, :],
                                   two_lanes(wide[...]))
            ah_ref[at, cols] = o.T.astype(b16)
            lse_ref[p, :, at] = jnp.concatenate(logs + [jnp.zeros((6, R), f32)], axis=0)
            for n, names in enumerate(late):
                if names:
                    @pl.when(it == n)
                    def _():
                        for name in names:
                            steps[name]()
            return carry
        lax.fori_loop(0, W // PAIR * C, body, 0)

    mine = pl.ds(pl.multiple_of(me.c * half, half), half)
    theirs = pl.ds(pl.multiple_of((1 - me.c) * half, half), half)
    heads = pl.ds(pl.multiple_of(me.c * W, W), W)

    def swap():
        sends.go(ah_ref.at[theirs, :], ar_ref.at[:, heads], csem.at[len(loads)], me.dev(c=1 - me.c))
        ar_ref[:, heads] = ah_ref[mine, :]
    steps["swap"] = swap
    early, late, end = FRONT_PLAN
    for name in early:
        steps[name]()
    attention(late)
    for name in end:
        steps[name]()
    arrived(ar_ref.at[:, heads], csem.at[len(loads)], me)
    sends.finish(me)


FRONT_PLAN = (
    ('1a0', '1a1', '1a2', '1a3', '1x0', '2a0', '1x1', '2a1', '1x2', '2a2', 'Xo', '1x3', '2a3', '1c0', '2x0',
     '1c1', '2x1', '1c2', '1c3', 'Xw', '1l', 'Xe', 'filled', 'load', '2x2', 'vectors', 'project', 'ready'),
    (('2x3',), (), ('Co',), ('2c0',), (), ('2c1',), (), ('2c2',), ('2c3',)),
    ('swap', '2l', 'Cw', 'Ce'),
)


def front(cfg, x, cot, segs, weights, small):
    sizes, S, W, H, chunk = cfg
    F, C, T = sizes
    _, R, D = x.shape
    X = F // 2
    L = C * R
    n = T * H // chunk
    f32, b = jnp.float32, jnp.bfloat16
    dma = pltpu.SemaphoreType.DMA
    r = weights[0].shape[0]
    n1, n2 = 3 * W + VEC, 2 * H + W
    sds = jax.ShapeDtypeStruct
    v = pltpu.VMEM
    return pl.pallas_call(
        functools.partial(front_kernel, cfg),
        in_specs=[ANY] * 2 + [VM] * (1 + len(weights) + len(small)),
        out_specs=[VM] * 6 + [ANY] * 5 + [VM] * 2 + [ANY],
        out_shape=[sds((L, W), b)] * 4 + [sds((L // 2, T * W), b), sds((W // PAIR, 8, L), f32),
                                          sds((C, R, D), b), sds((C // 2, R, D), b), sds((C, 8, R), f32),
                                          sds((T, X, 2, C, r, n1), b), sds((T, X, 2, C, r, n2), b),
                                          sds((8, D), f32), sds((n, 1, chunk), f32), sds((C // 2, R, D), b)],
        scratch_shapes=[v((R, D), b), v((8, R), f32), v((C, R, D), b), v((X, 2, C, r, n1), b),
                        v((T * F * C, r, VEC), b), v((C, 8, R), f32), v((L, 128), f32), v((W // PAIR, PAIR, L), b),
                        v((r, n1), b), v((r, n2), b), v((S, 8, R), f32), v((16, VEC), f32),
                        dma((2 * gather_count(sizes) + 1,)), dma((T * F * C,)), dma((T * F * C,)), dma((2,)),
                        dma((3, S + C // 2)), dma((3, C)), dma((3 + 3 * C,)), dma((5 + T * F * C,))],
        compiler_params=pltpu.CompilerParams(collective_id=0, has_side_effects=True,
                                             vmem_limit_bytes=60 * 2**20),
    )(x, cot, segs, *weights, *small)


def take(vec, index, width):
    n = vec.shape[1]
    wide = jnp.broadcast_to(vec, (8, n))
    return pltpu.roll(wide, lax.rem(n - index * width, n), 1)[0:1, :VEC]


def rest_kernel(cfg, q_ref, k_ref, v_ref, ah_ref, lse_ref, sf_ref, ar_ref, vec_ref, ub_ref,
                xm_ref, cf_ref, xf_ref, g1_ref, g2_ref,
                res_out, ing_out, oq_ref, oup_ref, odn_ref, oo_ref, vs_ref,
                xb, cb, unit, fac, low, low_t, acc, fl, fl_t, hid, act, slope, hl, wbuf, wo, sums, gub, tmp, stage,
                doh, away_o, away_q, got_part, vec, vacc, vgot, soon, sacc, sgot, *scr):
    sizes, S, W, H, chunk = cfg
    bf, bo, bq = scr[:7], scr[7:14], scr[14:21]
    ssem, rf, ro, rq, rv, ru, fc, fs, oc, qc, tss, trs, tls, csem, wsem = scr[21:]
    me = Place(sizes)
    C, X, T = me.C, me.X, me.T
    R, D = xb.shape[1:]
    L = C * R
    half = L // 2
    J = H // chunk
    n = T * J
    r = away_q.shape[3]
    f32, b16 = jnp.float32, jnp.bfloat16
    n_pairs = W // PAIR
    row = lambda i: vec_ref[i:i + 1, :]
    me.greet(True)
    sends = Sends(ssem)
    tok = Tokens(me, S)
    other = me.dev(c=1 - me.c)
    mine = pl.ds(pl.multiple_of(me.c * half, half), half)
    theirs = pl.ds(pl.multiple_of((1 - me.c) * half, half), half)
    heads = pl.ds(pl.multiple_of(me.c * W, W), W)

    def which(i):
        return jnp.where(i < J, 1 - me.y, me.y), lax.rem(i, J)

    def fetch(i, slot):
        t, j = which(i)
        return [pltpu.make_async_copy(
            g2_ref.at[t, :, pl.ds(pl.multiple_of(kind * H + j * chunk, chunk), chunk)],
            wbuf.at[2 * slot + kind], wsem.at[2 * slot + kind]) for kind in range(2)]

    loads = [pltpu.make_async_copy(a, b, csem.at[2 + i]) for i, (a, b) in enumerate(
        [(xm_ref, xb), (cf_ref, cb)] + [(g2_ref.at[t, :, pl.ds(2 * H, W)], wo.at[t]) for t in range(T)])]
    for cp in loads:
        cp.start()
    for cp in fetch(0, 0):
        cp.start()

    def put_ff(i, total):
        j, kind = i // 2, i % 2
        (oup_ref, odn_ref)[kind][:, j * chunk:(j + 1) * chunk] = total

    def put_o(i, total):
        oo_ref[...] = total

    def put_q(i, total):
        oq_ref[...] = total

    acc_f, rc_f = bf[:2]
    acc_o, rc_o = bo[:2]
    acc_q = bq[0]

    def parts_f(t, x):
        return [(rc_f.at[t, x, pl.ds(2 * j, 2)], fc.at[(t * X + x) * J + j]) for j in range(J)]

    def parts_o(t, x):
        return [(rc_o.at[t, x], oc.at[t * X + x])]

    def parts_q(t, x):
        return [(acc_q.at[t, x], qc.at[x])]

    def deal(cols, own_to, away_to):
        rows = C * r
        for x in range(X):
            own = pl.ds(pl.multiple_of((2 * x + me.c) * rows, r), rows)
            away = pl.ds(pl.multiple_of((2 * x + 1 - me.c) * rows, r), rows)
            own_to(x, tmp[own, :cols].reshape(C, r, cols))
            away_to(x, tmp[away, :cols].reshape(C, r, cols))

    def store(ref, *index):
        def put(x, block):
            ref[tuple(x if i is None else i for i in index)] = block
        return put

    steps = {}
    for name, group in (("f", reduce_events(me, False, bf, sends, rf, put_ff, parts_f)),
                        ("o", reduce_events(me, False, bo, sends, ro, put_o, parts_o)),
                        ("q", reduce_events(me, True, bq, sends, rq, put_q, parts_q)),
                        ("t", total_events(me, vec, (vacc, vgot), vec, sends, rv)),
                        ("u", total_events(me, soon, (sacc, sgot), soon, sends, ru))):
        for key, step in group.items():
            steps[name + key] = step
    for name, item in (("R", (xb, res_out, tss.at[0], trs.at[0], tls.at[0])),
                       ("I", (cb, ing_out, tss.at[1], trs.at[1], tls.at[1]))):
        steps[name + "o"] = lambda item=item: tok.back(*item)
        for p in range(S * CUT):
            steps[name + str(p)] = lambda item=item, p=p: tok.back_pass(p % S, p // S, *item)
        steps[name + "e"] = lambda item=item: tok.back_end(*item)
    mid_plan, gap_plan, att_plan, end_plan = REST_PLAN

    def at_step(i, plan):
        for m, names in enumerate(plan):
            if names:
                @pl.when(i == m)
                def _():
                    for name in names:
                        steps[name]()

    def strips(body):
        per = R // STRIP

        def step(i, carry):
            at = pl.ds(pl.multiple_of(i * STRIP, STRIP), STRIP)
            body(at, (i // per, pl.ds(pl.multiple_of(lax.rem(i, per) * STRIP, STRIP), STRIP)))
            return carry
        lax.fori_loop(0, half // STRIP, step, 0)

    for cp in loads:
        cp.wait()
    for t in range(T):
        part = nt(ar_ref[:, t * W:(t + 1) * W], wo[t])
        acc[...] = part if t == 0 else acc[...] + part

    def first_norm(at, qat):
        u, factor = unit_of(xb[qat].astype(f32) + acc[at, :] + row(0))
        unit[at, :] = u
        fac[at, :] = jnp.broadcast_to(factor, (STRIP, 128))
        low[at, :] = (u * row(2) + row(3)).astype(b16)
        acc[at, :] = jnp.zeros((STRIP, D), f32)
    strips(first_norm)
    flip(low, low_t)

    def forward(i, carry):
        slot = lax.rem(i, 2)
        t, j = which(i)
        for cp in fetch(i, slot):
            cp.wait()
        for cp in fetch(lax.rem(i + 1, n), 1 - slot):
            cp.start()
        hid[...] = nn(low[...], wbuf[2 * slot])
        bias = ub_ref[t * J + j]
        base = i * half

        def units(at, qat):
            h = hid[at, :] + bias
            phi = 0.5 + 0.5 * lax.erf(h * (0.5 ** 0.5))
            dens = jnp.exp(-0.5 * h * h) * 0.3989422804014327
            to = pl.ds(pl.multiple_of(base + at.start, STRIP), STRIP)
            act[to, :] = (h * phi).astype(b16)
            slope[to, :] = (phi + h * dens).astype(b16)
        strips(units)
        acc[...] += nt(act[pl.ds(pl.multiple_of(base, half), half), :], wbuf[2 * slot + 1])
        return carry
    lax.fori_loop(0, n, forward, 0)

    sums[...] = jnp.zeros_like(sums)

    def second_norm(at, qat):
        u, factor = unit_of(unit[at, :] * row(2) + row(3) + acc[at, :] + row(1))
        g = cb[qat].astype(f32)
        xb[qat] = (u * row(4) + row(5)).astype(b16)
        g2 = back_of(g, u, factor, row(4))
        l2 = g2.astype(b16)
        fl[at, :] = l2
        acc[at, :] = g2
        sums[1] += fold(l2.astype(f32))
        sums[4] += fold(g * u)
        sums[5] += fold(g)
    strips(second_norm)
    flip(fl, fl_t)
    steps["Ro"]()

    def stage_copy(i, x):
        t, j = which(i)
        slot = lax.rem(i, 2)
        return pltpu.make_async_remote_copy(
            src_ref=stage.at[slot, x], dst_ref=rc_f.at[t, x, pl.ds(2 * j, 2)], send_sem=fs.at[slot * X + x],
            recv_sem=fc.at[(t * X + x) * J + j], device_id=other, device_id_type=MESH)

    def backward(i, carry):
        slot = lax.rem(i, 2)
        t, j = which(i)
        for cp in fetch(i, slot):
            cp.wait()

        @pl.when(i + 1 < n)
        def _():
            for cp in fetch(i + 1, 1 - slot):
                cp.start()
        hid[...] = nn(fl[...], wbuf[2 * slot + 1])
        base = i * half
        gub[t * J + j] = jnp.zeros_like(gub[0])

        def units(at, qat):
            to = pl.ds(pl.multiple_of(base + at.start, STRIP), STRIP)
            v = (hid[at, :] * slope[to, :].astype(f32)).astype(b16)
            hl[at, :] = v
            gub[t * J + j] += fold(v.astype(f32))
        strips(units)

        @pl.when(i >= 2)
        def _():
            for x in range(X):
                stage_copy(i, x).wait_send()
        for kind in range(2):
            if kind == 0:
                tmp[...] = nn(low_t[...], hl[...]).astype(b16)
            else:
                tmp[...] = nn(fl_t[...], act[pl.ds(pl.multiple_of(base, half), half), :]).astype(b16)
            deal(chunk, store(acc_f, t, None, 2 * j + kind), store(stage, slot, None, kind))
        for x in range(X):
            stage_copy(i, x).start()
        acc[...] += nt(hl[...], wbuf[2 * slot])
        at_step(i, mid_plan)
        return carry
    lax.fori_loop(0, n, backward, 0)

    def first_back(at, qat):
        g = acc[at, :]
        u = unit[at, :]
        g1 = back_of(g, u, fac[at, 0:1], row(2))
        acc[at, :] = g1
        l1 = g1.astype(b16)
        fl[at, :] = l1
        sums[0] += fold(l1.astype(f32))
        sums[2] += fold(g * u)
        sums[3] += fold(g)
    strips(first_back)
    hl[:, :W] = nn(fl[...], wo[1 - me.c]).astype(b16)
    sends.go(hl.at[:, pl.ds(0, W)], doh.at[mine, :], csem.at[0], other)
    doh[mine, :] = nn(fl[...], wo[me.c]).astype(b16)
    flip(fl, fl_t)
    for t in range(T):
        tmp[:, :W] = nn(fl_t[...], ar_ref[:, t * W:(t + 1) * W]).astype(b16)
        deal(W, store(acc_o, t, None, 0), store(away_o, t, None, 0))
        for x in range(X):
            sends.go(away_o.at[t, x], rc_o.at[t, x], oc.at[t * X + x], other)
    for i in (n - 2, n - 1):
        for x in range(X):
            stage_copy(i, x).wait_send()
    turn = [pltpu.make_async_copy(g1_ref.at[me.c, :, pl.ds(m * W, W)], wbuf.at[m, :, pl.ds(0, W)], wsem.at[m])
            for m in range(3)]
    for cp in turn:
        cp.start()
    for h in range(2):
        for i in range(0, half, 128):
            a, b = (h * half + i) // R, (h * half + i) % R
            unit[i:i + 128, (4 + h) * PAIR:(5 + h) * PAIR] = jnp.broadcast_to(sf_ref[a, 0:1, b:b + 128], (128, 128)).T
        for p in range(n_pairs):
            low_t[(2 * p + h) * PAIR:(2 * p + h + 1) * PAIR, :] = (
                k_ref[h * half:(h + 1) * half, p * PAIR:(p + 1) * PAIR].astype(f32).T.astype(b16))
    def tokens(h):
        return [pltpu.make_async_copy(xf_ref.at[h * (C // 2) + i], low.at[pl.ds(i * R, R), :], csem.at[2 + i])
                for i in range(C // 2)]

    def turn_tokens(h):
        def run():
            for cp in tokens(h):
                cp.wait()
            for i in range(0, half, 128):
                at = h * half + i
                act[at // chunk * D:(at // chunk + 1) * D, at % chunk:at % chunk + 128] = (
                    low[i:i + 128, :].astype(f32).T.astype(b16))
            if h == 0:
                for cp in tokens(1):
                    cp.start()
        return run
    steps["x0"] = turn_tokens(0)
    steps["x1"] = turn_tokens(1)
    for cp in tokens(0):
        cp.start()

    def projections():
        for m in range(3):
            out = None
            for h in range(L // chunk):
                term = nn(act[h * D:(h + 1) * D, :], slope[m * L + h * chunk:m * L + (h + 1) * chunk, :W])
                out = term if out is None else out + term
            tmp[:, :W] = out.astype(b16)
            cols = slice(m * W, (m + 1) * W)
            every = slice(None)
            deal(W, store(acc_q, me.c, None, 0, every, every, cols), store(away_q, None, 0, every, every, cols))
        for x in range(X):
            sends.go(away_q.at[x], acc_q.at[me.c, x], qc.at[x], other)
    steps["gq"] = projections

    def back_project(who):
        out = None
        for m in range(3):
            rows = pl.ds(pl.multiple_of(m * L + who * half, half), half)
            term = nt(slope[rows, :W], wbuf[m, :, :W])
            out = term if out is None else out + term
        return out

    def give():
        for cp in turn:
            cp.wait()
        fl[...] = back_project(1 - me.c).astype(b16)
        sends.go(fl, got_part, csem.at[1], other)
    steps["give"] = give

    def keep():
        acc[...] += back_project(me.c)
    steps["keep"] = keep

    def join():
        arrived(got_part, csem.at[1], me)
        for i in range(C // 2):
            at = slice(i * R, (i + 1) * R)
            cb[i] = (acc[at, :] + got_part[at, :].astype(f32)).astype(b16)
    steps["join"] = join
    n_late, n_soon = 2 * T * W, T * H + 6 * D

    def lay(ref, flat, count):
        flat = jnp.concatenate(flat, axis=1)
        for i in range(count // 128):
            ref[i:i + 1, :] = flat[:, i * 128:(i + 1) * 128]
        if ref.shape[0] * 128 > count:
            ref[count // 128:, :] = jnp.zeros((ref.shape[0] - count // 128, 128), f32)

    def early_sums():
        lay(soon, [jnp.sum(gub[i], axis=0, keepdims=True) for i in range(n)]
            + [jnp.sum(sums[i], axis=0, keepdims=True) for i in range(6)], n_soon)
    steps["usums"] = early_sums

    def token_sums():
        zeros = jnp.zeros((1, W), f32)
        ones = jnp.ones((8, L), b16)
        first = me.c == 0
        flat = []
        for m in (0, 2):
            v = nn(ones, slope[m * L:(m + 1) * L, :W])[0:1]
            flat += [jnp.where(first, v, zeros), jnp.where(first, zeros, v)]
        lay(vec, flat, n_late)
    steps["sums"] = token_sums

    def vectors():
        fz = (2 * me.x + me.c) * C + me.z
        tfz = me.y * (X * 2 * C) + fz
        n_dev = T * X * 2 * C
        qw, uw = T * W // n_dev, T * H // n_dev
        out = 0
        for ref, count, kinds in ((vec, n_late, [(T * W, qw, tfz)] * 2),
                                  (soon, n_soon, [(T * H, uw, tfz)] + [(D, r, fz)] * 6)):
            total = jnp.concatenate([ref[i:i + 1, :] for i in range(count // 128)], axis=1)
            at = 0
            for m, w, here in kinds:
                vs_ref[out:out + 1, :] = take(total[:, at:at + m], here, w)
                at += m
                out += 1
    steps["vectors"] = vectors
    for name in gap_plan:
        steps[name]()
    arrived(doh.at[theirs, :], csem.at[0], me)

    def attention(it, carry):
        p, i = it // C, lax.rem(it, C)
        at = pl.ds(pl.multiple_of(i * R, R), R)
        cols = pl.ds(pl.multiple_of(p * PAIR, PAIR), PAIR)
        wide = jnp.concatenate([unit[:, (4 + h) * PAIR:(5 + h) * PAIR] for h in range(2)], axis=0)
        k_t = jnp.concatenate([low_t[pl.ds(pl.multiple_of((2 * p + h) * PAIR, PAIR), PAIR), :] for h in range(2)],
                              axis=1)
        dq, dk, dv = attend_back_block(q_ref[at, cols], k_ref[:, cols], k_t, v_ref[:, cols], doh[at, cols],
                                       ah_ref[at, cols], lse_ref[p, :, at], sf_ref[i, 0:1, :], two_lanes(wide))
        slope[at, cols] = dq.astype(b16)
        lanes = [slice(m * PAIR, (m + 1) * PAIR) for m in range(4)]
        halves = [dk[:half], dk[half:], dv[:half], dv[half:]]

        @pl.when(i == 0)
        def _():
            for m in range(4):
                unit[:, lanes[m]] = halves[m]

        @pl.when(i > 0)
        def _():
            for m in range(4):
                unit[:, lanes[m]] += halves[m]

        @pl.when(i == C - 1)
        def _():
            for m in range(4):
                slope[L + m * half:L + (m + 1) * half, cols] = unit[:, lanes[m]].astype(b16)

        at_step(it, att_plan)
        return carry
    lax.fori_loop(0, n_pairs * C, attention, 0)

    for name in end_plan:
        steps[name]()
    sends.finish(me)


REST_PLAN = (
    ((), (), (), ('fc', 'fd2'), ('fd3',), ('fd0',)),
    ('fd1', 'usums', 'u0'),
    (('fa', 'fy3'), ('u1', 'fb', 'fw3'), ('fw1',), ('fy1',), ('u2', 'fw2', 'fo'), (), ('fz3', 'fy0'), (),
     ('fw0',), ('fz1',), ('oc',), ('fy2',)),
    ('give', 'od3', 'R0', 'u3', 'R1', 'keep', 'join', 'Io', 'od0', 'od2', 'x0', 'sums', 'R2', 'R3', 'u4', 'x1',
     'gq', 'fz2', 'fz0', 'od1', 'I0', 't0', 'qc', 'qd0', 'qd1', 'qd3', 'qa', 'qb', 'qy0', 'qy1', 'qy3', 'qd2',
     'qw3', 'qw0', 'qo', 't1', 't2', 'R4', 'qy2', 't3', 'oa', 'oy0', 'oy1', 'oy2', 'oy3', 'qw2', 'qz3', 'I1',
     'qw1', 'I2', 'ob', 'ow1', 'ow2', 'ow3', 'ow0', 'qz1', 'I3', 'I4', 'I5', 'qz2', 'qz0', 't4', 'fl', 'oo',
     'oz0', 'oz1', 'oz3', 'R5', 'vectors', 'oz2', 'ql', 'Re', 'Ie', 'ol'),
)


def rest(cfg, q, k, v, ah, lse, sf, ar, vec, ub, xm, cf, xf, g1, g2):
    sizes, S, W, H, chunk = cfg
    F, C, T = sizes
    X = F // 2
    _, R, D = xf.shape
    L = C * R
    half = L // 2
    J = H // chunk
    n = T * J
    r = D // (F * C)
    f32, b = jnp.float32, jnp.bfloat16
    dma = pltpu.SemaphoreType.DMA
    sds = jax.ShapeDtypeStruct
    vm = pltpu.VMEM
    steps = total_count(sizes)
    n_vec = -(-2 * T * W // 1024) * 8
    n_soon = -(-(T * H + 6 * D) // 1024) * 8
    sems = reduce_sems(sizes)
    tall = max(n * half, 3 * L, L // chunk * D)
    return pl.pallas_call(
        functools.partial(rest_kernel, cfg),
        in_specs=[VM] * 9 + [ANY] * 5,
        out_specs=[ANY] * 2 + [VM] * 5,
        out_shape=[sds((S, R, D), b), sds((S, R, D), b), sds((r, 3 * W), f32), sds((r, H), f32), sds((r, H), f32),
                   sds((r, W), f32), sds((16, VEC), f32)],
        scratch_shapes=[vm((C // 2, R, D), b), vm((C // 2, R, D), b), vm((half, D), f32), vm((half, 128), f32),
                        vm((half, D), b), vm((D, half), b), vm((half, D), f32), vm((half, D), b), vm((D, half), b),
                        vm((half, chunk), f32), vm((tall, chunk), b), vm((tall, chunk), b), vm((half, chunk), b),
                        vm((4, D, chunk), b), vm((T, D, W), b), vm((6, 8, D), f32), vm((n, 8, chunk), f32),
                        vm((D, chunk), b), vm((2, X, 2, C, r, chunk), b),
                        vm((L, W), b), vm((T, X, 1, C, r, W), b),
                        vm((X, 1, C, r, 3 * W), b), vm((half, D), b),
                        vm((n_vec, 128), f32), vm((4, n_vec, 128), f32), vm((steps, n_vec, 128), f32),
                        vm((n_soon, 128), f32), vm((4, n_soon, 128), f32), vm((steps, n_soon, 128), f32)]
        + reduce_scratch(sizes, 2 * J, r, chunk, False) + reduce_scratch(sizes, 1, r, W, False)
        + reduce_scratch(sizes, 1, r, 3 * W, True)
        + [dma((3 * reduce_count(sizes) + T * X + X + 2 * steps + 2,)),
           dma((sems,)), dma((sems,)), dma((sems,)), dma((steps,)), dma((steps,)), dma((T * X * J,)), dma((2 * X,)),
           dma((T * X,)), dma((X,)), dma((2, (C // 2 + S) * CUT)), dma((2, S * CUT)), dma((2,)), dma((4 + T + C,)), dma((4,))],
        compiler_params=pltpu.CompilerParams(collective_id=1, has_side_effects=True,
                                             vmem_limit_bytes=60 * 2**20 + 512 * 2**10),
    )(q, k, v, ah, lse, sf, ar, vec, ub, xm, cf, xf, g1, g2)


def finish_kernel(W, res_in, ing_in, oq_in, oup_in, odn_in, oo_in, vs_in,
                  res, ing, oq, ok, ov, oo, oup, odn, *small):
    res[...] = res_in[...]
    ing[...] = ing_in[...].astype(jnp.float32)

    @pl.when(pl.program_id(0) == 0)
    def _():
        oq[...] = oq_in[:, :W]
        ok[...] = oq_in[:, W:2 * W]
        ov[...] = oq_in[:, 2 * W:]
        oup[...] = oup_in[...]
        oo[...] = oo_in[...]
        odn[...] = odn_in[...]
        for i, ref in enumerate(small):
            ref[...] = vs_in[i:i + 1, :ref.shape[1]]


def finish(cfg, widths, *arrays):
    sizes, S, W, H, chunk = cfg
    res, ing, oq = arrays[:3]
    r = oq.shape[0]
    R, D = res.shape[1:]
    f32 = jnp.float32
    token = pl.BlockSpec((1, R, D), lambda i: (i, 0, 0))
    whole = lambda shape: pl.BlockSpec(shape, lambda i: (0,) * len(shape))
    shapes = [(r, W)] * 4 + [(r, H), (r, H)] + [(1, w) for w in widths]
    return pl.pallas_call(
        functools.partial(finish_kernel, W),
        grid=(S,),
        in_specs=[token, token] + [whole(a.shape) for a in arrays[2:]],
        out_specs=[token, token] + [whole(shape) for shape in shapes],
        out_shape=[jax.ShapeDtypeStruct((S, R, D), jnp.bfloat16), jax.ShapeDtypeStruct((S, R, D), f32)]
        + [jax.ShapeDtypeStruct(shape, f32) for shape in shapes],
        compiler_params=pltpu.CompilerParams(vmem_limit_bytes=62 * 2**20),
    )(*arrays)


def chunk_of(H):
    for w in (512, 384, 256, 128):
        if H % w == 0:
            return w
    return H


def on_device(sizes, inputs, segments, cotangent, query_weight, key_weight, value_weight,
              output_weight, up_weight, down_weight, *small):
    F, C, T = sizes
    X = F // 2
    S, R, D = inputs.shape
    W = query_weight.shape[1]
    H = up_weight.shape[1]
    r = query_weight.shape[0]
    chunk = chunk_of(H)
    cfg = (sizes, S, W, H, chunk)
    weights = (query_weight, key_weight, value_weight, output_weight.T, up_weight, down_weight.T)
    widths = [v.shape[0] for v in small]
    small = [v.reshape(1, -1) for v in small]
    q, k, v, ah, ar, lse, xf, cf, sf, g1, g2, vec, ub, xm = front(
        cfg, inputs, cotangent, segments, weights, small)
    landed = rest(cfg, q, k, v, ah, lse, sf, ar, vec, ub, xm, cf, xf,
                  g1.reshape(T, D, -1), g2.reshape(T, D, -1))
    outs = finish(cfg, widths, *landed)
    return tuple(outs[:5]) + (outs[5].T, outs[6], outs[7].T) + tuple(v.reshape(-1) for v in outs[8:])


def solution(mesh):
    sizes = (mesh.shape["fsdp"], mesh.shape["ctx"], mesh.shape["tp"])
    every = ("fsdp", "ctx")
    rows, cols, one, three = P(every, "tp"), P("tp", every), P(every), P(("tp",) + every)
    token = P("fsdp", "ctx", None)
    weights = (rows, rows, rows, cols, rows, cols)
    vectors = (three, three, three) + (one,) * 6
    return jax.shard_map(
        functools.partial(on_device, sizes), mesh=mesh,
        in_specs=(token, P("fsdp", "ctx"), token) + weights + vectors,
        out_specs=(token, token) + weights + vectors, check_vma=False)
```

```python
import functools
import jax
import jax.numpy as jnp
from jax import lax
from jax.sharding import PartitionSpec as P
from jax.experimental import pallas as pl
from jax.experimental.pallas import tpu as pltpu

MESH = pl.DeviceIdType.MESH
ANY = pl.BlockSpec(memory_space=pl.ANY)
VM = pl.BlockSpec(memory_space=pltpu.VMEM)


class Place:
    def __init__(self, sizes):
        self.F, self.C, self.T = sizes
        self.X = self.F // 2
        f = lax.axis_index("fsdp")
        self.x = f // 2
        self.c = lax.rem(f, 2)
        self.z = lax.axis_index("ctx")
        self.y = lax.axis_index("tp")

    def dev(self, x=None, c=None, z=None, y=None):
        x = self.x if x is None else x
        c = self.c if c is None else c
        return (2 * x + c, self.z if z is None else z, self.y if y is None else y)

    def z_off(self, d):
        return lax.rem(self.z + d + self.C, self.C)

    def x_off(self, d):
        return lax.rem(self.x + d + self.X, self.X)

    def greet(self, chip_wide):
        bar = pltpu.get_barrier_semaphore()
        devs = [self.dev(c=1 - self.c), self.dev(y=1 - self.y)]
        devs += [self.dev(x=self.x_off(d)) for d in range(1, self.X)]
        for d in range(1, self.C):
            devs.append(self.dev(z=self.z_off(d)))
            if chip_wide:
                devs.append(self.dev(z=self.z_off(d), c=1 - self.c))
        for d in devs:
            pl.semaphore_signal(bar, inc=1, device_id=d, device_id_type=MESH)
        pl.semaphore_wait(bar, len(devs))


class Sends:
    def __init__(self, sems):
        self.sems, self.n, self.waits = sems, 0, []

    def go(self, src, dst, recv, dev, like=None, when=None):
        pltpu.make_async_remote_copy(
            src_ref=src, dst_ref=dst, send_sem=self.sems.at[self.n], recv_sem=recv,
            device_id=dev, device_id_type=MESH).start()
        self.n += 1
        self.waits.append((src if like is None else like, when))

    def finish(self, me):
        for n, (like, when) in enumerate(self.waits):
            def wait():
                pltpu.make_async_remote_copy(
                    src_ref=like, dst_ref=like, send_sem=self.sems.at[n], recv_sem=self.sems.at[n],
                    device_id=me.dev(c=1 - me.c), device_id_type=MESH).wait_send()
            given(when, wait)
        self.waits = []


def given(when, body):
    if when is None:
        body()
    else:
        pl.when(when())(body)


def arrived(dst, recv, pl_):
    pltpu.make_async_remote_copy(
        src_ref=dst, dst_ref=dst, send_sem=recv, recv_sem=recv,
        device_id=pl_.dev(c=1 - pl_.c), device_id_type=MESH).wait_recv()


def line_order(C, z):
    return [z] + [z + sign * k for k in range(1, C) for sign in (-1, 1) if 0 <= z + sign * k < C]


def pick(index, table):
    out = table[-1]
    for i in reversed(range(len(table) - 1)):
        out = jnp.where(index == i, table[i], out)
    return jnp.int32(out)


def gather_events(me, own, full, sends, recv, lsem):
    C, X = me.C, me.X
    sem = lambda t, x, c, z: recv.at[((t * X + x) * 2 + c) * C + z]
    r = own.shape[0]

    def slot(t, x, c, z):
        if len(full.shape) == 6:
            return full.at[t, x, c, z]
        row = ((x * 2 + c) * C + z) * r
        return full.at[t, pl.ds(row if isinstance(row, int) else pl.multiple_of(row, r), r), :]

    like = slot(0, 0, 0, 0)
    orders = [line_order(C, z) for z in range(C)]
    where = lambda m: pick(me.z, [o[m] for o in orders])

    def push(src, at, dev, when=None):
        sends.go(src, slot(*at), sem(*at), dev, like, when)

    def wait(at):
        arrived(slot(*at), sem(*at), me)

    core, side = me.dev(c=1 - me.c), me.dev(y=1 - me.y)
    xs = [(me.x_off(d), me.dev(x=me.x_off(d))) for d in range(1, X)]
    local = pltpu.make_async_copy(own, slot(me.y, me.x, me.c, me.z), lsem)

    def along(m):
        def run():
            zz = where(m)
            at = (me.y, me.x, me.c, zz)
            src = slot(*at) if m else own
            if m:
                wait(at)
            for sign in (-1, 1):
                def onward(sign=sign):
                    zz = where(m)
                    return ((zz - me.z) * sign <= 0) & (me.z + sign >= 0) & (me.z + sign < C)

                @pl.when(onward())
                def _():
                    push(src, at, me.dev(z=me.z + sign), onward)
            for _, dev in xs:
                push(src, at, dev)
            push(src, at, side)
            push(src, at, core)
            if not m:
                local.start()
        return run

    def across(m):
        def run():
            zz = where(m)
            at = (1 - me.y, me.x, me.c, zz)
            wait(at)
            if m < C // 2:
                for _, dev in xs:
                    push(slot(*at), at, dev)
            push(slot(*at), at, core)
            for xo, _ in xs:
                at = (me.y, xo, me.c, zz)
                wait(at)
                if m >= C // 2:
                    push(slot(*at), at, side)
                push(slot(*at), at, core)
        return run

    def corner(m):
        def run():
            zz = where(m)
            for xo, _ in xs:
                at = (1 - me.y, xo, me.c, zz)
                wait(at)
                push(slot(*at), at, core)
        return run

    def last():
        for t in range(me.T):
            for xx in range(X):
                for zz in range(C):
                    wait((t, xx, 1 - me.c, zz))
        local.wait()

    steps = {"l": last}
    for m in range(C):
        steps["a%d" % m] = along(m)
        steps["x%d" % m] = across(m)
        steps["c%d" % m] = corner(m)
    return steps


def gather_count(sizes):
    F, C, T = sizes
    X = F // 2
    return C * (4 * X + 4)


CUT = 2


class Tokens:
    def __init__(self, me, seqs):
        self.me, self.S = me, seqs
        self.half = me.C // 2
        self.lo = me.y * (me.C - seqs)
        self.busy = (me.z >= self.lo) & (me.z < self.lo + seqs)
        self.owner = me.c == me.y

    def out(self, src, dst, full, ssem, rsem, lsem):
        me, half = self.me, self.half
        k = me.z // half
        at = me.z if full else lax.rem(me.z, half)

        @pl.when(self.owner)
        def _():
            for s in range(self.S):
                here = (self.lo + s == me.z) & (k == me.c)

                @pl.when(here)
                def _():
                    pltpu.make_async_copy(src.at[s], dst.at[at], lsem).start()

                @pl.when(jnp.logical_not(here))
                def _():
                    pltpu.make_async_remote_copy(
                        src_ref=src.at[s], dst_ref=dst.at[at], send_sem=ssem.at[s],
                        recv_sem=rsem.at[lax.rem(me.z, half)],
                        device_id=me.dev(c=k, z=self.lo + s), device_id_type=MESH).start()

    def out_done(self, src, dst, full, ssem, rsem, lsem):
        me, half = self.me, self.half

        @pl.when(self.busy)
        def _():
            for i in range(half):
                zq = me.c * half + i
                at = zq if full else i
                here = (zq == me.z) & (me.c == me.y)

                @pl.when(here)
                def _():
                    pltpu.make_async_copy(src.at[0], dst.at[at], lsem).wait()

                @pl.when(jnp.logical_not(here))
                def _():
                    arrived(dst.at[at], rsem.at[i], me)

                if full:
                    pltpu.make_async_remote_copy(
                        src_ref=dst.at[at], dst_ref=dst.at[at], send_sem=ssem.at[self.S + i],
                        recv_sem=rsem.at[half + i], device_id=me.dev(c=1 - me.c),
                        device_id_type=MESH).start()

    def out_end(self, src, dst, full, ssem, rsem, lsem):
        me, half = self.me, self.half
        k = me.z // half

        @pl.when(self.owner)
        def _():
            for s in range(self.S):
                here = (self.lo + s == me.z) & (k == me.c)

                @pl.when(jnp.logical_not(here))
                def _():
                    pltpu.make_async_remote_copy(
                        src_ref=src.at[s], dst_ref=dst.at[0], send_sem=ssem.at[s],
                        recv_sem=rsem.at[0], device_id=me.dev(c=1 - me.c),
                        device_id_type=MESH).wait_send()

        if full:
            @pl.when(self.busy)
            def _():
                for i in range(half):
                    zq = (1 - me.c) * half + i
                    arrived(dst.at[zq], rsem.at[half + i], me)
                    pltpu.make_async_remote_copy(
                        src_ref=dst.at[0], dst_ref=dst.at[0], send_sem=ssem.at[self.S + i],
                        recv_sem=rsem.at[0], device_id=me.dev(c=1 - me.c),
                        device_id_type=MESH).wait_send()

    def back(self, src, dst, ssem, rsem, lsem):
        me, half = self.me, self.half
        size = src.shape[1] // CUT

        @pl.when(self.busy)
        def _():
            at = me.z - self.lo
            for h in range(CUT):
                piece = pl.ds(h * size, size)
                for i in range(half):
                    zq = me.c * half + i
                    here = (zq == me.z) & (me.c == me.y)

                    @pl.when(here)
                    def _():
                        if h == 0:
                            pltpu.make_async_copy(src.at[i], dst.at[at], lsem).start()

                    @pl.when(jnp.logical_not(here))
                    def _():
                        pltpu.make_async_remote_copy(
                            src_ref=src.at[i, piece], dst_ref=dst.at[at, piece], send_sem=ssem.at[i * CUT + h],
                            recv_sem=rsem.at[at * CUT + h], device_id=me.dev(c=me.y, z=zq),
                            device_id_type=MESH).start()

    def back_pass(self, s, h, src, dst, ssem, rsem, lsem):
        me, half = self.me, self.half
        size = src.shape[1] // CUT
        piece = pl.ds(h * size, size)

        @pl.when(self.owner)
        def _():
            here = (self.lo + s == me.z) & (me.z // half == me.c)

            @pl.when(here)
            def _():
                if h == 0:
                    pltpu.make_async_copy(src.at[0], dst.at[s], lsem).wait()

            @pl.when(jnp.logical_not(here))
            def _():
                arrived(dst.at[s, piece], rsem.at[s * CUT + h], me)

            pltpu.make_async_remote_copy(
                src_ref=dst.at[s, piece], dst_ref=dst.at[s, piece], send_sem=ssem.at[(half + s) * CUT + h],
                recv_sem=rsem.at[s * CUT + h], device_id=me.dev(y=1 - me.y), device_id_type=MESH).start()

    def back_end(self, src, dst, ssem, rsem, lsem):
        me, half = self.me, self.half
        size = src.shape[1] // CUT
        piece = pl.ds(0, size)

        @pl.when(self.busy)
        def _():
            for i in range(half):
                here = (me.c * half + i == me.z) & (me.c == me.y)

                @pl.when(jnp.logical_not(here))
                def _():
                    for h in range(CUT):
                        pltpu.make_async_remote_copy(
                            src_ref=src.at[i, piece], dst_ref=dst.at[0, piece], send_sem=ssem.at[i * CUT + h],
                            recv_sem=rsem.at[0], device_id=me.dev(c=1 - me.c), device_id_type=MESH).wait_send()

        @pl.when(self.owner)
        def _():
            for n in range(self.S * CUT):
                pltpu.make_async_remote_copy(
                    src_ref=dst.at[0, piece], dst_ref=dst.at[0, piece], send_sem=ssem.at[half * CUT + n],
                    recv_sem=rsem.at[0], device_id=me.dev(y=1 - me.y), device_id_type=MESH).wait_send()

        @pl.when(jnp.logical_not(self.owner))
        def _():
            for n in range(self.S * CUT):
                arrived(dst.at[n // CUT, pl.ds(n % CUT * size, size)], rsem.at[n], me)


def reduce_events(me, split, bufs, sends, recv, finish, parts):
    acc, rc, xd, yd, xr, yr, zr = bufs
    C, X = me.C, me.X
    half = C // 2
    n_cols = acc.shape[2]
    like = acc.at[0, 0, :, 0]
    side = me.dev(y=1 - me.y)
    base = 0
    s_d = lambda d, j: recv.at[base + (d - 1) * C + j]
    base2 = base + (X - 1) * C
    s_xr = lambda d, j: recv.at[base2 + (d - 1) * C + j]
    base3 = base2 + (X - 1) * C
    s_yr = lambda j: recv.at[base3 + j]
    s_zr = lambda j: recv.at[base3 + C + j]
    quads = ([(1 - me.y, me.x_off(d)) for d in range(1, X)] + [(1 - me.y, me.x)]
             + [(me.y, me.x_off(d)) for d in range(1, X)] + [(me.y, me.x)])

    def add(a, b):
        def body(i, carry):
            a[i] = a[i] + b[i]
            return carry
        lax.fori_loop(0, n_cols, body, 0)

    def ready(n):
        t, x = quads[n]
        if split:
            if n == 0:
                for xo in [me.x_off(d) for d in range(1, X)] + [me.x]:
                    for view, sem in parts(1 - me.c, xo):
                        arrived(view, sem, me)
            return
        for view, sem in parts(t, x):
            arrived(view, sem, me)

        def body(i, carry):
            for z in range(C):
                acc[t, x, i, z] = acc[t, x, i, z] + rc[t, x, i, z]
            return carry
        lax.fori_loop(0, n_cols, body, 0)

    by_x = range(1, C)

    def ready_corner():
        for d in range(1, X):
            ready(d - 1)

    def corner(j):
        def run():
            zj = me.z_off(-j)
            for d in range(1, X):
                t, x = quads[d - 1]
                if j in by_x:
                    sends.go(acc.at[t, x, :, zj], xd.at[d - 1, j - 1], s_d(d, j), me.dev(x=x), like)
                else:
                    sends.go(acc.at[t, x, :, zj], yd.at[d - 1, 0], s_d(d, j), side, like)
        return run

    def ready_x():
        for n in range(X, 2 * X - 1):
            ready(n)

    def over_x(j):
        def run():
            zj = me.z_off(-j)
            for d in range(1, X):
                xo = me.x_off(d)
                if j not in by_x:
                    arrived(yd.at[d - 1, 0], s_d(d, j), me)
                    add(acc.at[me.y, xo, :, zj], yd.at[d - 1, 0])
                sends.go(acc.at[me.y, xo, :, zj], xr.at[d - 1, j], s_xr(d, j), me.dev(x=xo), like)
        return run

    def over_y(j):
        def run():
            zj = me.z_off(-j)
            if j in by_x:
                for d in range(1, X):
                    arrived(xd.at[d - 1, j - 1], s_d(d, j), me)
                    add(acc.at[1 - me.y, me.x, :, zj], xd.at[d - 1, j - 1])
            sends.go(acc.at[1 - me.y, me.x, :, zj], yr.at[j], s_yr(j), side, like)
        return run

    def to_z(j):
        def run():
            t, x = me.y, me.x
            zj = me.z_off(-j)
            for d in range(1, X):
                arrived(xr.at[d - 1, j], s_xr(d, j), me)
                add(acc.at[t, x, :, zj], xr.at[d - 1, j])
            arrived(yr.at[j], s_yr(j), me)
            add(acc.at[t, x, :, zj], yr.at[j])
            if j:
                sends.go(acc.at[t, x, :, zj], zr.at[j - 1], s_zr(j - 1), me.dev(z=zj), like)
        return run

    def last():
        for j in range(1, C):
            arrived(zr.at[j - 1], s_zr(j - 1), me)
        for i in range(n_cols):
            total = acc[me.y, me.x, i, me.z].astype(jnp.float32)
            for j in range(1, C):
                total = total + zr[j - 1, i].astype(jnp.float32)
            finish(i, total)

    steps = {"c": ready_corner, "a": lambda: ready(X - 1), "b": ready_x, "o": lambda: ready(2 * X - 1), "l": last}
    for j in range(C):
        steps["d%d" % j] = corner(j)
        steps["w%d" % j] = over_x(j)
        steps["y%d" % j] = over_y(j)
        steps["z%d" % j] = to_z(j)
    return steps


def reduce_scratch(sizes, n, r, w, split):
    F, C, T = sizes
    X = F // 2
    half = C // 2
    v = lambda shape: pltpu.VMEM(shape, jnp.bfloat16)
    return [v((T, X, n, C, r, w)), v((1, 1, 1, 1, 16, 128) if split else (T, X, n, C, r, w)),
            v((X - 1, C - 1, n, r, w)), v((X - 1, 1, n, r, w)), v((X - 1, C, n, r, w)),
            v((C, n, r, w)), v((C - 1, n, r, w))]


def reduce_sems(sizes):
    F, C, T = sizes
    X = F // 2
    return 2 * (X - 1) * C + 2 * C


def reduce_count(sizes):
    F, C, T = sizes
    X = F // 2
    return 2 * (X - 1) * C + C + C - 1


def total_events(me, own, bufs, out, sends, recv):
    C, X = me.C, me.X
    acc, got = bufs
    groups = [[me.dev(c=1 - me.c)], [me.dev(x=me.x_off(d)) for d in range(1, X)],
              [me.dev(y=1 - me.y)], [me.dev(z=me.z_off(d)) for d in range(1, C)]]
    like = acc.at[0]
    bases = [sum(len(g) for g in groups[:i]) for i in range(len(groups))]

    def start(gi):
        for i, dev in enumerate(groups[gi]):
            sends.go(acc.at[gi], got.at[bases[gi] + i], recv.at[bases[gi] + i], dev, like)

    def first():
        acc[0] = own[...]
        start(0)

    steps = {"0": first}
    for gi in range(len(groups)):
        def step(gi=gi):
            total = acc[gi]
            for i in range(len(groups[gi])):
                arrived(got.at[bases[gi] + i], recv.at[bases[gi] + i], me)
                total = total + got[bases[gi] + i]
            if gi + 1 < len(groups):
                acc[gi + 1] = total
                start(gi + 1)
            else:
                out[...] = total
        steps[str(gi + 1)] = step
    return steps


def total_count(sizes):
    F, C, T = sizes
    return 1 + F // 2 - 1 + 1 + C - 1

HEAD = 64
PAIR = 2 * HEAD
SCALE = HEAD ** (-0.5)
norm_eps = 1e-12
masked_score = -1000000000.0


def nt(a, b):
    return lax.dot_general(a, b, (((1,), (1,)), ((), ())), preferred_element_type=jnp.float32)


def nn(a, b):
    return lax.dot_general(a, b, (((1,), (0,)), ((), ())), preferred_element_type=jnp.float32)


def spread_segments(seg_ref, wide):
    C, _, R = seg_ref.shape
    for i in range(C):
        for j in range(0, R, 128):
            row = jnp.broadcast_to(seg_ref[i, 0:1, j:j + 128], (128, 128))
            wide[i * R + j:i * R + j + 128, :] = row.T


def lanes_of(h, like):
    lane = lax.broadcasted_iota(jnp.int32, like.shape, like.ndim - 1)
    return jnp.where(lane // HEAD == h, like, jnp.zeros_like(like))


def two_lanes(wide):
    return jnp.concatenate([wide, wide], axis=1)


def attend_block(q, k, v_t, seg_q, seg_k):
    same = seg_k == seg_q
    outs, logs = [], []
    for h in range(2):
        s = nt(k, lanes_of(h, q) * jnp.bfloat16(SCALE))
        s = jnp.where(same, s, masked_score)
        peak = jnp.max(s, axis=0, keepdims=True)
        e = jnp.exp(s - peak)
        total = jnp.sum(e, axis=0, keepdims=True)
        o = nn(v_t, e.astype(jnp.bfloat16))
        outs.append(o[h * HEAD:(h + 1) * HEAD] * (1.0 / total))
        logs.append(peak + jnp.log(total))
    return jnp.concatenate(outs, axis=0), logs


def attend_back_block(q, k, k_t, v, do, o, lse, seg_q, seg_k):
    same = seg_k == seg_q
    prod = (do.astype(jnp.float32) * o.astype(jnp.float32)).T
    dq, dk, dv = [], None, None
    for h in range(2):
        qh = lanes_of(h, q) * jnp.bfloat16(SCALE)
        doh = lanes_of(h, do)
        s = nt(k, qh)
        p = jnp.exp(jnp.where(same, s, masked_score) - lse[h:h + 1])
        dp = nt(v, doh)
        inner = jnp.sum(prod[h * HEAD:(h + 1) * HEAD], axis=0, keepdims=True)
        ds = (p * (dp - inner)).astype(jnp.bfloat16)
        dv_h = nn(p.astype(jnp.bfloat16), doh)
        dk_h = nn(ds, qh)
        dv = dv_h if dv is None else dv + dv_h
        dk = dk_h if dk is None else dk + dk_h
        dq.append(nn(k_t, ds)[h * HEAD:(h + 1) * HEAD])
    return jnp.concatenate(dq, axis=0).T * SCALE, dk, dv

STRIP = 64


def fold(value):
    total = value[0:8]
    for i in range(8, value.shape[0], 8):
        total = total + value[i:i + 8]
    return total


def mean(value):
    return jnp.mean(value, axis=-1, keepdims=True)


def unit_of(value):
    centred = value - mean(value)
    factor = lax.rsqrt(mean(centred * centred) + norm_eps)
    return centred * factor, factor


def back_of(upstream, unit, factor, gain):
    along = upstream * gain
    return factor * (along - mean(along) - unit * mean(along * unit))


def flip(ref, out):
    rows = ref.shape[0]
    for i in range(0, rows, 128):
        out[:, i:i + 128] = ref[i:i + 128, :].astype(jnp.float32).T.astype(jnp.bfloat16)


VEC = 128


def spread_pieces(blocks, width, first, total):
    n, lanes = blocks.shape
    i = lax.broadcasted_iota(jnp.int32, (lanes, total), 0)
    col = lax.broadcasted_iota(jnp.int32, (lanes, total), 1)
    pick = jnp.where(i - first == lax.rem(col, width), 1.0, 0.0).astype(jnp.bfloat16)
    wide = nn(blocks, pick)
    dev = lax.broadcasted_iota(jnp.int32, (n, total), 0)
    col = lax.broadcasted_iota(jnp.int32, (n, total), 1)
    return jnp.sum(jnp.where(dev == col // width, wide, 0.0), axis=0, keepdims=True)


def pack(widths):
    offs, at = [], 0
    for w in widths:
        if at % VEC + w > VEC:
            at += VEC - at % VEC
        offs.append(at)
        at += w
    return offs, -(-at // VEC)


def small_widths(sizes, D, W, H):
    F, C, T = sizes
    n_dev = T * F * C
    return [T * W // n_dev, T * W // n_dev, T * H // n_dev] + [D // (F * C)] * 6


def front_part(cfg, me, sends, tok, steps, ins, outs, scratch, sems):
    sizes, S, W, H, chunk = cfg
    x_ref, cot_ref, segs_ref, wq_in, wk_in, wv_in, wo_in, up_in, dn_in = ins[:9]
    small_refs = ins[9:18]
    (q_ref, k_ref, v_ref, ah_ref, ar_ref, lse_ref, xf_ref, cf_ref, sf_ref, g1_ref, g2_ref, g3_ref,
     vec_ref, ub_ref) = outs
    zero, zseg, xv, wv, pv, sv, wide, v_t, w1_ref, w2_ref, seg_ref, rows = scratch
    r1, r2, r3, lsem, tss, trs, tls, csem = sems
    C, X, T = me.C, me.X, me.T
    R, D = xv.shape[1:]
    r = wq_in.shape[0]
    L = C * R
    f32, b16 = jnp.float32, jnp.bfloat16
    offs, n_rows = pack([ref.shape[1] for ref in small_refs])
    w1_ref[:, :W] = wq_in[...]
    w1_ref[:, W:2 * W] = wk_in[...]
    w1_ref[:, 2 * W:3 * W] = wv_in[...]
    w2_ref[:, :H] = up_in[...]
    w2_ref[:, H:] = wo_in[...]
    rows[...] = jnp.zeros_like(rows)
    for i, ref in enumerate(small_refs):
        rows[i:i + 1, :ref.shape[1]] = ref[...].astype(f32)
    block = [jnp.zeros((1, VEC), f32) for _ in range(n_rows)]
    for i, off in enumerate(offs):
        one = jnp.broadcast_to(rows[i:i + 1, :], (8, VEC))
        block[off // VEC] += (pltpu.roll(one, off % VEC, 1) if off % VEC else one)[0:1]
    pad = [jnp.zeros((r - n_rows, VEC), f32)] if r > n_rows else []
    w1_ref[:, 3 * W:] = jnp.concatenate(block + pad, axis=0).astype(b16)
    for i in range(S):
        seg_ref[i] = jnp.broadcast_to(segs_ref[i:i + 1, :].astype(f32), (8, R))
    me.greet(True)
    items = [(x_ref, xf_ref, True, tss.at[0], trs.at[0], tls.at[0]),
             (seg_ref, sf_ref, True, tss.at[1], trs.at[1], tls.at[1]),
             (cot_ref, cf_ref, False, tss.at[2], trs.at[2], tls.at[2])]
    idle = jnp.logical_not(tok.busy)
    fills = ([(zero, xf_ref.at[i]) for i in range(C)] + [(zseg, sf_ref.at[i]) for i in range(C)]
             + [(zero, cf_ref.at[i]) for i in range(C // 2)])

    @pl.when(idle)
    def _():
        zero[...] = jnp.zeros_like(zero)
        zseg[...] = jnp.zeros_like(zseg)
        for i, (a, b) in enumerate(fills):
            pltpu.make_async_copy(a, b, tls.at[3 + i]).start()

    for group, w_ref, g_ref, recv, n in (("1", w1_ref, g1_ref, r1, 0), ("2", w2_ref, g2_ref, r2, 1),
                                         ("3", dn_in, g3_ref, r3, 2)):
        for name, step in gather_events(me, w_ref, g_ref, sends, recv, lsem.at[n]).items():
            steps[group + name] = step
    half = L // 2

    def each(f, its):
        return lambda: [f(*it) for it in its]

    for name, its in (("X", items[:2]), ("C", items[2:])):
        steps[name + "o"] = each(tok.out, its)
        steps[name + "w"] = each(tok.out_done, its)
        steps[name + "e"] = each(tok.out_end, its)

    def filled():
        @pl.when(idle)
        def _():
            for i, (a, b) in enumerate(fills):
                pltpu.make_async_copy(a, b, tls.at[3 + i]).wait()
    steps["filled"] = filled

    loads = [(xf_ref, xv), (sf_ref, sv), (g1_ref.at[me.c], wv)]
    blocks = [(t, xx, cc, zz) for t in range(T) for xx in range(X) for cc in range(2) for zz in range(C)]
    if len(g1_ref.shape) == 6:
        pieces = [(g1_ref.at[at + (slice(None), pl.ds(3 * W, VEC))], pv.at[i]) for i, at in enumerate(blocks)]
    else:
        per = len(blocks) // T
        pieces = [(g1_ref.at[i // per, pl.ds(i % per * r, r), pl.ds(3 * W, VEC)], pv.at[i])
                  for i in range(len(blocks))]
    loads = [pltpu.make_async_copy(a, b, csem.at[i]) for i, (a, b) in enumerate(loads + pieces)]

    def load():
        for cp in loads:
            cp.start()
    steps["load"] = load

    def vectors():
        for cp in loads:
            cp.wait()
        blocks = jnp.concatenate([pv[:, i, :] for i in range(n_rows)], axis=1)
        n_dev = blocks.shape[0]
        qw, uw = T * W // n_dev, T * H // n_dev
        qb = spread_pieces(blocks, qw, offs[0], T * W)
        vb = spread_pieces(blocks, qw, offs[1], T * W)
        ub = spread_pieces(blocks, uw, offs[2], T * H)
        for i in range(T * H // chunk):
            ub_ref[i] = ub[:, i * chunk:(i + 1) * chunk]
        once = blocks[:n_dev // T]
        for i in range(6):
            vec_ref[i:i + 1, :] = spread_pieces(once, r, offs[3 + i], D)
        first = me.c == 0
        vec_ref[6:7, :W] = jnp.where(first, qb[:, :W], qb[:, W:])
        vec_ref[7:8, :W] = jnp.where(first, vb[:, :W], vb[:, W:])
    steps["vectors"] = vectors

    def project():
        weights = wv[...].reshape(D, wv.shape[-1])[:, :3 * W]

        def body(i, carry):
            at = pl.ds(pl.multiple_of(i * R, R), R)
            out = nn(xv[i], weights)
            q_ref[at, :] = (out[:, :W] + vec_ref[6:7, :W]).astype(b16)
            k_ref[at, :] = out[:, W:2 * W].astype(b16)
            v_ref[at, :] = (out[:, 2 * W:] + vec_ref[7:8, :W]).astype(b16)
            return carry
        lax.fori_loop(0, C, body, 0)
    steps["project"] = project

    def ready():
        spread_segments(sv, wide)
        for p in range(W // PAIR):
            v_t[p] = v_ref[:, p * PAIR:(p + 1) * PAIR].astype(f32).T.astype(b16)
    steps["ready"] = ready

    def attention(late):
        def body(it, carry):
            p, i = it // C, lax.rem(it, C)
            at = pl.ds(pl.multiple_of(i * R, R), R)
            cols = pl.ds(pl.multiple_of(p * PAIR, PAIR), PAIR)
            o, logs = attend_block(q_ref[at, cols], k_ref[:, cols], v_t[p], sv[i, 0:1, :],
                                   two_lanes(wide[...]))
            ah_ref[at, cols] = o.T.astype(b16)
            lse_ref[p, :, at] = jnp.concatenate(logs + [jnp.zeros((6, R), f32)], axis=0)
            for n, names in enumerate(late):
                if names:
                    @pl.when(it == n)
                    def _():
                        for name in names:
                            steps[name]()
            return carry
        lax.fori_loop(0, W // PAIR * C, body, 0)

    mine = pl.ds(pl.multiple_of(me.c * half, half), half)
    theirs = pl.ds(pl.multiple_of((1 - me.c) * half, half), half)
    heads = pl.ds(pl.multiple_of(me.c * W, W), W)

    def swap():
        sends.go(ah_ref.at[theirs, :], ar_ref.at[:, heads], csem.at[len(loads)], me.dev(c=1 - me.c))
        ar_ref[:, heads] = ah_ref[mine, :]
    steps["swap"] = swap
    steps["attention"] = attention

    def swapped():
        arrived(ar_ref.at[:, heads], csem.at[len(loads)], me)
    steps["swapped"] = swapped


def front_kernel(cfg, *refs):
    sizes, S, W, H, chunk = cfg
    ins, outs, scratch, (ssem, *sems) = refs[:18], refs[18:32], refs[32:44], refs[44:]
    me = Place(sizes)
    sends = Sends(ssem)
    steps = {}
    front_part(cfg, me, sends, Tokens(me, S), steps, ins, outs, scratch, sems)
    early, late, (pre, *_) = ONE_PLAN
    for name in early:
        steps[name]()
    steps["attention"](late)
    steps["swap"]()
    for name in pre[0] + pre[1] + sum(pre[2], ()) + pre[3]:
        steps[name]()
    sends.finish(me)


def front_shapes(cfg, R, D, r, rows):
    sizes, S, W, H, chunk = cfg
    F, C, T = sizes
    X = F // 2
    L = C * R
    n = T * H // chunk
    f32, b = jnp.float32, jnp.bfloat16
    dma = pltpu.SemaphoreType.DMA
    v = pltpu.VMEM
    n1, n2 = 3 * W + VEC, H + W
    full = lambda w: ((T, D, w) if rows else (T, X, 2, C, r, w), b)
    outs = ([((L, W), b)] * 4 + [((L // 2, T * W), b), ((W // PAIR, 8, L), f32)]
            + [((C, R, D), b), ((C // 2, R, D), b), ((C, 8, R), f32), full(n1), full(n2), full(H)]
            + [((8, D), f32), ((n, 1, chunk), f32)])
    scratch = [v((R, D), b), v((8, R), f32), v((C, R, D), b), v((D, n1) if rows else (X, 2, C, r, n1), b),
               v((T * F * C, r, VEC), b), v((C, 8, R), f32), v((L, 128), f32), v((W // PAIR, PAIR, L), b),
               v((r, n1), b), v((r, n2), b), v((S, 8, R), f32), v((16, VEC), f32)]
    sems = [dma((T * F * C,))] * 3 + [dma((3,)), dma((3, S + C // 2)), dma((3, C)), dma((3 + 3 * C,)),
                                      dma((5 + T * F * C,))]
    return outs, scratch, sems, 3 * gather_count(sizes) + 1


def front(cfg, x, cot, segs, weights, small):
    sizes, S, W, H, chunk = cfg
    outs, scratch, sems, count = front_shapes(cfg, x.shape[1], x.shape[2], weights[0].shape[0], False)
    return pl.pallas_call(
        functools.partial(front_kernel, cfg),
        in_specs=[ANY] * 2 + [VM] * (1 + len(weights) + len(small)),
        out_specs=[VM] * 6 + [ANY] * 6 + [VM] * 2,
        out_shape=[jax.ShapeDtypeStruct(*o) for o in outs],
        scratch_shapes=scratch + [pltpu.SemaphoreType.DMA((count,))] + sems,
        compiler_params=pltpu.CompilerParams(collective_id=0, has_side_effects=True,
                                             vmem_limit_bytes=60 * 2**20),
    )(x, cot, segs, *weights, *small)


def take(vec, index, width):
    n = vec.shape[1]
    wide = jnp.broadcast_to(vec, (8, n))
    return pltpu.roll(wide, lax.rem(n - index * width, n), 1)[0:1, :VEC]


def rest_part(cfg, me, sends, tok, steps, plan, ins, outs, scratch, sems):
    sizes, S, W, H, chunk = cfg
    q_ref, k_ref, v_ref, ah_ref, lse_ref, sf_ref, ar_ref, vec_ref, ub_ref, cf_ref, xf_ref, g1_ref, g2_ref, g3_ref = ins
    res_out, ing_out, oq_ref, oup_ref, odn_ref, oo_ref, vs_ref = outs
    (xb, cb, unit, fac, low, low_t, acc, fl, fl_t, hid, act, slope, hl, wbuf, wo, sums, gub, tmp, stage,
     doh, away_o, away_q, got_part, vec, vacc, vgot, soon, sacc, sgot) = scratch[:29]
    bf, bo, bq = scratch[29:36], scratch[36:43], scratch[43:50]
    rf, ro, rq, rv, ru, fc, fs, oc, qc, tss, trs, tls, csem, wsem = sems
    C, X, T = me.C, me.X, me.T
    R, D = xb.shape[1:]
    L = C * R
    half = L // 2
    J = H // chunk
    n = T * J
    r = away_q.shape[3]
    f32, b16 = jnp.float32, jnp.bfloat16
    n_pairs = W // PAIR
    row = lambda i: vec_ref[i:i + 1, :]
    pre_plan, mid_plan, gap_plan, att_plan, end_plan = plan
    other = me.dev(c=1 - me.c)
    mine = pl.ds(pl.multiple_of(me.c * half, half), half)
    theirs = pl.ds(pl.multiple_of((1 - me.c) * half, half), half)
    heads = pl.ds(pl.multiple_of(me.c * W, W), W)

    def which(i):
        return jnp.where(i < J, 1 - me.y, me.y), lax.rem(i, J)

    def fetch(i, slot, kinds=(0, 1)):
        t, j = which(i)
        cols = pl.ds(pl.multiple_of(j * chunk, chunk), chunk)
        return [pltpu.make_async_copy((g2_ref, g3_ref)[kind].at[t, :, cols], wbuf.at[2 * slot + kind],
                                      wsem.at[2 * slot + kind]) for kind in kinds]

    own_rows = pl.ds(me.c * (C // 2), C // 2)
    load_x = [pltpu.make_async_copy(xf_ref.at[own_rows], xb, csem.at[2])]
    load_c = [pltpu.make_async_copy(cf_ref, cb, csem.at[3])]
    load_wo = [pltpu.make_async_copy(g2_ref.at[t, :, pl.ds(H, W)], wo.at[t], csem.at[4 + t]) for t in range(T)]
    for cp in load_x:
        cp.start()
    for name in pre_plan[0]:
        steps[name]()
    for cp in load_wo + fetch(0, 0, (0,)):
        cp.start()

    def put_ff(i, total):
        j, kind = i // 2, i % 2
        (oup_ref, odn_ref)[kind][:, j * chunk:(j + 1) * chunk] = total

    def put_o(i, total):
        oo_ref[...] = total

    def put_q(i, total):
        oq_ref[...] = total

    acc_f, rc_f = bf[:2]
    acc_o, rc_o = bo[:2]
    acc_q = bq[0]

    def parts_f(t, x):
        return [(rc_f.at[t, x, pl.ds(2 * j, 2)], fc.at[(t * X + x) * J + j]) for j in range(J)]

    def parts_o(t, x):
        return [(rc_o.at[t, x], oc.at[t * X + x])]

    def parts_q(t, x):
        return [(acc_q.at[t, x], qc.at[x])]

    def deal(cols, own_to, away_to):
        rows = C * r
        for x in range(X):
            own = pl.ds(pl.multiple_of((2 * x + me.c) * rows, r), rows)
            away = pl.ds(pl.multiple_of((2 * x + 1 - me.c) * rows, r), rows)
            own_to(x, tmp[own, :cols].reshape(C, r, cols))
            away_to(x, tmp[away, :cols].reshape(C, r, cols))

    def store(ref, *index):
        def put(x, block):
            ref[tuple(x if i is None else i for i in index)] = block
        return put

    for name, group in (("f", reduce_events(me, False, bf, sends, rf, put_ff, parts_f)),
                        ("o", reduce_events(me, False, bo, sends, ro, put_o, parts_o)),
                        ("q", reduce_events(me, True, bq, sends, rq, put_q, parts_q)),
                        ("t", total_events(me, vec, (vacc, vgot), vec, sends, rv)),
                        ("u", total_events(me, soon, (sacc, sgot), soon, sends, ru))):
        for key, step in group.items():
            steps[name + key] = step
    for name, item in (("R", (xb, res_out, tss.at[0], trs.at[0], tls.at[0])),
                       ("I", (cb, ing_out, tss.at[1], trs.at[1], tls.at[1]))):
        steps[name + "o"] = lambda item=item: tok.back(*item)
        for p in range(S * CUT):
            steps[name + str(p)] = lambda item=item, p=p: tok.back_pass(p % S, p // S, *item)
        steps[name + "e"] = lambda item=item: tok.back_end(*item)

    def at_step(i, plan):
        for m, names in enumerate(plan):
            if names:
                @pl.when(i == m)
                def _():
                    for name in names:
                        steps[name]()

    def strips(body):
        per = R // STRIP

        def step(i, carry):
            at = pl.ds(pl.multiple_of(i * STRIP, STRIP), STRIP)
            body(at, (i // per, pl.ds(pl.multiple_of(lax.rem(i, per) * STRIP, STRIP), STRIP)))
            return carry
        lax.fori_loop(0, half // STRIP, step, 0)

    for cp in load_x + load_wo:
        cp.wait()
    for t in range(T):
        part = nt(ar_ref[:, t * W:(t + 1) * W], wo[t])
        acc[...] = part if t == 0 else acc[...] + part

    def first_norm(at, qat):
        u, factor = unit_of(xb[qat].astype(f32) + acc[at, :] + row(0))
        unit[at, :] = u
        fac[at, :] = jnp.broadcast_to(factor, (STRIP, 128))
        low[at, :] = (u * row(2) + row(3)).astype(b16)
        acc[at, :] = jnp.zeros((STRIP, D), f32)
    strips(first_norm)
    flip(low, low_t)

    for name in pre_plan[1]:
        steps[name]()

    def up(i, carry):
        slot = lax.rem(i, 2)
        t, j = which(i)
        for cp in fetch(i, slot, (0,)):
            cp.wait()

        @pl.when(i + 1 < n)
        def _():
            for cp in fetch(i + 1, 1 - slot, (0,)):
                cp.start()
        hid[...] = nn(low[...], wbuf[2 * slot])
        bias = ub_ref[t * J + j]
        base = i * half

        def units(at, qat):
            h = hid[at, :] + bias
            phi = 0.5 + 0.5 * lax.erf(h * (0.5 ** 0.5))
            dens = jnp.exp(-0.5 * h * h) * 0.3989422804014327
            to = pl.ds(pl.multiple_of(base + at.start, STRIP), STRIP)
            act[to, :] = (h * phi).astype(b16)
            slope[to, :] = (phi + h * dens).astype(b16)
        strips(units)
        at_step(i, pre_plan[2])
        return carry
    lax.fori_loop(0, n, up, 0)
    for name in pre_plan[3]:
        steps[name]()
    for cp in load_c + fetch(0, 0, (1,)):
        cp.start()

    def down(i, carry):
        slot = lax.rem(i, 2)
        for cp in fetch(i, slot, (1,)):
            cp.wait()

        @pl.when(i + 1 < n)
        def _():
            for cp in fetch(i + 1, 1 - slot, (1,)):
                cp.start()
        acc[...] += nt(act[pl.ds(pl.multiple_of(i * half, half), half), :], wbuf[2 * slot + 1])
        return carry
    lax.fori_loop(0, n, down, 0)
    for cp in fetch(0, 0):
        cp.start()
    for cp in load_c:
        cp.wait()

    sums[...] = jnp.zeros_like(sums)

    def second_norm(at, qat):
        u, factor = unit_of(unit[at, :] * row(2) + row(3) + acc[at, :] + row(1))
        g = cb[qat].astype(f32)
        xb[qat] = (u * row(4) + row(5)).astype(b16)
        g2 = back_of(g, u, factor, row(4))
        l2 = g2.astype(b16)
        fl[at, :] = l2
        acc[at, :] = g2
        sums[1] += fold(l2.astype(f32))
        sums[4] += fold(g * u)
        sums[5] += fold(g)
    strips(second_norm)
    flip(fl, fl_t)
    steps["Ro"]()

    def stage_copy(i, x):
        t, j = which(i)
        slot = lax.rem(i, 2)
        return pltpu.make_async_remote_copy(
            src_ref=stage.at[slot, x], dst_ref=rc_f.at[t, x, pl.ds(2 * j, 2)], send_sem=fs.at[slot * X + x],
            recv_sem=fc.at[(t * X + x) * J + j], device_id=other, device_id_type=MESH)

    def backward(i, carry):
        slot = lax.rem(i, 2)
        t, j = which(i)
        for cp in fetch(i, slot):
            cp.wait()

        @pl.when(i + 1 < n)
        def _():
            for cp in fetch(i + 1, 1 - slot):
                cp.start()
        hid[...] = nn(fl[...], wbuf[2 * slot + 1])
        base = i * half
        gub[t * J + j] = jnp.zeros_like(gub[0])

        def units(at, qat):
            to = pl.ds(pl.multiple_of(base + at.start, STRIP), STRIP)
            v = (hid[at, :] * slope[to, :].astype(f32)).astype(b16)
            hl[at, :] = v
            gub[t * J + j] += fold(v.astype(f32))
        strips(units)

        @pl.when(i >= 2)
        def _():
            for x in range(X):
                stage_copy(i, x).wait_send()
        for kind in range(2):
            if kind == 0:
                tmp[...] = nn(low_t[...], hl[...]).astype(b16)
            else:
                tmp[...] = nn(fl_t[...], act[pl.ds(pl.multiple_of(base, half), half), :]).astype(b16)
            deal(chunk, store(acc_f, t, None, 2 * j + kind), store(stage, slot, None, kind))
        for x in range(X):
            stage_copy(i, x).start()
        acc[...] += nt(hl[...], wbuf[2 * slot])
        at_step(i, mid_plan)
        return carry
    lax.fori_loop(0, n, backward, 0)

    def first_back(at, qat):
        g = acc[at, :]
        u = unit[at, :]
        g1 = back_of(g, u, fac[at, 0:1], row(2))
        acc[at, :] = g1
        l1 = g1.astype(b16)
        fl[at, :] = l1
        sums[0] += fold(l1.astype(f32))
        sums[2] += fold(g * u)
        sums[3] += fold(g)
    strips(first_back)
    hl[:, :W] = nn(fl[...], wo[1 - me.c]).astype(b16)
    sends.go(hl.at[:, pl.ds(0, W)], doh.at[mine, :], csem.at[0], other)
    doh[mine, :] = nn(fl[...], wo[me.c]).astype(b16)
    flip(fl, fl_t)
    for t in range(T):
        tmp[:, :W] = nn(fl_t[...], ar_ref[:, t * W:(t + 1) * W]).astype(b16)
        deal(W, store(acc_o, t, None, 0), store(away_o, t, None, 0))
        for x in range(X):
            sends.go(away_o.at[t, x], rc_o.at[t, x], oc.at[t * X + x], other)
    for i in (n - 2, n - 1):
        for x in range(X):
            stage_copy(i, x).wait_send()
    turn = [pltpu.make_async_copy(g1_ref.at[me.c, :, pl.ds(m * W, W)], wbuf.at[m, :, pl.ds(0, W)], wsem.at[m])
            for m in range(3)]
    for cp in turn:
        cp.start()
    for h in range(2):
        for i in range(0, half, 128):
            a, b = (h * half + i) // R, (h * half + i) % R
            unit[i:i + 128, (4 + h) * PAIR:(5 + h) * PAIR] = jnp.broadcast_to(sf_ref[a, 0:1, b:b + 128], (128, 128)).T
        for p in range(n_pairs):
            low_t[(2 * p + h) * PAIR:(2 * p + h + 1) * PAIR, :] = (
                k_ref[h * half:(h + 1) * half, p * PAIR:(p + 1) * PAIR].astype(f32).T.astype(b16))
    def tokens(h):
        return [pltpu.make_async_copy(xf_ref.at[h * (C // 2) + i], low.at[pl.ds(i * R, R), :], csem.at[2 + i])
                for i in range(C // 2)]

    def turn_tokens(h):
        def run():
            for cp in tokens(h):
                cp.wait()
            for i in range(0, half, 128):
                at = h * half + i
                act[at // chunk * D:(at // chunk + 1) * D, at % chunk:at % chunk + 128] = (
                    low[i:i + 128, :].astype(f32).T.astype(b16))
            if h == 0:
                for cp in tokens(1):
                    cp.start()
        return run
    steps["x0"] = turn_tokens(0)
    steps["x1"] = turn_tokens(1)
    for cp in tokens(0):
        cp.start()

    def projections():
        for m in range(3):
            out = None
            for h in range(L // chunk):
                term = nn(act[h * D:(h + 1) * D, :], slope[m * L + h * chunk:m * L + (h + 1) * chunk, :W])
                out = term if out is None else out + term
            tmp[:, :W] = out.astype(b16)
            cols = slice(m * W, (m + 1) * W)
            every = slice(None)
            deal(W, store(acc_q, me.c, None, 0, every, every, cols), store(away_q, None, 0, every, every, cols))
        for x in range(X):
            sends.go(away_q.at[x], acc_q.at[me.c, x], qc.at[x], other)
    steps["gq"] = projections

    def back_project(who):
        out = None
        for m in range(3):
            rows = pl.ds(pl.multiple_of(m * L + who * half, half), half)
            term = nt(slope[rows, :W], wbuf[m, :, :W])
            out = term if out is None else out + term
        return out

    def give():
        for cp in turn:
            cp.wait()
        fl[...] = back_project(1 - me.c).astype(b16)
        sends.go(fl, got_part, csem.at[1], other)
    steps["give"] = give

    def keep():
        acc[...] += back_project(me.c)
    steps["keep"] = keep

    def join():
        arrived(got_part, csem.at[1], me)
        for i in range(C // 2):
            at = slice(i * R, (i + 1) * R)
            cb[i] = (acc[at, :] + got_part[at, :].astype(f32)).astype(b16)
    steps["join"] = join
    n_late, n_soon = 2 * T * W, T * H + 6 * D

    def lay(ref, flat, count):
        flat = jnp.concatenate(flat, axis=1)
        for i in range(count // 128):
            ref[i:i + 1, :] = flat[:, i * 128:(i + 1) * 128]
        if ref.shape[0] * 128 > count:
            ref[count // 128:, :] = jnp.zeros((ref.shape[0] - count // 128, 128), f32)

    def early_sums():
        lay(soon, [jnp.sum(gub[i], axis=0, keepdims=True) for i in range(n)]
            + [jnp.sum(sums[i], axis=0, keepdims=True) for i in range(6)], n_soon)
    steps["usums"] = early_sums

    def token_sums():
        zeros = jnp.zeros((1, W), f32)
        ones = jnp.ones((8, L), b16)
        first = me.c == 0
        flat = []
        for m in (0, 2):
            v = nn(ones, slope[m * L:(m + 1) * L, :W])[0:1]
            flat += [jnp.where(first, v, zeros), jnp.where(first, zeros, v)]
        lay(vec, flat, n_late)
    steps["sums"] = token_sums

    def vectors():
        fz = (2 * me.x + me.c) * C + me.z
        tfz = me.y * (X * 2 * C) + fz
        n_dev = T * X * 2 * C
        qw, uw = T * W // n_dev, T * H // n_dev
        out = 0
        for ref, count, kinds in ((vec, n_late, [(T * W, qw, tfz)] * 2),
                                  (soon, n_soon, [(T * H, uw, tfz)] + [(D, r, fz)] * 6)):
            total = jnp.concatenate([ref[i:i + 1, :] for i in range(count // 128)], axis=1)
            at = 0
            for m, w, here in kinds:
                vs_ref[out:out + 1, :] = take(total[:, at:at + m], here, w)
                at += m
                out += 1
    steps["pieces"] = vectors
    for name in gap_plan:
        steps[name]()
    arrived(doh.at[theirs, :], csem.at[0], me)

    def attention(it, carry):
        p, i = it // C, lax.rem(it, C)
        at = pl.ds(pl.multiple_of(i * R, R), R)
        cols = pl.ds(pl.multiple_of(p * PAIR, PAIR), PAIR)
        wide = jnp.concatenate([unit[:, (4 + h) * PAIR:(5 + h) * PAIR] for h in range(2)], axis=0)
        k_t = jnp.concatenate([low_t[pl.ds(pl.multiple_of((2 * p + h) * PAIR, PAIR), PAIR), :] for h in range(2)],
                              axis=1)
        dq, dk, dv = attend_back_block(q_ref[at, cols], k_ref[:, cols], k_t, v_ref[:, cols], doh[at, cols],
                                       ah_ref[at, cols], lse_ref[p, :, at], sf_ref[i, 0:1, :], two_lanes(wide))
        slope[at, cols] = dq.astype(b16)
        lanes = [slice(m * PAIR, (m + 1) * PAIR) for m in range(4)]
        halves = [dk[:half], dk[half:], dv[:half], dv[half:]]

        @pl.when(i == 0)
        def _():
            for m in range(4):
                unit[:, lanes[m]] = halves[m]

        @pl.when(i > 0)
        def _():
            for m in range(4):
                unit[:, lanes[m]] += halves[m]

        @pl.when(i == C - 1)
        def _():
            for m in range(4):
                slope[L + m * half:L + (m + 1) * half, cols] = unit[:, lanes[m]].astype(b16)

        at_step(it, att_plan)
        return carry
    lax.fori_loop(0, n_pairs * C, attention, 0)

    for name in end_plan:
        steps[name]()


def rest_kernel(cfg, *refs):
    sizes, S, W, H, chunk = cfg
    ins, outs, scratch, (ssem, *sems) = refs[:14], refs[14:21], refs[21:71], refs[71:]
    me = Place(sizes)
    me.greet(True)
    sends = Sends(ssem)
    none = ((), (), (), ())
    rest_part(cfg, me, sends, Tokens(me, S), {}, (none,) + ONE_PLAN[2][1:], ins, outs, scratch, sems)
    sends.finish(me)


def rest_shapes(cfg, R, D, r):
    sizes, S, W, H, chunk = cfg
    F, C, T = sizes
    X = F // 2
    L = C * R
    half = L // 2
    J = H // chunk
    n = T * J
    f32, b = jnp.float32, jnp.bfloat16
    dma = pltpu.SemaphoreType.DMA
    vm = pltpu.VMEM
    steps = total_count(sizes)
    n_vec = -(-2 * T * W // 1024) * 8
    n_soon = -(-(T * H + 6 * D) // 1024) * 8
    sems = reduce_sems(sizes)
    tall = max(n * half, 3 * L, L // chunk * D)
    outs = [((S, R, D), b), ((S, R, D), b), ((r, 3 * W), f32), ((r, H), f32), ((r, H), f32), ((r, W), f32),
            ((16, VEC), f32)]
    scratch = [vm((C // 2, R, D), b), vm((C // 2, R, D), b), vm((half, D), f32), vm((half, 128), f32),
               vm((half, D), b), vm((D, half), b), vm((half, D), f32), vm((half, D), b), vm((D, half), b),
               vm((half, chunk), f32), vm((tall, chunk), b), vm((tall, chunk), b), vm((half, chunk), b),
               vm((4, D, chunk), b), vm((T, D, W), b), vm((6, 8, D), f32), vm((n, 8, chunk), f32),
               vm((D, chunk), b), vm((2, X, 2, C, r, chunk), b),
               vm((L, W), b), vm((T, X, 1, C, r, W), b), vm((X, 1, C, r, 3 * W), b), vm((half, D), b),
               vm((n_vec, 128), f32), vm((4, n_vec, 128), f32), vm((steps, n_vec, 128), f32),
               vm((n_soon, 128), f32), vm((4, n_soon, 128), f32), vm((steps, n_soon, 128), f32)]
    scratch += (reduce_scratch(sizes, 2 * J, r, chunk, False) + reduce_scratch(sizes, 1, r, W, False)
                + reduce_scratch(sizes, 1, r, 3 * W, True))
    semas = [dma((sems,)), dma((sems,)), dma((sems,)), dma((steps,)), dma((steps,)), dma((T * X * J,)),
             dma((2 * X,)), dma((T * X,)), dma((X,)), dma((2, (C // 2 + S) * CUT)), dma((2, S * CUT)), dma((2,)),
             dma((4 + T + C,)), dma((4,))]
    return outs, scratch, semas, 3 * reduce_count(sizes) + T * X + X + 2 * steps + 2


def rest(cfg, q, k, v, ah, lse, sf, ar, vec, ub, cf, xf, g1, g2, g3):
    F, C, T = cfg[0]
    _, R, D = xf.shape
    outs, scratch, sems, count = rest_shapes(cfg, R, D, D // (F * C))
    return pl.pallas_call(
        functools.partial(rest_kernel, cfg),
        in_specs=[VM] * 9 + [ANY] * 5,
        out_specs=[ANY] * 2 + [VM] * 5,
        out_shape=[jax.ShapeDtypeStruct(*o) for o in outs],
        scratch_shapes=scratch + [pltpu.SemaphoreType.DMA((count,))] + sems,
        compiler_params=pltpu.CompilerParams(collective_id=1, has_side_effects=True,
                                             vmem_limit_bytes=60 * 2**20 + 512 * 2**10),
    )(q, k, v, ah, lse, sf, ar, vec, ub, cf, xf, g1, g2, g3)


ONE_PLAN = (
    ('1a0', '2a0', '1a1', '1a2', '1a3', 'Xo', '2a1', '1x0', '1x1', '1x2', '1x3', '2x0', '2x1', '1c0', '1c1',
     '1c2', '1c3', '2a2', '1l', 'Xw', '3a0', 'filled', 'Xe', 'load', 'vectors', 'project', '2a3', 'ready'),
    ((), ('2x2',), (), (), ('3x0',), ('2x3', '2c0', '2c1', '3a1'), (), ('3a2',), ('2c2',), ('3a3',), ('2c3',
     '3x1'), ()),
    ((('Co', '3c0', '2l', 'swapped'), ('3x2',), ((), ('3x3',), (), (), ('3c1', '3c2', '3c3'), ('Cw',)), ('Ce',
     '3l')), ((), (), (), ('fc', 'fd2', 'fd3'), ('fd1', 'fd0'), ('fa',)), ('fy2',), (('fb',), ('fo', 'fw3'),
     ('fy3',), (), (), ('fy1',), ('fw0',), ('fz3',), (), ('fy0',), (), ()), ('give', 'fw2', 'oc', 'od0', 'x0',
     'keep', 'join', 'Io', 'R0', 'R1', 'R2', 'x1', 'R3', 'gq', 'qc', 'qd0', 'qd1', 'usums', 'fz2', 'qd2',
     'od3', 'u0', 'u1', 'qa', 'qy2', 'qd3', 'qy0', 'oa', 'qb', 'qw1', 'qo', 'fz0', 'qw3', 'I0', 'ob', 'oy0',
     'fw1', 'sums', 't0', 't1', 'qy1', 'I1', 'qw0', 'qw2', 'fz1', 'I2', 'I3', 'u2', 'qy3', 'u3', 'qz3', 'I4',
     'ow1', 'od2', 't2', 'R4', 'oy2', 'oy3', 'qz2', 'I5', 'fl', 'ow2', 'od1', 'qz1', 'ow0', 't3', 'ow3', 'u4',
     'oy1', 'R5', 'oo', 'oz3', 'oz0', 'oz1', 'oz2', 'qz0', 'Ie', 'Re', 't4', 'pieces', 'ql', 'ol')),
)


def layer_kernel(cfg, *refs):
    sizes, S, W, H, chunk = cfg
    refs = list(refs)
    take_refs = lambda n: [refs.pop(0) for _ in range(n)]
    ins, moved, results = take_refs(18), take_refs(6), take_refs(7)
    kept, front_scratch, rest_scratch, ssem = take_refs(8), take_refs(12), take_refs(50), take_refs(1)[0]
    front_sems, rest_sems = take_refs(8), take_refs(14)
    me = Place(sizes)
    sends = Sends(ssem)
    tok = Tokens(me, S)
    steps = {}
    q, k, v, ah, ar, lse, vec, ub = kept
    xf, cf, sf, g1, g2, g3 = moved
    outs = [q, k, v, ah, ar, lse] + moved + [vec, ub]
    front_part(cfg, me, sends, tok, steps, ins, outs, front_scratch, front_sems)
    early, late, plan = ONE_PLAN
    for name in early:
        steps[name]()
    steps["attention"](late)
    steps["swap"]()
    rest_part(cfg, me, sends, tok, steps, plan, [q, k, v, ah, lse, front_scratch[5], ar, vec, ub, cf, xf, g1, g2, g3],
              results, rest_scratch, rest_sems)
    sends.finish(me)


def layer(cfg, x, cot, segs, weights, small):
    sizes, S, W, H, chunk = cfg
    _, R, D = x.shape
    r = weights[0].shape[0]
    front_outs, front_scratch, front_sems, n_front = front_shapes(cfg, R, D, r, True)
    outs, scratch, sems, n_rest = rest_shapes(cfg, R, D, r)
    moved = front_outs[6:12]
    kept = [pltpu.VMEM(*o) for o in front_outs[:6] + front_outs[12:]]
    return pl.pallas_call(
        functools.partial(layer_kernel, cfg),
        in_specs=[ANY] * 2 + [VM] * (1 + len(weights) + len(small)),
        out_specs=[ANY] * 6 + [ANY] * 2 + [VM] * 5,
        out_shape=[jax.ShapeDtypeStruct(*o) for o in moved + outs],
        scratch_shapes=kept + front_scratch + scratch + [pltpu.SemaphoreType.DMA((n_front + n_rest,))]
        + front_sems + sems,
        compiler_params=pltpu.CompilerParams(collective_id=0, has_side_effects=True,
                                             vmem_limit_bytes=62 * 2**20),
    )(x, cot, segs, *weights, *small)[6:]


def finish_kernel(W, res_in, ing_in, oq_in, oup_in, odn_in, oo_in, vs_in,
                  res, ing, oq, ok, ov, oo, oup, odn, *small):
    res[...] = res_in[...]
    ing[...] = ing_in[...].astype(jnp.float32)

    @pl.when(pl.program_id(0) == 0)
    def _():
        oq[...] = oq_in[:, :W]
        ok[...] = oq_in[:, W:2 * W]
        ov[...] = oq_in[:, 2 * W:]
        oup[...] = oup_in[...]
        oo[...] = oo_in[...]
        odn[...] = odn_in[...]
        for i, ref in enumerate(small):
            ref[...] = vs_in[i:i + 1, :ref.shape[1]]


def finish(cfg, widths, *arrays):
    sizes, S, W, H, chunk = cfg
    res, ing, oq = arrays[:3]
    r = oq.shape[0]
    R, D = res.shape[1:]
    f32 = jnp.float32
    token = pl.BlockSpec((1, R, D), lambda i: (i, 0, 0))
    whole = lambda shape: pl.BlockSpec(shape, lambda i: (0,) * len(shape))
    shapes = [(r, W)] * 4 + [(r, H), (r, H)] + [(1, w) for w in widths]
    return pl.pallas_call(
        functools.partial(finish_kernel, W),
        grid=(S,),
        in_specs=[token, token] + [whole(a.shape) for a in arrays[2:]],
        out_specs=[token, token] + [whole(shape) for shape in shapes],
        out_shape=[jax.ShapeDtypeStruct((S, R, D), jnp.bfloat16), jax.ShapeDtypeStruct((S, R, D), f32)]
        + [jax.ShapeDtypeStruct(shape, f32) for shape in shapes],
        compiler_params=pltpu.CompilerParams(vmem_limit_bytes=62 * 2**20),
    )(*arrays)


def chunk_of(H):
    for w in (512, 384, 256, 128):
        if H % w == 0:
            return w
    return H


def on_device(sizes, inputs, segments, cotangent, query_weight, key_weight, value_weight,
              output_weight, up_weight, down_weight, *small):
    F, C, T = sizes
    X = F // 2
    S, R, D = inputs.shape
    W = query_weight.shape[1]
    H = up_weight.shape[1]
    r = query_weight.shape[0]
    chunk = chunk_of(H)
    cfg = (sizes, S, W, H, chunk)
    weights = (query_weight, key_weight, value_weight, output_weight.T, up_weight, down_weight.T)
    widths = [v.shape[0] for v in small]
    small = [v.reshape(1, -1) for v in small]
    if r % 16 == 0:
        landed = layer(cfg, inputs, cotangent, segments, weights, small)
    else:
        q, k, v, ah, ar, lse, xf, cf, sf, g1, g2, g3, vec, ub = front(
            cfg, inputs, cotangent, segments, weights, small)
        landed = rest(cfg, q, k, v, ah, lse, sf, ar, vec, ub, cf, xf,
                      g1.reshape(T, D, -1), g2.reshape(T, D, -1), g3.reshape(T, D, -1))
    outs = finish(cfg, widths, *landed)
    return tuple(outs[:5]) + (outs[5].T, outs[6], outs[7].T) + tuple(v.reshape(-1) for v in outs[8:])


def solution(mesh):
    sizes = (mesh.shape["fsdp"], mesh.shape["ctx"], mesh.shape["tp"])
    every = ("fsdp", "ctx")
    rows, cols, one, three = P(every, "tp"), P("tp", every), P(every), P(("tp",) + every)
    token = P("fsdp", "ctx", None)
    weights = (rows, rows, rows, cols, rows, cols)
    vectors = (three, three, three) + (one,) * 6
    return jax.shard_map(
        functools.partial(on_device, sizes), mesh=mesh,
        in_specs=(token, P("fsdp", "ctx"), token) + weights + vectors,
        out_specs=(token, token) + weights + vectors, check_vma=False)
```

```python
import functools
import jax
import jax.numpy as jnp
from jax import lax
from jax.sharding import PartitionSpec as P
from jax.experimental import pallas as pl
from jax.experimental.pallas import tpu as pltpu

MESH = pl.DeviceIdType.MESH
ANY = pl.BlockSpec(memory_space=pl.ANY)
VM = pl.BlockSpec(memory_space=pltpu.VMEM)


class Place:
    def __init__(self, sizes):
        self.F, self.C, self.T = sizes
        self.X = self.F // 2
        f = lax.axis_index("fsdp")
        self.x = f // 2
        self.c = lax.rem(f, 2)
        self.z = lax.axis_index("ctx")
        self.y = lax.axis_index("tp")

    def dev(self, x=None, c=None, z=None, y=None):
        x = self.x if x is None else x
        c = self.c if c is None else c
        return (2 * x + c, self.z if z is None else z, self.y if y is None else y)

    def z_off(self, d):
        return lax.rem(self.z + d + self.C, self.C)

    def x_off(self, d):
        return lax.rem(self.x + d + self.X, self.X)

    def greet(self, chip_wide):
        bar = pltpu.get_barrier_semaphore()
        devs = [self.dev(c=1 - self.c), self.dev(y=1 - self.y)]
        devs += [self.dev(x=self.x_off(d)) for d in range(1, self.X)]
        for d in range(1, self.C):
            devs.append(self.dev(z=self.z_off(d)))
            if chip_wide:
                devs.append(self.dev(z=self.z_off(d), c=1 - self.c))
        for d in devs:
            pl.semaphore_signal(bar, inc=1, device_id=d, device_id_type=MESH)
        pl.semaphore_wait(bar, len(devs))


class Sends:
    def __init__(self, sems):
        self.sems, self.n, self.waits = sems, 0, []

    def go(self, src, dst, recv, dev, like=None, when=None):
        pltpu.make_async_remote_copy(
            src_ref=src, dst_ref=dst, send_sem=self.sems.at[self.n], recv_sem=recv,
            device_id=dev, device_id_type=MESH).start()
        self.n += 1
        self.waits.append((src if like is None else like, when))

    def finish(self, me):
        for n, (like, when) in enumerate(self.waits):
            def wait():
                pltpu.make_async_remote_copy(
                    src_ref=like, dst_ref=like, send_sem=self.sems.at[n], recv_sem=self.sems.at[n],
                    device_id=me.dev(c=1 - me.c), device_id_type=MESH).wait_send()
            given(when, wait)
        self.waits = []


def given(when, body):
    if when is None:
        body()
    else:
        pl.when(when())(body)


def arrived(dst, recv, pl_):
    pltpu.make_async_remote_copy(
        src_ref=dst, dst_ref=dst, send_sem=recv, recv_sem=recv,
        device_id=pl_.dev(c=1 - pl_.c), device_id_type=MESH).wait_recv()


def line_order(C, z):
    return [z] + [z + sign * k for k in range(1, C) for sign in (-1, 1) if 0 <= z + sign * k < C]


def pick(index, table):
    out = table[-1]
    for i in reversed(range(len(table) - 1)):
        out = jnp.where(index == i, table[i], out)
    return jnp.int32(out)


def gather_events(me, own, full, sends, recv, lsem):
    C, X = me.C, me.X
    sem = lambda t, x, c, z: recv.at[((t * X + x) * 2 + c) * C + z]
    r = own.shape[0]

    def slot(t, x, c, z):
        if len(full.shape) == 6:
            return full.at[t, x, c, z]
        row = ((x * 2 + c) * C + z) * r
        return full.at[t, pl.ds(row if isinstance(row, int) else pl.multiple_of(row, r), r), :]

    like = slot(0, 0, 0, 0)
    orders = [line_order(C, z) for z in range(C)]
    where = lambda m: pick(me.z, [o[m] for o in orders])

    def push(src, at, dev, when=None):
        sends.go(src, slot(*at), sem(*at), dev, like, when)

    def wait(at):
        arrived(slot(*at), sem(*at), me)

    core, side = me.dev(c=1 - me.c), me.dev(y=1 - me.y)
    xs = [(me.x_off(d), me.dev(x=me.x_off(d))) for d in range(1, X)]
    local = pltpu.make_async_copy(own, slot(me.y, me.x, me.c, me.z), lsem)

    def along(m):
        def run():
            zz = where(m)
            at = (me.y, me.x, me.c, zz)
            src = slot(*at) if m else own
            if m:
                wait(at)
            for sign in (-1, 1):
                def onward(sign=sign):
                    zz = where(m)
                    return ((zz - me.z) * sign <= 0) & (me.z + sign >= 0) & (me.z + sign < C)

                @pl.when(onward())
                def _():
                    push(src, at, me.dev(z=me.z + sign), onward)
            for _, dev in xs:
                push(src, at, dev)
            push(src, at, side)
            push(src, at, core)
            if not m:
                local.start()
        return run

    def across(m):
        def run():
            zz = where(m)
            at = (1 - me.y, me.x, me.c, zz)
            wait(at)
            if m < C // 2:
                for _, dev in xs:
                    push(slot(*at), at, dev)
            push(slot(*at), at, core)
            for xo, _ in xs:
                at = (me.y, xo, me.c, zz)
                wait(at)
                if m >= C // 2:
                    push(slot(*at), at, side)
                push(slot(*at), at, core)
        return run

    def corner(m):
        def run():
            zz = where(m)
            for xo, _ in xs:
                at = (1 - me.y, xo, me.c, zz)
                wait(at)
                push(slot(*at), at, core)
        return run

    def last():
        for t in range(me.T):
            for xx in range(X):
                for zz in range(C):
                    wait((t, xx, 1 - me.c, zz))
        local.wait()

    steps = {"l": last}
    for m in range(C):
        steps["a%d" % m] = along(m)
        steps["x%d" % m] = across(m)
        steps["c%d" % m] = corner(m)
    return steps


def gather_count(sizes):
    F, C, T = sizes
    X = F // 2
    return C * (4 * X + 4)


CUT = 2


class Tokens:
    def __init__(self, me, seqs):
        self.me, self.S = me, seqs
        self.half = me.C // 2
        self.lo = me.y * (me.C - seqs)
        self.busy = (me.z >= self.lo) & (me.z < self.lo + seqs)
        self.owner = me.c == me.y

    def out(self, src, dst, full, ssem, rsem, lsem):
        me, half = self.me, self.half
        k = me.z // half
        at = me.z if full else lax.rem(me.z, half)

        @pl.when(self.owner)
        def _():
            for s in range(self.S):
                here = (self.lo + s == me.z) & (k == me.c)

                @pl.when(here)
                def _():
                    pltpu.make_async_copy(src.at[s], dst.at[at], lsem).start()

                @pl.when(jnp.logical_not(here))
                def _():
                    pltpu.make_async_remote_copy(
                        src_ref=src.at[s], dst_ref=dst.at[at], send_sem=ssem.at[s],
                        recv_sem=rsem.at[lax.rem(me.z, half)],
                        device_id=me.dev(c=k, z=self.lo + s), device_id_type=MESH).start()

    def out_done(self, src, dst, full, ssem, rsem, lsem):
        me, half = self.me, self.half

        @pl.when(self.busy)
        def _():
            for i in range(half):
                zq = me.c * half + i
                at = zq if full else i
                here = (zq == me.z) & (me.c == me.y)

                @pl.when(here)
                def _():
                    pltpu.make_async_copy(src.at[0], dst.at[at], lsem).wait()

                @pl.when(jnp.logical_not(here))
                def _():
                    arrived(dst.at[at], rsem.at[i], me)

                if full:
                    pltpu.make_async_remote_copy(
                        src_ref=dst.at[at], dst_ref=dst.at[at], send_sem=ssem.at[self.S + i],
                        recv_sem=rsem.at[half + i], device_id=me.dev(c=1 - me.c),
                        device_id_type=MESH).start()

    def out_end(self, src, dst, full, ssem, rsem, lsem):
        me, half = self.me, self.half
        k = me.z // half

        @pl.when(self.owner)
        def _():
            for s in range(self.S):
                here = (self.lo + s == me.z) & (k == me.c)

                @pl.when(jnp.logical_not(here))
                def _():
                    pltpu.make_async_remote_copy(
                        src_ref=src.at[s], dst_ref=dst.at[0], send_sem=ssem.at[s],
                        recv_sem=rsem.at[0], device_id=me.dev(c=1 - me.c),
                        device_id_type=MESH).wait_send()

        if full:
            @pl.when(self.busy)
            def _():
                for i in range(half):
                    zq = (1 - me.c) * half + i
                    arrived(dst.at[zq], rsem.at[half + i], me)
                    pltpu.make_async_remote_copy(
                        src_ref=dst.at[0], dst_ref=dst.at[0], send_sem=ssem.at[self.S + i],
                        recv_sem=rsem.at[0], device_id=me.dev(c=1 - me.c),
                        device_id_type=MESH).wait_send()

    def back(self, src, dst, ssem, rsem, lsem):
        me, half = self.me, self.half
        size = src.shape[1] // CUT

        @pl.when(self.busy)
        def _():
            at = me.z - self.lo
            for h in range(CUT):
                piece = pl.ds(h * size, size)
                for i in range(half):
                    zq = me.c * half + i
                    here = (zq == me.z) & (me.c == me.y)

                    @pl.when(here)
                    def _():
                        if h == 0:
                            pltpu.make_async_copy(src.at[i], dst.at[at], lsem).start()

                    @pl.when(jnp.logical_not(here))
                    def _():
                        pltpu.make_async_remote_copy(
                            src_ref=src.at[i, piece], dst_ref=dst.at[at, piece], send_sem=ssem.at[i * CUT + h],
                            recv_sem=rsem.at[at * CUT + h], device_id=me.dev(c=me.y, z=zq),
                            device_id_type=MESH).start()

    def back_pass(self, s, h, src, dst, ssem, rsem, lsem):
        me, half = self.me, self.half
        size = src.shape[1] // CUT
        piece = pl.ds(h * size, size)

        @pl.when(self.owner)
        def _():
            here = (self.lo + s == me.z) & (me.z // half == me.c)

            @pl.when(here)
            def _():
                if h == 0:
                    pltpu.make_async_copy(src.at[0], dst.at[s], lsem).wait()

            @pl.when(jnp.logical_not(here))
            def _():
                arrived(dst.at[s, piece], rsem.at[s * CUT + h], me)

            pltpu.make_async_remote_copy(
                src_ref=dst.at[s, piece], dst_ref=dst.at[s, piece], send_sem=ssem.at[(half + s) * CUT + h],
                recv_sem=rsem.at[s * CUT + h], device_id=me.dev(y=1 - me.y), device_id_type=MESH).start()

    def back_end(self, src, dst, ssem, rsem, lsem):
        me, half = self.me, self.half
        size = src.shape[1] // CUT
        piece = pl.ds(0, size)

        @pl.when(self.busy)
        def _():
            for i in range(half):
                here = (me.c * half + i == me.z) & (me.c == me.y)

                @pl.when(jnp.logical_not(here))
                def _():
                    for h in range(CUT):
                        pltpu.make_async_remote_copy(
                            src_ref=src.at[i, piece], dst_ref=dst.at[0, piece], send_sem=ssem.at[i * CUT + h],
                            recv_sem=rsem.at[0], device_id=me.dev(c=1 - me.c), device_id_type=MESH).wait_send()

        @pl.when(self.owner)
        def _():
            for n in range(self.S * CUT):
                pltpu.make_async_remote_copy(
                    src_ref=dst.at[0, piece], dst_ref=dst.at[0, piece], send_sem=ssem.at[half * CUT + n],
                    recv_sem=rsem.at[0], device_id=me.dev(y=1 - me.y), device_id_type=MESH).wait_send()

        @pl.when(jnp.logical_not(self.owner))
        def _():
            for n in range(self.S * CUT):
                arrived(dst.at[n // CUT, pl.ds(n % CUT * size, size)], rsem.at[n], me)


def reduce_events(me, split, bufs, sends, recv, finish, parts):
    acc, rc, xd, yd, xr, yr, zr = bufs
    C, X = me.C, me.X
    half = C // 2
    n_cols = acc.shape[2]
    like = acc.at[0, 0, :, 0]
    side = me.dev(y=1 - me.y)
    base = 0
    s_d = lambda d, j: recv.at[base + (d - 1) * C + j]
    base2 = base + (X - 1) * C
    s_xr = lambda d, j: recv.at[base2 + (d - 1) * C + j]
    base3 = base2 + (X - 1) * C
    s_yr = lambda j: recv.at[base3 + j]
    s_zr = lambda j: recv.at[base3 + C + j]
    quads = ([(1 - me.y, me.x_off(d)) for d in range(1, X)] + [(1 - me.y, me.x)]
             + [(me.y, me.x_off(d)) for d in range(1, X)] + [(me.y, me.x)])

    def add(a, b):
        def body(i, carry):
            a[i] = a[i] + b[i]
            return carry
        lax.fori_loop(0, n_cols, body, 0)

    def ready(n):
        t, x = quads[n]
        if split:
            if n == 0:
                for xo in [me.x_off(d) for d in range(1, X)] + [me.x]:
                    for view, sem in parts(1 - me.c, xo):
                        arrived(view, sem, me)
            return
        for view, sem in parts(t, x):
            arrived(view, sem, me)

        def body(i, carry):
            for z in range(C):
                acc[t, x, i, z] = acc[t, x, i, z] + rc[t, x, i, z]
            return carry
        lax.fori_loop(0, n_cols, body, 0)

    by_x = range(1, C)

    def ready_corner():
        for d in range(1, X):
            ready(d - 1)

    def corner(j):
        def run():
            zj = me.z_off(-j)
            for d in range(1, X):
                t, x = quads[d - 1]
                if j in by_x:
                    sends.go(acc.at[t, x, :, zj], xd.at[d - 1, j - 1], s_d(d, j), me.dev(x=x), like)
                else:
                    sends.go(acc.at[t, x, :, zj], yd.at[d - 1, 0], s_d(d, j), side, like)
        return run

    def ready_x():
        for n in range(X, 2 * X - 1):
            ready(n)

    def over_x(j):
        def run():
            zj = me.z_off(-j)
            for d in range(1, X):
                xo = me.x_off(d)
                if j not in by_x:
                    arrived(yd.at[d - 1, 0], s_d(d, j), me)
                    add(acc.at[me.y, xo, :, zj], yd.at[d - 1, 0])
                sends.go(acc.at[me.y, xo, :, zj], xr.at[d - 1, j], s_xr(d, j), me.dev(x=xo), like)
        return run

    def over_y(j):
        def run():
            zj = me.z_off(-j)
            if j in by_x:
                for d in range(1, X):
                    arrived(xd.at[d - 1, j - 1], s_d(d, j), me)
                    add(acc.at[1 - me.y, me.x, :, zj], xd.at[d - 1, j - 1])
            sends.go(acc.at[1 - me.y, me.x, :, zj], yr.at[j], s_yr(j), side, like)
        return run

    def to_z(j):
        def run():
            t, x = me.y, me.x
            zj = me.z_off(-j)
            for d in range(1, X):
                arrived(xr.at[d - 1, j], s_xr(d, j), me)
                add(acc.at[t, x, :, zj], xr.at[d - 1, j])
            arrived(yr.at[j], s_yr(j), me)
            add(acc.at[t, x, :, zj], yr.at[j])
            if j:
                sends.go(acc.at[t, x, :, zj], zr.at[j - 1], s_zr(j - 1), me.dev(z=zj), like)
        return run

    def last():
        for j in range(1, C):
            arrived(zr.at[j - 1], s_zr(j - 1), me)
        for i in range(n_cols):
            total = acc[me.y, me.x, i, me.z].astype(jnp.float32)
            for j in range(1, C):
                total = total + zr[j - 1, i].astype(jnp.float32)
            finish(i, total)

    steps = {"c": ready_corner, "a": lambda: ready(X - 1), "b": ready_x, "o": lambda: ready(2 * X - 1), "l": last}
    for j in range(C):
        steps["d%d" % j] = corner(j)
        steps["w%d" % j] = over_x(j)
        steps["y%d" % j] = over_y(j)
        steps["z%d" % j] = to_z(j)
    return steps


def reduce_scratch(sizes, n, r, w, split):
    F, C, T = sizes
    X = F // 2
    half = C // 2
    v = lambda shape: pltpu.VMEM(shape, jnp.bfloat16)
    return [v((T, X, n, C, r, w)), v((1, 1, 1, 1, 16, 128) if split else (T, X, n, C, r, w)),
            v((X - 1, C - 1, n, r, w)), v((X - 1, 1, n, r, w)), v((X - 1, C, n, r, w)),
            v((C, n, r, w)), v((C - 1, n, r, w))]


def reduce_sems(sizes):
    F, C, T = sizes
    X = F // 2
    return 2 * (X - 1) * C + 2 * C


def reduce_count(sizes):
    F, C, T = sizes
    X = F // 2
    return 2 * (X - 1) * C + C + C - 1


def total_events(me, own, bufs, out, sends, recv):
    C, X = me.C, me.X
    acc, got = bufs
    groups = [[me.dev(c=1 - me.c)], [me.dev(x=me.x_off(d)) for d in range(1, X)],
              [me.dev(y=1 - me.y)], [me.dev(z=me.z_off(d)) for d in range(1, C)]]
    like = acc.at[0]
    bases = [sum(len(g) for g in groups[:i]) for i in range(len(groups))]

    def start(gi):
        for i, dev in enumerate(groups[gi]):
            sends.go(acc.at[gi], got.at[bases[gi] + i], recv.at[bases[gi] + i], dev, like)

    def first():
        acc[0] = own[...]
        start(0)

    steps = {"0": first}
    for gi in range(len(groups)):
        def step(gi=gi):
            total = acc[gi]
            for i in range(len(groups[gi])):
                arrived(got.at[bases[gi] + i], recv.at[bases[gi] + i], me)
                total = total + got[bases[gi] + i]
            if gi + 1 < len(groups):
                acc[gi + 1] = total
                start(gi + 1)
            else:
                out[...] = total
        steps[str(gi + 1)] = step
    return steps


def total_count(sizes):
    F, C, T = sizes
    return 1 + F // 2 - 1 + 1 + C - 1

HEAD = 64
PAIR = 2 * HEAD
SCALE = HEAD ** (-0.5)
norm_eps = 1e-12
masked_score = -1000000000.0


def nt(a, b):
    return lax.dot_general(a, b, (((1,), (1,)), ((), ())), preferred_element_type=jnp.float32)


def nn(a, b):
    return lax.dot_general(a, b, (((1,), (0,)), ((), ())), preferred_element_type=jnp.float32)


def spread_segments(seg_ref, wide):
    C, _, R = seg_ref.shape
    for i in range(C):
        for j in range(0, R, 128):
            row = jnp.broadcast_to(seg_ref[i, 0:1, j:j + 128], (128, 128))
            wide[i * R + j:i * R + j + 128, :] = row.T


def lanes_of(h, like):
    lane = lax.broadcasted_iota(jnp.int32, like.shape, like.ndim - 1)
    return jnp.where(lane // HEAD == h, like, jnp.zeros_like(like))


def two_lanes(wide):
    return jnp.concatenate([wide, wide], axis=1)


def attend_block(q, k, v_t, seg_q, seg_k):
    same = seg_k == seg_q
    outs, logs = [], []
    for h in range(2):
        s = nt(k, lanes_of(h, q) * jnp.bfloat16(SCALE))
        s = jnp.where(same, s, masked_score)
        peak = jnp.max(s, axis=0, keepdims=True)
        e = jnp.exp(s - peak)
        total = jnp.sum(e, axis=0, keepdims=True)
        o = nn(v_t, e.astype(jnp.bfloat16))
        outs.append(o[h * HEAD:(h + 1) * HEAD] * (1.0 / total))
        logs.append(peak + jnp.log(total))
    return jnp.concatenate(outs, axis=0), logs


def attend_back_block(q, k, k_t, v, do, o, lse, seg_q, seg_k):
    same = seg_k == seg_q
    prod = (do.astype(jnp.float32) * o.astype(jnp.float32)).T
    dq, dk, dv = [], None, None
    for h in range(2):
        qh = lanes_of(h, q) * jnp.bfloat16(SCALE)
        doh = lanes_of(h, do)
        s = nt(k, qh)
        p = jnp.exp(jnp.where(same, s, masked_score) - lse[h:h + 1])
        dp = nt(v, doh)
        inner = jnp.sum(prod[h * HEAD:(h + 1) * HEAD], axis=0, keepdims=True)
        ds = (p * (dp - inner)).astype(jnp.bfloat16)
        dv_h = nn(p.astype(jnp.bfloat16), doh)
        dk_h = nn(ds, qh)
        dv = dv_h if dv is None else dv + dv_h
        dk = dk_h if dk is None else dk + dk_h
        dq.append(nn(k_t, ds)[h * HEAD:(h + 1) * HEAD])
    return jnp.concatenate(dq, axis=0).T * SCALE, dk, dv

STRIP = 64


def fold(value):
    total = value[0:8]
    for i in range(8, value.shape[0], 8):
        total = total + value[i:i + 8]
    return total


def mean(value):
    return jnp.mean(value, axis=-1, keepdims=True)


def unit_of(value):
    centred = value - mean(value)
    factor = lax.rsqrt(mean(centred * centred) + norm_eps)
    return centred * factor, factor


def back_of(upstream, unit, factor, gain):
    along = upstream * gain
    return factor * (along - mean(along) - unit * mean(along * unit))


def flip(ref, out):
    rows = ref.shape[0]
    for i in range(0, rows, 128):
        out[:, i:i + 128] = ref[i:i + 128, :].astype(jnp.float32).T.astype(jnp.bfloat16)


VEC = 128


def spread_pieces(blocks, width, first, total):
    n, lanes = blocks.shape
    i = lax.broadcasted_iota(jnp.int32, (lanes, total), 0)
    col = lax.broadcasted_iota(jnp.int32, (lanes, total), 1)
    pick = jnp.where(i - first == lax.rem(col, width), 1.0, 0.0).astype(jnp.bfloat16)
    wide = nn(blocks, pick)
    dev = lax.broadcasted_iota(jnp.int32, (n, total), 0)
    col = lax.broadcasted_iota(jnp.int32, (n, total), 1)
    return jnp.sum(jnp.where(dev == col // width, wide, 0.0), axis=0, keepdims=True)


def pack(widths):
    offs, at = [], 0
    for w in widths:
        if at % VEC + w > VEC:
            at += VEC - at % VEC
        offs.append(at)
        at += w
    return offs, -(-at // VEC)


def small_widths(sizes, D, W, H):
    F, C, T = sizes
    n_dev = T * F * C
    return [T * W // n_dev, T * W // n_dev, T * H // n_dev] + [D // (F * C)] * 6


def front_part(cfg, me, sends, tok, steps, ins, outs, scratch, sems):
    sizes, S, W, H, chunk = cfg
    x_ref, cot_ref, segs_ref, wq_in, wk_in, wv_in, wo_in, up_in, dn_in = ins[:9]
    small_refs = ins[9:18]
    (q_ref, k_ref, v_ref, ah_ref, ar_ref, lse_ref, xf_ref, cf_ref, sf_ref, g1_ref, g2_ref, g3_ref,
     vec_ref, ub_ref) = outs
    zero, zseg, xv, wv, pv, sv, wide, v_t, w1_ref, w2_ref, seg_ref, rows = scratch
    r1, r2, r3, lsem, tss, trs, tls, csem = sems
    C, X, T = me.C, me.X, me.T
    R, D = xv.shape[1:]
    r = wq_in.shape[0]
    L = C * R
    f32, b16 = jnp.float32, jnp.bfloat16
    offs, n_rows = pack([ref.shape[1] for ref in small_refs])
    w1_ref[:, :W] = wq_in[...]
    w1_ref[:, W:2 * W] = wk_in[...]
    w1_ref[:, 2 * W:3 * W] = wv_in[...]
    w2_ref[:, :H] = up_in[...]
    w2_ref[:, H:] = wo_in[...]
    rows[...] = jnp.zeros_like(rows)
    for i, ref in enumerate(small_refs):
        rows[i:i + 1, :ref.shape[1]] = ref[...].astype(f32)
    block = [jnp.zeros((1, VEC), f32) for _ in range(n_rows)]
    for i, off in enumerate(offs):
        one = jnp.broadcast_to(rows[i:i + 1, :], (8, VEC))
        block[off // VEC] += (pltpu.roll(one, off % VEC, 1) if off % VEC else one)[0:1]
    pad = [jnp.zeros((r - n_rows, VEC), f32)] if r > n_rows else []
    w1_ref[:, 3 * W:] = jnp.concatenate(block + pad, axis=0).astype(b16)
    for i in range(S):
        seg_ref[i] = jnp.broadcast_to(segs_ref[i:i + 1, :].astype(f32), (8, R))
    me.greet(True)
    items = [(x_ref, xf_ref, True, tss.at[0], trs.at[0], tls.at[0]),
             (seg_ref, sf_ref, True, tss.at[1], trs.at[1], tls.at[1]),
             (cot_ref, cf_ref, False, tss.at[2], trs.at[2], tls.at[2])]
    idle = jnp.logical_not(tok.busy)
    fills = ([(zero, xf_ref.at[i]) for i in range(C)] + [(zseg, sf_ref.at[i]) for i in range(C)]
             + [(zero, cf_ref.at[i]) for i in range(C // 2)])

    @pl.when(idle)
    def _():
        zero[...] = jnp.zeros_like(zero)
        zseg[...] = jnp.zeros_like(zseg)
        for i, (a, b) in enumerate(fills):
            pltpu.make_async_copy(a, b, tls.at[3 + i]).start()

    for group, w_ref, g_ref, recv, n in (("1", w1_ref, g1_ref, r1, 0), ("2", w2_ref, g2_ref, r2, 1),
                                         ("3", dn_in, g3_ref, r3, 2)):
        for name, step in gather_events(me, w_ref, g_ref, sends, recv, lsem.at[n]).items():
            steps[group + name] = step
    half = L // 2

    def each(f, its):
        return lambda: [f(*it) for it in its]

    for name, its in (("X", items[:2]), ("C", items[2:])):
        steps[name + "o"] = each(tok.out, its)
        steps[name + "w"] = each(tok.out_done, its)
        steps[name + "e"] = each(tok.out_end, its)

    def filled():
        @pl.when(idle)
        def _():
            for i, (a, b) in enumerate(fills):
                pltpu.make_async_copy(a, b, tls.at[3 + i]).wait()
    steps["filled"] = filled

    loads = [(xf_ref, xv), (sf_ref, sv), (g1_ref.at[me.c], wv)]
    blocks = [(t, xx, cc, zz) for t in range(T) for xx in range(X) for cc in range(2) for zz in range(C)]
    if len(g1_ref.shape) == 6:
        pieces = [(g1_ref.at[at + (slice(None), pl.ds(3 * W, VEC))], pv.at[i]) for i, at in enumerate(blocks)]
    else:
        per = len(blocks) // T
        pieces = [(g1_ref.at[i // per, pl.ds(i % per * r, r), pl.ds(3 * W, VEC)], pv.at[i])
                  for i in range(len(blocks))]
    loads = [pltpu.make_async_copy(a, b, csem.at[i]) for i, (a, b) in enumerate(loads + pieces)]

    def load():
        for cp in loads:
            cp.start()
    steps["load"] = load

    def vectors():
        for cp in loads:
            cp.wait()
        blocks = jnp.concatenate([pv[:, i, :] for i in range(n_rows)], axis=1)
        n_dev = blocks.shape[0]
        qw, uw = T * W // n_dev, T * H // n_dev
        qb = spread_pieces(blocks, qw, offs[0], T * W)
        vb = spread_pieces(blocks, qw, offs[1], T * W)
        ub = spread_pieces(blocks, uw, offs[2], T * H)
        for i in range(T * H // chunk):
            ub_ref[i] = ub[:, i * chunk:(i + 1) * chunk]
        once = blocks[:n_dev // T]
        for i in range(6):
            vec_ref[i:i + 1, :] = spread_pieces(once, r, offs[3 + i], D)
        first = me.c == 0
        vec_ref[6:7, :W] = jnp.where(first, qb[:, :W], qb[:, W:])
        vec_ref[7:8, :W] = jnp.where(first, vb[:, :W], vb[:, W:])
    steps["vectors"] = vectors

    def project():
        weights = wv[...].reshape(D, wv.shape[-1])[:, :3 * W]

        def body(i, carry):
            at = pl.ds(pl.multiple_of(i * R, R), R)
            out = nn(xv[i], weights)
            q_ref[at, :] = (out[:, :W] + vec_ref[6:7, :W]).astype(b16)
            k_ref[at, :] = out[:, W:2 * W].astype(b16)
            v_ref[at, :] = (out[:, 2 * W:] + vec_ref[7:8, :W]).astype(b16)
            return carry
        lax.fori_loop(0, C, body, 0)
    steps["project"] = project

    def ready():
        spread_segments(sv, wide)
        for p in range(W // PAIR):
            v_t[p] = v_ref[:, p * PAIR:(p + 1) * PAIR].astype(f32).T.astype(b16)
    steps["ready"] = ready

    def attention(late):
        def body(it, carry):
            p, i = it // C, lax.rem(it, C)
            at = pl.ds(pl.multiple_of(i * R, R), R)
            cols = pl.ds(pl.multiple_of(p * PAIR, PAIR), PAIR)
            o, logs = attend_block(q_ref[at, cols], k_ref[:, cols], v_t[p], sv[i, 0:1, :],
                                   two_lanes(wide[...]))
            ah_ref[at, cols] = o.T.astype(b16)
            lse_ref[p, :, at] = jnp.concatenate(logs + [jnp.zeros((6, R), f32)], axis=0)
            for n, names in enumerate(late):
                if names:
                    @pl.when(it == n)
                    def _():
                        for name in names:
                            steps[name]()
            return carry
        lax.fori_loop(0, W // PAIR * C, body, 0)

    mine = pl.ds(pl.multiple_of(me.c * half, half), half)
    theirs = pl.ds(pl.multiple_of((1 - me.c) * half, half), half)
    heads = pl.ds(pl.multiple_of(me.c * W, W), W)

    def swap():
        sends.go(ah_ref.at[theirs, :], ar_ref.at[:, heads], csem.at[len(loads)], me.dev(c=1 - me.c))
        ar_ref[:, heads] = ah_ref[mine, :]
    steps["swap"] = swap
    steps["attention"] = attention

    def swapped():
        arrived(ar_ref.at[:, heads], csem.at[len(loads)], me)
    steps["swapped"] = swapped


def front_kernel(cfg, *refs):
    sizes, S, W, H, chunk = cfg
    ins, outs, scratch, (ssem, *sems) = refs[:18], refs[18:32], refs[32:44], refs[44:]
    me = Place(sizes)
    sends = Sends(ssem)
    steps = {}
    front_part(cfg, me, sends, Tokens(me, S), steps, ins, outs, scratch, sems)
    early, late, (pre, *_) = ONE_PLAN
    for name in early:
        steps[name]()
    steps["attention"](late)
    steps["swap"]()
    for name in pre[0] + pre[1] + sum(pre[2], ()) + pre[3]:
        steps[name]()
    sends.finish(me)


def front_shapes(cfg, R, D, r, rows):
    sizes, S, W, H, chunk = cfg
    F, C, T = sizes
    X = F // 2
    L = C * R
    n = T * H // chunk
    f32, b = jnp.float32, jnp.bfloat16
    dma = pltpu.SemaphoreType.DMA
    v = pltpu.VMEM
    n1, n2 = 3 * W + VEC, H + W
    full = lambda w: ((T, D, w) if rows else (T, X, 2, C, r, w), b)
    outs = ([((L, W), b)] * 4 + [((L // 2, T * W), b), ((W // PAIR, 8, L), f32)]
            + [((C, R, D), b), ((C // 2, R, D), b), ((C, 8, R), f32), full(n1), full(n2), full(H)]
            + [((8, D), f32), ((n, 1, chunk), f32)])
    scratch = [v((R, D), b), v((8, R), f32), v((C, R, D), b), v((D, n1) if rows else (X, 2, C, r, n1), b),
               v((T * F * C, r, VEC), b), v((C, 8, R), f32), v((L, 128), f32), v((W // PAIR, PAIR, L), b),
               v((r, n1), b), v((r, n2), b), v((S, 8, R), f32), v((16, VEC), f32)]
    sems = [dma((T * F * C,))] * 3 + [dma((3,)), dma((3, S + C // 2)), dma((3, C)), dma((3 + 3 * C,)),
                                      dma((5 + T * F * C,))]
    return outs, scratch, sems, 3 * gather_count(sizes) + 1


def front(cfg, x, cot, segs, weights, small):
    sizes, S, W, H, chunk = cfg
    outs, scratch, sems, count = front_shapes(cfg, x.shape[1], x.shape[2], weights[0].shape[0], False)
    return pl.pallas_call(
        functools.partial(front_kernel, cfg),
        in_specs=[ANY] * 2 + [VM] * (1 + len(weights) + len(small)),
        out_specs=[VM] * 6 + [ANY] * 6 + [VM] * 2,
        out_shape=[jax.ShapeDtypeStruct(*o) for o in outs],
        scratch_shapes=scratch + [pltpu.SemaphoreType.DMA((count,))] + sems,
        compiler_params=pltpu.CompilerParams(collective_id=0, has_side_effects=True,
                                             vmem_limit_bytes=60 * 2**20),
    )(x, cot, segs, *weights, *small)


def take(vec, index, width):
    n = vec.shape[1]
    wide = jnp.broadcast_to(vec, (8, n))
    return pltpu.roll(wide, lax.rem(n - index * width, n), 1)[0:1, :VEC]


def rest_part(cfg, me, sends, tok, steps, plan, ins, outs, scratch, sems):
    sizes, S, W, H, chunk = cfg
    q_ref, k_ref, v_ref, ah_ref, lse_ref, sf_ref, ar_ref, vec_ref, ub_ref, cf_ref, xf_ref, g1_ref, g2_ref, g3_ref = ins
    res_out, ing_out, oq_ref, oup_ref, odn_ref, oo_ref, vs_ref = outs
    (xb, cb, unit, fac, low, low_t, acc, fl, fl_t, hid, act, slope, hl, wbuf, wo, sums, gub, tmp, stage,
     doh, away_o, away_q, got_part, vec, vacc, vgot, soon, sacc, sgot) = scratch[:29]
    bf, bo, bq = scratch[29:36], scratch[36:43], scratch[43:50]
    rf, ro, rq, rv, ru, fc, fs, oc, qc, tss, trs, tls, csem, wsem = sems
    C, X, T = me.C, me.X, me.T
    R, D = xb.shape[1:]
    L = C * R
    half = L // 2
    J = H // chunk
    n = T * J
    r = away_q.shape[3]
    f32, b16 = jnp.float32, jnp.bfloat16
    n_pairs = W // PAIR
    row = lambda i: vec_ref[i:i + 1, :]
    pre_plan, mid_plan, gap_plan, att_plan, end_plan = plan
    other = me.dev(c=1 - me.c)
    mine = pl.ds(pl.multiple_of(me.c * half, half), half)
    theirs = pl.ds(pl.multiple_of((1 - me.c) * half, half), half)
    heads = pl.ds(pl.multiple_of(me.c * W, W), W)

    def which(i):
        return jnp.where(i < J, 1 - me.y, me.y), lax.rem(i, J)

    def fetch(i, slot, kinds=(0, 1)):
        t, j = which(i)
        cols = pl.ds(pl.multiple_of(j * chunk, chunk), chunk)
        return [pltpu.make_async_copy((g2_ref, g3_ref)[kind].at[t, :, cols], wbuf.at[2 * slot + kind],
                                      wsem.at[2 * slot + kind]) for kind in kinds]

    own_rows = pl.ds(me.c * (C // 2), C // 2)
    load_x = [pltpu.make_async_copy(xf_ref.at[own_rows], xb, csem.at[2])]
    load_c = [pltpu.make_async_copy(cf_ref, cb, csem.at[3])]
    load_wo = [pltpu.make_async_copy(g2_ref.at[t, :, pl.ds(H, W)], wo.at[t], csem.at[4 + t]) for t in range(T)]
    for cp in load_x:
        cp.start()
    for name in pre_plan[0]:
        steps[name]()
    for cp in load_wo + fetch(0, 0, (0,)):
        cp.start()

    def put_ff(i, total):
        j, kind = i // 2, i % 2
        (oup_ref, odn_ref)[kind][:, j * chunk:(j + 1) * chunk] = total

    def put_o(i, total):
        oo_ref[...] = total

    def put_q(i, total):
        oq_ref[...] = total

    acc_f, rc_f = bf[:2]
    acc_o, rc_o = bo[:2]
    acc_q = bq[0]

    def parts_f(t, x):
        return [(rc_f.at[t, x, pl.ds(2 * j, 2)], fc.at[(t * X + x) * J + j]) for j in range(J)]

    def parts_o(t, x):
        return [(rc_o.at[t, x], oc.at[t * X + x])]

    def parts_q(t, x):
        return [(acc_q.at[t, x], qc.at[x])]

    def deal(cols, own_to, away_to):
        rows = C * r
        for x in range(X):
            own = pl.ds(pl.multiple_of((2 * x + me.c) * rows, r), rows)
            away = pl.ds(pl.multiple_of((2 * x + 1 - me.c) * rows, r), rows)
            own_to(x, tmp[own, :cols].reshape(C, r, cols))
            away_to(x, tmp[away, :cols].reshape(C, r, cols))

    def store(ref, *index):
        def put(x, block):
            ref[tuple(x if i is None else i for i in index)] = block
        return put

    for name, group in (("f", reduce_events(me, False, bf, sends, rf, put_ff, parts_f)),
                        ("o", reduce_events(me, False, bo, sends, ro, put_o, parts_o)),
                        ("q", reduce_events(me, True, bq, sends, rq, put_q, parts_q)),
                        ("t", total_events(me, vec, (vacc, vgot), vec, sends, rv)),
                        ("u", total_events(me, soon, (sacc, sgot), soon, sends, ru))):
        for key, step in group.items():
            steps[name + key] = step
    for name, item in (("R", (xb, res_out, tss.at[0], trs.at[0], tls.at[0])),
                       ("I", (cb, ing_out, tss.at[1], trs.at[1], tls.at[1]))):
        steps[name + "o"] = lambda item=item: tok.back(*item)
        for p in range(S * CUT):
            steps[name + str(p)] = lambda item=item, p=p: tok.back_pass(p % S, p // S, *item)
        steps[name + "e"] = lambda item=item: tok.back_end(*item)

    def at_step(i, plan):
        for m, names in enumerate(plan):
            if names:
                @pl.when(i == m)
                def _():
                    for name in names:
                        steps[name]()

    def strips(body):
        per = R // STRIP

        def step(i, carry):
            at = pl.ds(pl.multiple_of(i * STRIP, STRIP), STRIP)
            body(at, (i // per, pl.ds(pl.multiple_of(lax.rem(i, per) * STRIP, STRIP), STRIP)))
            return carry
        lax.fori_loop(0, half // STRIP, step, 0)

    for cp in load_x + load_wo:
        cp.wait()
    for t in range(T):
        part = nt(ar_ref[:, t * W:(t + 1) * W], wo[t])
        acc[...] = part if t == 0 else acc[...] + part

    def first_norm(at, qat):
        u, factor = unit_of(xb[qat].astype(f32) + acc[at, :] + row(0))
        unit[at, :] = u
        fac[at, :] = jnp.broadcast_to(factor, (STRIP, 128))
        low[at, :] = (u * row(2) + row(3)).astype(b16)
        acc[at, :] = jnp.zeros((STRIP, D), f32)
    strips(first_norm)
    flip(low, low_t)

    for name in pre_plan[1]:
        steps[name]()

    def up(i, carry):
        slot = lax.rem(i, 2)
        t, j = which(i)
        for cp in fetch(i, slot, (0,)):
            cp.wait()

        @pl.when(i + 1 < n)
        def _():
            for cp in fetch(i + 1, 1 - slot, (0,)):
                cp.start()
        hid[...] = nn(low[...], wbuf[2 * slot])
        bias = ub_ref[t * J + j]
        base = i * half

        def units(at, qat):
            h = hid[at, :] + bias
            phi = 0.5 + 0.5 * lax.erf(h * (0.5 ** 0.5))
            dens = jnp.exp(-0.5 * h * h) * 0.3989422804014327
            to = pl.ds(pl.multiple_of(base + at.start, STRIP), STRIP)
            act[to, :] = (h * phi).astype(b16)
            slope[to, :] = (phi + h * dens).astype(b16)
        strips(units)
        at_step(i, pre_plan[2])
        return carry
    lax.fori_loop(0, n, up, 0)
    for name in pre_plan[3]:
        steps[name]()
    for cp in load_c + fetch(0, 0, (1,)):
        cp.start()

    def down(i, carry):
        slot = lax.rem(i, 2)
        for cp in fetch(i, slot, (1,)):
            cp.wait()

        @pl.when(i + 1 < n)
        def _():
            for cp in fetch(i + 1, 1 - slot, (1,)):
                cp.start()
        acc[...] += nt(act[pl.ds(pl.multiple_of(i * half, half), half), :], wbuf[2 * slot + 1])
        return carry
    lax.fori_loop(0, n, down, 0)
    for cp in fetch(0, 0):
        cp.start()
    for cp in load_c:
        cp.wait()

    sums[...] = jnp.zeros_like(sums)

    def second_norm(at, qat):
        u, factor = unit_of(unit[at, :] * row(2) + row(3) + acc[at, :] + row(1))
        g = cb[qat].astype(f32)
        xb[qat] = (u * row(4) + row(5)).astype(b16)
        g2 = back_of(g, u, factor, row(4))
        l2 = g2.astype(b16)
        fl[at, :] = l2
        acc[at, :] = g2
        sums[1] += fold(l2.astype(f32))
        sums[4] += fold(g * u)
        sums[5] += fold(g)
    strips(second_norm)
    flip(fl, fl_t)
    steps["Ro"]()

    def stage_copy(i, x):
        t, j = which(i)
        slot = lax.rem(i, 2)
        return pltpu.make_async_remote_copy(
            src_ref=stage.at[slot, x], dst_ref=rc_f.at[t, x, pl.ds(2 * j, 2)], send_sem=fs.at[slot * X + x],
            recv_sem=fc.at[(t * X + x) * J + j], device_id=other, device_id_type=MESH)

    def backward(i, carry):
        slot = lax.rem(i, 2)
        t, j = which(i)
        for cp in fetch(i, slot):
            cp.wait()

        @pl.when(i + 1 < n)
        def _():
            for cp in fetch(i + 1, 1 - slot):
                cp.start()
        hid[...] = nn(fl[...], wbuf[2 * slot + 1])
        base = i * half
        gub[t * J + j] = jnp.zeros_like(gub[0])

        def units(at, qat):
            to = pl.ds(pl.multiple_of(base + at.start, STRIP), STRIP)
            v = (hid[at, :] * slope[to, :].astype(f32)).astype(b16)
            hl[at, :] = v
            gub[t * J + j] += fold(v.astype(f32))
        strips(units)

        @pl.when(i >= 2)
        def _():
            for x in range(X):
                stage_copy(i, x).wait_send()
        for kind in range(2):
            if kind == 0:
                tmp[...] = nn(low_t[...], hl[...]).astype(b16)
            else:
                tmp[...] = nn(fl_t[...], act[pl.ds(pl.multiple_of(base, half), half), :]).astype(b16)
            deal(chunk, store(acc_f, t, None, 2 * j + kind), store(stage, slot, None, kind))
        for x in range(X):
            stage_copy(i, x).start()
        acc[...] += nt(hl[...], wbuf[2 * slot])
        at_step(i, mid_plan)
        return carry
    lax.fori_loop(0, n, backward, 0)

    def first_back(at, qat):
        g = acc[at, :]
        u = unit[at, :]
        g1 = back_of(g, u, fac[at, 0:1], row(2))
        acc[at, :] = g1
        l1 = g1.astype(b16)
        fl[at, :] = l1
        sums[0] += fold(l1.astype(f32))
        sums[2] += fold(g * u)
        sums[3] += fold(g)
    strips(first_back)
    hl[:, :W] = nn(fl[...], wo[1 - me.c]).astype(b16)
    sends.go(hl.at[:, pl.ds(0, W)], doh.at[mine, :], csem.at[0], other)
    doh[mine, :] = nn(fl[...], wo[me.c]).astype(b16)
    flip(fl, fl_t)
    for t in range(T):
        tmp[:, :W] = nn(fl_t[...], ar_ref[:, t * W:(t + 1) * W]).astype(b16)
        deal(W, store(acc_o, t, None, 0), store(away_o, t, None, 0))
        for x in range(X):
            sends.go(away_o.at[t, x], rc_o.at[t, x], oc.at[t * X + x], other)
    for i in (n - 2, n - 1):
        for x in range(X):
            stage_copy(i, x).wait_send()
    turn = [pltpu.make_async_copy(g1_ref.at[me.c, :, pl.ds(m * W, W)], wbuf.at[m, :, pl.ds(0, W)], wsem.at[m])
            for m in range(3)]
    for cp in turn:
        cp.start()
    for h in range(2):
        for i in range(0, half, 128):
            a, b = (h * half + i) // R, (h * half + i) % R
            unit[i:i + 128, (4 + h) * PAIR:(5 + h) * PAIR] = jnp.broadcast_to(sf_ref[a, 0:1, b:b + 128], (128, 128)).T
        for p in range(n_pairs):
            low_t[(2 * p + h) * PAIR:(2 * p + h + 1) * PAIR, :] = (
                k_ref[h * half:(h + 1) * half, p * PAIR:(p + 1) * PAIR].astype(f32).T.astype(b16))
    def tokens(h):
        return [pltpu.make_async_copy(xf_ref.at[h * (C // 2) + i], low.at[pl.ds(i * R, R), :], csem.at[2 + i])
                for i in range(C // 2)]

    def turn_tokens(h):
        def run():
            for cp in tokens(h):
                cp.wait()
            for i in range(0, half, 128):
                at = h * half + i
                act[at // chunk * D:(at // chunk + 1) * D, at % chunk:at % chunk + 128] = (
                    low[i:i + 128, :].astype(f32).T.astype(b16))
            if h == 0:
                for cp in tokens(1):
                    cp.start()
        return run
    steps["x0"] = turn_tokens(0)
    steps["x1"] = turn_tokens(1)
    for cp in tokens(0):
        cp.start()

    def projections():
        for m in range(3):
            out = None
            for h in range(L // chunk):
                term = nn(act[h * D:(h + 1) * D, :], slope[m * L + h * chunk:m * L + (h + 1) * chunk, :W])
                out = term if out is None else out + term
            tmp[:, :W] = out.astype(b16)
            cols = slice(m * W, (m + 1) * W)
            every = slice(None)
            deal(W, store(acc_q, me.c, None, 0, every, every, cols), store(away_q, None, 0, every, every, cols))
        for x in range(X):
            sends.go(away_q.at[x], acc_q.at[me.c, x], qc.at[x], other)
    steps["gq"] = projections

    def back_project(who):
        out = None
        for m in range(3):
            rows = pl.ds(pl.multiple_of(m * L + who * half, half), half)
            term = nt(slope[rows, :W], wbuf[m, :, :W])
            out = term if out is None else out + term
        return out

    def give():
        for cp in turn:
            cp.wait()
        fl[...] = back_project(1 - me.c).astype(b16)
        sends.go(fl, got_part, csem.at[1], other)
    steps["give"] = give

    def keep():
        acc[...] += back_project(me.c)
    steps["keep"] = keep

    def join():
        arrived(got_part, csem.at[1], me)
        for i in range(C // 2):
            at = slice(i * R, (i + 1) * R)
            cb[i] = (acc[at, :] + got_part[at, :].astype(f32)).astype(b16)
    steps["join"] = join
    n_late, n_soon = 2 * T * W, T * H + 6 * D

    def lay(ref, flat, count):
        flat = jnp.concatenate(flat, axis=1)
        for i in range(count // 128):
            ref[i:i + 1, :] = flat[:, i * 128:(i + 1) * 128]
        if ref.shape[0] * 128 > count:
            ref[count // 128:, :] = jnp.zeros((ref.shape[0] - count // 128, 128), f32)

    def early_sums():
        lay(soon, [jnp.sum(gub[i], axis=0, keepdims=True) for i in range(n)]
            + [jnp.sum(sums[i], axis=0, keepdims=True) for i in range(6)], n_soon)
    steps["usums"] = early_sums

    def token_sums():
        zeros = jnp.zeros((1, W), f32)
        ones = jnp.ones((8, L), b16)
        first = me.c == 0
        flat = []
        for m in (0, 2):
            v = nn(ones, slope[m * L:(m + 1) * L, :W])[0:1]
            flat += [jnp.where(first, v, zeros), jnp.where(first, zeros, v)]
        lay(vec, flat, n_late)
    steps["sums"] = token_sums

    def vectors():
        fz = (2 * me.x + me.c) * C + me.z
        tfz = me.y * (X * 2 * C) + fz
        n_dev = T * X * 2 * C
        qw, uw = T * W // n_dev, T * H // n_dev
        out = 0
        for ref, count, kinds in ((vec, n_late, [(T * W, qw, tfz)] * 2),
                                  (soon, n_soon, [(T * H, uw, tfz)] + [(D, r, fz)] * 6)):
            total = jnp.concatenate([ref[i:i + 1, :] for i in range(count // 128)], axis=1)
            at = 0
            for m, w, here in kinds:
                vs_ref[out:out + 1, :] = take(total[:, at:at + m], here, w)
                at += m
                out += 1
    steps["pieces"] = vectors
    for name in gap_plan:
        steps[name]()
    arrived(doh.at[theirs, :], csem.at[0], me)

    def attention(it, carry):
        p, i = it // C, lax.rem(it, C)
        at = pl.ds(pl.multiple_of(i * R, R), R)
        cols = pl.ds(pl.multiple_of(p * PAIR, PAIR), PAIR)
        wide = jnp.concatenate([unit[:, (4 + h) * PAIR:(5 + h) * PAIR] for h in range(2)], axis=0)
        k_t = jnp.concatenate([low_t[pl.ds(pl.multiple_of((2 * p + h) * PAIR, PAIR), PAIR), :] for h in range(2)],
                              axis=1)
        dq, dk, dv = attend_back_block(q_ref[at, cols], k_ref[:, cols], k_t, v_ref[:, cols], doh[at, cols],
                                       ah_ref[at, cols], lse_ref[p, :, at], sf_ref[i, 0:1, :], two_lanes(wide))
        slope[at, cols] = dq.astype(b16)
        lanes = [slice(m * PAIR, (m + 1) * PAIR) for m in range(4)]
        halves = [dk[:half], dk[half:], dv[:half], dv[half:]]

        @pl.when(i == 0)
        def _():
            for m in range(4):
                unit[:, lanes[m]] = halves[m]

        @pl.when(i > 0)
        def _():
            for m in range(4):
                unit[:, lanes[m]] += halves[m]

        @pl.when(i == C - 1)
        def _():
            for m in range(4):
                slope[L + m * half:L + (m + 1) * half, cols] = unit[:, lanes[m]].astype(b16)

        at_step(it, att_plan)
        return carry
    lax.fori_loop(0, n_pairs * C, attention, 0)

    for name in end_plan:
        steps[name]()


def rest_kernel(cfg, *refs):
    sizes, S, W, H, chunk = cfg
    ins, outs, scratch, (ssem, *sems) = refs[:14], refs[14:21], refs[21:71], refs[71:]
    me = Place(sizes)
    me.greet(True)
    sends = Sends(ssem)
    none = ((), (), (), ())
    rest_part(cfg, me, sends, Tokens(me, S), {}, (none,) + ONE_PLAN[2][1:], ins, outs, scratch, sems)
    sends.finish(me)


def rest_shapes(cfg, R, D, r):
    sizes, S, W, H, chunk = cfg
    F, C, T = sizes
    X = F // 2
    L = C * R
    half = L // 2
    J = H // chunk
    n = T * J
    f32, b = jnp.float32, jnp.bfloat16
    dma = pltpu.SemaphoreType.DMA
    vm = pltpu.VMEM
    steps = total_count(sizes)
    n_vec = -(-2 * T * W // 1024) * 8
    n_soon = -(-(T * H + 6 * D) // 1024) * 8
    sems = reduce_sems(sizes)
    tall = max(n * half, 3 * L, L // chunk * D)
    outs = [((S, R, D), b), ((S, R, D), b), ((r, 3 * W), f32), ((r, H), f32), ((r, H), f32), ((r, W), f32),
            ((16, VEC), f32)]
    scratch = [vm((C // 2, R, D), b), vm((C // 2, R, D), b), vm((half, D), f32), vm((half, 128), f32),
               vm((half, D), b), vm((D, half), b), vm((half, D), f32), vm((half, D), b), vm((D, half), b),
               vm((half, chunk), f32), vm((tall, chunk), b), vm((tall, chunk), b), vm((half, chunk), b),
               vm((4, D, chunk), b), vm((T, D, W), b), vm((6, 8, D), f32), vm((n, 8, chunk), f32),
               vm((D, chunk), b), vm((2, X, 2, C, r, chunk), b),
               vm((L, W), b), vm((T, X, 1, C, r, W), b), vm((X, 1, C, r, 3 * W), b), vm((half, D), b),
               vm((n_vec, 128), f32), vm((4, n_vec, 128), f32), vm((steps, n_vec, 128), f32),
               vm((n_soon, 128), f32), vm((4, n_soon, 128), f32), vm((steps, n_soon, 128), f32)]
    scratch += (reduce_scratch(sizes, 2 * J, r, chunk, False) + reduce_scratch(sizes, 1, r, W, False)
                + reduce_scratch(sizes, 1, r, 3 * W, True))
    semas = [dma((sems,)), dma((sems,)), dma((sems,)), dma((steps,)), dma((steps,)), dma((T * X * J,)),
             dma((2 * X,)), dma((T * X,)), dma((X,)), dma((2, (C // 2 + S) * CUT)), dma((2, S * CUT)), dma((2,)),
             dma((4 + T + C,)), dma((4,))]
    return outs, scratch, semas, 3 * reduce_count(sizes) + T * X + X + 2 * steps + 2


def rest(cfg, q, k, v, ah, lse, sf, ar, vec, ub, cf, xf, g1, g2, g3):
    F, C, T = cfg[0]
    _, R, D = xf.shape
    outs, scratch, sems, count = rest_shapes(cfg, R, D, D // (F * C))
    return pl.pallas_call(
        functools.partial(rest_kernel, cfg),
        in_specs=[VM] * 9 + [ANY] * 5,
        out_specs=[ANY] * 2 + [VM] * 5,
        out_shape=[jax.ShapeDtypeStruct(*o) for o in outs],
        scratch_shapes=scratch + [pltpu.SemaphoreType.DMA((count,))] + sems,
        compiler_params=pltpu.CompilerParams(collective_id=1, has_side_effects=True,
                                             vmem_limit_bytes=60 * 2**20 + 512 * 2**10),
    )(q, k, v, ah, lse, sf, ar, vec, ub, cf, xf, g1, g2, g3)


ONE_PLAN = (
    ('1a0', '2a0', '1a1', '1a2', '1a3', 'Xo', '2a1', '1x0', '1x1', '1x2', '1x3', '2x0', '2x1', '1c0', '1c1',
     '1c2', '1c3', '2a2', '1l', 'Xw', '3a0', 'filled', 'Xe', 'load', 'vectors', 'project', '2a3', 'ready'),
    ((), ('2x2',), (), (), ('3x0',), ('2x3', '2c0', '2c1', '3a1'), (), ('3a2',), ('2c2',), ('3a3',), ('2c3',
     '3x1'), ()),
    ((('Co', '3c0', '2l', 'swapped'), ('3x2',), ((), ('3x3',), (), (), ('3c1', '3c2', '3c3'), ('Cw',)), ('Ce',
     '3l')), ((), (), (), ('fc', 'fd1'), ('fd0',), ('fd3', 'fa')), ('fd2',), (('usums', 'R0', 'u0'), ('fy3',),
     ('fb', 'fw3'), ('u1', 'fo', 'fw1', 'oc'), ('fy1', 'od2', 'fw2'), ('fz3', 'fw0'), ('fy2', 'u2', 'x0'), (),
     ('fz1',), ('fy0',), ('od0',), ()), ('give', 'sums', 'keep', 'u3', 'R1', 'join', 'R2', 'Io', 'od1', 'R3',
     'R4', 'fz2', 'x1', 'gq', 'qc', 'qd0', 't0', 'qd3', 'R5', 'oa', 'oy0', 'qa', 'qb', 'qd2', 'ob', 'ow1',
     'qy2', 'qd1', 'qw3', 'qy3', 'qy1', 'qo', 't1', 'qw1', 't2', 'oy1', 'oy2', 'qz3', 'od3', 'qy0', 'qw0',
     'qz1', 'oy3', 'qw2', 'ow2', 'oo', 't3', 'u4', 'I0', 'I1', 'qz2', 'I2', 'I3', 'ow0', 'I4', 'I5', 'ow3',
     'qz0', 'oz1', 'oz0', 'oz3', 'Re', 'fz0', 'oz2', 'fl', 'Ie', 't4', 'pieces', 'ql', 'ol')),
)


def layer_kernel(cfg, *refs):
    sizes, S, W, H, chunk = cfg
    refs = list(refs)
    take_refs = lambda n: [refs.pop(0) for _ in range(n)]
    ins, moved, results = take_refs(18), take_refs(6), take_refs(7)
    kept, front_scratch, rest_scratch, ssem = take_refs(8), take_refs(12), take_refs(50), take_refs(1)[0]
    front_sems, rest_sems = take_refs(8), take_refs(14)
    me = Place(sizes)
    sends = Sends(ssem)
    tok = Tokens(me, S)
    steps = {}
    q, k, v, ah, ar, lse, vec, ub = kept
    xf, cf, sf, g1, g2, g3 = moved
    outs = [q, k, v, ah, ar, lse] + moved + [vec, ub]
    front_part(cfg, me, sends, tok, steps, ins, outs, front_scratch, front_sems)
    early, late, plan = ONE_PLAN
    for name in early:
        steps[name]()
    steps["attention"](late)
    steps["swap"]()
    rest_part(cfg, me, sends, tok, steps, plan, [q, k, v, ah, lse, front_scratch[5], ar, vec, ub, cf, xf, g1, g2, g3],
              results, rest_scratch, rest_sems)
    sends.finish(me)


def layer(cfg, x, cot, segs, weights, small):
    sizes, S, W, H, chunk = cfg
    _, R, D = x.shape
    r = weights[0].shape[0]
    front_outs, front_scratch, front_sems, n_front = front_shapes(cfg, R, D, r, True)
    outs, scratch, sems, n_rest = rest_shapes(cfg, R, D, r)
    moved = front_outs[6:12]
    kept = [pltpu.VMEM(*o) for o in front_outs[:6] + front_outs[12:]]
    return pl.pallas_call(
        functools.partial(layer_kernel, cfg),
        in_specs=[ANY] * 2 + [VM] * (1 + len(weights) + len(small)),
        out_specs=[ANY] * 6 + [ANY] * 2 + [VM] * 5,
        out_shape=[jax.ShapeDtypeStruct(*o) for o in moved + outs],
        scratch_shapes=kept + front_scratch + scratch + [pltpu.SemaphoreType.DMA((n_front + n_rest,))]
        + front_sems + sems,
        compiler_params=pltpu.CompilerParams(collective_id=0, has_side_effects=True,
                                             vmem_limit_bytes=62 * 2**20),
    )(x, cot, segs, *weights, *small)[6:]


def finish_kernel(W, res_in, ing_in, oq_in, oup_in, odn_in, oo_in, vs_in,
                  res, ing, oq, ok, ov, oo, oup, odn, *small):
    res[...] = res_in[...]
    ing[...] = ing_in[...].astype(jnp.float32)

    @pl.when(pl.program_id(0) == 0)
    def _():
        oq[...] = oq_in[:, :W]
        ok[...] = oq_in[:, W:2 * W]
        ov[...] = oq_in[:, 2 * W:]
        oup[...] = oup_in[...]
        oo[...] = oo_in[...]
        odn[...] = odn_in[...]
        for i, ref in enumerate(small):
            ref[...] = vs_in[i:i + 1, :ref.shape[1]]


def finish(cfg, widths, *arrays):
    sizes, S, W, H, chunk = cfg
    res, ing, oq = arrays[:3]
    r = oq.shape[0]
    R, D = res.shape[1:]
    f32 = jnp.float32
    token = pl.BlockSpec((1, R, D), lambda i: (i, 0, 0))
    whole = lambda shape: pl.BlockSpec(shape, lambda i: (0,) * len(shape))
    shapes = [(r, W)] * 4 + [(r, H), (r, H)] + [(1, w) for w in widths]
    return pl.pallas_call(
        functools.partial(finish_kernel, W),
        grid=(S,),
        in_specs=[token, token] + [whole(a.shape) for a in arrays[2:]],
        out_specs=[token, token] + [whole(shape) for shape in shapes],
        out_shape=[jax.ShapeDtypeStruct((S, R, D), jnp.bfloat16), jax.ShapeDtypeStruct((S, R, D), f32)]
        + [jax.ShapeDtypeStruct(shape, f32) for shape in shapes],
        compiler_params=pltpu.CompilerParams(vmem_limit_bytes=62 * 2**20),
    )(*arrays)


def chunk_of(H):
    for w in (512, 384, 256, 128):
        if H % w == 0:
            return w
    return H


def on_device(sizes, inputs, segments, cotangent, query_weight, key_weight, value_weight,
              output_weight, up_weight, down_weight, *small):
    F, C, T = sizes
    X = F // 2
    S, R, D = inputs.shape
    W = query_weight.shape[1]
    H = up_weight.shape[1]
    r = query_weight.shape[0]
    chunk = chunk_of(H)
    cfg = (sizes, S, W, H, chunk)
    weights = (query_weight, key_weight, value_weight, output_weight.T, up_weight, down_weight.T)
    widths = [v.shape[0] for v in small]
    small = [v.reshape(1, -1) for v in small]
    if r % 16 == 0:
        landed = layer(cfg, inputs, cotangent, segments, weights, small)
    else:
        q, k, v, ah, ar, lse, xf, cf, sf, g1, g2, g3, vec, ub = front(
            cfg, inputs, cotangent, segments, weights, small)
        landed = rest(cfg, q, k, v, ah, lse, sf, ar, vec, ub, cf, xf,
                      g1.reshape(T, D, -1), g2.reshape(T, D, -1), g3.reshape(T, D, -1))
    outs = finish(cfg, widths, *landed)
    return tuple(outs[:5]) + (outs[5].T, outs[6], outs[7].T) + tuple(v.reshape(-1) for v in outs[8:])


def solution(mesh):
    sizes = (mesh.shape["fsdp"], mesh.shape["ctx"], mesh.shape["tp"])
    every = ("fsdp", "ctx")
    rows, cols, one, three = P(every, "tp"), P("tp", every), P(every), P(("tp",) + every)
    token = P("fsdp", "ctx", None)
    weights = (rows, rows, rows, cols, rows, cols)
    vectors = (three, three, three) + (one,) * 6
    return jax.shard_map(
        functools.partial(on_device, sizes), mesh=mesh,
        in_specs=(token, P("fsdp", "ctx"), token) + weights + vectors,
        out_specs=(token, token) + weights + vectors, check_vma=False)
```
